32 devices in a mesh: section: 2 (over core), seq: 4 (over y, x), head: 4 (over z).
Axes of the slice: x: 2, y: 2, z: 4, core: 2. Of those that a mesh axis runs over, the one named last changes fastest.
Arguments:
- inputs: bfloat16 [2, 2048, 2048], P(None, ('seq', 'head')), may hold values from -6 to 6
- cotangent: bfloat16 [2, 2048, 2048], P(None, ('seq', 'head')), may hold values from -6 to 6
- starts: int32 [2, 2048], P(None, 'seq'), may hold values from 0 to 1, as said below
- live: int32 [2, 2048], P(None, 'seq'), may hold values from 0 to 1, as said below
- norm_gain: float32 [2, 2048], P('section'), may hold values from 0.5 to 1.5
- w_gate: bfloat16 [2, 2048, 4096], P('section', None, 'head'), may hold values from -0.125 to 0.125
- w_in: bfloat16 [2, 2048, 4096], P('section', None, 'head'), may hold values from -0.125 to 0.125
- w_bc: bfloat16 [2, 2048, 256], P('section'), may hold values from -0.125 to 0.125
- w_dt: bfloat16 [2, 2048, 64], P('section', None, 'head'), may hold values from -0.125 to 0.125
- conv_x: bfloat16 [2, 4, 4096], P('section', None, 'head'), may hold values from -3 to 3
- conv_x_bias: float32 [2, 4096], P('section', 'head'), may hold values from -3 to 3
- conv_bc: bfloat16 [2, 4, 256], P('section'), may hold values from -3 to 3
- conv_bc_bias: float32 [2, 256], P('section'), may hold values from -3 to 3
- dt_bias: float32 [2, 64], P('section', 'head'), may hold values from -7 to -1
- a_log: float32 [2, 64], P('section', 'head'), may hold values from -4.5 to 2
- skip: float32 [2, 64], P('section', 'head'), may hold values from 0.5 to 1.5
- gate_gain: float32 [2, 4096], P('section', 'head'), may hold values from 0.5 to 1.5
- w_out: bfloat16 [2, 4096, 2048], P('section', 'head'), may hold values from -0.09375 to 0.09375
Outputs:
- acts: float32 [2, 2, 2048, 2048], P('section', None, ('seq', 'head'))
- in_grads: float32 [2, 2, 2048, 2048], P('section', None, ('seq', 'head'))
- g_norm_gain: float32 [2, 2048], P('section')
- g_w_gate: float32 [2, 2048, 4096], P('section', None, 'head')
- g_w_in: float32 [2, 2048, 4096], P('section', None, 'head')
- g_w_bc: float32 [2, 2048, 256], P('section')
- g_w_dt: float32 [2, 2048, 64], P('section', None, 'head')
- g_conv_x: float32 [2, 4, 4096], P('section', None, 'head')
- g_conv_x_bias: float32 [2, 4096], P('section', 'head')
- g_conv_bc: float32 [2, 4, 256], P('section')
- g_conv_bc_bias: float32 [2, 256], P('section')
- g_dt_bias: float32 [2, 64], P('section', 'head')
- g_a_log: float32 [2, 64], P('section', 'head')
- g_skip: float32 [2, 64], P('section', 'head')
- g_gate_gain: float32 [2, 4096], P('section', 'head')
- g_w_out: float32 [2, 4096, 2048], P('section', 'head')
The draws below stay inside these ranges and needn't reach their ends.
Inputs may be any that keep to these rules, and one draw needn't show every extreme that they name: A micro-batch of even index holds three sequences in three buckets: the first begins at position 0, the first two hold 512 to 682 positions each, the third the rest; one of odd index holds one sequence in one bucket; starts is 1 exactly at each bucket's first position. In each bucket live is 1 on a leading run of half of its positions or more and 0 after it; in every micro-batch of even index one bucket is live throughout.
All inputs are finite; a program needn't handle non-finite values.
Results may differ from the reference program's by a relative error of at most 0.019.
Values may be sent and summed in bfloat16 or wider, within the bound.
A program may use at most 320 MiB of HBM per device.

```python
from functools import partial
import jax
import jax.numpy as jnp
from jax import lax

D = 2048
DI = 4096
H = 64
P_SIZE = 64
N = 128
KW = 4
SCAN_BLOCK = 256
MICRO = 2
LAYERS = 2
MB_TOK = 2048


def bucket_layout(key):
    position = jnp.arange(MB_TOK)
    base_key = jax.random.fold_in(key, 11)
    start_rows = []
    live_rows = []
    for micro_index in range(MICRO):
        micro_key = jax.random.fold_in(base_key, micro_index)
        key_len, key_full, key_one, key_first, key_second = jax.random.split(micro_key, 5)
        first = jax.random.randint(key_first, (), MB_TOK // 4, MB_TOK // 3 + 1)
        second = first + jax.random.randint(key_second, (), MB_TOK // 4, MB_TOK // 3 + 1)
        bucket_begins = jnp.stack([jnp.zeros((), first.dtype), first, second])
        bucket_ends = jnp.stack([first, second, jnp.full((), MB_TOK, first.dtype)])
        bucket_sizes = bucket_ends - bucket_begins
        bucket = (position >= first).astype(jnp.int32) + (position >= second).astype(jnp.int32)
        bucket_begin = bucket_begins[bucket]
        drawn_len = jax.random.randint(key_len, (3,), (bucket_sizes + 1) // 2, bucket_sizes + 1)
        full_pick = jax.random.randint(key_full, (), 0, 3)
        lengths = jnp.where(jnp.arange(3) == full_pick, bucket_sizes, drawn_len)
        single = jax.random.randint(key_one, (), (MB_TOK + 1) // 2, MB_TOK + 1)
        if micro_index % 2 == 0:
            start_rows.append((position == bucket_begin).astype(jnp.int32))
            live_rows.append((position - bucket_begin < lengths[bucket]).astype(jnp.int32))
        else:
            start_rows.append((position == 0).astype(jnp.int32))
            live_rows.append((position < single).astype(jnp.int32))
    return (jnp.stack(start_rows), jnp.stack(live_rows))


def draw_starts(key, part):
    return bucket_layout(key)[0]


def draw_live(key, part):
    return bucket_layout(key)[1]


def draw_a_log(key, part):
    return jax.random.uniform(key, (LAYERS, H), jnp.float32, -4.0, 2.0)


def draw_dt_bias(key, part):
    return jax.random.uniform(key, (LAYERS, H), jnp.float32, -6.0, -1.0)


def shard_levels(rng, shape, cuts, least, high):
    level, own = 1.0, jax.random.fold_in(rng, 6)
    for axis_at, parts in cuts:
        heights = jnp.exp(jax.random.uniform(jax.random.fold_in(own, axis_at), (parts,), jnp.float32, least / len(cuts), high / len(cuts)))
        level = level * jnp.repeat(heights, shape[axis_at] // parts).reshape([-1 if axis == axis_at else 1 for axis in range(len(shape))])
    return level


def scatter_about(key, shape, deviation, most, cuts=(), kind=jnp.bfloat16):
    result = jax.random.normal(key, shape, jnp.float32) * deviation
    if len(cuts) > 0:
        result = shard_levels(key, shape, cuts, -0.22, 0.18) * result
    return jnp.clip(result, min=-most, max=most).astype(kind)


def setup_inputs(seed: int = 0) -> dict:
    streams_of = jax.random.split(jax.random.key(seed), 19)
    inputs = scatter_about(streams_of[0], (MICRO, MB_TOK, D), 1.0, 6.0, ((1, 16),))
    cotangent = scatter_about(streams_of[1], (MICRO, MB_TOK, D), 1.0, 6.0, ((1, 16),))
    starts = draw_starts(jax.random.fold_in(streams_of[18], 71), 0)
    live = draw_live(jax.random.fold_in(streams_of[18], 71), 0)
    norm_gain = jnp.clip(1.0 + 0.1 * jax.random.normal(streams_of[4], (LAYERS, D), jnp.float32), 0.5, 1.5)
    w_gate = scatter_about(streams_of[5], (LAYERS, D, DI), D ** -0.5, 0.125, ((0, 2), (2, 4)))
    w_in = scatter_about(streams_of[6], (LAYERS, D, DI), D ** -0.5, 0.125, ((0, 2), (2, 4)))
    w_bc = scatter_about(streams_of[7], (LAYERS, D, 2 * N), D ** -0.5, 0.125, ((0, 2),))
    w_dt = scatter_about(streams_of[8], (LAYERS, D, H), D ** -0.5, 0.125, ((0, 2), (2, 4)))
    conv_x = scatter_about(streams_of[9], (LAYERS, KW, DI), 0.5, 3.0, ((0, 2), (2, 4)))
    conv_x_bias = scatter_about(streams_of[10], (LAYERS, DI), 0.3, 3.0, ((0, 2), (1, 4)), jnp.float32)
    conv_bc = scatter_about(streams_of[11], (LAYERS, KW, 2 * N), 0.5, 3.0, ((0, 2),))
    conv_bc_bias = scatter_about(streams_of[12], (LAYERS, 2 * N), 0.3, 3.0, ((0, 2),), jnp.float32)
    dt_bias = draw_dt_bias(jax.random.fold_in(streams_of[18], 71), 0)
    a_log = draw_a_log(jax.random.fold_in(streams_of[18], 71), 0)
    skip = jnp.clip(0.5 + 1.0 * jax.random.uniform(streams_of[15], (LAYERS, H), jnp.float32) ** shard_levels(streams_of[15], (LAYERS, H), ((0, 2), (1, 4)), -0.2, 0.2), 0.5, 1.5)
    gate_gain = jnp.clip(1.0 + 0.1 * jax.random.normal(streams_of[16], (LAYERS, DI), jnp.float32), 0.5, 1.5)
    w_out = scatter_about(streams_of[17], (LAYERS, DI, D), DI ** -0.5, 0.09375, ((0, 2), (1, 4)))
    return {"inputs": inputs, "cotangent": cotangent, "starts": starts, "live": live, "norm_gain": norm_gain, "w_gate": w_gate, "w_in": w_in, "w_bc": w_bc, "w_dt": w_dt, "conv_x": conv_x, "conv_x_bias": conv_x_bias, "conv_bc": conv_bc, "conv_bc_bias": conv_bc_bias, "dt_bias": dt_bias, "a_log": a_log, "skip": skip, "gate_gain": gate_gain, "w_out": w_out}


@jax.custom_vjp
def low(v):
    return lax.optimization_barrier(v.astype(jnp.bfloat16)).astype(jnp.float32)

@jax.custom_vjp
def low_back(v):
    return v

def low_keep(v):
    return (low(v), None)

def low_pass(kept, grad):
    return (grad,)

def back_keep(v):
    return (v, None)

def back_low(kept, grad):
    return (low(grad),)
low.defvjp(low_keep, low_pass)
low_back.defvjp(back_keep, back_low)
norm_eps = 1e-05
far_below = -1e+30
highest = lax.Precision.HIGHEST

def product(left_mat, right_mat):
    return jnp.dot(left_mat, right_mat, precision=highest)

def rms_scale(values):
    return lax.rsqrt(lax.optimization_barrier(jnp.mean(values * values, axis=-1, keepdims=True)) + norm_eps)

def causal_conv(pre_conv, start_marks, weight, conv_bias):
    tap_count = weight.shape[0]
    length = pre_conv.shape[0]
    padded = jnp.concatenate([jnp.zeros((tap_count - 1, pre_conv.shape[1]), jnp.float32), pre_conv], axis=0)
    marks_ext = jnp.concatenate([jnp.zeros((tap_count - 1,), jnp.int32), start_marks], axis=0)
    counts = jnp.cumsum(marks_ext)
    conv_sum = jnp.zeros_like(pre_conv) + conv_bias
    for tap_index in range(tap_count):
        linked = (counts[tap_count - 1:] == counts[tap_index:tap_index + length]).astype(jnp.float32)
        conv_sum = conv_sum + linked[:, None] * weight[tap_index] * padded[tap_index:tap_index + length]
    return conv_sum

def block_step(chain_state, block_item):
    x_blk, dt_blk, decay_blk, b_blk, c_blk, flag_blk = block_item
    mark_count = jnp.cumsum(flag_blk)
    cum_decay = jnp.cumsum(decay_blk, axis=0)
    arange_pos = jnp.arange(SCAN_BLOCK)
    linked = (arange_pos[:, None] >= arange_pos[None, :]) & (mark_count[:, None] == mark_count[None, :])
    spread = jnp.where(linked[:, :, None], cum_decay[:, None, :] - cum_decay[None, :, :], far_below)
    inner_prod = jnp.dot(c_blk, b_blk.T, precision=highest)
    weights = jnp.exp(spread) * inner_prod[:, :, None] * dt_blk[None, :, :]
    y_intra = jnp.einsum('ijh,jhp->ihp', weights, x_blk, precision=highest)
    carry_in = jnp.exp(cum_decay) * (mark_count == 0).astype(jnp.float32)[:, None]
    y_inter = jnp.einsum('in,hpn->ihp', c_blk, chain_state, precision=highest) * carry_in[:, :, None]
    same_end = (mark_count == mark_count[-1]).astype(jnp.float32)
    end_weight = jnp.exp(cum_decay[-1][None, :] - cum_decay) * same_end[:, None] * dt_blk
    fresh_state = jnp.einsum('jh,jhp,jn->hpn', end_weight, x_blk, b_blk, precision=highest)
    factor = jnp.exp(cum_decay[-1]) * (mark_count[-1] == 0).astype(jnp.float32)
    return (factor[:, None, None] * chain_state + fresh_state, y_intra + y_inter)

def scan_heads(inner_act, step_size, log_decay, b_mat, c_mat, start_marks):
    length = inner_act.shape[0]
    blocks = length // SCAN_BLOCK
    pieces = (inner_act.reshape(blocks, SCAN_BLOCK, H, P_SIZE), step_size.reshape(blocks, SCAN_BLOCK, H), log_decay.reshape(blocks, SCAN_BLOCK, H), b_mat.reshape(blocks, SCAN_BLOCK, N), c_mat.reshape(blocks, SCAN_BLOCK, N), start_marks.reshape(blocks, SCAN_BLOCK))
    initial = jnp.zeros((H, P_SIZE, N), jnp.float32)
    _, mixed_out = lax.scan(jax.checkpoint(block_step), initial, pieces)
    return mixed_out.reshape(length, H, P_SIZE)

def mixer_layer(stream, layer_weights, start_marks, alive_mask):
    norm_gain, w_gate, w_in, w_bc, w_dt, conv_x, conv_x_bias, conv_bc, conv_bc_bias, dt_bias, a_log, skip, gate_gain, w_out = layer_weights
    length = stream.shape[0]
    normed = low(stream * rms_scale(stream) * norm_gain)
    gate_pre = low_back(product(normed, w_gate))
    inner_pre = low_back(product(normed, w_in))
    bc_pre = product(normed, w_bc)
    dt_pre = low_back(product(normed, w_dt))
    conv_in = jnp.concatenate([inner_pre, bc_pre], axis=1)
    conv_weight = jnp.concatenate([conv_x, conv_bc], axis=1)
    conv_bias = jnp.concatenate([conv_x_bias, conv_bc_bias], axis=0)
    activated = jax.nn.silu(causal_conv(conv_in, start_marks, conv_weight, conv_bias))
    inner_act = activated[:, :DI] * alive_mask[:, None]
    b_mat = activated[:, DI:DI + N]
    c_mat = activated[:, DI + N:]
    step_size = jax.nn.softplus(dt_pre + dt_bias) * alive_mask[:, None]
    log_decay = -step_size * jnp.exp(a_log)
    mixed_out = scan_heads(inner_act, step_size, log_decay, b_mat, c_mat, start_marks)
    mixed_out = mixed_out + skip[None, :, None] * inner_act.reshape(length, H, P_SIZE)
    gated_mix = mixed_out.reshape(length, DI) * jax.nn.silu(gate_pre)
    normed_out = low(gated_mix * rms_scale(gated_mix) * gate_gain)
    branch = low_back(product(normed_out, w_out))
    return stream + branch

def stacked_layers(start_marks, alive_mask, first_stream, weights, shifts):
    stream = first_stream
    outputs = []
    for layer_index in range(LAYERS):
        layer_weights = tuple((member[layer_index] for member in weights))
        stream = mixer_layer(stream + shifts[layer_index], layer_weights, start_marks, alive_mask)
        outputs.append(stream)
    return jnp.stack(outputs)

def reference(inputs, cotangent, starts, live, norm_gain, w_gate, w_in, w_bc, w_dt, conv_x, conv_x_bias, conv_bc, conv_bc_bias, dt_bias, a_log, skip, gate_gain, w_out):
    weights = tuple((member.astype(jnp.float32) for member in (norm_gain, w_gate, w_in, w_bc, w_dt, conv_x, conv_x_bias, conv_bc, conv_bc_bias, dt_bias, a_log, skip, gate_gain, w_out)))
    acts_list = []
    grads_list = []
    grad_total = weights
    for micro_index in range(MICRO):
        first_stream = inputs[micro_index].astype(jnp.float32)
        start_marks = starts[micro_index]
        alive_mask = live[micro_index].astype(jnp.float32)
        shifts = jnp.zeros((LAYERS,) + first_stream.shape, jnp.float32)
        stacked, pull_back = jax.vjp(partial(stacked_layers, start_marks, alive_mask), first_stream, weights, shifts)
        grad_seed = jnp.concatenate([jnp.zeros((LAYERS - 1,) + first_stream.shape, jnp.float32), cotangent[micro_index].astype(jnp.float32)[None]], axis=0)
        unused_first, weight_grads, shift_grads = pull_back(grad_seed)
        acts_list.append(stacked)
        grads_list.append(shift_grads)
        if micro_index == 0:
            grad_total = weight_grads
        else:
            grad_total = tuple((former + latter for former, latter in zip(grad_total, weight_grads)))
    acts = jnp.stack(acts_list, axis=1)
    in_grads = jnp.stack(grads_list, axis=1)
    return (acts, in_grads, grad_total[0], grad_total[1], grad_total[2], grad_total[3], grad_total[4], grad_total[5], grad_total[6], grad_total[7], grad_total[8], grad_total[9], grad_total[10], grad_total[11], grad_total[12], grad_total[13])
```

```python
from functools import partial

import jax
import jax.numpy as jnp
from jax import lax
from jax.sharding import PartitionSpec as P

DI = 4096
P_SIZE = 64
N = 128
KW = 4
SCAN_BLOCK = 256


norm_eps = 1e-05
far_below = -1e30
highest = lax.Precision.HIGHEST


def shifted(value, axis, by):
    count = lax.axis_size(axis)
    pairs = [(i, i + by) for i in range(count) if 0 <= i + by < count]
    return lax.ppermute(value, axis, pairs)


def entering(value, axis, combine, identity):
    count, mine = (lax.axis_size(axis), lax.axis_index(axis))
    everything = jax.tree.map(lambda part: lax.all_gather(part, axis), value)
    before = jax.tree.map(
        lambda part, zero: jnp.broadcast_to(jnp.asarray(zero, part.dtype), part.shape),
        value,
        identity,
    )
    for k in range(count - 1):
        reached = k < mine
        new = combine(before, jax.tree.map(lambda part: part[k], everything))
        before = jax.tree.map(lambda a, b: jnp.where(reached, a, b), new, before)
    return before


def entering_2(value, axis, join, neutral):
    count = lax.axis_size(axis)
    place = lax.axis_index(axis)
    ahead = count - 1 - place
    gathered = jax.tree.map(
        lambda a, kind: lax.all_gather(a.astype(kind), axis),
        value,
        jax.tree.map(lambda a: jnp.bfloat16 if a.dtype == jnp.float32 else a.dtype, value),
    )
    state = jax.tree.map(lambda a, e: jnp.zeros_like(a) + jnp.asarray(e, a.dtype), value, neutral)
    for lap in range(count - 1):
        source = count - 1 - lap
        new = join(
            state,
            jax.tree.map(lambda a, own: a[source].astype(own.dtype), gathered, value),
        )
        active = lap < ahead
        state = jax.tree.map(lambda a, b: jnp.where(active, a, b), new, state)
    return state


def rms_scale(values):
    return lax.rsqrt(jnp.mean(values * values, axis=-1, keepdims=True) + norm_eps)


def silu_slope(values):
    logistic = jax.nn.sigmoid(values)
    return logistic * (1.0 + values * (1.0 - logistic))


def causal_conv(extended, marks_ext, weight, conv_bias):
    tap_count = weight.shape[0]
    length = extended.shape[0] - tap_count + 1
    counts = jnp.cumsum(marks_ext)
    conv_sum = jnp.zeros((length, extended.shape[1]), jnp.float32) + conv_bias
    for tap_index in range(tap_count):
        linked = (counts[tap_count - 1 :] == counts[tap_index : tap_index + length]).astype(
            jnp.float32
        )
        conv_sum = (
            conv_sum
            + linked[:, None] * weight[tap_index] * extended[tap_index : tap_index + length]
        )
    return conv_sum


def prepare(extended, dt_pre, marks_ext, alive_mask, conv_weight, conv_bias, dt_bias, a_log):
    inner_width = dt_pre.shape[1] * P_SIZE
    activated = jax.nn.silu(causal_conv(extended, marks_ext, conv_weight, conv_bias))
    inner_act = activated[:, :inner_width] * alive_mask[:, None]
    b_mat = activated[:, inner_width : inner_width + N]
    c_mat = activated[:, inner_width + N :]
    step_size = jax.nn.softplus(dt_pre + dt_bias) * alive_mask[:, None]
    log_decay = -step_size * jnp.exp(a_log)
    return (inner_act, step_size, log_decay, b_mat, c_mat)


def block_terms(inner_act, step_size, log_decay, b_mat, start_marks):
    blocks = inner_act.shape[0] // SCAN_BLOCK
    head_count = step_size.shape[1]
    x_blocks = inner_act.reshape(blocks, SCAN_BLOCK, head_count, P_SIZE)
    dt_blocks = step_size.reshape(blocks, SCAN_BLOCK, head_count)
    cum_decay = jnp.cumsum(log_decay.reshape(blocks, SCAN_BLOCK, head_count), axis=1)
    mark_count = jnp.cumsum(start_marks.reshape(blocks, SCAN_BLOCK), axis=1)
    b_blocks = b_mat.reshape(blocks, SCAN_BLOCK, N)
    last_cum = cum_decay[:, -1]
    last_mark = mark_count[:, -1]
    same_end = (mark_count == last_mark[:, None]).astype(jnp.float32)
    end_weight = jnp.exp(last_cum[:, None, :] - cum_decay) * same_end[:, :, None] * dt_blocks
    block_states = jnp.einsum(
        "cjh,cjhp,cjn->chpn", end_weight, x_blocks, b_blocks, precision=highest
    )
    block_decay = jnp.exp(last_cum) * (last_mark == 0).astype(jnp.float32)[:, None]
    return (block_decay, block_states, cum_decay, mark_count, x_blocks, dt_blocks)


def compose_blocks(block_decay, block_states, start_state):
    chain_state = start_state
    incoming = []
    for block_index in range(block_decay.shape[0]):
        incoming.append(chain_state)
        chain_state = (
            block_decay[block_index][:, None, None] * chain_state + block_states[block_index]
        )
    return (chain_state, jnp.stack(incoming))


def block_output(block_parts, b_mat, c_mat, skip, incoming):
    block_decay, block_states, cum_decay, mark_count, x_blocks, dt_blocks = block_parts
    blocks = cum_decay.shape[0]
    head_count = cum_decay.shape[2]
    b_blocks = b_mat.reshape(blocks, SCAN_BLOCK, N)
    c_blocks = c_mat.reshape(blocks, SCAN_BLOCK, N)
    inner_prod = jnp.einsum("cin,cjn->cij", c_blocks, b_blocks, precision=highest)
    arange_pos = jnp.arange(SCAN_BLOCK)
    linked = (arange_pos[:, None] >= arange_pos[None, :])[None] & (
        mark_count[:, :, None] == mark_count[:, None, :]
    )
    spread = jnp.where(
        linked[..., None], cum_decay[:, :, None, :] - cum_decay[:, None, :, :], far_below
    )
    weights = jnp.exp(spread) * inner_prod[..., None] * dt_blocks[:, None, :, :]
    y_intra = jnp.einsum("cijh,cjhp->cihp", weights, x_blocks, precision=highest)
    carry_in = jnp.exp(cum_decay) * (mark_count == 0).astype(jnp.float32)[:, :, None]
    y_inter = (
        jnp.einsum("cin,chpn->cihp", c_blocks, incoming, precision=highest) * carry_in[..., None]
    )
    mixed_out = y_intra + y_inter + skip[None, None, :, None] * x_blocks
    return mixed_out.reshape(blocks * SCAN_BLOCK, head_count * P_SIZE)


def local_front(marks_ext, alive_mask, extended, dt_pre, conv_weight, conv_bias, dt_bias, a_log):
    inner_act, step_size, log_decay, b_mat, c_mat = prepare(
        extended, dt_pre, marks_ext, alive_mask, conv_weight, conv_bias, dt_bias, a_log
    )
    block_parts = block_terms(inner_act, step_size, log_decay, b_mat, marks_ext[KW - 1 :])
    zero_state = jnp.zeros(block_parts[1].shape[1:], jnp.float32)
    total_state, _ = compose_blocks(block_parts[0], block_parts[1], zero_state)
    total_decay = jnp.prod(block_parts[0], axis=0)
    return (block_parts, b_mat, c_mat, total_decay, total_state)


def local_rear(block_parts, b_mat, c_mat, skip, start_state):
    _, incoming = compose_blocks(block_parts[0], block_parts[1], start_state)
    return block_output(block_parts, b_mat, c_mat, skip, incoming)


def local_pass(
    marks_ext,
    alive_mask,
    extended,
    dt_pre,
    conv_weight,
    conv_bias,
    dt_bias,
    a_log,
    skip,
    start_state,
):
    block_parts, b_mat, c_mat, total_decay, total_state = local_front(
        marks_ext, alive_mask, extended, dt_pre, conv_weight, conv_bias, dt_bias, a_log
    )
    return (local_rear(block_parts, b_mat, c_mat, skip, start_state), total_decay, total_state)


def chain_combine(earlier, later):
    return (earlier[0] * later[0], later[0][:, None, None] * earlier[1] + later[1])


def extend(pre_conv, start_marks, edge_rows, edge_marks):
    extended = jnp.concatenate([edge_rows, pre_conv], axis=0)
    marks_ext = jnp.concatenate([edge_marks.astype(jnp.int32), start_marks], axis=0)
    return (extended, marks_ext)


def mixer_forward(stream, start_marks, alive_mask, layer_weights):
    (
        norm_gain,
        w_main,
        w_low,
        w_bc,
        conv_weight,
        conv_bias,
        dt_bias,
        a_log,
        skip,
        gate_gain,
        w_out,
    ) = layer_weights
    inner_width = w_out.shape[0]
    normed = (stream * rms_scale(stream) * norm_gain).astype(jnp.bfloat16)
    gathered = lax.all_gather(normed, "head", axis=0, tiled=True)
    projected = jnp.dot(gathered, w_main, preferred_element_type=jnp.float32)
    gate_pre = projected[:, :inner_width]
    pre_conv = projected[:, inner_width : 2 * inner_width + 2 * N]
    dt_pre = projected[:, 2 * inner_width + 2 * N :]
    marks_float = start_marks.astype(jnp.float32)
    tail_from = pre_conv.shape[0] - KW + 1
    edge_parts = shifted((pre_conv[tail_from:], marks_float[tail_from:]), "seq", 1)
    extended, marks_ext = extend(pre_conv, start_marks, edge_parts[0], edge_parts[1])
    front_fn = partial(local_front, marks_ext, alive_mask)
    front_out, front_pull = jax.vjp(
        front_fn, extended, dt_pre, conv_weight, conv_bias, dt_bias, a_log
    )
    block_parts, b_mat, c_mat, total_decay, total_state = front_out
    neutral = (jnp.ones_like(total_decay), jnp.zeros_like(total_state))
    prefix = entering((total_decay, total_state), "seq", chain_combine, neutral)
    start_state = prefix[1]
    mixed_out, rear_pull = jax.vjp(local_rear, block_parts, b_mat, c_mat, skip, start_state)
    silu_gate = jax.nn.silu(gate_pre)
    gated_mix = mixed_out * silu_gate
    square_total = lax.psum(jnp.sum(gated_mix * gated_mix, axis=-1), "head")
    scale_out = lax.rsqrt(square_total / DI + norm_eps)
    normed_out = (gated_mix * scale_out[:, None] * gate_gain).astype(jnp.bfloat16)
    branch = lax.psum_scatter(
        jnp.dot(normed_out, w_out, preferred_element_type=jnp.float32),
        "head",
        scatter_dimension=0,
        tiled=True,
    )
    saved = (
        stream,
        gathered,
        gate_pre,
        mixed_out,
        silu_gate,
        gated_mix,
        scale_out,
        normed_out,
        total_decay,
        start_state,
        front_pull,
        rear_pull,
    )
    return stream + branch, saved


def mixer_backward(grad_next, layer_weights, saved):
    (
        norm_gain,
        w_main,
        w_low,
        w_bc,
        conv_weight,
        conv_bias,
        dt_bias,
        a_log,
        skip,
        gate_gain,
        w_out,
    ) = layer_weights
    (
        stream,
        gathered,
        gate_pre,
        mixed_out,
        silu_gate,
        gated_mix,
        scale_out,
        normed_out,
        total_decay,
        start_state,
        front_pull,
        rear_pull,
    ) = saved
    inner_width = w_out.shape[0]
    grad_branch = grad_next.astype(jnp.bfloat16)
    shard_rows = lax.all_gather(grad_branch, "head", axis=0, tiled=True)
    g_w_out = lax.dot_general(
        normed_out, shard_rows, (((0,), (0,)), ((), ())), preferred_element_type=jnp.float32
    )
    grad_normed = lax.dot_general(
        shard_rows, w_out, (((1,), (1,)), ((), ())), preferred_element_type=jnp.float32
    )
    weighted = grad_normed * gate_gain
    g_gate_gain = jnp.sum(grad_normed * gated_mix * scale_out[:, None], axis=0)
    cross_sum = lax.psum(jnp.sum(weighted * gated_mix, axis=-1), "head")
    grad_gated = (
        scale_out[:, None] * weighted - gated_mix * (scale_out**3 * cross_sum / DI)[:, None]
    )
    grad_mixed = grad_gated * silu_gate
    grad_gate = (grad_gated * mixed_out * silu_slope(gate_pre)).astype(jnp.bfloat16)
    g_parts, g_b_mat, g_c_mat, g_skip, g_start = rear_pull(grad_mixed)
    neutral = (jnp.ones_like(total_decay), jnp.zeros_like(g_start))
    suffix = entering_2((total_decay, g_start), "seq", chain_combine, neutral)
    after_state = suffix[1]
    grad_decay = jnp.sum(after_state * start_state, axis=(1, 2))
    grad_ext, grad_dt_pre, g_conv_w, g_conv_b, g_dt_bias, g_a_log = front_pull(
        (g_parts, g_b_mat, g_c_mat, grad_decay, after_state)
    )
    returned = shifted(grad_ext[: KW - 1], "seq", -1)
    grad_pre = grad_ext[KW - 1 :]
    tail_from = grad_pre.shape[0] - KW + 1
    grad_pre = jnp.concatenate([grad_pre[:tail_from], grad_pre[tail_from:] + returned], axis=0)
    grad_inner = grad_pre[:, :inner_width].astype(jnp.bfloat16)
    grad_bc = grad_pre[:, inner_width:]
    grad_low = jnp.concatenate([grad_gate, grad_inner, grad_dt_pre.astype(jnp.bfloat16)], axis=1)
    w_bc_float = w_bc.astype(jnp.float32)
    g_low = lax.dot_general(
        gathered, grad_low, (((0,), (0,)), ((), ())), preferred_element_type=jnp.float32
    )
    g_w_bc = lax.dot_general(
        gathered.astype(jnp.float32),
        grad_bc,
        (((0,), (0,)), ((), ())),
        precision=highest,
        preferred_element_type=jnp.float32,
    )
    main_term = lax.dot_general(
        grad_low, w_low, (((1,), (1,)), ((), ())), preferred_element_type=jnp.float32
    )
    side_term = lax.dot_general(
        grad_bc,
        w_bc_float,
        (((1,), (1,)), ((), ())),
        precision=highest,
        preferred_element_type=jnp.float32,
    )
    grad_normed_in = lax.psum_scatter(
        (main_term + side_term).astype(jnp.bfloat16), "head", scatter_dimension=0, tiled=True
    ).astype(jnp.float32)
    scale_in = rms_scale(stream)
    g_norm_gain = jnp.sum(grad_normed_in * stream * scale_in, axis=0)
    weighted_in = grad_normed_in * norm_gain
    grad_stream = (
        grad_next
        + scale_in * weighted_in
        - stream * scale_in**3 * jnp.mean(weighted_in * stream, axis=-1, keepdims=True)
    )
    head_part = (
        g_low[:, :inner_width],
        g_low[:, inner_width : 2 * inner_width],
        g_low[:, 2 * inner_width :],
        g_w_out,
        g_conv_w[:, :inner_width],
        g_conv_b[:inner_width],
        g_dt_bias,
        g_a_log,
        g_skip,
        g_gate_gain,
    )
    shared_part = (g_norm_gain, g_w_bc, g_conv_w[:, inner_width:], g_conv_b[inner_width:])
    return (grad_stream, head_part, shared_part)


def reduce_grads(head_part, shared_part):
    head_sum = tuple(
        lax.psum(member.astype(jnp.bfloat16), "seq").astype(jnp.float32) for member in head_part
    )
    shared_sum = lax.psum(tuple(shared_part), ("seq", "head"))
    return (head_sum, tuple(shared_sum))


def store_slot(buffer, value, slot_index, is_valid):
    current = lax.dynamic_index_in_dim(buffer, slot_index, 0, False)
    return lax.dynamic_update_index_in_dim(
        buffer, jnp.where(is_valid, value, current), slot_index, 0
    )


def on_device(
    inputs,
    cotangent,
    starts,
    live,
    norm_gain,
    w_gate,
    w_in,
    w_bc,
    w_dt,
    conv_x,
    conv_x_bias,
    conv_bc,
    conv_bc_bias,
    dt_bias,
    a_log,
    skip,
    gate_gain,
    w_out,
):
    section_count = lax.axis_size("section")
    section_index = lax.axis_index("section")
    micro_count = inputs.shape[0]
    tick_count = micro_count + section_count - 1
    w_main = jnp.concatenate([w_gate[0], w_in[0], w_bc[0], w_dt[0]], axis=1)
    w_low = jnp.concatenate([w_gate[0], w_in[0], w_dt[0]], axis=1)
    conv_weight = jnp.concatenate([conv_x[0], conv_bc[0]], axis=1).astype(jnp.float32)
    conv_bias = jnp.concatenate([conv_x_bias[0], conv_bc_bias[0]], axis=0)
    layer_weights = (
        norm_gain[0],
        w_main,
        w_low,
        w_bc[0],
        conv_weight,
        conv_bias,
        dt_bias[0],
        a_log[0],
        skip[0],
        gate_gain[0],
        w_out[0],
    )
    row_shape = inputs.shape[1:]
    outputs_all = jnp.zeros((micro_count,) + row_shape, jnp.float32)
    arrived = jnp.zeros(row_shape, jnp.float32)
    ticks = []
    for tick_index in range(tick_count):
        slot_index = tick_index - section_index
        is_valid = (slot_index >= 0) & (slot_index < micro_count)
        clipped = jnp.clip(slot_index, 0, micro_count - 1)
        fresh_rows = lax.dynamic_index_in_dim(inputs, clipped, 0, False).astype(jnp.float32)
        stream = jnp.where(section_index == 0, fresh_rows, arrived)
        start_marks = lax.dynamic_index_in_dim(starts, clipped, 0, False)
        alive_mask = lax.dynamic_index_in_dim(live, clipped, 0, False).astype(jnp.float32)
        result, saved = mixer_forward(stream, start_marks, alive_mask, layer_weights)
        outputs_all = store_slot(outputs_all, result, clipped, is_valid)
        ticks.append((clipped, is_valid, saved))
        if tick_index + 1 < tick_count:
            arrived = shifted(result, "section", 1)
    back_arrived = jnp.zeros(row_shape, jnp.float32)
    input_grads = jnp.zeros((micro_count,) + row_shape, jnp.float32)
    head_total = ()
    shared_total = ()
    for tick_index in range(tick_count):
        clipped, is_valid, saved = ticks[tick_count - 1 - tick_index]
        outer_grad = lax.dynamic_index_in_dim(cotangent, clipped, 0, False).astype(jnp.float32)
        grad_next = jnp.where(section_index == section_count - 1, outer_grad, back_arrived)
        grad_stream, head_part, shared_part = mixer_backward(grad_next, layer_weights, saved)
        mask_value = is_valid.astype(jnp.float32)
        head_part = tuple((member * mask_value for member in head_part))
        shared_part = tuple((member * mask_value for member in shared_part))
        if tick_index == 0:
            head_total = head_part
            shared_total = shared_part
        else:
            head_total = tuple((former + latter for former, latter in zip(head_total, head_part)))
            shared_total = tuple(
                (former + latter for former, latter in zip(shared_total, shared_part))
            )
        input_grads = store_slot(input_grads, grad_stream, clipped, is_valid)
        if tick_index + 1 < tick_count:
            back_arrived = shifted(grad_stream.astype(jnp.bfloat16), "section", -1).astype(
                grad_stream.dtype
            )
    head_total, shared_total = reduce_grads(head_total, shared_total)
    return (
        outputs_all[None],
        input_grads[None],
        shared_total[0][None],
        head_total[0][None],
        head_total[1][None],
        shared_total[1][None],
        head_total[2][None],
        head_total[4][None],
        head_total[5][None],
        shared_total[2][None],
        shared_total[3][None],
        head_total[6][None],
        head_total[7][None],
        head_total[8][None],
        head_total[9][None],
        head_total[3][None],
    )


def solution(mesh):
    return jax.shard_map(
        on_device,
        mesh=mesh,
        in_specs=(
            P(None, ("seq", "head"), None),
            P(None, ("seq", "head"), None),
            P(None, "seq"),
            P(None, "seq"),
            P("section", None),
            P("section", None, "head"),
            P("section", None, "head"),
            P("section", None, None),
            P("section", None, "head"),
            P("section", None, "head"),
            P("section", "head"),
            P("section", None, None),
            P("section", None),
            P("section", "head"),
            P("section", "head"),
            P("section", "head"),
            P("section", "head"),
            P("section", "head", None),
        ),
        out_specs=(
            P("section", None, ("seq", "head"), None),
            P("section", None, ("seq", "head"), None),
            P("section", None),
            P("section", None, "head"),
            P("section", None, "head"),
            P("section", None, None),
            P("section", None, "head"),
            P("section", None, "head"),
            P("section", "head"),
            P("section", None, None),
            P("section", None),
            P("section", "head"),
            P("section", "head"),
            P("section", "head"),
            P("section", "head"),
            P("section", "head", None),
        ),
        check_vma=False,
    )
```

```python
from functools import partial

import jax
import jax.numpy as jnp
from jax import lax
from jax.sharding import PartitionSpec as P

DI = 4096
P_SIZE = 64
N = 128
KW = 4
SCAN_BLOCK = 256


norm_eps = 1e-05
far_below = -1e30
highest = lax.Precision.HIGHEST


def shifted(value, axis, by):
    count = lax.axis_size(axis)
    pairs = [(i, i + by) for i in range(count) if 0 <= i + by < count]
    return lax.ppermute(value, axis, pairs)


def entering(value, axis, combine, identity):
    count, mine = (lax.axis_size(axis), lax.axis_index(axis))
    everything = jax.tree.map(lambda part: lax.all_gather(part, axis), value)
    before = jax.tree.map(
        lambda part, zero: jnp.broadcast_to(jnp.asarray(zero, part.dtype), part.shape),
        value,
        identity,
    )
    for k in range(count - 1):
        reached = k < mine
        new = combine(before, jax.tree.map(lambda part: part[k], everything))
        before = jax.tree.map(lambda a, b: jnp.where(reached, a, b), new, before)
    return before


def entering_2(value, axis, join, neutral):
    count = lax.axis_size(axis)
    place = lax.axis_index(axis)
    ahead = count - 1 - place
    gathered = jax.tree.map(
        lambda a, kind: lax.all_gather(a.astype(kind), axis),
        value,
        jax.tree.map(lambda a: jnp.bfloat16 if a.dtype == jnp.float32 else a.dtype, value),
    )
    state = jax.tree.map(lambda a, e: jnp.zeros_like(a) + jnp.asarray(e, a.dtype), value, neutral)
    for lap in range(count - 1):
        source = count - 1 - lap
        new = join(
            state,
            jax.tree.map(lambda a, own: a[source].astype(own.dtype), gathered, value),
        )
        active = lap < ahead
        state = jax.tree.map(lambda a, b: jnp.where(active, a, b), new, state)
    return state


def rms_scale(values):
    return lax.rsqrt(jnp.mean(values * values, axis=-1, keepdims=True) + norm_eps)


def silu_slope(values):
    logistic = jax.nn.sigmoid(values)
    return logistic * (1.0 + values * (1.0 - logistic))


def causal_conv(extended, marks_ext, weight, conv_bias):
    tap_count = weight.shape[0]
    length = extended.shape[0] - tap_count + 1
    counts = jnp.cumsum(marks_ext)
    conv_sum = jnp.zeros((length, extended.shape[1]), jnp.float32) + conv_bias
    for tap_index in range(tap_count):
        linked = (counts[tap_count - 1 :] == counts[tap_index : tap_index + length]).astype(
            jnp.float32
        )
        conv_sum = (
            conv_sum
            + linked[:, None] * weight[tap_index] * extended[tap_index : tap_index + length]
        )
    return conv_sum


def prepare(extended, dt_pre, marks_ext, alive_mask, conv_weight, conv_bias, dt_bias, a_log):
    inner_width = dt_pre.shape[1] * P_SIZE
    activated = jax.nn.silu(causal_conv(extended, marks_ext, conv_weight, conv_bias))
    inner_act = activated[:, :inner_width] * alive_mask[:, None]
    b_mat = activated[:, inner_width : inner_width + N]
    c_mat = activated[:, inner_width + N :]
    step_size = jax.nn.softplus(dt_pre + dt_bias) * alive_mask[:, None]
    log_decay = -step_size * jnp.exp(a_log)
    return (inner_act, step_size, log_decay, b_mat, c_mat)


def block_terms(inner_act, step_size, log_decay, b_mat, start_marks):
    blocks = inner_act.shape[0] // SCAN_BLOCK
    head_count = step_size.shape[1]
    x_blocks = inner_act.reshape(blocks, SCAN_BLOCK, head_count, P_SIZE)
    dt_blocks = step_size.reshape(blocks, SCAN_BLOCK, head_count)
    cum_decay = jnp.cumsum(log_decay.reshape(blocks, SCAN_BLOCK, head_count), axis=1)
    mark_count = jnp.cumsum(start_marks.reshape(blocks, SCAN_BLOCK), axis=1)
    b_blocks = b_mat.reshape(blocks, SCAN_BLOCK, N)
    last_cum = cum_decay[:, -1]
    last_mark = mark_count[:, -1]
    same_end = (mark_count == last_mark[:, None]).astype(jnp.float32)
    end_weight = jnp.exp(last_cum[:, None, :] - cum_decay) * same_end[:, :, None] * dt_blocks
    block_states = jnp.einsum(
        "cjh,cjhp,cjn->chpn", end_weight, x_blocks, b_blocks, precision=highest
    )
    block_decay = jnp.exp(last_cum) * (last_mark == 0).astype(jnp.float32)[:, None]
    return (block_decay, block_states, cum_decay, mark_count, x_blocks, dt_blocks)


def compose_blocks(block_decay, block_states, start_state):
    chain_state = start_state
    incoming = []
    for block_index in range(block_decay.shape[0]):
        incoming.append(chain_state)
        chain_state = (
            block_decay[block_index][:, None, None] * chain_state + block_states[block_index]
        )
    return (chain_state, jnp.stack(incoming))


def block_output(block_parts, b_mat, c_mat, skip, incoming):
    block_decay, block_states, cum_decay, mark_count, x_blocks, dt_blocks = block_parts
    blocks = cum_decay.shape[0]
    head_count = cum_decay.shape[2]
    b_blocks = b_mat.reshape(blocks, SCAN_BLOCK, N)
    c_blocks = c_mat.reshape(blocks, SCAN_BLOCK, N)
    inner_prod = jnp.einsum("cin,cjn->cij", c_blocks, b_blocks, precision=highest)
    arange_pos = jnp.arange(SCAN_BLOCK)
    linked = (arange_pos[:, None] >= arange_pos[None, :])[None] & (
        mark_count[:, :, None] == mark_count[:, None, :]
    )
    spread = jnp.where(
        linked[..., None], cum_decay[:, :, None, :] - cum_decay[:, None, :, :], far_below
    )
    weights = jnp.exp(spread) * inner_prod[..., None] * dt_blocks[:, None, :, :]
    y_intra = jnp.einsum("cijh,cjhp->cihp", weights, x_blocks, precision=highest)
    carry_in = jnp.exp(cum_decay) * (mark_count == 0).astype(jnp.float32)[:, :, None]
    y_inter = (
        jnp.einsum("cin,chpn->cihp", c_blocks, incoming, precision=highest) * carry_in[..., None]
    )
    mixed_out = y_intra + y_inter + skip[None, None, :, None] * x_blocks
    return mixed_out.reshape(blocks * SCAN_BLOCK, head_count * P_SIZE)


def local_front(marks_ext, alive_mask, extended, dt_pre, conv_weight, conv_bias, dt_bias, a_log):
    inner_act, step_size, log_decay, b_mat, c_mat = prepare(
        extended, dt_pre, marks_ext, alive_mask, conv_weight, conv_bias, dt_bias, a_log
    )
    block_parts = block_terms(inner_act, step_size, log_decay, b_mat, marks_ext[KW - 1 :])
    zero_state = jnp.zeros(block_parts[1].shape[1:], jnp.float32)
    total_state, _ = compose_blocks(block_parts[0], block_parts[1], zero_state)
    total_decay = jnp.prod(block_parts[0], axis=0)
    return (block_parts, b_mat, c_mat, total_decay, total_state)


def local_rear(block_parts, b_mat, c_mat, skip, start_state):
    _, incoming = compose_blocks(block_parts[0], block_parts[1], start_state)
    return block_output(block_parts, b_mat, c_mat, skip, incoming)


def local_pass(
    marks_ext,
    alive_mask,
    extended,
    dt_pre,
    conv_weight,
    conv_bias,
    dt_bias,
    a_log,
    skip,
    start_state,
):
    block_parts, b_mat, c_mat, total_decay, total_state = local_front(
        marks_ext, alive_mask, extended, dt_pre, conv_weight, conv_bias, dt_bias, a_log
    )
    return (local_rear(block_parts, b_mat, c_mat, skip, start_state), total_decay, total_state)


def chain_combine(earlier, later):
    return (earlier[0] * later[0], later[0][:, None, None] * earlier[1] + later[1])


def extend(pre_conv, start_marks, edge_rows, edge_marks):
    extended = jnp.concatenate([edge_rows, pre_conv], axis=0)
    marks_ext = jnp.concatenate([edge_marks.astype(jnp.int32), start_marks], axis=0)
    return (extended, marks_ext)


def mixer_forward(stream, start_marks, alive_mask, layer_weights):
    (
        norm_gain,
        w_main,
        w_low,
        w_bc,
        conv_weight,
        conv_bias,
        dt_bias,
        a_log,
        skip,
        gate_gain,
        w_out,
    ) = layer_weights
    inner_width = w_out.shape[0]
    normed = (stream * rms_scale(stream) * norm_gain).astype(jnp.bfloat16)
    gathered = lax.all_gather(normed, "head", axis=0, tiled=True)
    projected = jnp.dot(gathered, w_main, preferred_element_type=jnp.float32)
    gate_pre = projected[:, :inner_width]
    pre_conv = projected[:, inner_width : 2 * inner_width + 2 * N]
    dt_pre = projected[:, 2 * inner_width + 2 * N :]
    marks_float = start_marks.astype(jnp.float32)
    tail_from = pre_conv.shape[0] - KW + 1
    edge_parts = shifted((pre_conv[tail_from:], marks_float[tail_from:]), "seq", 1)
    extended, marks_ext = extend(pre_conv, start_marks, edge_parts[0], edge_parts[1])
    front_fn = partial(local_front, marks_ext, alive_mask)
    front_out, front_pull = jax.vjp(
        front_fn, extended, dt_pre, conv_weight, conv_bias, dt_bias, a_log
    )
    block_parts, b_mat, c_mat, total_decay, total_state = front_out
    neutral = (jnp.ones_like(total_decay), jnp.zeros_like(total_state))
    prefix = entering((total_decay, total_state), "seq", chain_combine, neutral)
    start_state = prefix[1]
    mixed_out, rear_pull = jax.vjp(local_rear, block_parts, b_mat, c_mat, skip, start_state)
    silu_gate = jax.nn.silu(gate_pre)
    gated_mix = mixed_out * silu_gate
    square_total = lax.psum(jnp.sum(gated_mix * gated_mix, axis=-1), "head")
    scale_out = lax.rsqrt(square_total / DI + norm_eps)
    normed_out = (gated_mix * scale_out[:, None] * gate_gain).astype(jnp.bfloat16)
    branch = lax.psum_scatter(
        jnp.dot(normed_out, w_out, preferred_element_type=jnp.float32).astype(jnp.bfloat16),
        "head",
        scatter_dimension=0,
        tiled=True,
    ).astype(jnp.float32)
    saved = (
        stream,
        gathered,
        gate_pre,
        mixed_out,
        silu_gate,
        gated_mix,
        scale_out,
        normed_out,
        total_decay,
        start_state,
        front_pull,
        rear_pull,
    )
    return stream + branch, saved


def mixer_backward(grad_next, layer_weights, saved, mask_value):
    (
        norm_gain,
        w_main,
        w_low,
        w_bc,
        conv_weight,
        conv_bias,
        dt_bias,
        a_log,
        skip,
        gate_gain,
        w_out,
    ) = layer_weights
    (
        stream,
        gathered,
        gate_pre,
        mixed_out,
        silu_gate,
        gated_mix,
        scale_out,
        normed_out,
        total_decay,
        start_state,
        front_pull,
        rear_pull,
    ) = saved
    inner_width = w_out.shape[0]
    grad_branch = grad_next.astype(jnp.bfloat16)
    shard_rows = lax.all_gather(grad_branch, "head", axis=0, tiled=True)
    g_w_out = lax.dot_general(
        normed_out, shard_rows, (((0,), (0,)), ((), ())), preferred_element_type=jnp.float32
    ) * mask_value
    grad_normed = lax.dot_general(
        shard_rows, w_out, (((1,), (1,)), ((), ())), preferred_element_type=jnp.float32
    )
    weighted = grad_normed * gate_gain
    g_gate_gain = jnp.sum(grad_normed * gated_mix * scale_out[:, None], axis=0)
    cross_sum = lax.psum(jnp.sum(weighted * gated_mix, axis=-1), "head")
    grad_gated = (
        scale_out[:, None] * weighted - gated_mix * (scale_out**3 * cross_sum / DI)[:, None]
    )
    grad_mixed = grad_gated * silu_gate
    grad_gate = (grad_gated * mixed_out * silu_slope(gate_pre)).astype(jnp.bfloat16)
    g_parts, g_b_mat, g_c_mat, g_skip, g_start = rear_pull(grad_mixed)
    neutral = (jnp.ones_like(total_decay), jnp.zeros_like(g_start))
    suffix = entering_2((total_decay, g_start), "seq", chain_combine, neutral)
    after_state = suffix[1]
    grad_decay = jnp.sum(after_state * start_state, axis=(1, 2))
    grad_ext, grad_dt_pre, g_conv_w, g_conv_b, g_dt_bias, g_a_log = front_pull(
        (g_parts, g_b_mat, g_c_mat, grad_decay, after_state)
    )
    returned = shifted(grad_ext[: KW - 1], "seq", -1)
    grad_pre = grad_ext[KW - 1 :]
    tail_from = grad_pre.shape[0] - KW + 1
    grad_pre = jnp.concatenate([grad_pre[:tail_from], grad_pre[tail_from:] + returned], axis=0)
    grad_inner = grad_pre[:, :inner_width].astype(jnp.bfloat16)
    grad_bc = grad_pre[:, inner_width:]
    grad_low = jnp.concatenate([grad_gate, grad_inner, grad_dt_pre.astype(jnp.bfloat16)], axis=1)
    w_bc_float = w_bc.astype(jnp.float32)
    g_low = lax.dot_general(
        gathered, grad_low, (((0,), (0,)), ((), ())), preferred_element_type=jnp.float32
    )
    g_w_bc = lax.dot_general(
        gathered.astype(jnp.float32),
        grad_bc,
        (((0,), (0,)), ((), ())),
        precision=highest,
        preferred_element_type=jnp.float32,
    )
    main_term = lax.dot_general(
        grad_low, w_low, (((1,), (1,)), ((), ())), preferred_element_type=jnp.float32
    )
    side_term = lax.dot_general(
        grad_bc,
        w_bc_float,
        (((1,), (1,)), ((), ())),
        precision=highest,
        preferred_element_type=jnp.float32,
    )
    grad_normed_in = lax.psum_scatter(
        (main_term + side_term).astype(jnp.bfloat16), "head", scatter_dimension=0, tiled=True
    ).astype(jnp.float32)
    scale_in = rms_scale(stream)
    g_norm_gain = jnp.sum(grad_normed_in * stream * scale_in, axis=0)
    weighted_in = grad_normed_in * norm_gain
    grad_stream = (
        grad_next
        + scale_in * weighted_in
        - stream * scale_in**3 * jnp.mean(weighted_in * stream, axis=-1, keepdims=True)
    )
    head_part = (
        g_low[:, :inner_width],
        g_low[:, inner_width : 2 * inner_width],
        g_low[:, 2 * inner_width :],
        g_conv_w[:, :inner_width],
        g_conv_b[:inner_width],
        g_dt_bias,
        g_a_log,
        g_skip,
        g_gate_gain,
    )
    shared_part = (g_norm_gain, g_w_bc, g_conv_w[:, inner_width:], g_conv_b[inner_width:])
    return (grad_stream, head_part, shared_part, g_w_out)


def reduce_grads(head_part, shared_part):
    head_sum = tuple(
        lax.psum(member.astype(jnp.bfloat16), "seq").astype(jnp.float32) for member in head_part
    )
    shared_sum = lax.psum(tuple(shared_part), ("seq", "head"))
    return (head_sum, tuple(shared_sum))


def store_slot(buffer, value, slot_index, is_valid):
    current = lax.dynamic_index_in_dim(buffer, slot_index, 0, False)
    return lax.dynamic_update_index_in_dim(
        buffer, jnp.where(is_valid, value, current), slot_index, 0
    )


def on_device(
    inputs,
    cotangent,
    starts,
    live,
    norm_gain,
    w_gate,
    w_in,
    w_bc,
    w_dt,
    conv_x,
    conv_x_bias,
    conv_bc,
    conv_bc_bias,
    dt_bias,
    a_log,
    skip,
    gate_gain,
    w_out,
):
    section_count = lax.axis_size("section")
    section_index = lax.axis_index("section")
    micro_count = inputs.shape[0]
    tick_count = micro_count + section_count - 1
    w_main = jnp.concatenate([w_gate[0], w_in[0], w_bc[0], w_dt[0]], axis=1)
    w_low = jnp.concatenate([w_gate[0], w_in[0], w_dt[0]], axis=1)
    conv_weight = jnp.concatenate([conv_x[0], conv_bc[0]], axis=1).astype(jnp.float32)
    conv_bias = jnp.concatenate([conv_x_bias[0], conv_bc_bias[0]], axis=0)
    layer_weights = (
        norm_gain[0],
        w_main,
        w_low,
        w_bc[0],
        conv_weight,
        conv_bias,
        dt_bias[0],
        a_log[0],
        skip[0],
        gate_gain[0],
        w_out[0],
    )
    row_shape = inputs.shape[1:]
    outputs_all = jnp.zeros((micro_count,) + row_shape, jnp.float32)
    arrived = jnp.zeros(row_shape, jnp.float32)
    ticks = []
    for tick_index in range(tick_count):
        slot_index = tick_index - section_index
        is_valid = (slot_index >= 0) & (slot_index < micro_count)
        clipped = jnp.clip(slot_index, 0, micro_count - 1)
        fresh_rows = lax.dynamic_index_in_dim(inputs, clipped, 0, False).astype(jnp.float32)
        stream = jnp.where(section_index == 0, fresh_rows, arrived)
        start_marks = lax.dynamic_index_in_dim(starts, clipped, 0, False)
        alive_mask = lax.dynamic_index_in_dim(live, clipped, 0, False).astype(jnp.float32)
        result, saved = mixer_forward(stream, start_marks, alive_mask, layer_weights)
        outputs_all = store_slot(outputs_all, result, clipped, is_valid)
        ticks.append((clipped, is_valid, saved))
        if tick_index + 1 < tick_count:
            arrived = shifted(result, "section", 1)
    back_arrived = jnp.zeros(row_shape, jnp.float32)
    input_grads = jnp.zeros((micro_count,) + row_shape, jnp.float32)
    head_total = ()
    shared_total = ()
    for tick_index in range(tick_count):
        clipped, is_valid, saved = ticks[tick_count - 1 - tick_index]
        outer_grad = lax.dynamic_index_in_dim(cotangent, clipped, 0, False).astype(jnp.float32)
        grad_next = jnp.where(section_index == section_count - 1, outer_grad, back_arrived)
        mask_value = is_valid.astype(jnp.float32)
        grad_stream, head_part, shared_part, out_part = mixer_backward(
            grad_next, layer_weights, saved, mask_value
        )
        if tick_index == 0:
            out_total = out_part
        else:
            out_total = out_total + out_part
        if tick_index + 1 == tick_count:
            out_total = lax.psum(out_total.astype(jnp.bfloat16), "seq")
        head_part = tuple((member * mask_value for member in head_part))
        shared_part = tuple((member * mask_value for member in shared_part))
        if tick_index == 0:
            head_total = head_part
            shared_total = shared_part
        else:
            head_total = tuple((former + latter for former, latter in zip(head_total, head_part)))
            shared_total = tuple(
                (former + latter for former, latter in zip(shared_total, shared_part))
            )
        input_grads = store_slot(input_grads, grad_stream, clipped, is_valid)
        if tick_index + 1 < tick_count:
            back_arrived = shifted(grad_stream.astype(jnp.bfloat16), "section", -1).astype(
                grad_stream.dtype
            )
    anchor = out_total[0, 0].astype(jnp.float32) * 0.0
    head_total = (head_total[0] + anchor,) + head_total[1:]
    head_total, shared_total = reduce_grads(head_total, shared_total)
    head_total = head_total[:3] + (out_total.astype(jnp.float32),) + head_total[3:]
    return (
        outputs_all[None],
        input_grads[None],
        shared_total[0][None],
        head_total[0][None],
        head_total[1][None],
        shared_total[1][None],
        head_total[2][None],
        head_total[4][None],
        head_total[5][None],
        shared_total[2][None],
        shared_total[3][None],
        head_total[6][None],
        head_total[7][None],
        head_total[8][None],
        head_total[9][None],
        head_total[3][None],
    )


def solution(mesh):
    return jax.shard_map(
        on_device,
        mesh=mesh,
        in_specs=(
            P(None, ("seq", "head"), None),
            P(None, ("seq", "head"), None),
            P(None, "seq"),
            P(None, "seq"),
            P("section", None),
            P("section", None, "head"),
            P("section", None, "head"),
            P("section", None, None),
            P("section", None, "head"),
            P("section", None, "head"),
            P("section", "head"),
            P("section", None, None),
            P("section", None),
            P("section", "head"),
            P("section", "head"),
            P("section", "head"),
            P("section", "head"),
            P("section", "head", None),
        ),
        out_specs=(
            P("section", None, ("seq", "head"), None),
            P("section", None, ("seq", "head"), None),
            P("section", None),
            P("section", None, "head"),
            P("section", None, "head"),
            P("section", None, None),
            P("section", None, "head"),
            P("section", None, "head"),
            P("section", "head"),
            P("section", None, None),
            P("section", None),
            P("section", "head"),
            P("section", "head"),
            P("section", "head"),
            P("section", "head"),
            P("section", "head", None),
        ),
        check_vma=False,
    )
```

```python
from functools import partial

import functools

import jax
import jax.numpy as jnp
from jax import lax
from jax.experimental import pallas as pl
from jax.experimental.pallas import tpu as pltpu
from jax.sharding import PartitionSpec as P

DI = 4096
P_SIZE = 64
N = 128
KW = 4
SCAN_BLOCK = 256


MESH = pl.DeviceIdType.MESH


def _tick_valid(offset, sign, count):
    slot = offset + sign * lax.axis_index("section")
    return jnp.logical_and(slot >= 0, slot < count)


def _enter(barrier, h, n):
    @pl.when(h > 0)
    def _():
        pl.semaphore_signal(barrier, 1, device_id={"head": h - 1}, device_id_type=MESH)

    @pl.when(h < n - 1)
    def _():
        pl.semaphore_signal(barrier, 1, device_id={"head": h + 1}, device_id_type=MESH)

    @pl.when(jnp.logical_and(h > 0, h < n - 1))
    def _():
        pl.semaphore_wait(barrier, 2)

    @pl.when(jnp.logical_or(h == 0, h == n - 1))
    def _():
        pl.semaphore_wait(barrier, 1)


def gather_body(n, tick, x_ref, o_ref, land, send_r, send_l, recv):
    h = lax.axis_index("head")
    valid = _tick_valid(*tick)

    @pl.when(valid)
    def _():
        _enter(pltpu.get_barrier_semaphore(), h, n)

        def copy_right(s, k):
            src = x_ref if s == 0 else land.at[k]
            return pltpu.make_async_remote_copy(
                src_ref=src, dst_ref=land.at[k], send_sem=send_r.at[s], recv_sem=recv.at[k],
                device_id={"head": h + 1}, device_id_type=MESH)

        def copy_left(s, k):
            src = x_ref if s == 0 else land.at[k]
            return pltpu.make_async_remote_copy(
                src_ref=src, dst_ref=land.at[k], send_sem=send_l.at[s], recv_sem=recv.at[k],
                device_id={"head": h - 1}, device_id_type=MESH)

        for s in range(n):
            k_r = h - s
            k_l = h + s
            if s >= 1:
                @pl.when(k_r >= 0)
                def _():
                    pltpu.make_async_remote_copy(
                        src_ref=land.at[k_r], dst_ref=land.at[k_r], send_sem=send_r.at[0],
                        recv_sem=recv.at[k_r], device_id={"head": h}, device_id_type=MESH
                    ).wait_recv()

                @pl.when(k_l <= n - 1)
                def _():
                    pltpu.make_async_remote_copy(
                        src_ref=land.at[k_l], dst_ref=land.at[k_l], send_sem=send_l.at[0],
                        recv_sem=recv.at[k_l], device_id={"head": h}, device_id_type=MESH
                    ).wait_recv()
            if s <= n - 2:
                @pl.when(jnp.logical_and(k_r >= 0, h < n - 1))
                def _():
                    copy_right(s, k_r).start()

                @pl.when(jnp.logical_and(k_l <= n - 1, h > 0))
                def _():
                    copy_left(s, k_l).start()
        land[h] = x_ref[...]
        for s in range(n - 1):
            k_r = h - s
            k_l = h + s

            @pl.when(jnp.logical_and(k_r >= 0, h < n - 1))
            def _():
                copy_right(s, k_r).wait_send()

            @pl.when(jnp.logical_and(k_l <= n - 1, h > 0))
            def _():
                copy_left(s, k_l).wait_send()
        o_ref[...] = land[...]

    @pl.when(jnp.logical_not(valid))
    def _():
        o_ref[...] = jnp.zeros(o_ref.shape, o_ref.dtype)


def head_gather(x, tick, cid):
    n = lax.axis_size("head")
    rows, cols = x.shape
    return pl.pallas_call(
        functools.partial(gather_body, n, tick),
        out_shape=jax.ShapeDtypeStruct((n, rows, cols), x.dtype),
        in_specs=[pl.BlockSpec(memory_space=pltpu.VMEM)],
        out_specs=pl.BlockSpec(memory_space=pltpu.VMEM),
        scratch_shapes=[
            pltpu.VMEM((n, rows, cols), x.dtype),
            pltpu.SemaphoreType.DMA((n,)),
            pltpu.SemaphoreType.DMA((n,)),
            pltpu.SemaphoreType.DMA((n,)),
        ],
        compiler_params=pltpu.CompilerParams(collective_id=cid, has_side_effects=True),
    )(x)


def scatter_body(n, tick, p_ref, o_ref, recv_l, recv_r, send_l, send_r, ssem_l, ssem_r, rsem_l, rsem_r):
    h = lax.axis_index("head")
    valid = _tick_valid(*tick)
    link = send_r.dtype

    @pl.when(valid)
    def _():
        _enter(pltpu.get_barrier_semaphore(), h, n)

        def to_right(k):
            return pltpu.make_async_remote_copy(
                src_ref=send_r.at[k], dst_ref=recv_l.at[k], send_sem=ssem_r.at[k],
                recv_sem=rsem_l.at[k], device_id={"head": h + 1}, device_id_type=MESH)

        def to_left(k):
            return pltpu.make_async_remote_copy(
                src_ref=send_l.at[k], dst_ref=recv_r.at[k], send_sem=ssem_l.at[k],
                recv_sem=rsem_r.at[k], device_id={"head": h - 1}, device_id_type=MESH)

        for s in range(n - 1):
            k_r = n - 1 - s
            k_l = s

            @pl.when(k_r > h)
            def _():
                @pl.when(h > 0)
                def _():
                    to_right(k_r).wait_recv()
                    send_r[k_r] = (p_ref[k_r] + recv_l[k_r].astype(jnp.float32)).astype(link)

                @pl.when(h == 0)
                def _():
                    send_r[k_r] = p_ref[k_r].astype(link)

                to_right(k_r).start()

            @pl.when(k_l < h)
            def _():
                @pl.when(h < n - 1)
                def _():
                    to_left(k_l).wait_recv()
                    send_l[k_l] = (p_ref[k_l] + recv_r[k_l].astype(jnp.float32)).astype(link)

                @pl.when(h == n - 1)
                def _():
                    send_l[k_l] = p_ref[k_l].astype(link)

                to_left(k_l).start()
        total = p_ref[h]

        @pl.when(h > 0)
        def _():
            to_right(h).wait_recv()

        @pl.when(h < n - 1)
        def _():
            to_left(h).wait_recv()

        left_part = jnp.where(h > 0, recv_l[h].astype(jnp.float32), 0.0)
        right_part = jnp.where(h < n - 1, recv_r[h].astype(jnp.float32), 0.0)
        o_ref[...] = (total + left_part + right_part).astype(o_ref.dtype)
        for s in range(n - 1):
            k_r = n - 1 - s
            k_l = s

            @pl.when(k_r > h)
            def _():
                to_right(k_r).wait_send()

            @pl.when(k_l < h)
            def _():
                to_left(k_l).wait_send()

    @pl.when(jnp.logical_not(valid))
    def _():
        o_ref[...] = jnp.zeros(o_ref.shape, o_ref.dtype)


def head_scatter(parts, tick, cid, link=jnp.bfloat16):
    n = lax.axis_size("head")
    _, rows, cols = parts.shape
    return pl.pallas_call(
        functools.partial(scatter_body, n, tick),
        out_shape=jax.ShapeDtypeStruct((rows, cols), jnp.float32),
        in_specs=[pl.BlockSpec(memory_space=pltpu.VMEM)],
        out_specs=pl.BlockSpec(memory_space=pltpu.VMEM),
        scratch_shapes=[
            pltpu.VMEM((n, rows, cols), link),
            pltpu.VMEM((n, rows, cols), link),
            pltpu.VMEM((n, rows, cols), link),
            pltpu.VMEM((n, rows, cols), link),
            pltpu.SemaphoreType.DMA((n,)),
            pltpu.SemaphoreType.DMA((n,)),
            pltpu.SemaphoreType.DMA((n,)),
            pltpu.SemaphoreType.DMA((n,)),
        ],
        compiler_params=pltpu.CompilerParams(collective_id=cid, has_side_effects=True),
    )(parts)


norm_eps = 1e-05
far_below = -1e30
highest = lax.Precision.HIGHEST


def shifted(value, axis, by):
    count = lax.axis_size(axis)
    pairs = [(i, i + by) for i in range(count) if 0 <= i + by < count]
    return lax.ppermute(value, axis, pairs)


def entering(value, axis, combine, identity):
    count, mine = (lax.axis_size(axis), lax.axis_index(axis))
    everything = jax.tree.map(lambda part: lax.all_gather(part, axis), value)
    before = jax.tree.map(
        lambda part, zero: jnp.broadcast_to(jnp.asarray(zero, part.dtype), part.shape),
        value,
        identity,
    )
    for k in range(count - 1):
        reached = k < mine
        new = combine(before, jax.tree.map(lambda part: part[k], everything))
        before = jax.tree.map(lambda a, b: jnp.where(reached, a, b), new, before)
    return before


def entering_2(value, axis, join, neutral):
    count = lax.axis_size(axis)
    place = lax.axis_index(axis)
    ahead = count - 1 - place
    gathered = jax.tree.map(
        lambda a, kind: lax.all_gather(a.astype(kind), axis),
        value,
        jax.tree.map(lambda a: jnp.bfloat16 if a.dtype == jnp.float32 else a.dtype, value),
    )
    state = jax.tree.map(lambda a, e: jnp.zeros_like(a) + jnp.asarray(e, a.dtype), value, neutral)
    for lap in range(count - 1):
        source = count - 1 - lap
        new = join(
            state,
            jax.tree.map(lambda a, own: a[source].astype(own.dtype), gathered, value),
        )
        active = lap < ahead
        state = jax.tree.map(lambda a, b: jnp.where(active, a, b), new, state)
    return state


def rms_scale(values):
    return lax.rsqrt(jnp.mean(values * values, axis=-1, keepdims=True) + norm_eps)


def silu_slope(values):
    logistic = jax.nn.sigmoid(values)
    return logistic * (1.0 + values * (1.0 - logistic))


def causal_conv(extended, marks_ext, weight, conv_bias):
    tap_count = weight.shape[0]
    length = extended.shape[0] - tap_count + 1
    counts = jnp.cumsum(marks_ext)
    conv_sum = jnp.zeros((length, extended.shape[1]), jnp.float32) + conv_bias
    for tap_index in range(tap_count):
        linked = (counts[tap_count - 1 :] == counts[tap_index : tap_index + length]).astype(
            jnp.float32
        )
        conv_sum = (
            conv_sum
            + linked[:, None] * weight[tap_index] * extended[tap_index : tap_index + length]
        )
    return conv_sum


def prepare(extended, dt_pre, marks_ext, alive_mask, conv_weight, conv_bias, dt_bias, a_log):
    inner_width = dt_pre.shape[1] * P_SIZE
    activated = jax.nn.silu(causal_conv(extended, marks_ext, conv_weight, conv_bias))
    inner_act = activated[:, :inner_width] * alive_mask[:, None]
    b_mat = activated[:, inner_width : inner_width + N]
    c_mat = activated[:, inner_width + N :]
    step_size = jax.nn.softplus(dt_pre + dt_bias) * alive_mask[:, None]
    log_decay = -step_size * jnp.exp(a_log)
    return (inner_act, step_size, log_decay, b_mat, c_mat)


def block_terms(inner_act, step_size, log_decay, b_mat, start_marks):
    blocks = inner_act.shape[0] // SCAN_BLOCK
    head_count = step_size.shape[1]
    x_blocks = inner_act.reshape(blocks, SCAN_BLOCK, head_count, P_SIZE)
    dt_blocks = step_size.reshape(blocks, SCAN_BLOCK, head_count)
    cum_decay = jnp.cumsum(log_decay.reshape(blocks, SCAN_BLOCK, head_count), axis=1)
    mark_count = jnp.cumsum(start_marks.reshape(blocks, SCAN_BLOCK), axis=1)
    b_blocks = b_mat.reshape(blocks, SCAN_BLOCK, N)
    last_cum = cum_decay[:, -1]
    last_mark = mark_count[:, -1]
    same_end = (mark_count == last_mark[:, None]).astype(jnp.float32)
    end_weight = jnp.exp(last_cum[:, None, :] - cum_decay) * same_end[:, :, None] * dt_blocks
    block_states = jnp.einsum(
        "cjh,cjhp,cjn->chpn", end_weight, x_blocks, b_blocks, precision=highest
    )
    block_decay = jnp.exp(last_cum) * (last_mark == 0).astype(jnp.float32)[:, None]
    return (block_decay, block_states, cum_decay, mark_count, x_blocks, dt_blocks)


def compose_blocks(block_decay, block_states, start_state):
    chain_state = start_state
    incoming = []
    for block_index in range(block_decay.shape[0]):
        incoming.append(chain_state)
        chain_state = (
            block_decay[block_index][:, None, None] * chain_state + block_states[block_index]
        )
    return (chain_state, jnp.stack(incoming))


def block_output(block_parts, b_mat, c_mat, skip, incoming):
    block_decay, block_states, cum_decay, mark_count, x_blocks, dt_blocks = block_parts
    blocks = cum_decay.shape[0]
    head_count = cum_decay.shape[2]
    b_blocks = b_mat.reshape(blocks, SCAN_BLOCK, N)
    c_blocks = c_mat.reshape(blocks, SCAN_BLOCK, N)
    inner_prod = jnp.einsum("cin,cjn->cij", c_blocks, b_blocks, precision=highest)
    arange_pos = jnp.arange(SCAN_BLOCK)
    linked = (arange_pos[:, None] >= arange_pos[None, :])[None] & (
        mark_count[:, :, None] == mark_count[:, None, :]
    )
    spread = jnp.where(
        linked[..., None], cum_decay[:, :, None, :] - cum_decay[:, None, :, :], far_below
    )
    weights = jnp.exp(spread) * inner_prod[..., None] * dt_blocks[:, None, :, :]
    y_intra = jnp.einsum("cijh,cjhp->cihp", weights, x_blocks, precision=highest)
    carry_in = jnp.exp(cum_decay) * (mark_count == 0).astype(jnp.float32)[:, :, None]
    y_inter = (
        jnp.einsum("cin,chpn->cihp", c_blocks, incoming, precision=highest) * carry_in[..., None]
    )
    mixed_out = y_intra + y_inter + skip[None, None, :, None] * x_blocks
    return mixed_out.reshape(blocks * SCAN_BLOCK, head_count * P_SIZE)


def local_front(marks_ext, alive_mask, extended, dt_pre, conv_weight, conv_bias, dt_bias, a_log):
    inner_act, step_size, log_decay, b_mat, c_mat = prepare(
        extended, dt_pre, marks_ext, alive_mask, conv_weight, conv_bias, dt_bias, a_log
    )
    block_parts = block_terms(inner_act, step_size, log_decay, b_mat, marks_ext[KW - 1 :])
    zero_state = jnp.zeros(block_parts[1].shape[1:], jnp.float32)
    total_state, _ = compose_blocks(block_parts[0], block_parts[1], zero_state)
    total_decay = jnp.prod(block_parts[0], axis=0)
    return (block_parts, b_mat, c_mat, total_decay, total_state)


def local_rear(block_parts, b_mat, c_mat, skip, start_state):
    _, incoming = compose_blocks(block_parts[0], block_parts[1], start_state)
    return block_output(block_parts, b_mat, c_mat, skip, incoming)


def local_pass(
    marks_ext,
    alive_mask,
    extended,
    dt_pre,
    conv_weight,
    conv_bias,
    dt_bias,
    a_log,
    skip,
    start_state,
):
    block_parts, b_mat, c_mat, total_decay, total_state = local_front(
        marks_ext, alive_mask, extended, dt_pre, conv_weight, conv_bias, dt_bias, a_log
    )
    return (local_rear(block_parts, b_mat, c_mat, skip, start_state), total_decay, total_state)


def chain_combine(earlier, later):
    return (earlier[0] * later[0], later[0][:, None, None] * earlier[1] + later[1])


def extend(pre_conv, start_marks, edge_rows, edge_marks):
    extended = jnp.concatenate([edge_rows, pre_conv], axis=0)
    marks_ext = jnp.concatenate([edge_marks.astype(jnp.int32), start_marks], axis=0)
    return (extended, marks_ext)


def mixer_forward(stream, start_marks, alive_mask, layer_weights, tick, ids):
    (
        norm_gain,
        w_main,
        w_low,
        w_bc,
        conv_weight,
        conv_bias,
        dt_bias,
        a_log,
        skip,
        gate_gain,
        w_out,
    ) = layer_weights
    inner_width = w_out.shape[0]
    normed = (stream * rms_scale(stream) * norm_gain).astype(jnp.bfloat16)
    gathered = head_gather(normed, tick, ids[0])
    gathered = gathered.reshape(-1, gathered.shape[-1])
    projected = jnp.dot(gathered, w_main, preferred_element_type=jnp.float32)
    gate_pre = projected[:, :inner_width]
    pre_conv = projected[:, inner_width : 2 * inner_width + 2 * N]
    dt_pre = projected[:, 2 * inner_width + 2 * N :]
    marks_float = start_marks.astype(jnp.float32)
    tail_from = pre_conv.shape[0] - KW + 1
    edge_parts = shifted((pre_conv[tail_from:], marks_float[tail_from:]), "seq", 1)
    extended, marks_ext = extend(pre_conv, start_marks, edge_parts[0], edge_parts[1])
    front_fn = partial(local_front, marks_ext, alive_mask)
    front_out, front_pull = jax.vjp(
        front_fn, extended, dt_pre, conv_weight, conv_bias, dt_bias, a_log
    )
    block_parts, b_mat, c_mat, total_decay, total_state = front_out
    neutral = (jnp.ones_like(total_decay), jnp.zeros_like(total_state))
    prefix = entering((total_decay, total_state), "seq", chain_combine, neutral)
    start_state = prefix[1]
    mixed_out, rear_pull = jax.vjp(local_rear, block_parts, b_mat, c_mat, skip, start_state)
    silu_gate = jax.nn.silu(gate_pre)
    gated_mix = mixed_out * silu_gate
    square_total = lax.psum(jnp.sum(gated_mix * gated_mix, axis=-1), "head")
    scale_out = lax.rsqrt(square_total / DI + norm_eps)
    normed_out = (gated_mix * scale_out[:, None] * gate_gain).astype(jnp.bfloat16)
    head_count = lax.axis_size("head")
    branch = head_scatter(
        jnp.dot(normed_out, w_out, preferred_element_type=jnp.float32).reshape(
            head_count, -1, w_out.shape[1]
        ),
        tick,
        ids[1],
    )
    saved = (
        stream,
        gathered,
        gate_pre,
        mixed_out,
        silu_gate,
        gated_mix,
        scale_out,
        normed_out,
        total_decay,
        start_state,
        front_pull,
        rear_pull,
    )
    return stream + branch, saved


def mixer_backward(grad_next, layer_weights, saved, mask_value, tick, ids):
    (
        norm_gain,
        w_main,
        w_low,
        w_bc,
        conv_weight,
        conv_bias,
        dt_bias,
        a_log,
        skip,
        gate_gain,
        w_out,
    ) = layer_weights
    (
        stream,
        gathered,
        gate_pre,
        mixed_out,
        silu_gate,
        gated_mix,
        scale_out,
        normed_out,
        total_decay,
        start_state,
        front_pull,
        rear_pull,
    ) = saved
    inner_width = w_out.shape[0]
    grad_branch = grad_next.astype(jnp.bfloat16)
    shard_rows = head_gather(grad_branch, tick, ids[0])
    shard_rows = shard_rows.reshape(-1, shard_rows.shape[-1])
    g_w_out = lax.dot_general(
        normed_out, shard_rows, (((0,), (0,)), ((), ())), preferred_element_type=jnp.float32
    ) * mask_value
    grad_normed = lax.dot_general(
        shard_rows, w_out, (((1,), (1,)), ((), ())), preferred_element_type=jnp.float32
    )
    weighted = grad_normed * gate_gain
    g_gate_gain = jnp.sum(grad_normed * gated_mix * scale_out[:, None], axis=0)
    cross_sum = lax.psum(jnp.sum(weighted * gated_mix, axis=-1), "head")
    grad_gated = (
        scale_out[:, None] * weighted - gated_mix * (scale_out**3 * cross_sum / DI)[:, None]
    )
    grad_mixed = grad_gated * silu_gate
    grad_gate = (grad_gated * mixed_out * silu_slope(gate_pre)).astype(jnp.bfloat16)
    g_parts, g_b_mat, g_c_mat, g_skip, g_start = rear_pull(grad_mixed)
    neutral = (jnp.ones_like(total_decay), jnp.zeros_like(g_start))
    suffix = entering_2((total_decay, g_start), "seq", chain_combine, neutral)
    after_state = suffix[1]
    grad_decay = jnp.sum(after_state * start_state, axis=(1, 2))
    grad_ext, grad_dt_pre, g_conv_w, g_conv_b, g_dt_bias, g_a_log = front_pull(
        (g_parts, g_b_mat, g_c_mat, grad_decay, after_state)
    )
    returned = shifted(grad_ext[: KW - 1], "seq", -1)
    grad_pre = grad_ext[KW - 1 :]
    tail_from = grad_pre.shape[0] - KW + 1
    grad_pre = jnp.concatenate([grad_pre[:tail_from], grad_pre[tail_from:] + returned], axis=0)
    grad_inner = grad_pre[:, :inner_width].astype(jnp.bfloat16)
    grad_bc = grad_pre[:, inner_width:]
    grad_low = jnp.concatenate([grad_gate, grad_inner, grad_dt_pre.astype(jnp.bfloat16)], axis=1)
    w_bc_float = w_bc.astype(jnp.float32)
    g_low = lax.dot_general(
        gathered, grad_low, (((0,), (0,)), ((), ())), preferred_element_type=jnp.float32
    )
    g_w_bc = lax.dot_general(
        gathered.astype(jnp.float32),
        grad_bc,
        (((0,), (0,)), ((), ())),
        precision=highest,
        preferred_element_type=jnp.float32,
    )
    main_term = lax.dot_general(
        grad_low, w_low, (((1,), (1,)), ((), ())), preferred_element_type=jnp.float32
    )
    side_term = lax.dot_general(
        grad_bc,
        w_bc_float,
        (((1,), (1,)), ((), ())),
        precision=highest,
        preferred_element_type=jnp.float32,
    )
    head_count = lax.axis_size("head")
    grad_normed_in = head_scatter(
        (main_term + side_term).reshape(head_count, -1, main_term.shape[1]), tick, ids[1]
    )
    scale_in = rms_scale(stream)
    g_norm_gain = jnp.sum(grad_normed_in * stream * scale_in, axis=0)
    weighted_in = grad_normed_in * norm_gain
    grad_stream = (
        grad_next
        + scale_in * weighted_in
        - stream * scale_in**3 * jnp.mean(weighted_in * stream, axis=-1, keepdims=True)
    )
    head_part = (
        g_low[:, :inner_width],
        g_low[:, inner_width : 2 * inner_width],
        g_low[:, 2 * inner_width :],
        g_conv_w[:, :inner_width],
        g_conv_b[:inner_width],
        g_dt_bias,
        g_a_log,
        g_skip,
        g_gate_gain,
    )
    shared_part = (g_norm_gain, g_w_bc, g_conv_w[:, inner_width:], g_conv_b[inner_width:])
    return (grad_stream, head_part, shared_part, g_w_out)


def reduce_grads(head_part, shared_part):
    head_sum = tuple(
        lax.psum(member.astype(jnp.bfloat16), "seq").astype(jnp.float32) for member in head_part
    )
    shared_sum = lax.psum(tuple(shared_part), ("seq", "head"))
    return (head_sum, tuple(shared_sum))


def store_slot(buffer, value, slot_index, is_valid):
    current = lax.dynamic_index_in_dim(buffer, slot_index, 0, False)
    return lax.dynamic_update_index_in_dim(
        buffer, jnp.where(is_valid, value, current), slot_index, 0
    )


def on_device(
    inputs,
    cotangent,
    starts,
    live,
    norm_gain,
    w_gate,
    w_in,
    w_bc,
    w_dt,
    conv_x,
    conv_x_bias,
    conv_bc,
    conv_bc_bias,
    dt_bias,
    a_log,
    skip,
    gate_gain,
    w_out,
):
    section_count = lax.axis_size("section")
    section_index = lax.axis_index("section")
    micro_count = inputs.shape[0]
    tick_count = micro_count + section_count - 1
    w_main = jnp.concatenate([w_gate[0], w_in[0], w_bc[0], w_dt[0]], axis=1)
    w_low = jnp.concatenate([w_gate[0], w_in[0], w_dt[0]], axis=1)
    conv_weight = jnp.concatenate([conv_x[0], conv_bc[0]], axis=1).astype(jnp.float32)
    conv_bias = jnp.concatenate([conv_x_bias[0], conv_bc_bias[0]], axis=0)
    layer_weights = (
        norm_gain[0],
        w_main,
        w_low,
        w_bc[0],
        conv_weight,
        conv_bias,
        dt_bias[0],
        a_log[0],
        skip[0],
        gate_gain[0],
        w_out[0],
    )
    row_shape = inputs.shape[1:]
    outputs_all = jnp.zeros((micro_count,) + row_shape, jnp.float32)
    arrived = jnp.zeros(row_shape, jnp.float32)
    ticks = []
    for tick_index in range(tick_count):
        slot_index = tick_index - section_index
        is_valid = (slot_index >= 0) & (slot_index < micro_count)
        clipped = jnp.clip(slot_index, 0, micro_count - 1)
        fresh_rows = lax.dynamic_index_in_dim(inputs, clipped, 0, False).astype(jnp.float32)
        stream = jnp.where(section_index == 0, fresh_rows, arrived)
        start_marks = lax.dynamic_index_in_dim(starts, clipped, 0, False)
        alive_mask = lax.dynamic_index_in_dim(live, clipped, 0, False).astype(jnp.float32)
        result, saved = mixer_forward(
            stream,
            start_marks,
            alive_mask,
            layer_weights,
            (tick_index, -1, micro_count),
            (tick_index, tick_count + tick_index),
        )
        outputs_all = store_slot(outputs_all, result, clipped, is_valid)
        ticks.append((clipped, is_valid, saved))
        if tick_index + 1 < tick_count:
            arrived = shifted(result, "section", 1)
    back_arrived = jnp.zeros(row_shape, jnp.float32)
    input_grads = jnp.zeros((micro_count,) + row_shape, jnp.float32)
    head_total = ()
    shared_total = ()
    for tick_index in range(tick_count):
        clipped, is_valid, saved = ticks[tick_count - 1 - tick_index]
        outer_grad = lax.dynamic_index_in_dim(cotangent, clipped, 0, False).astype(jnp.float32)
        grad_next = jnp.where(section_index == section_count - 1, outer_grad, back_arrived)
        mask_value = is_valid.astype(jnp.float32)
        grad_stream, head_part, shared_part, out_part = mixer_backward(
            grad_next,
            layer_weights,
            saved,
            mask_value,
            (tick_count - 1 - tick_index, -1, micro_count),
            (2 * tick_count + tick_index, 3 * tick_count + tick_index),
        )
        if tick_index == 0:
            out_total = out_part
        else:
            out_total = out_total + out_part
        if tick_index + 1 == tick_count:
            out_total = lax.psum(out_total.astype(jnp.bfloat16), "seq")
        head_part = tuple((member * mask_value for member in head_part))
        shared_part = tuple((member * mask_value for member in shared_part))
        if tick_index == 0:
            head_total = head_part
            shared_total = shared_part
        else:
            head_total = tuple((former + latter for former, latter in zip(head_total, head_part)))
            shared_total = tuple(
                (former + latter for former, latter in zip(shared_total, shared_part))
            )
        input_grads = store_slot(input_grads, grad_stream, clipped, is_valid)
        if tick_index + 1 < tick_count:
            back_arrived = shifted(grad_stream.astype(jnp.bfloat16), "section", -1).astype(
                grad_stream.dtype
            )
    anchor = out_total[0, 0].astype(jnp.float32) * 0.0
    head_total = (head_total[0] + anchor,) + head_total[1:]
    head_total, shared_total = reduce_grads(head_total, shared_total)
    head_total = head_total[:3] + (out_total.astype(jnp.float32),) + head_total[3:]
    return (
        outputs_all[None],
        input_grads[None],
        shared_total[0][None],
        head_total[0][None],
        head_total[1][None],
        shared_total[1][None],
        head_total[2][None],
        head_total[4][None],
        head_total[5][None],
        shared_total[2][None],
        shared_total[3][None],
        head_total[6][None],
        head_total[7][None],
        head_total[8][None],
        head_total[9][None],
        head_total[3][None],
    )


def solution(mesh):
    return jax.shard_map(
        on_device,
        mesh=mesh,
        in_specs=(
            P(None, ("seq", "head"), None),
            P(None, ("seq", "head"), None),
            P(None, "seq"),
            P(None, "seq"),
            P("section", None),
            P("section", None, "head"),
            P("section", None, "head"),
            P("section", None, None),
            P("section", None, "head"),
            P("section", None, "head"),
            P("section", "head"),
            P("section", None, None),
            P("section", None),
            P("section", "head"),
            P("section", "head"),
            P("section", "head"),
            P("section", "head"),
            P("section", "head", None),
        ),
        out_specs=(
            P("section", None, ("seq", "head"), None),
            P("section", None, ("seq", "head"), None),
            P("section", None),
            P("section", None, "head"),
            P("section", None, "head"),
            P("section", None, None),
            P("section", None, "head"),
            P("section", None, "head"),
            P("section", "head"),
            P("section", None, None),
            P("section", None),
            P("section", "head"),
            P("section", "head"),
            P("section", "head"),
            P("section", "head"),
            P("section", "head", None),
        ),
        check_vma=False,
    )
```

```python
from functools import partial

import functools

import jax
import jax.numpy as jnp
from jax import lax
from jax.experimental import pallas as pl
from jax.experimental.pallas import tpu as pltpu
from jax.sharding import PartitionSpec as P

DI = 4096
P_SIZE = 64
N = 128
KW = 4
SCAN_BLOCK = 256


MESH = pl.DeviceIdType.MESH


def _tick_valid(offset, sign, count):
    slot = offset + sign * lax.axis_index("section")
    return jnp.logical_and(slot >= 0, slot < count)


def _enter(barrier, h, n):
    @pl.when(h > 0)
    def _():
        pl.semaphore_signal(barrier, 1, device_id={"head": h - 1}, device_id_type=MESH)

    @pl.when(h < n - 1)
    def _():
        pl.semaphore_signal(barrier, 1, device_id={"head": h + 1}, device_id_type=MESH)

    @pl.when(jnp.logical_and(h > 0, h < n - 1))
    def _():
        pl.semaphore_wait(barrier, 2)

    @pl.when(jnp.logical_or(h == 0, h == n - 1))
    def _():
        pl.semaphore_wait(barrier, 1)


def gather_body(n, tick, x_ref, o_ref, land, send_r, send_l, recv):
    h = lax.axis_index("head")
    valid = _tick_valid(*tick)

    @pl.when(valid)
    def _():
        _enter(pltpu.get_barrier_semaphore(), h, n)

        def copy_right(s, k):
            src = x_ref if s == 0 else land.at[k]
            return pltpu.make_async_remote_copy(
                src_ref=src, dst_ref=land.at[k], send_sem=send_r.at[s], recv_sem=recv.at[k],
                device_id={"head": h + 1}, device_id_type=MESH)

        def copy_left(s, k):
            src = x_ref if s == 0 else land.at[k]
            return pltpu.make_async_remote_copy(
                src_ref=src, dst_ref=land.at[k], send_sem=send_l.at[s], recv_sem=recv.at[k],
                device_id={"head": h - 1}, device_id_type=MESH)

        for s in range(n):
            k_r = h - s
            k_l = h + s
            if s >= 1:
                @pl.when(k_r >= 0)
                def _():
                    pltpu.make_async_remote_copy(
                        src_ref=land.at[k_r], dst_ref=land.at[k_r], send_sem=send_r.at[0],
                        recv_sem=recv.at[k_r], device_id={"head": h}, device_id_type=MESH
                    ).wait_recv()

                @pl.when(k_l <= n - 1)
                def _():
                    pltpu.make_async_remote_copy(
                        src_ref=land.at[k_l], dst_ref=land.at[k_l], send_sem=send_l.at[0],
                        recv_sem=recv.at[k_l], device_id={"head": h}, device_id_type=MESH
                    ).wait_recv()
            if s <= n - 2:
                @pl.when(jnp.logical_and(k_r >= 0, h < n - 1))
                def _():
                    copy_right(s, k_r).start()

                @pl.when(jnp.logical_and(k_l <= n - 1, h > 0))
                def _():
                    copy_left(s, k_l).start()
        land[h] = x_ref[...]
        for s in range(n - 1):
            k_r = h - s
            k_l = h + s

            @pl.when(jnp.logical_and(k_r >= 0, h < n - 1))
            def _():
                copy_right(s, k_r).wait_send()

            @pl.when(jnp.logical_and(k_l <= n - 1, h > 0))
            def _():
                copy_left(s, k_l).wait_send()
        o_ref[...] = land[...]

    @pl.when(jnp.logical_not(valid))
    def _():
        o_ref[...] = jnp.zeros(o_ref.shape, o_ref.dtype)


def head_gather(x, tick, cid):
    n = lax.axis_size("head")
    rows, cols = x.shape
    return pl.pallas_call(
        functools.partial(gather_body, n, tick),
        out_shape=jax.ShapeDtypeStruct((n, rows, cols), x.dtype),
        in_specs=[pl.BlockSpec(memory_space=pltpu.VMEM)],
        out_specs=pl.BlockSpec(memory_space=pltpu.VMEM),
        scratch_shapes=[
            pltpu.VMEM((n, rows, cols), x.dtype),
            pltpu.SemaphoreType.DMA((n,)),
            pltpu.SemaphoreType.DMA((n,)),
            pltpu.SemaphoreType.DMA((n,)),
        ],
        compiler_params=pltpu.CompilerParams(collective_id=cid, has_side_effects=True),
    )(x)


def scatter_body(n, tick, p_ref, o_ref, recv_l, recv_r, send_l, send_r, ssem_l, ssem_r, rsem_l, rsem_r):
    h = lax.axis_index("head")
    valid = _tick_valid(*tick)
    link = send_r.dtype

    @pl.when(valid)
    def _():
        _enter(pltpu.get_barrier_semaphore(), h, n)

        def to_right(k):
            return pltpu.make_async_remote_copy(
                src_ref=send_r.at[k], dst_ref=recv_l.at[k], send_sem=ssem_r.at[k],
                recv_sem=rsem_l.at[k], device_id={"head": h + 1}, device_id_type=MESH)

        def to_left(k):
            return pltpu.make_async_remote_copy(
                src_ref=send_l.at[k], dst_ref=recv_r.at[k], send_sem=ssem_l.at[k],
                recv_sem=rsem_r.at[k], device_id={"head": h - 1}, device_id_type=MESH)

        for s in range(n - 1):
            k_r = n - 1 - s
            k_l = s

            @pl.when(k_r > h)
            def _():
                @pl.when(h > 0)
                def _():
                    to_right(k_r).wait_recv()
                    send_r[k_r] = (p_ref[k_r] + recv_l[k_r].astype(jnp.float32)).astype(link)

                @pl.when(h == 0)
                def _():
                    send_r[k_r] = p_ref[k_r].astype(link)

                to_right(k_r).start()

            @pl.when(k_l < h)
            def _():
                @pl.when(h < n - 1)
                def _():
                    to_left(k_l).wait_recv()
                    send_l[k_l] = (p_ref[k_l] + recv_r[k_l].astype(jnp.float32)).astype(link)

                @pl.when(h == n - 1)
                def _():
                    send_l[k_l] = p_ref[k_l].astype(link)

                to_left(k_l).start()
        total = p_ref[h]

        @pl.when(h > 0)
        def _():
            to_right(h).wait_recv()

        @pl.when(h < n - 1)
        def _():
            to_left(h).wait_recv()

        left_part = jnp.where(h > 0, recv_l[h].astype(jnp.float32), 0.0)
        right_part = jnp.where(h < n - 1, recv_r[h].astype(jnp.float32), 0.0)
        o_ref[...] = (total + left_part + right_part).astype(o_ref.dtype)
        for s in range(n - 1):
            k_r = n - 1 - s
            k_l = s

            @pl.when(k_r > h)
            def _():
                to_right(k_r).wait_send()

            @pl.when(k_l < h)
            def _():
                to_left(k_l).wait_send()

    @pl.when(jnp.logical_not(valid))
    def _():
        o_ref[...] = jnp.zeros(o_ref.shape, o_ref.dtype)


def head_scatter(parts, tick, cid, link=jnp.bfloat16):
    n = lax.axis_size("head")
    _, rows, cols = parts.shape
    return pl.pallas_call(
        functools.partial(scatter_body, n, tick),
        out_shape=jax.ShapeDtypeStruct((rows, cols), jnp.float32),
        in_specs=[pl.BlockSpec(memory_space=pltpu.VMEM)],
        out_specs=pl.BlockSpec(memory_space=pltpu.VMEM),
        scratch_shapes=[
            pltpu.VMEM((n, rows, cols), link),
            pltpu.VMEM((n, rows, cols), link),
            pltpu.VMEM((n, rows, cols), link),
            pltpu.VMEM((n, rows, cols), link),
            pltpu.SemaphoreType.DMA((n,)),
            pltpu.SemaphoreType.DMA((n,)),
            pltpu.SemaphoreType.DMA((n,)),
            pltpu.SemaphoreType.DMA((n,)),
        ],
        compiler_params=pltpu.CompilerParams(collective_id=cid, has_side_effects=True),
    )(parts)


norm_eps = 1e-05
far_below = -1e30
highest = lax.Precision.HIGHEST


def shifted(value, axis, by):
    count = lax.axis_size(axis)
    pairs = [(i, i + by) for i in range(count) if 0 <= i + by < count]
    return lax.ppermute(value, axis, pairs)


def gather_flat(value, axis, kind):
    leaves, tree = jax.tree.flatten(value)
    slabs = []
    for leaf in leaves:
        flat = leaf.reshape(-1).astype(kind or leaf.dtype)
        flat = jnp.pad(flat, (0, -flat.size % 1024))
        slabs.append(flat.reshape(-1, 128))
    everything = lax.all_gather(jnp.concatenate(slabs, axis=0), axis)
    pieces = []
    start = 0
    for leaf, slab in zip(leaves, slabs):
        rows = everything[:, start : start + slab.shape[0]].reshape(everything.shape[0], -1)
        pieces.append(rows[:, : leaf.size].reshape((-1,) + leaf.shape))
        start += slab.shape[0]
    return jax.tree.unflatten(tree, pieces)


def entering(value, axis, combine, identity):
    count, mine = (lax.axis_size(axis), lax.axis_index(axis))
    everything = gather_flat(value, axis, None)
    before = jax.tree.map(
        lambda part, zero: jnp.broadcast_to(jnp.asarray(zero, part.dtype), part.shape),
        value,
        identity,
    )
    for k in range(count - 1):
        reached = k < mine
        new = combine(before, jax.tree.map(lambda part: part[k], everything))
        before = jax.tree.map(lambda a, b: jnp.where(reached, a, b), new, before)
    return before


def entering_2(value, axis, join, neutral):
    count = lax.axis_size(axis)
    place = lax.axis_index(axis)
    ahead = count - 1 - place
    gathered = gather_flat(value, axis, jnp.bfloat16)
    state = jax.tree.map(lambda a, e: jnp.zeros_like(a) + jnp.asarray(e, a.dtype), value, neutral)
    for lap in range(count - 1):
        source = count - 1 - lap
        new = join(
            state,
            jax.tree.map(lambda a, own: a[source].astype(own.dtype), gathered, value),
        )
        active = lap < ahead
        state = jax.tree.map(lambda a, b: jnp.where(active, a, b), new, state)
    return state


def rms_scale(values):
    return lax.rsqrt(jnp.mean(values * values, axis=-1, keepdims=True) + norm_eps)


def silu_slope(values):
    logistic = jax.nn.sigmoid(values)
    return logistic * (1.0 + values * (1.0 - logistic))


def causal_conv(extended, marks_ext, weight, conv_bias):
    tap_count = weight.shape[0]
    length = extended.shape[0] - tap_count + 1
    counts = jnp.cumsum(marks_ext)
    conv_sum = jnp.zeros((length, extended.shape[1]), jnp.float32) + conv_bias
    for tap_index in range(tap_count):
        linked = (counts[tap_count - 1 :] == counts[tap_index : tap_index + length]).astype(
            jnp.float32
        )
        conv_sum = (
            conv_sum
            + linked[:, None] * weight[tap_index] * extended[tap_index : tap_index + length]
        )
    return conv_sum


def prepare(extended, dt_pre, marks_ext, alive_mask, conv_weight, conv_bias, dt_bias, a_log):
    inner_width = dt_pre.shape[1] * P_SIZE
    activated = jax.nn.silu(causal_conv(extended, marks_ext, conv_weight, conv_bias))
    inner_act = activated[:, :inner_width] * alive_mask[:, None]
    b_mat = activated[:, inner_width : inner_width + N]
    c_mat = activated[:, inner_width + N :]
    step_size = jax.nn.softplus(dt_pre + dt_bias) * alive_mask[:, None]
    log_decay = -step_size * jnp.exp(a_log)
    return (inner_act, step_size, log_decay, b_mat, c_mat)


def block_terms(inner_act, step_size, log_decay, b_mat, start_marks):
    blocks = inner_act.shape[0] // SCAN_BLOCK
    head_count = step_size.shape[1]
    x_blocks = inner_act.reshape(blocks, SCAN_BLOCK, head_count, P_SIZE)
    dt_blocks = step_size.reshape(blocks, SCAN_BLOCK, head_count)
    cum_decay = jnp.cumsum(log_decay.reshape(blocks, SCAN_BLOCK, head_count), axis=1)
    mark_count = jnp.cumsum(start_marks.reshape(blocks, SCAN_BLOCK), axis=1)
    b_blocks = b_mat.reshape(blocks, SCAN_BLOCK, N)
    last_cum = cum_decay[:, -1]
    last_mark = mark_count[:, -1]
    same_end = (mark_count == last_mark[:, None]).astype(jnp.float32)
    end_weight = jnp.exp(last_cum[:, None, :] - cum_decay) * same_end[:, :, None] * dt_blocks
    block_states = jnp.einsum(
        "cjh,cjhp,cjn->chpn", end_weight, x_blocks, b_blocks, precision=highest
    )
    block_decay = jnp.exp(last_cum) * (last_mark == 0).astype(jnp.float32)[:, None]
    return (block_decay, block_states, cum_decay, mark_count, x_blocks, dt_blocks)


def compose_blocks(block_decay, block_states, start_state):
    chain_state = start_state
    incoming = []
    for block_index in range(block_decay.shape[0]):
        incoming.append(chain_state)
        chain_state = (
            block_decay[block_index][:, None, None] * chain_state + block_states[block_index]
        )
    return (chain_state, jnp.stack(incoming))


def block_output(block_parts, b_mat, c_mat, skip, incoming):
    block_decay, block_states, cum_decay, mark_count, x_blocks, dt_blocks = block_parts
    blocks = cum_decay.shape[0]
    head_count = cum_decay.shape[2]
    b_blocks = b_mat.reshape(blocks, SCAN_BLOCK, N)
    c_blocks = c_mat.reshape(blocks, SCAN_BLOCK, N)
    inner_prod = jnp.einsum("cin,cjn->cij", c_blocks, b_blocks, precision=highest)
    arange_pos = jnp.arange(SCAN_BLOCK)
    linked = (arange_pos[:, None] >= arange_pos[None, :])[None] & (
        mark_count[:, :, None] == mark_count[:, None, :]
    )
    spread = jnp.where(
        linked[..., None], cum_decay[:, :, None, :] - cum_decay[:, None, :, :], far_below
    )
    weights = jnp.exp(spread) * inner_prod[..., None] * dt_blocks[:, None, :, :]
    y_intra = jnp.einsum("cijh,cjhp->cihp", weights, x_blocks, precision=highest)
    carry_in = jnp.exp(cum_decay) * (mark_count == 0).astype(jnp.float32)[:, :, None]
    y_inter = (
        jnp.einsum("cin,chpn->cihp", c_blocks, incoming, precision=highest) * carry_in[..., None]
    )
    mixed_out = y_intra + y_inter + skip[None, None, :, None] * x_blocks
    return mixed_out.reshape(blocks * SCAN_BLOCK, head_count * P_SIZE)


def local_front(marks_ext, alive_mask, extended, dt_pre, conv_weight, conv_bias, dt_bias, a_log):
    inner_act, step_size, log_decay, b_mat, c_mat = prepare(
        extended, dt_pre, marks_ext, alive_mask, conv_weight, conv_bias, dt_bias, a_log
    )
    block_parts = block_terms(inner_act, step_size, log_decay, b_mat, marks_ext[KW - 1 :])
    zero_state = jnp.zeros(block_parts[1].shape[1:], jnp.float32)
    total_state, _ = compose_blocks(block_parts[0], block_parts[1], zero_state)
    total_decay = jnp.prod(block_parts[0], axis=0)
    return (block_parts, b_mat, c_mat, total_decay, total_state)


def local_rear(block_parts, b_mat, c_mat, skip, start_state):
    _, incoming = compose_blocks(block_parts[0], block_parts[1], start_state)
    return block_output(block_parts, b_mat, c_mat, skip, incoming)


def local_pass(
    marks_ext,
    alive_mask,
    extended,
    dt_pre,
    conv_weight,
    conv_bias,
    dt_bias,
    a_log,
    skip,
    start_state,
):
    block_parts, b_mat, c_mat, total_decay, total_state = local_front(
        marks_ext, alive_mask, extended, dt_pre, conv_weight, conv_bias, dt_bias, a_log
    )
    return (local_rear(block_parts, b_mat, c_mat, skip, start_state), total_decay, total_state)


def chain_combine(earlier, later):
    return (earlier[0] * later[0], later[0][:, None, None] * earlier[1] + later[1])


def extend(pre_conv, start_marks, edge_rows, edge_marks):
    extended = jnp.concatenate([edge_rows, pre_conv], axis=0)
    marks_ext = jnp.concatenate([edge_marks.astype(jnp.int32), start_marks], axis=0)
    return (extended, marks_ext)


def mixer_forward(stream, start_marks, alive_mask, layer_weights, tick, ids):
    (
        norm_gain,
        w_main,
        w_low,
        w_bc,
        conv_weight,
        conv_bias,
        dt_bias,
        a_log,
        skip,
        gate_gain,
        w_out,
    ) = layer_weights
    inner_width = w_out.shape[0]
    normed = (stream * rms_scale(stream) * norm_gain).astype(jnp.bfloat16)
    gathered = head_gather(normed, tick, ids[0])
    gathered = gathered.reshape(-1, gathered.shape[-1])
    projected = jnp.dot(gathered, w_main, preferred_element_type=jnp.float32)
    gate_pre = projected[:, :inner_width]
    pre_conv = projected[:, inner_width : 2 * inner_width + 2 * N]
    dt_pre = projected[:, 2 * inner_width + 2 * N :]
    marks_float = start_marks.astype(jnp.float32)
    tail_from = pre_conv.shape[0] - KW + 1
    edge_parts = shifted((pre_conv[tail_from:], marks_float[tail_from:]), "seq", 1)
    extended, marks_ext = extend(pre_conv, start_marks, edge_parts[0], edge_parts[1])
    front_fn = partial(local_front, marks_ext, alive_mask)
    front_out, front_pull = jax.vjp(
        front_fn, extended, dt_pre, conv_weight, conv_bias, dt_bias, a_log
    )
    block_parts, b_mat, c_mat, total_decay, total_state = front_out
    neutral = (jnp.ones_like(total_decay), jnp.zeros_like(total_state))
    prefix = entering((total_decay, total_state), "seq", chain_combine, neutral)
    start_state = prefix[1]
    mixed_out, rear_pull = jax.vjp(local_rear, block_parts, b_mat, c_mat, skip, start_state)
    silu_gate = jax.nn.silu(gate_pre)
    gated_mix = mixed_out * silu_gate
    square_total = lax.psum(jnp.sum(gated_mix * gated_mix, axis=-1), "head")
    scale_out = lax.rsqrt(square_total / DI + norm_eps)
    normed_out = (gated_mix * scale_out[:, None] * gate_gain).astype(jnp.bfloat16)
    head_count = lax.axis_size("head")
    branch = head_scatter(
        jnp.dot(normed_out, w_out, preferred_element_type=jnp.float32).reshape(
            head_count, -1, w_out.shape[1]
        ),
        tick,
        ids[1],
    )
    saved = (
        stream,
        gathered,
        gate_pre,
        mixed_out,
        silu_gate,
        gated_mix,
        scale_out,
        normed_out,
        total_decay,
        start_state,
        front_pull,
        rear_pull,
    )
    return stream + branch, saved


def mixer_backward(grad_next, layer_weights, saved, mask_value, tick, ids):
    (
        norm_gain,
        w_main,
        w_low,
        w_bc,
        conv_weight,
        conv_bias,
        dt_bias,
        a_log,
        skip,
        gate_gain,
        w_out,
    ) = layer_weights
    (
        stream,
        gathered,
        gate_pre,
        mixed_out,
        silu_gate,
        gated_mix,
        scale_out,
        normed_out,
        total_decay,
        start_state,
        front_pull,
        rear_pull,
    ) = saved
    inner_width = w_out.shape[0]
    grad_branch = grad_next.astype(jnp.bfloat16)
    shard_rows = head_gather(grad_branch, tick, ids[0])
    shard_rows = shard_rows.reshape(-1, shard_rows.shape[-1])
    g_w_out = lax.dot_general(
        normed_out, shard_rows, (((0,), (0,)), ((), ())), preferred_element_type=jnp.float32
    ) * mask_value
    grad_normed = lax.dot_general(
        shard_rows, w_out, (((1,), (1,)), ((), ())), preferred_element_type=jnp.float32
    )
    weighted = grad_normed * gate_gain
    g_gate_gain = jnp.sum(grad_normed * gated_mix * scale_out[:, None], axis=0)
    cross_sum = lax.psum(jnp.sum(weighted * gated_mix, axis=-1), "head")
    grad_gated = (
        scale_out[:, None] * weighted - gated_mix * (scale_out**3 * cross_sum / DI)[:, None]
    )
    grad_mixed = grad_gated * silu_gate
    grad_gate = (grad_gated * mixed_out * silu_slope(gate_pre)).astype(jnp.bfloat16)
    g_parts, g_b_mat, g_c_mat, g_skip, g_start = rear_pull(grad_mixed)
    neutral = (jnp.ones_like(total_decay), jnp.zeros_like(g_start))
    suffix = entering_2((total_decay, g_start), "seq", chain_combine, neutral)
    after_state = suffix[1]
    grad_decay = jnp.sum(after_state * start_state, axis=(1, 2))
    grad_ext, grad_dt_pre, g_conv_w, g_conv_b, g_dt_bias, g_a_log = front_pull(
        (g_parts, g_b_mat, g_c_mat, grad_decay, after_state)
    )
    returned = shifted(grad_ext[: KW - 1], "seq", -1)
    grad_pre = grad_ext[KW - 1 :]
    tail_from = grad_pre.shape[0] - KW + 1
    grad_pre = jnp.concatenate([grad_pre[:tail_from], grad_pre[tail_from:] + returned], axis=0)
    grad_inner = grad_pre[:, :inner_width].astype(jnp.bfloat16)
    grad_bc = grad_pre[:, inner_width:]
    grad_low = jnp.concatenate([grad_gate, grad_inner, grad_dt_pre.astype(jnp.bfloat16)], axis=1)
    w_bc_float = w_bc.astype(jnp.float32)
    g_low = lax.dot_general(
        gathered, grad_low, (((0,), (0,)), ((), ())), preferred_element_type=jnp.float32
    )
    g_w_bc = lax.dot_general(
        gathered.astype(jnp.float32),
        grad_bc,
        (((0,), (0,)), ((), ())),
        precision=highest,
        preferred_element_type=jnp.float32,
    )
    main_term = lax.dot_general(
        grad_low, w_low, (((1,), (1,)), ((), ())), preferred_element_type=jnp.float32
    )
    side_term = lax.dot_general(
        grad_bc,
        w_bc_float,
        (((1,), (1,)), ((), ())),
        precision=highest,
        preferred_element_type=jnp.float32,
    )
    head_count = lax.axis_size("head")
    grad_normed_in = head_scatter(
        (main_term + side_term).reshape(head_count, -1, main_term.shape[1]), tick, ids[1]
    )
    scale_in = rms_scale(stream)
    g_norm_gain = jnp.sum(grad_normed_in * stream * scale_in, axis=0)
    weighted_in = grad_normed_in * norm_gain
    grad_stream = (
        grad_next
        + scale_in * weighted_in
        - stream * scale_in**3 * jnp.mean(weighted_in * stream, axis=-1, keepdims=True)
    )
    head_part = (
        g_low[:, :inner_width],
        g_low[:, inner_width : 2 * inner_width],
        g_low[:, 2 * inner_width :],
        g_conv_w[:, :inner_width],
        g_conv_b[:inner_width],
        g_dt_bias,
        g_a_log,
        g_skip,
        g_gate_gain,
    )
    shared_part = (g_norm_gain, g_w_bc, g_conv_w[:, inner_width:], g_conv_b[inner_width:])
    return (grad_stream, head_part, shared_part, g_w_out)


def psum_flat(members, axes, kind):
    flat = jnp.concatenate([member.reshape(-1).astype(kind) for member in members])
    total = lax.psum(flat, axes).astype(jnp.float32)
    pieces = []
    start = 0
    for member in members:
        pieces.append(total[start : start + member.size].reshape(member.shape))
        start += member.size
    return tuple(pieces)


def reduce_grads(head_part, shared_part):
    head_sum = psum_flat(head_part, "seq", jnp.bfloat16)
    shared_sum = psum_flat(shared_part, ("seq", "head"), jnp.float32)
    return (head_sum, shared_sum)


def store_slot(buffer, value, slot_index, is_valid):
    current = lax.dynamic_index_in_dim(buffer, slot_index, 0, False)
    return lax.dynamic_update_index_in_dim(
        buffer, jnp.where(is_valid, value, current), slot_index, 0
    )


def on_device(
    inputs,
    cotangent,
    starts,
    live,
    norm_gain,
    w_gate,
    w_in,
    w_bc,
    w_dt,
    conv_x,
    conv_x_bias,
    conv_bc,
    conv_bc_bias,
    dt_bias,
    a_log,
    skip,
    gate_gain,
    w_out,
):
    section_count = lax.axis_size("section")
    section_index = lax.axis_index("section")
    micro_count = inputs.shape[0]
    tick_count = micro_count + section_count - 1
    w_main = jnp.concatenate([w_gate[0], w_in[0], w_bc[0], w_dt[0]], axis=1)
    w_low = jnp.concatenate([w_gate[0], w_in[0], w_dt[0]], axis=1)
    conv_weight = jnp.concatenate([conv_x[0], conv_bc[0]], axis=1).astype(jnp.float32)
    conv_bias = jnp.concatenate([conv_x_bias[0], conv_bc_bias[0]], axis=0)
    layer_weights = (
        norm_gain[0],
        w_main,
        w_low,
        w_bc[0],
        conv_weight,
        conv_bias,
        dt_bias[0],
        a_log[0],
        skip[0],
        gate_gain[0],
        w_out[0],
    )
    row_shape = inputs.shape[1:]
    outputs_all = jnp.zeros((micro_count,) + row_shape, jnp.float32)
    arrived = jnp.zeros(row_shape, jnp.float32)
    ticks = []
    for tick_index in range(tick_count):
        slot_index = tick_index - section_index
        is_valid = (slot_index >= 0) & (slot_index < micro_count)
        clipped = jnp.clip(slot_index, 0, micro_count - 1)
        fresh_rows = lax.dynamic_index_in_dim(inputs, clipped, 0, False).astype(jnp.float32)
        stream = jnp.where(section_index == 0, fresh_rows, arrived)
        start_marks = lax.dynamic_index_in_dim(starts, clipped, 0, False)
        alive_mask = lax.dynamic_index_in_dim(live, clipped, 0, False).astype(jnp.float32)
        result, saved = mixer_forward(
            stream,
            start_marks,
            alive_mask,
            layer_weights,
            (tick_index, -1, micro_count),
            (tick_index, tick_count + tick_index),
        )
        outputs_all = store_slot(outputs_all, result, clipped, is_valid)
        ticks.append((clipped, is_valid, saved))
        if tick_index + 1 < tick_count:
            arrived = shifted(result, "section", 1)
    back_arrived = jnp.zeros(row_shape, jnp.float32)
    input_grads = jnp.zeros((micro_count,) + row_shape, jnp.float32)
    head_total = ()
    shared_total = ()
    for tick_index in range(tick_count):
        clipped, is_valid, saved = ticks[tick_count - 1 - tick_index]
        outer_grad = lax.dynamic_index_in_dim(cotangent, clipped, 0, False).astype(jnp.float32)
        grad_next = jnp.where(section_index == section_count - 1, outer_grad, back_arrived)
        mask_value = is_valid.astype(jnp.float32)
        grad_stream, head_part, shared_part, out_part = mixer_backward(
            grad_next,
            layer_weights,
            saved,
            mask_value,
            (tick_count - 1 - tick_index, -1, micro_count),
            (2 * tick_count + tick_index, 3 * tick_count + tick_index),
        )
        if tick_index == 0:
            out_total = out_part
        else:
            out_total = out_total + out_part
        if tick_index + 1 == tick_count:
            out_total = lax.psum(out_total.astype(jnp.bfloat16), "seq")
        head_part = tuple((member * mask_value for member in head_part))
        shared_part = tuple((member * mask_value for member in shared_part))
        if tick_index == 0:
            head_total = head_part
            shared_total = shared_part
        else:
            head_total = tuple((former + latter for former, latter in zip(head_total, head_part)))
            shared_total = tuple(
                (former + latter for former, latter in zip(shared_total, shared_part))
            )
        input_grads = store_slot(input_grads, grad_stream, clipped, is_valid)
        if tick_index + 1 < tick_count:
            back_arrived = shifted(grad_stream.astype(jnp.bfloat16), "section", -1).astype(
                grad_stream.dtype
            )
    anchor = out_total[0, 0].astype(jnp.float32) * 0.0
    head_total = (head_total[0] + anchor,) + head_total[1:]
    head_total, shared_total = reduce_grads(head_total, shared_total)
    head_total = head_total[:3] + (out_total.astype(jnp.float32),) + head_total[3:]
    return (
        outputs_all[None],
        input_grads[None],
        shared_total[0][None],
        head_total[0][None],
        head_total[1][None],
        shared_total[1][None],
        head_total[2][None],
        head_total[4][None],
        head_total[5][None],
        shared_total[2][None],
        shared_total[3][None],
        head_total[6][None],
        head_total[7][None],
        head_total[8][None],
        head_total[9][None],
        head_total[3][None],
    )


def solution(mesh):
    return jax.shard_map(
        on_device,
        mesh=mesh,
        in_specs=(
            P(None, ("seq", "head"), None),
            P(None, ("seq", "head"), None),
            P(None, "seq"),
            P(None, "seq"),
            P("section", None),
            P("section", None, "head"),
            P("section", None, "head"),
            P("section", None, None),
            P("section", None, "head"),
            P("section", None, "head"),
            P("section", "head"),
            P("section", None, None),
            P("section", None),
            P("section", "head"),
            P("section", "head"),
            P("section", "head"),
            P("section", "head"),
            P("section", "head", None),
        ),
        out_specs=(
            P("section", None, ("seq", "head"), None),
            P("section", None, ("seq", "head"), None),
            P("section", None),
            P("section", None, "head"),
            P("section", None, "head"),
            P("section", None, None),
            P("section", None, "head"),
            P("section", None, "head"),
            P("section", "head"),
            P("section", None, None),
            P("section", None),
            P("section", "head"),
            P("section", "head"),
            P("section", "head"),
            P("section", "head"),
            P("section", "head", None),
        ),
        check_vma=False,
    )
```

```python
from functools import partial

import functools

import jax
import jax.numpy as jnp
from jax import lax
from jax.experimental import pallas as pl
from jax.experimental.pallas import tpu as pltpu
from jax.sharding import PartitionSpec as P

DI = 4096
P_SIZE = 64
N = 128
KW = 4
SCAN_BLOCK = 256


MESH = pl.DeviceIdType.MESH


def _tick_valid(offset, sign, count):
    slot = offset + sign * lax.axis_index("section")
    return jnp.logical_and(slot >= 0, slot < count)


def _enter(barrier, h, n):
    @pl.when(h > 0)
    def _():
        pl.semaphore_signal(barrier, 1, device_id={"head": h - 1}, device_id_type=MESH)

    @pl.when(h < n - 1)
    def _():
        pl.semaphore_signal(barrier, 1, device_id={"head": h + 1}, device_id_type=MESH)

    @pl.when(jnp.logical_and(h > 0, h < n - 1))
    def _():
        pl.semaphore_wait(barrier, 2)

    @pl.when(jnp.logical_or(h == 0, h == n - 1))
    def _():
        pl.semaphore_wait(barrier, 1)


def gather_body(n, tick, x_ref, o_ref, land, send_r, send_l, recv):
    h = lax.axis_index("head")
    valid = _tick_valid(*tick)

    @pl.when(valid)
    def _():
        _enter(pltpu.get_barrier_semaphore(), h, n)

        def copy_right(s, k):
            src = x_ref if s == 0 else land.at[k]
            return pltpu.make_async_remote_copy(
                src_ref=src, dst_ref=land.at[k], send_sem=send_r.at[s], recv_sem=recv.at[k],
                device_id={"head": h + 1}, device_id_type=MESH)

        def copy_left(s, k):
            src = x_ref if s == 0 else land.at[k]
            return pltpu.make_async_remote_copy(
                src_ref=src, dst_ref=land.at[k], send_sem=send_l.at[s], recv_sem=recv.at[k],
                device_id={"head": h - 1}, device_id_type=MESH)

        for s in range(n):
            k_r = h - s
            k_l = h + s
            if s >= 1:
                @pl.when(k_r >= 0)
                def _():
                    pltpu.make_async_remote_copy(
                        src_ref=land.at[k_r], dst_ref=land.at[k_r], send_sem=send_r.at[0],
                        recv_sem=recv.at[k_r], device_id={"head": h}, device_id_type=MESH
                    ).wait_recv()

                @pl.when(k_l <= n - 1)
                def _():
                    pltpu.make_async_remote_copy(
                        src_ref=land.at[k_l], dst_ref=land.at[k_l], send_sem=send_l.at[0],
                        recv_sem=recv.at[k_l], device_id={"head": h}, device_id_type=MESH
                    ).wait_recv()
            if s <= n - 2:
                @pl.when(jnp.logical_and(k_r >= 0, h < n - 1))
                def _():
                    copy_right(s, k_r).start()

                @pl.when(jnp.logical_and(k_l <= n - 1, h > 0))
                def _():
                    copy_left(s, k_l).start()
        land[h] = x_ref[...]
        for s in range(n - 1):
            k_r = h - s
            k_l = h + s

            @pl.when(jnp.logical_and(k_r >= 0, h < n - 1))
            def _():
                copy_right(s, k_r).wait_send()

            @pl.when(jnp.logical_and(k_l <= n - 1, h > 0))
            def _():
                copy_left(s, k_l).wait_send()
        o_ref[...] = land[...]

    @pl.when(jnp.logical_not(valid))
    def _():
        o_ref[...] = jnp.zeros(o_ref.shape, o_ref.dtype)


def head_gather(x, tick, cid):
    n = lax.axis_size("head")
    rows, cols = x.shape
    return pl.pallas_call(
        functools.partial(gather_body, n, tick),
        out_shape=jax.ShapeDtypeStruct((n, rows, cols), x.dtype),
        in_specs=[pl.BlockSpec(memory_space=pltpu.VMEM)],
        out_specs=pl.BlockSpec(memory_space=pltpu.VMEM),
        scratch_shapes=[
            pltpu.VMEM((n, rows, cols), x.dtype),
            pltpu.SemaphoreType.DMA((n,)),
            pltpu.SemaphoreType.DMA((n,)),
            pltpu.SemaphoreType.DMA((n,)),
        ],
        compiler_params=pltpu.CompilerParams(collective_id=cid, has_side_effects=True),
    )(x)


def scatter_body(n, tick, p_ref, o_ref, recv_l, recv_r, send_l, send_r, ssem_l, ssem_r, rsem_l, rsem_r):
    h = lax.axis_index("head")
    valid = _tick_valid(*tick)
    link = send_r.dtype

    @pl.when(valid)
    def _():
        _enter(pltpu.get_barrier_semaphore(), h, n)

        def to_right(k):
            return pltpu.make_async_remote_copy(
                src_ref=send_r.at[k], dst_ref=recv_l.at[k], send_sem=ssem_r.at[k],
                recv_sem=rsem_l.at[k], device_id={"head": h + 1}, device_id_type=MESH)

        def to_left(k):
            return pltpu.make_async_remote_copy(
                src_ref=send_l.at[k], dst_ref=recv_r.at[k], send_sem=ssem_l.at[k],
                recv_sem=rsem_r.at[k], device_id={"head": h - 1}, device_id_type=MESH)

        for s in range(n - 1):
            k_r = n - 1 - s
            k_l = s

            @pl.when(k_r > h)
            def _():
                @pl.when(h > 0)
                def _():
                    to_right(k_r).wait_recv()
                    send_r[k_r] = (p_ref[k_r] + recv_l[k_r].astype(jnp.float32)).astype(link)

                @pl.when(h == 0)
                def _():
                    send_r[k_r] = p_ref[k_r].astype(link)

                to_right(k_r).start()

            @pl.when(k_l < h)
            def _():
                @pl.when(h < n - 1)
                def _():
                    to_left(k_l).wait_recv()
                    send_l[k_l] = (p_ref[k_l] + recv_r[k_l].astype(jnp.float32)).astype(link)

                @pl.when(h == n - 1)
                def _():
                    send_l[k_l] = p_ref[k_l].astype(link)

                to_left(k_l).start()
        total = p_ref[h]

        @pl.when(h > 0)
        def _():
            to_right(h).wait_recv()

        @pl.when(h < n - 1)
        def _():
            to_left(h).wait_recv()

        left_part = jnp.where(h > 0, recv_l[h].astype(jnp.float32), 0.0)
        right_part = jnp.where(h < n - 1, recv_r[h].astype(jnp.float32), 0.0)
        o_ref[...] = (total + left_part + right_part).astype(o_ref.dtype)
        for s in range(n - 1):
            k_r = n - 1 - s
            k_l = s

            @pl.when(k_r > h)
            def _():
                to_right(k_r).wait_send()

            @pl.when(k_l < h)
            def _():
                to_left(k_l).wait_send()

    @pl.when(jnp.logical_not(valid))
    def _():
        o_ref[...] = jnp.zeros(o_ref.shape, o_ref.dtype)


def head_scatter(parts, tick, cid, link=jnp.bfloat16):
    n = lax.axis_size("head")
    _, rows, cols = parts.shape
    return pl.pallas_call(
        functools.partial(scatter_body, n, tick),
        out_shape=jax.ShapeDtypeStruct((rows, cols), jnp.float32),
        in_specs=[pl.BlockSpec(memory_space=pltpu.VMEM)],
        out_specs=pl.BlockSpec(memory_space=pltpu.VMEM),
        scratch_shapes=[
            pltpu.VMEM((n, rows, cols), link),
            pltpu.VMEM((n, rows, cols), link),
            pltpu.VMEM((n, rows, cols), link),
            pltpu.VMEM((n, rows, cols), link),
            pltpu.SemaphoreType.DMA((n,)),
            pltpu.SemaphoreType.DMA((n,)),
            pltpu.SemaphoreType.DMA((n,)),
            pltpu.SemaphoreType.DMA((n,)),
        ],
        compiler_params=pltpu.CompilerParams(collective_id=cid, has_side_effects=True),
    )(parts)


norm_eps = 1e-05
far_below = -1e30
highest = lax.Precision.HIGHEST


def shifted(value, axis, by):
    count = lax.axis_size(axis)
    pairs = [(i, i + by) for i in range(count) if 0 <= i + by < count]
    return lax.ppermute(value, axis, pairs)


def gather_flat(value, axis, kind):
    leaves, tree = jax.tree.flatten(value)
    slabs = []
    for leaf in leaves:
        flat = leaf.reshape(-1).astype(kind or leaf.dtype)
        flat = jnp.pad(flat, (0, -flat.size % 1024))
        slabs.append(flat.reshape(-1, 128))
    everything = lax.all_gather(jnp.concatenate(slabs, axis=0), axis)
    pieces = []
    start = 0
    for leaf, slab in zip(leaves, slabs):
        rows = everything[:, start : start + slab.shape[0]].reshape(everything.shape[0], -1)
        pieces.append(rows[:, : leaf.size].reshape((-1,) + leaf.shape))
        start += slab.shape[0]
    return jax.tree.unflatten(tree, pieces)


def entering(value, axis, combine, identity):
    count, mine = (lax.axis_size(axis), lax.axis_index(axis))
    everything = gather_flat(value, axis, None)
    before = jax.tree.map(
        lambda part, zero: jnp.broadcast_to(jnp.asarray(zero, part.dtype), part.shape),
        value,
        identity,
    )
    for k in range(count - 1):
        reached = k < mine
        new = combine(before, jax.tree.map(lambda part: part[k], everything))
        before = jax.tree.map(lambda a, b: jnp.where(reached, a, b), new, before)
    return before


def entering_2(value, axis, join, neutral):
    count = lax.axis_size(axis)
    place = lax.axis_index(axis)
    ahead = count - 1 - place
    gathered = gather_flat(value, axis, jnp.bfloat16)
    state = jax.tree.map(lambda a, e: jnp.zeros_like(a) + jnp.asarray(e, a.dtype), value, neutral)
    for lap in range(count - 1):
        source = count - 1 - lap
        new = join(
            state,
            jax.tree.map(lambda a, own: a[source].astype(own.dtype), gathered, value),
        )
        active = lap < ahead
        state = jax.tree.map(lambda a, b: jnp.where(active, a, b), new, state)
    return state


def rms_scale(values):
    return lax.rsqrt(jnp.mean(values * values, axis=-1, keepdims=True) + norm_eps)


def silu_slope(values):
    logistic = jax.nn.sigmoid(values)
    return logistic * (1.0 + values * (1.0 - logistic))


def causal_conv(extended, marks_ext, weight, conv_bias):
    tap_count = weight.shape[0]
    length = extended.shape[0] - tap_count + 1
    counts = jnp.cumsum(marks_ext)
    conv_sum = jnp.zeros((length, extended.shape[1]), jnp.float32) + conv_bias
    for tap_index in range(tap_count):
        linked = (counts[tap_count - 1 :] == counts[tap_index : tap_index + length]).astype(
            jnp.float32
        )
        conv_sum = (
            conv_sum
            + linked[:, None] * weight[tap_index] * extended[tap_index : tap_index + length]
        )
    return conv_sum


def prepare(extended, dt_pre, marks_ext, alive_mask, conv_weight, conv_bias, dt_bias, a_log):
    inner_width = dt_pre.shape[1] * P_SIZE
    activated = jax.nn.silu(causal_conv(extended, marks_ext, conv_weight, conv_bias))
    inner_act = activated[:, :inner_width] * alive_mask[:, None]
    b_mat = activated[:, inner_width : inner_width + N]
    c_mat = activated[:, inner_width + N :]
    step_size = jax.nn.softplus(dt_pre + dt_bias) * alive_mask[:, None]
    log_decay = -step_size * jnp.exp(a_log)
    return (inner_act, step_size, log_decay, b_mat, c_mat)


def block_terms(inner_act, step_size, log_decay, b_mat, start_marks):
    blocks = inner_act.shape[0] // SCAN_BLOCK
    head_count = step_size.shape[1]
    x_blocks = inner_act.reshape(blocks, SCAN_BLOCK, head_count, P_SIZE)
    dt_blocks = step_size.reshape(blocks, SCAN_BLOCK, head_count)
    cum_decay = jnp.cumsum(log_decay.reshape(blocks, SCAN_BLOCK, head_count), axis=1)
    mark_count = jnp.cumsum(start_marks.reshape(blocks, SCAN_BLOCK), axis=1)
    b_blocks = b_mat.reshape(blocks, SCAN_BLOCK, N)
    last_cum = cum_decay[:, -1]
    last_mark = mark_count[:, -1]
    same_end = (mark_count == last_mark[:, None]).astype(jnp.float32)
    end_weight = jnp.exp(last_cum[:, None, :] - cum_decay) * same_end[:, :, None] * dt_blocks
    block_states = jnp.einsum(
        "cjh,cjhp,cjn->chpn", end_weight, x_blocks, b_blocks, precision=highest
    )
    block_decay = jnp.exp(last_cum) * (last_mark == 0).astype(jnp.float32)[:, None]
    return (block_decay, block_states, cum_decay, mark_count, x_blocks, dt_blocks)


def compose_blocks(block_decay, block_states, start_state):
    chain_state = start_state
    incoming = []
    for block_index in range(block_decay.shape[0]):
        incoming.append(chain_state)
        chain_state = (
            block_decay[block_index][:, None, None] * chain_state + block_states[block_index]
        )
    return (chain_state, jnp.stack(incoming))


def block_output(block_parts, b_mat, c_mat, skip, incoming):
    block_decay, block_states, cum_decay, mark_count, x_blocks, dt_blocks = block_parts
    blocks = cum_decay.shape[0]
    head_count = cum_decay.shape[2]
    b_blocks = b_mat.reshape(blocks, SCAN_BLOCK, N)
    c_blocks = c_mat.reshape(blocks, SCAN_BLOCK, N)
    inner_prod = jnp.einsum("cin,cjn->cij", c_blocks, b_blocks, precision=highest)
    arange_pos = jnp.arange(SCAN_BLOCK)
    linked = (arange_pos[:, None] >= arange_pos[None, :])[None] & (
        mark_count[:, :, None] == mark_count[:, None, :]
    )
    spread = jnp.where(
        linked[..., None], cum_decay[:, :, None, :] - cum_decay[:, None, :, :], far_below
    )
    weights = jnp.exp(spread) * inner_prod[..., None] * dt_blocks[:, None, :, :]
    y_intra = jnp.einsum("cijh,cjhp->cihp", weights, x_blocks, precision=highest)
    carry_in = jnp.exp(cum_decay) * (mark_count == 0).astype(jnp.float32)[:, :, None]
    y_inter = (
        jnp.einsum("cin,chpn->cihp", c_blocks, incoming, precision=highest) * carry_in[..., None]
    )
    mixed_out = y_intra + y_inter + skip[None, None, :, None] * x_blocks
    return mixed_out.reshape(blocks * SCAN_BLOCK, head_count * P_SIZE)


def local_front(marks_ext, alive_mask, extended, dt_pre, conv_weight, conv_bias, dt_bias, a_log):
    inner_act, step_size, log_decay, b_mat, c_mat = prepare(
        extended, dt_pre, marks_ext, alive_mask, conv_weight, conv_bias, dt_bias, a_log
    )
    block_parts = block_terms(inner_act, step_size, log_decay, b_mat, marks_ext[KW - 1 :])
    zero_state = jnp.zeros(block_parts[1].shape[1:], jnp.float32)
    total_state, _ = compose_blocks(block_parts[0], block_parts[1], zero_state)
    total_decay = jnp.prod(block_parts[0], axis=0)
    return (block_parts, b_mat, c_mat, total_decay, total_state)


def local_rear(block_parts, b_mat, c_mat, skip, start_state):
    _, incoming = compose_blocks(block_parts[0], block_parts[1], start_state)
    return block_output(block_parts, b_mat, c_mat, skip, incoming)


def local_pass(
    marks_ext,
    alive_mask,
    extended,
    dt_pre,
    conv_weight,
    conv_bias,
    dt_bias,
    a_log,
    skip,
    start_state,
):
    block_parts, b_mat, c_mat, total_decay, total_state = local_front(
        marks_ext, alive_mask, extended, dt_pre, conv_weight, conv_bias, dt_bias, a_log
    )
    return (local_rear(block_parts, b_mat, c_mat, skip, start_state), total_decay, total_state)


def chain_combine(earlier, later):
    return (earlier[0] * later[0], later[0][:, None, None] * earlier[1] + later[1])


def extend(pre_conv, start_marks, edge_rows, edge_marks):
    extended = jnp.concatenate([edge_rows, pre_conv], axis=0)
    marks_ext = jnp.concatenate([edge_marks.astype(jnp.int32), start_marks], axis=0)
    return (extended, marks_ext)


def mixer_forward(stream, start_marks, alive_mask, layer_weights, tick, ids):
    (
        norm_gain,
        w_main,
        w_low,
        w_bc,
        conv_weight,
        conv_bias,
        dt_bias,
        a_log,
        skip,
        gate_gain,
        w_out,
    ) = layer_weights
    inner_width = w_out.shape[0]
    normed = (stream * rms_scale(stream) * norm_gain).astype(jnp.bfloat16)
    gathered = head_gather(normed, tick, ids[0])
    gathered = gathered.reshape(-1, gathered.shape[-1])
    projected = jnp.dot(gathered, w_main, preferred_element_type=jnp.float32)
    gate_pre = projected[:, :inner_width]
    pre_conv = projected[:, inner_width : 2 * inner_width + 2 * N]
    dt_pre = projected[:, 2 * inner_width + 2 * N :]
    marks_float = start_marks.astype(jnp.float32)
    tail_from = pre_conv.shape[0] - KW + 1
    edge_parts = shifted((pre_conv[tail_from:], marks_float[tail_from:]), "seq", 1)
    extended, marks_ext = extend(pre_conv, start_marks, edge_parts[0], edge_parts[1])
    front_fn = partial(local_front, marks_ext, alive_mask)
    front_out, front_pull = jax.vjp(
        front_fn, extended, dt_pre, conv_weight, conv_bias, dt_bias, a_log
    )
    block_parts, b_mat, c_mat, total_decay, total_state = front_out
    neutral = (jnp.ones_like(total_decay), jnp.zeros_like(total_state))
    prefix = entering((total_decay, total_state), "seq", chain_combine, neutral)
    start_state = prefix[1]
    mixed_out, rear_pull = jax.vjp(local_rear, block_parts, b_mat, c_mat, skip, start_state)
    silu_gate = jax.nn.silu(gate_pre)
    gated_mix = mixed_out * silu_gate
    square_total = lax.psum(jnp.sum(gated_mix * gated_mix, axis=-1), "head")
    scale_out = lax.rsqrt(square_total / DI + norm_eps)
    normed_out = (gated_mix * scale_out[:, None] * gate_gain).astype(jnp.bfloat16)
    head_count = lax.axis_size("head")
    branch = head_scatter(
        jnp.dot(normed_out, w_out, preferred_element_type=jnp.float32).reshape(
            head_count, -1, w_out.shape[1]
        ),
        tick,
        ids[1],
    )
    saved = (
        stream,
        gathered,
        gate_pre,
        mixed_out,
        silu_gate,
        gated_mix,
        scale_out,
        normed_out,
        total_decay,
        start_state,
        front_pull,
        rear_pull,
    )
    return stream + branch, saved


def mixer_backward(grad_next, layer_weights, saved, mask_value, tick, ids):
    (
        norm_gain,
        w_main,
        w_low,
        w_bc,
        conv_weight,
        conv_bias,
        dt_bias,
        a_log,
        skip,
        gate_gain,
        w_out,
    ) = layer_weights
    (
        stream,
        gathered,
        gate_pre,
        mixed_out,
        silu_gate,
        gated_mix,
        scale_out,
        normed_out,
        total_decay,
        start_state,
        front_pull,
        rear_pull,
    ) = saved
    inner_width = w_out.shape[0]
    grad_branch = grad_next.astype(jnp.bfloat16)
    shard_rows = head_gather(grad_branch, tick, ids[0])
    shard_rows = shard_rows.reshape(-1, shard_rows.shape[-1])
    g_w_out = lax.dot_general(
        normed_out, shard_rows, (((0,), (0,)), ((), ())), preferred_element_type=jnp.float32
    ) * mask_value
    grad_normed = lax.dot_general(
        shard_rows, w_out, (((1,), (1,)), ((), ())), preferred_element_type=jnp.float32
    )
    weighted = grad_normed * gate_gain
    g_gate_gain = jnp.sum(grad_normed * gated_mix * scale_out[:, None], axis=0)
    cross_sum = lax.psum(jnp.sum(weighted * gated_mix, axis=-1), "head")
    grad_gated = (
        scale_out[:, None] * weighted - gated_mix * (scale_out**3 * cross_sum / DI)[:, None]
    )
    grad_mixed = grad_gated * silu_gate
    grad_gate = (grad_gated * mixed_out * silu_slope(gate_pre)).astype(jnp.bfloat16)
    g_parts, g_b_mat, g_c_mat, g_skip, g_start = rear_pull(grad_mixed)
    neutral = (jnp.ones_like(total_decay), jnp.zeros_like(g_start))
    suffix = entering_2((total_decay, g_start), "seq", chain_combine, neutral)
    after_state = suffix[1]
    grad_decay = jnp.sum(after_state * start_state, axis=(1, 2))
    grad_ext, grad_dt_pre, g_conv_w, g_conv_b, g_dt_bias, g_a_log = front_pull(
        (g_parts, g_b_mat, g_c_mat, grad_decay, after_state)
    )
    returned = shifted(grad_ext[: KW - 1], "seq", -1)
    grad_pre = grad_ext[KW - 1 :]
    tail_from = grad_pre.shape[0] - KW + 1
    grad_pre = jnp.concatenate([grad_pre[:tail_from], grad_pre[tail_from:] + returned], axis=0)
    grad_inner = grad_pre[:, :inner_width].astype(jnp.bfloat16)
    grad_bc = grad_pre[:, inner_width:]
    grad_low = jnp.concatenate([grad_gate, grad_inner, grad_dt_pre.astype(jnp.bfloat16)], axis=1)
    w_bc_float = w_bc.astype(jnp.float32)
    g_low = lax.dot_general(
        gathered, grad_low, (((0,), (0,)), ((), ())), preferred_element_type=jnp.float32
    )
    g_w_bc = lax.dot_general(
        gathered.astype(jnp.float32),
        grad_bc,
        (((0,), (0,)), ((), ())),
        precision=highest,
        preferred_element_type=jnp.float32,
    )
    main_term = lax.dot_general(
        grad_low, w_low, (((1,), (1,)), ((), ())), preferred_element_type=jnp.float32
    )
    side_term = lax.dot_general(
        grad_bc,
        w_bc_float,
        (((1,), (1,)), ((), ())),
        precision=highest,
        preferred_element_type=jnp.float32,
    )
    head_count = lax.axis_size("head")
    grad_normed_in = head_scatter(
        (main_term + side_term).reshape(head_count, -1, main_term.shape[1]), tick, ids[1]
    )
    scale_in = rms_scale(stream)
    g_norm_gain = jnp.sum(grad_normed_in * stream * scale_in, axis=0)
    weighted_in = grad_normed_in * norm_gain
    grad_stream = (
        grad_next
        + scale_in * weighted_in
        - stream * scale_in**3 * jnp.mean(weighted_in * stream, axis=-1, keepdims=True)
    )
    head_part = (
        g_low[:, :inner_width],
        g_low[:, inner_width : 2 * inner_width],
        g_low[:, 2 * inner_width :],
        g_conv_w[:, :inner_width],
        g_conv_b[:inner_width],
        g_dt_bias,
        g_a_log,
        g_skip,
        g_gate_gain,
    )
    shared_part = (g_norm_gain, g_w_bc, g_conv_w[:, inner_width:], g_conv_b[inner_width:])
    return (grad_stream, head_part, shared_part, g_w_out)


def psum_packed(big, small, axes, kind):
    host = big[0]
    width = host.shape[-1]
    flat = jnp.concatenate([member.reshape(-1).astype(kind) for member in small])
    flat = jnp.pad(flat, (0, -flat.size % (16 * width)))
    joined = jnp.concatenate([host.reshape(-1, width).astype(kind), flat.reshape(-1, width)])
    summed = lax.psum((joined,) + tuple(member.astype(kind) for member in big[1:]), axes)
    joined = summed[0].astype(jnp.float32)
    pieces = [joined[: host.size // width].reshape(host.shape)]
    pieces += [member.astype(jnp.float32) for member in summed[1:]]
    packed = joined[host.size // width :].reshape(-1)
    start = 0
    for member in small:
        pieces.append(packed[start : start + member.size].reshape(member.shape))
        start += member.size
    return tuple(pieces)


def reduce_grads(head_part, shared_part):
    head_sum = psum_packed(head_part[:3], head_part[3:], "seq", jnp.bfloat16)
    shared = psum_packed(
        (shared_part[1],), (shared_part[0],) + shared_part[2:], ("seq", "head"), jnp.float32
    )
    shared_sum = (shared[1], shared[0]) + shared[2:]
    return (head_sum, shared_sum)


def store_slot(buffer, value, slot_index, is_valid):
    current = lax.dynamic_index_in_dim(buffer, slot_index, 0, False)
    return lax.dynamic_update_index_in_dim(
        buffer, jnp.where(is_valid, value, current), slot_index, 0
    )


def on_device(
    inputs,
    cotangent,
    starts,
    live,
    norm_gain,
    w_gate,
    w_in,
    w_bc,
    w_dt,
    conv_x,
    conv_x_bias,
    conv_bc,
    conv_bc_bias,
    dt_bias,
    a_log,
    skip,
    gate_gain,
    w_out,
):
    section_count = lax.axis_size("section")
    section_index = lax.axis_index("section")
    micro_count = inputs.shape[0]
    tick_count = micro_count + section_count - 1
    w_main = jnp.concatenate([w_gate[0], w_in[0], w_bc[0], w_dt[0]], axis=1)
    w_low = jnp.concatenate([w_gate[0], w_in[0], w_dt[0]], axis=1)
    conv_weight = jnp.concatenate([conv_x[0], conv_bc[0]], axis=1).astype(jnp.float32)
    conv_bias = jnp.concatenate([conv_x_bias[0], conv_bc_bias[0]], axis=0)
    layer_weights = (
        norm_gain[0],
        w_main,
        w_low,
        w_bc[0],
        conv_weight,
        conv_bias,
        dt_bias[0],
        a_log[0],
        skip[0],
        gate_gain[0],
        w_out[0],
    )
    row_shape = inputs.shape[1:]
    outputs_all = jnp.zeros((micro_count,) + row_shape, jnp.float32)
    arrived = jnp.zeros(row_shape, jnp.float32)
    ticks = []
    for tick_index in range(tick_count):
        slot_index = tick_index - section_index
        is_valid = (slot_index >= 0) & (slot_index < micro_count)
        clipped = jnp.clip(slot_index, 0, micro_count - 1)
        fresh_rows = lax.dynamic_index_in_dim(inputs, clipped, 0, False).astype(jnp.float32)
        stream = jnp.where(section_index == 0, fresh_rows, arrived)
        start_marks = lax.dynamic_index_in_dim(starts, clipped, 0, False)
        alive_mask = lax.dynamic_index_in_dim(live, clipped, 0, False).astype(jnp.float32)
        result, saved = mixer_forward(
            stream,
            start_marks,
            alive_mask,
            layer_weights,
            (tick_index, -1, micro_count),
            (tick_index, tick_count + tick_index),
        )
        outputs_all = store_slot(outputs_all, result, clipped, is_valid)
        ticks.append((clipped, is_valid, saved))
        if tick_index + 1 < tick_count:
            arrived = shifted(result, "section", 1)
    back_arrived = jnp.zeros(row_shape, jnp.float32)
    input_grads = jnp.zeros((micro_count,) + row_shape, jnp.float32)
    head_total = ()
    shared_total = ()
    for tick_index in range(tick_count):
        clipped, is_valid, saved = ticks[tick_count - 1 - tick_index]
        outer_grad = lax.dynamic_index_in_dim(cotangent, clipped, 0, False).astype(jnp.float32)
        grad_next = jnp.where(section_index == section_count - 1, outer_grad, back_arrived)
        mask_value = is_valid.astype(jnp.float32)
        grad_stream, head_part, shared_part, out_part = mixer_backward(
            grad_next,
            layer_weights,
            saved,
            mask_value,
            (tick_count - 1 - tick_index, -1, micro_count),
            (2 * tick_count + tick_index, 3 * tick_count + tick_index),
        )
        if tick_index == 0:
            out_total = out_part
        else:
            out_total = out_total + out_part
        if tick_index + 1 == tick_count:
            out_total = lax.psum(out_total.astype(jnp.bfloat16), "seq")
        head_part = tuple((member * mask_value for member in head_part))
        shared_part = tuple((member * mask_value for member in shared_part))
        if tick_index == 0:
            head_total = head_part
            shared_total = shared_part
        else:
            head_total = tuple((former + latter for former, latter in zip(head_total, head_part)))
            shared_total = tuple(
                (former + latter for former, latter in zip(shared_total, shared_part))
            )
        input_grads = store_slot(input_grads, grad_stream, clipped, is_valid)
        if tick_index + 1 < tick_count:
            back_arrived = shifted(grad_stream.astype(jnp.bfloat16), "section", -1).astype(
                grad_stream.dtype
            )
    anchor = out_total[0, 0].astype(jnp.float32) * 0.0
    head_total = (head_total[0] + anchor,) + head_total[1:]
    head_total, shared_total = reduce_grads(head_total, shared_total)
    head_total = head_total[:3] + (out_total.astype(jnp.float32),) + head_total[3:]
    return (
        outputs_all[None],
        input_grads[None],
        shared_total[0][None],
        head_total[0][None],
        head_total[1][None],
        shared_total[1][None],
        head_total[2][None],
        head_total[4][None],
        head_total[5][None],
        shared_total[2][None],
        shared_total[3][None],
        head_total[6][None],
        head_total[7][None],
        head_total[8][None],
        head_total[9][None],
        head_total[3][None],
    )


def solution(mesh):
    return jax.shard_map(
        on_device,
        mesh=mesh,
        in_specs=(
            P(None, ("seq", "head"), None),
            P(None, ("seq", "head"), None),
            P(None, "seq"),
            P(None, "seq"),
            P("section", None),
            P("section", None, "head"),
            P("section", None, "head"),
            P("section", None, None),
            P("section", None, "head"),
            P("section", None, "head"),
            P("section", "head"),
            P("section", None, None),
            P("section", None),
            P("section", "head"),
            P("section", "head"),
            P("section", "head"),
            P("section", "head"),
            P("section", "head", None),
        ),
        out_specs=(
            P("section", None, ("seq", "head"), None),
            P("section", None, ("seq", "head"), None),
            P("section", None),
            P("section", None, "head"),
            P("section", None, "head"),
            P("section", None, None),
            P("section", None, "head"),
            P("section", None, "head"),
            P("section", "head"),
            P("section", None, None),
            P("section", None),
            P("section", "head"),
            P("section", "head"),
            P("section", "head"),
            P("section", "head"),
            P("section", "head", None),
        ),
        check_vma=False,
    )
```

```python
from functools import partial

import functools

import jax
import jax.numpy as jnp
from jax import lax
from jax.experimental import pallas as pl
from jax.experimental.pallas import tpu as pltpu
from jax.sharding import PartitionSpec as P

DI = 4096
P_SIZE = 64
N = 128
KW = 4
SCAN_BLOCK = 256


MESH = pl.DeviceIdType.MESH


def _tick_valid(offset, sign, count):
    slot = offset + sign * lax.axis_index("section")
    return jnp.logical_and(slot >= 0, slot < count)


def _enter(barrier, h, n):
    @pl.when(h > 0)
    def _():
        pl.semaphore_signal(barrier, 1, device_id={"head": h - 1}, device_id_type=MESH)

    @pl.when(h < n - 1)
    def _():
        pl.semaphore_signal(barrier, 1, device_id={"head": h + 1}, device_id_type=MESH)

    @pl.when(jnp.logical_and(h > 0, h < n - 1))
    def _():
        pl.semaphore_wait(barrier, 2)

    @pl.when(jnp.logical_or(h == 0, h == n - 1))
    def _():
        pl.semaphore_wait(barrier, 1)


def gather_body(n, tick, x_ref, o_ref, land, send_r, send_l, recv):
    h = lax.axis_index("head")
    valid = _tick_valid(*tick)

    @pl.when(valid)
    def _():
        _enter(pltpu.get_barrier_semaphore(), h, n)

        def copy_right(s, k):
            src = x_ref if s == 0 else land.at[k]
            return pltpu.make_async_remote_copy(
                src_ref=src, dst_ref=land.at[k], send_sem=send_r.at[s], recv_sem=recv.at[k],
                device_id={"head": h + 1}, device_id_type=MESH)

        def copy_left(s, k):
            src = x_ref if s == 0 else land.at[k]
            return pltpu.make_async_remote_copy(
                src_ref=src, dst_ref=land.at[k], send_sem=send_l.at[s], recv_sem=recv.at[k],
                device_id={"head": h - 1}, device_id_type=MESH)

        for s in range(n):
            k_r = h - s
            k_l = h + s
            if s >= 1:
                @pl.when(k_r >= 0)
                def _():
                    pltpu.make_async_remote_copy(
                        src_ref=land.at[k_r], dst_ref=land.at[k_r], send_sem=send_r.at[0],
                        recv_sem=recv.at[k_r], device_id={"head": h}, device_id_type=MESH
                    ).wait_recv()

                @pl.when(k_l <= n - 1)
                def _():
                    pltpu.make_async_remote_copy(
                        src_ref=land.at[k_l], dst_ref=land.at[k_l], send_sem=send_l.at[0],
                        recv_sem=recv.at[k_l], device_id={"head": h}, device_id_type=MESH
                    ).wait_recv()
            if s <= n - 2:
                @pl.when(jnp.logical_and(k_r >= 0, h < n - 1))
                def _():
                    copy_right(s, k_r).start()

                @pl.when(jnp.logical_and(k_l <= n - 1, h > 0))
                def _():
                    copy_left(s, k_l).start()
        land[h] = x_ref[...]
        for s in range(n - 1):
            k_r = h - s
            k_l = h + s

            @pl.when(jnp.logical_and(k_r >= 0, h < n - 1))
            def _():
                copy_right(s, k_r).wait_send()

            @pl.when(jnp.logical_and(k_l <= n - 1, h > 0))
            def _():
                copy_left(s, k_l).wait_send()
        o_ref[...] = land[...]

    @pl.when(jnp.logical_not(valid))
    def _():
        o_ref[...] = jnp.zeros(o_ref.shape, o_ref.dtype)


def head_gather(x, tick, cid):
    n = lax.axis_size("head")
    rows, cols = x.shape
    return pl.pallas_call(
        functools.partial(gather_body, n, tick),
        out_shape=jax.ShapeDtypeStruct((n, rows, cols), x.dtype),
        in_specs=[pl.BlockSpec(memory_space=pltpu.VMEM)],
        out_specs=pl.BlockSpec(memory_space=pltpu.VMEM),
        scratch_shapes=[
            pltpu.VMEM((n, rows, cols), x.dtype),
            pltpu.SemaphoreType.DMA((n,)),
            pltpu.SemaphoreType.DMA((n,)),
            pltpu.SemaphoreType.DMA((n,)),
        ],
        compiler_params=pltpu.CompilerParams(collective_id=cid, has_side_effects=True),
    )(x)


def scatter_body(n, tick, p_ref, o_ref, recv_l, recv_r, send_l, send_r, ssem_l, ssem_r, rsem_l, rsem_r):
    h = lax.axis_index("head")
    valid = _tick_valid(*tick)
    link = send_r.dtype

    @pl.when(valid)
    def _():
        _enter(pltpu.get_barrier_semaphore(), h, n)

        def to_right(k):
            return pltpu.make_async_remote_copy(
                src_ref=send_r.at[k], dst_ref=recv_l.at[k], send_sem=ssem_r.at[k],
                recv_sem=rsem_l.at[k], device_id={"head": h + 1}, device_id_type=MESH)

        def to_left(k):
            return pltpu.make_async_remote_copy(
                src_ref=send_l.at[k], dst_ref=recv_r.at[k], send_sem=ssem_l.at[k],
                recv_sem=rsem_r.at[k], device_id={"head": h - 1}, device_id_type=MESH)

        for s in range(n - 1):
            k_r = n - 1 - s
            k_l = s

            @pl.when(k_r > h)
            def _():
                @pl.when(h > 0)
                def _():
                    to_right(k_r).wait_recv()
                    send_r[k_r] = (p_ref[k_r] + recv_l[k_r].astype(jnp.float32)).astype(link)

                @pl.when(h == 0)
                def _():
                    send_r[k_r] = p_ref[k_r].astype(link)

                to_right(k_r).start()

            @pl.when(k_l < h)
            def _():
                @pl.when(h < n - 1)
                def _():
                    to_left(k_l).wait_recv()
                    send_l[k_l] = (p_ref[k_l] + recv_r[k_l].astype(jnp.float32)).astype(link)

                @pl.when(h == n - 1)
                def _():
                    send_l[k_l] = p_ref[k_l].astype(link)

                to_left(k_l).start()
        total = p_ref[h]

        @pl.when(h > 0)
        def _():
            to_right(h).wait_recv()

        @pl.when(h < n - 1)
        def _():
            to_left(h).wait_recv()

        left_part = jnp.where(h > 0, recv_l[h].astype(jnp.float32), 0.0)
        right_part = jnp.where(h < n - 1, recv_r[h].astype(jnp.float32), 0.0)
        o_ref[...] = (total + left_part + right_part).astype(o_ref.dtype)
        for s in range(n - 1):
            k_r = n - 1 - s
            k_l = s

            @pl.when(k_r > h)
            def _():
                to_right(k_r).wait_send()

            @pl.when(k_l < h)
            def _():
                to_left(k_l).wait_send()

    @pl.when(jnp.logical_not(valid))
    def _():
        o_ref[...] = jnp.zeros(o_ref.shape, o_ref.dtype)


def head_scatter(parts, tick, cid, link=jnp.bfloat16):
    n = lax.axis_size("head")
    _, rows, cols = parts.shape
    return pl.pallas_call(
        functools.partial(scatter_body, n, tick),
        out_shape=jax.ShapeDtypeStruct((rows, cols), jnp.float32),
        in_specs=[pl.BlockSpec(memory_space=pltpu.VMEM)],
        out_specs=pl.BlockSpec(memory_space=pltpu.VMEM),
        scratch_shapes=[
            pltpu.VMEM((n, rows, cols), link),
            pltpu.VMEM((n, rows, cols), link),
            pltpu.VMEM((n, rows, cols), link),
            pltpu.VMEM((n, rows, cols), link),
            pltpu.SemaphoreType.DMA((n,)),
            pltpu.SemaphoreType.DMA((n,)),
            pltpu.SemaphoreType.DMA((n,)),
            pltpu.SemaphoreType.DMA((n,)),
        ],
        compiler_params=pltpu.CompilerParams(collective_id=cid, has_side_effects=True),
    )(parts)


norm_eps = 1e-05
far_below = -1e30
highest = lax.Precision.HIGHEST


def shifted(value, axis, by):
    count = lax.axis_size(axis)
    pairs = [(i, i + by) for i in range(count) if 0 <= i + by < count]
    return lax.ppermute(value, axis, pairs)


def entering(value, axis, combine, identity):
    count, mine = (lax.axis_size(axis), lax.axis_index(axis))
    everything = jax.tree.map(lambda part: lax.all_gather(part, axis), value)
    before = jax.tree.map(
        lambda part, zero: jnp.broadcast_to(jnp.asarray(zero, part.dtype), part.shape),
        value,
        identity,
    )
    for k in range(count - 1):
        reached = k < mine
        new = combine(before, jax.tree.map(lambda part: part[k], everything))
        before = jax.tree.map(lambda a, b: jnp.where(reached, a, b), new, before)
    return before


def entering_2(value, axis, join, neutral):
    count = lax.axis_size(axis)
    place = lax.axis_index(axis)
    ahead = count - 1 - place
    gathered = jax.tree.map(
        lambda a, kind: lax.all_gather(a.astype(kind), axis),
        value,
        jax.tree.map(lambda a: jnp.bfloat16 if a.dtype == jnp.float32 else a.dtype, value),
    )
    state = jax.tree.map(lambda a, e: jnp.zeros_like(a) + jnp.asarray(e, a.dtype), value, neutral)
    for lap in range(count - 1):
        source = count - 1 - lap
        new = join(
            state,
            jax.tree.map(lambda a, own: a[source].astype(own.dtype), gathered, value),
        )
        active = lap < ahead
        state = jax.tree.map(lambda a, b: jnp.where(active, a, b), new, state)
    return state


def rms_scale(values):
    return lax.rsqrt(jnp.mean(values * values, axis=-1, keepdims=True) + norm_eps)


def silu_slope(values):
    logistic = jax.nn.sigmoid(values)
    return logistic * (1.0 + values * (1.0 - logistic))


def causal_conv(extended, marks_ext, weight, conv_bias):
    tap_count = weight.shape[0]
    length = extended.shape[0] - tap_count + 1
    counts = jnp.cumsum(marks_ext)
    conv_sum = jnp.zeros((length, extended.shape[1]), jnp.float32) + conv_bias
    for tap_index in range(tap_count):
        linked = (counts[tap_count - 1 :] == counts[tap_index : tap_index + length]).astype(
            jnp.float32
        )
        conv_sum = (
            conv_sum
            + linked[:, None] * weight[tap_index] * extended[tap_index : tap_index + length]
        )
    return conv_sum


def prepare(extended, dt_pre, marks_ext, alive_mask, conv_weight, conv_bias, dt_bias, a_log):
    inner_width = dt_pre.shape[1] * P_SIZE
    activated = jax.nn.silu(causal_conv(extended, marks_ext, conv_weight, conv_bias))
    inner_act = activated[:, :inner_width] * alive_mask[:, None]
    b_mat = activated[:, inner_width : inner_width + N]
    c_mat = activated[:, inner_width + N :]
    step_size = jax.nn.softplus(dt_pre + dt_bias) * alive_mask[:, None]
    log_decay = -step_size * jnp.exp(a_log)
    return (inner_act, step_size, log_decay, b_mat, c_mat)


def block_terms(inner_act, step_size, log_decay, b_mat, start_marks):
    blocks = inner_act.shape[0] // SCAN_BLOCK
    head_count = step_size.shape[1]
    x_blocks = inner_act.reshape(blocks, SCAN_BLOCK, head_count, P_SIZE)
    dt_blocks = step_size.reshape(blocks, SCAN_BLOCK, head_count)
    cum_decay = jnp.cumsum(log_decay.reshape(blocks, SCAN_BLOCK, head_count), axis=1)
    mark_count = jnp.cumsum(start_marks.reshape(blocks, SCAN_BLOCK), axis=1)
    b_blocks = b_mat.reshape(blocks, SCAN_BLOCK, N)
    last_cum = cum_decay[:, -1]
    last_mark = mark_count[:, -1]
    same_end = (mark_count == last_mark[:, None]).astype(jnp.float32)
    end_weight = jnp.exp(last_cum[:, None, :] - cum_decay) * same_end[:, :, None] * dt_blocks
    block_states = jnp.einsum(
        "cjh,cjhp,cjn->chpn", end_weight, x_blocks, b_blocks, precision=highest
    )
    block_decay = jnp.exp(last_cum) * (last_mark == 0).astype(jnp.float32)[:, None]
    return (block_decay, block_states, cum_decay, mark_count, x_blocks, dt_blocks)


def compose_blocks(block_decay, block_states, start_state):
    chain_state = start_state
    incoming = []
    for block_index in range(block_decay.shape[0]):
        incoming.append(chain_state)
        chain_state = (
            block_decay[block_index][:, None, None] * chain_state + block_states[block_index]
        )
    return (chain_state, jnp.stack(incoming))


def block_output(block_parts, b_mat, c_mat, skip, incoming):
    block_decay, block_states, cum_decay, mark_count, x_blocks, dt_blocks = block_parts
    blocks = cum_decay.shape[0]
    head_count = cum_decay.shape[2]
    b_blocks = b_mat.reshape(blocks, SCAN_BLOCK, N)
    c_blocks = c_mat.reshape(blocks, SCAN_BLOCK, N)
    inner_prod = jnp.einsum("cin,cjn->cij", c_blocks, b_blocks, precision=highest)
    arange_pos = jnp.arange(SCAN_BLOCK)
    linked = (arange_pos[:, None] >= arange_pos[None, :])[None] & (
        mark_count[:, :, None] == mark_count[:, None, :]
    )
    spread = jnp.where(
        linked[..., None], cum_decay[:, :, None, :] - cum_decay[:, None, :, :], far_below
    )
    weights = jnp.exp(spread) * inner_prod[..., None] * dt_blocks[:, None, :, :]
    y_intra = jnp.einsum("cijh,cjhp->cihp", weights, x_blocks, precision=highest)
    carry_in = jnp.exp(cum_decay) * (mark_count == 0).astype(jnp.float32)[:, :, None]
    y_inter = (
        jnp.einsum("cin,chpn->cihp", c_blocks, incoming, precision=highest) * carry_in[..., None]
    )
    mixed_out = y_intra + y_inter + skip[None, None, :, None] * x_blocks
    return mixed_out.reshape(blocks * SCAN_BLOCK, head_count * P_SIZE)


def local_front(marks_ext, alive_mask, extended, dt_pre, conv_weight, conv_bias, dt_bias, a_log):
    inner_act, step_size, log_decay, b_mat, c_mat = prepare(
        extended, dt_pre, marks_ext, alive_mask, conv_weight, conv_bias, dt_bias, a_log
    )
    block_parts = block_terms(inner_act, step_size, log_decay, b_mat, marks_ext[KW - 1 :])
    zero_state = jnp.zeros(block_parts[1].shape[1:], jnp.float32)
    total_state, _ = compose_blocks(block_parts[0], block_parts[1], zero_state)
    total_decay = jnp.prod(block_parts[0], axis=0)
    return (block_parts, b_mat, c_mat, total_decay, total_state)


def local_rear(block_parts, b_mat, c_mat, skip, start_state):
    _, incoming = compose_blocks(block_parts[0], block_parts[1], start_state)
    return block_output(block_parts, b_mat, c_mat, skip, incoming)


def local_pass(
    marks_ext,
    alive_mask,
    extended,
    dt_pre,
    conv_weight,
    conv_bias,
    dt_bias,
    a_log,
    skip,
    start_state,
):
    block_parts, b_mat, c_mat, total_decay, total_state = local_front(
        marks_ext, alive_mask, extended, dt_pre, conv_weight, conv_bias, dt_bias, a_log
    )
    return (local_rear(block_parts, b_mat, c_mat, skip, start_state), total_decay, total_state)


def chain_combine(earlier, later):
    return (earlier[0] * later[0], later[0][:, None, None] * earlier[1] + later[1])


def extend(pre_conv, start_marks, edge_rows, edge_marks):
    extended = jnp.concatenate([edge_rows, pre_conv], axis=0)
    marks_ext = jnp.concatenate([edge_marks.astype(jnp.int32), start_marks], axis=0)
    return (extended, marks_ext)


def mixer_forward(stream, start_marks, alive_mask, layer_weights, tick, ids):
    (
        norm_gain,
        w_main,
        w_low,
        w_bc,
        conv_weight,
        conv_bias,
        dt_bias,
        a_log,
        skip,
        gate_gain,
        w_out,
    ) = layer_weights
    inner_width = w_out.shape[0]
    normed = (stream * rms_scale(stream) * norm_gain).astype(jnp.bfloat16)
    gathered = head_gather(normed, tick, ids[0])
    gathered = gathered.reshape(-1, gathered.shape[-1])
    projected = jnp.dot(gathered, w_main, preferred_element_type=jnp.float32)
    gate_pre = projected[:, :inner_width]
    pre_conv = projected[:, inner_width : 2 * inner_width + 2 * N]
    dt_pre = projected[:, 2 * inner_width + 2 * N :]
    marks_float = start_marks.astype(jnp.float32)
    tail_from = pre_conv.shape[0] - KW + 1
    edge_parts = shifted((pre_conv[tail_from:], marks_float[tail_from:]), "seq", 1)
    extended, marks_ext = extend(pre_conv, start_marks, edge_parts[0], edge_parts[1])
    front_fn = partial(local_front, marks_ext, alive_mask)
    front_out, front_pull = jax.vjp(
        front_fn, extended, dt_pre, conv_weight, conv_bias, dt_bias, a_log
    )
    block_parts, b_mat, c_mat, total_decay, total_state = front_out
    neutral = (jnp.ones_like(total_decay), jnp.zeros_like(total_state))
    prefix = entering((total_decay, total_state), "seq", chain_combine, neutral)
    start_state = prefix[1]
    mixed_out, rear_pull = jax.vjp(local_rear, block_parts, b_mat, c_mat, skip, start_state)
    silu_gate = jax.nn.silu(gate_pre)
    gated_mix = mixed_out * silu_gate
    square_total = lax.psum(jnp.sum(gated_mix * gated_mix, axis=-1), "head")
    scale_out = lax.rsqrt(square_total / DI + norm_eps)
    normed_out = (gated_mix * scale_out[:, None] * gate_gain).astype(jnp.bfloat16)
    head_count = lax.axis_size("head")
    branch = head_scatter(
        jnp.dot(normed_out, w_out, preferred_element_type=jnp.float32).reshape(
            head_count, -1, w_out.shape[1]
        ),
        tick,
        ids[1],
    )
    saved = (
        stream,
        gathered,
        gate_pre,
        mixed_out,
        silu_gate,
        gated_mix,
        scale_out,
        normed_out,
        total_decay,
        start_state,
        front_pull,
        rear_pull,
    )
    return stream + branch, saved


def mixer_backward(grad_next, layer_weights, saved, mask_value, tick, ids):
    (
        norm_gain,
        w_main,
        w_low,
        w_bc,
        conv_weight,
        conv_bias,
        dt_bias,
        a_log,
        skip,
        gate_gain,
        w_out,
    ) = layer_weights
    (
        stream,
        gathered,
        gate_pre,
        mixed_out,
        silu_gate,
        gated_mix,
        scale_out,
        normed_out,
        total_decay,
        start_state,
        front_pull,
        rear_pull,
    ) = saved
    inner_width = w_out.shape[0]
    grad_branch = grad_next.astype(jnp.bfloat16)
    shard_rows = head_gather(grad_branch, tick, ids[0])
    shard_rows = shard_rows.reshape(-1, shard_rows.shape[-1])
    g_w_out = lax.dot_general(
        normed_out, shard_rows, (((0,), (0,)), ((), ())), preferred_element_type=jnp.float32
    ) * mask_value
    grad_normed = lax.dot_general(
        shard_rows, w_out, (((1,), (1,)), ((), ())), preferred_element_type=jnp.float32
    )
    weighted = grad_normed * gate_gain
    g_gate_gain = jnp.sum(grad_normed * gated_mix * scale_out[:, None], axis=0)
    cross_sum = lax.psum(jnp.sum(weighted * gated_mix, axis=-1), "head")
    grad_gated = (
        scale_out[:, None] * weighted - gated_mix * (scale_out**3 * cross_sum / DI)[:, None]
    )
    grad_mixed = grad_gated * silu_gate
    grad_gate = (grad_gated * mixed_out * silu_slope(gate_pre)).astype(jnp.bfloat16)
    g_parts, g_b_mat, g_c_mat, g_skip, g_start = rear_pull(grad_mixed)
    neutral = (jnp.ones_like(total_decay), jnp.zeros_like(g_start))
    suffix = entering_2((total_decay, g_start), "seq", chain_combine, neutral)
    after_state = suffix[1]
    grad_decay = jnp.sum(after_state * start_state, axis=(1, 2))
    grad_ext, grad_dt_pre, g_conv_w, g_conv_b, g_dt_bias, g_a_log = front_pull(
        (g_parts, g_b_mat, g_c_mat, grad_decay, after_state)
    )
    returned = shifted(grad_ext[: KW - 1], "seq", -1)
    grad_pre = grad_ext[KW - 1 :]
    tail_from = grad_pre.shape[0] - KW + 1
    grad_pre = jnp.concatenate([grad_pre[:tail_from], grad_pre[tail_from:] + returned], axis=0)
    grad_inner = grad_pre[:, :inner_width].astype(jnp.bfloat16)
    grad_bc = grad_pre[:, inner_width:]
    grad_low = jnp.concatenate([grad_gate, grad_inner, grad_dt_pre.astype(jnp.bfloat16)], axis=1)
    w_bc_float = w_bc.astype(jnp.float32)
    g_low = lax.dot_general(
        gathered, grad_low, (((0,), (0,)), ((), ())), preferred_element_type=jnp.float32
    )
    g_w_bc = lax.dot_general(
        gathered.astype(jnp.float32),
        grad_bc,
        (((0,), (0,)), ((), ())),
        precision=highest,
        preferred_element_type=jnp.float32,
    )
    main_term = lax.dot_general(
        grad_low, w_low, (((1,), (1,)), ((), ())), preferred_element_type=jnp.float32
    )
    side_term = lax.dot_general(
        grad_bc,
        w_bc_float,
        (((1,), (1,)), ((), ())),
        precision=highest,
        preferred_element_type=jnp.float32,
    )
    head_count = lax.axis_size("head")
    grad_normed_in = head_scatter(
        (main_term + side_term).reshape(head_count, -1, main_term.shape[1]), tick, ids[1]
    )
    scale_in = rms_scale(stream)
    g_norm_gain = jnp.sum(grad_normed_in * stream * scale_in, axis=0)
    weighted_in = grad_normed_in * norm_gain
    grad_stream = (
        grad_next
        + scale_in * weighted_in
        - stream * scale_in**3 * jnp.mean(weighted_in * stream, axis=-1, keepdims=True)
    )
    head_part = (
        g_low[:, :inner_width],
        g_low[:, inner_width : 2 * inner_width],
        g_low[:, 2 * inner_width :],
        g_conv_w[:, :inner_width],
        g_conv_b[:inner_width],
        g_dt_bias,
        g_a_log,
        g_skip,
        g_gate_gain,
    )
    shared_part = (g_norm_gain, g_w_bc, g_conv_w[:, inner_width:], g_conv_b[inner_width:])
    return (grad_stream, head_part, shared_part, g_w_out)


def reduce_grads(head_part, shared_part):
    head_sum = tuple(
        lax.psum(member.astype(jnp.bfloat16), "seq").astype(jnp.float32) for member in head_part
    )
    shared_sum = lax.psum(
        (shared_part[0], shared_part[1].astype(jnp.bfloat16)) + tuple(shared_part[2:]),
        ("seq", "head"),
    )
    shared_sum = (shared_sum[0], shared_sum[1].astype(jnp.float32)) + tuple(shared_sum[2:])
    return (head_sum, shared_sum)


def store_slot(buffer, value, slot_index, is_valid):
    current = lax.dynamic_index_in_dim(buffer, slot_index, 0, False)
    return lax.dynamic_update_index_in_dim(
        buffer, jnp.where(is_valid, value, current), slot_index, 0
    )


def on_device(
    inputs,
    cotangent,
    starts,
    live,
    norm_gain,
    w_gate,
    w_in,
    w_bc,
    w_dt,
    conv_x,
    conv_x_bias,
    conv_bc,
    conv_bc_bias,
    dt_bias,
    a_log,
    skip,
    gate_gain,
    w_out,
):
    section_count = lax.axis_size("section")
    section_index = lax.axis_index("section")
    micro_count = inputs.shape[0]
    tick_count = micro_count + section_count - 1
    w_main = jnp.concatenate([w_gate[0], w_in[0], w_bc[0], w_dt[0]], axis=1)
    w_low = jnp.concatenate([w_gate[0], w_in[0], w_dt[0]], axis=1)
    conv_weight = jnp.concatenate([conv_x[0], conv_bc[0]], axis=1).astype(jnp.float32)
    conv_bias = jnp.concatenate([conv_x_bias[0], conv_bc_bias[0]], axis=0)
    layer_weights = (
        norm_gain[0],
        w_main,
        w_low,
        w_bc[0],
        conv_weight,
        conv_bias,
        dt_bias[0],
        a_log[0],
        skip[0],
        gate_gain[0],
        w_out[0],
    )
    row_shape = inputs.shape[1:]
    outputs_all = jnp.zeros((micro_count,) + row_shape, jnp.float32)
    arrived = jnp.zeros(row_shape, jnp.float32)
    ticks = []
    for tick_index in range(tick_count):
        slot_index = tick_index - section_index
        is_valid = (slot_index >= 0) & (slot_index < micro_count)
        clipped = jnp.clip(slot_index, 0, micro_count - 1)
        fresh_rows = lax.dynamic_index_in_dim(inputs, clipped, 0, False).astype(jnp.float32)
        stream = jnp.where(section_index == 0, fresh_rows, arrived)
        start_marks = lax.dynamic_index_in_dim(starts, clipped, 0, False)
        alive_mask = lax.dynamic_index_in_dim(live, clipped, 0, False).astype(jnp.float32)
        result, saved = mixer_forward(
            stream,
            start_marks,
            alive_mask,
            layer_weights,
            (tick_index, -1, micro_count),
            (tick_index, tick_count + tick_index),
        )
        outputs_all = store_slot(outputs_all, result, clipped, is_valid)
        ticks.append((clipped, is_valid, saved))
        if tick_index + 1 < tick_count:
            arrived = shifted(result, "section", 1)
    back_arrived = jnp.zeros(row_shape, jnp.float32)
    input_grads = jnp.zeros((micro_count,) + row_shape, jnp.float32)
    head_total = ()
    shared_total = ()
    for tick_index in range(tick_count):
        clipped, is_valid, saved = ticks[tick_count - 1 - tick_index]
        outer_grad = lax.dynamic_index_in_dim(cotangent, clipped, 0, False).astype(jnp.float32)
        grad_next = jnp.where(section_index == section_count - 1, outer_grad, back_arrived)
        mask_value = is_valid.astype(jnp.float32)
        grad_stream, head_part, shared_part, out_part = mixer_backward(
            grad_next,
            layer_weights,
            saved,
            mask_value,
            (tick_count - 1 - tick_index, -1, micro_count),
            (2 * tick_count + tick_index, 3 * tick_count + tick_index),
        )
        if tick_index == 0:
            out_total = out_part
        else:
            out_total = out_total + out_part
        if tick_index + 1 == tick_count:
            out_total = lax.psum(out_total.astype(jnp.bfloat16), "seq")
        head_part = tuple((member * mask_value for member in head_part))
        shared_part = tuple((member * mask_value for member in shared_part))
        if tick_index == 0:
            head_total = head_part
            shared_total = shared_part
        else:
            head_total = tuple((former + latter for former, latter in zip(head_total, head_part)))
            shared_total = tuple(
                (former + latter for former, latter in zip(shared_total, shared_part))
            )
        input_grads = store_slot(input_grads, grad_stream, clipped, is_valid)
        if tick_index + 1 < tick_count:
            back_arrived = shifted(grad_stream.astype(jnp.bfloat16), "section", -1).astype(
                grad_stream.dtype
            )
    anchor = out_total[0, 0].astype(jnp.float32) * 0.0
    head_total = (head_total[0] + anchor,) + head_total[1:]
    head_total, shared_total = reduce_grads(head_total, shared_total)
    head_total = head_total[:3] + (out_total.astype(jnp.float32),) + head_total[3:]
    return (
        outputs_all[None],
        input_grads[None],
        shared_total[0][None],
        head_total[0][None],
        head_total[1][None],
        shared_total[1][None],
        head_total[2][None],
        head_total[4][None],
        head_total[5][None],
        shared_total[2][None],
        shared_total[3][None],
        head_total[6][None],
        head_total[7][None],
        head_total[8][None],
        head_total[9][None],
        head_total[3][None],
    )


def solution(mesh):
    return jax.shard_map(
        on_device,
        mesh=mesh,
        in_specs=(
            P(None, ("seq", "head"), None),
            P(None, ("seq", "head"), None),
            P(None, "seq"),
            P(None, "seq"),
            P("section", None),
            P("section", None, "head"),
            P("section", None, "head"),
            P("section", None, None),
            P("section", None, "head"),
            P("section", None, "head"),
            P("section", "head"),
            P("section", None, None),
            P("section", None),
            P("section", "head"),
            P("section", "head"),
            P("section", "head"),
            P("section", "head"),
            P("section", "head", None),
        ),
        out_specs=(
            P("section", None, ("seq", "head"), None),
            P("section", None, ("seq", "head"), None),
            P("section", None),
            P("section", None, "head"),
            P("section", None, "head"),
            P("section", None, None),
            P("section", None, "head"),
            P("section", None, "head"),
            P("section", "head"),
            P("section", None, None),
            P("section", None),
            P("section", "head"),
            P("section", "head"),
            P("section", "head"),
            P("section", "head"),
            P("section", "head", None),
        ),
        check_vma=False,
    )
```

```python
from functools import partial

import functools
import math

import jax
import jax.numpy as jnp
from jax import lax
from jax.experimental import pallas as pl
from jax.experimental.pallas import tpu as pltpu
from jax.sharding import PartitionSpec as P

DI = 4096
P_SIZE = 64
N = 128
KW = 4
SCAN_BLOCK = 256


MESH = pl.DeviceIdType.MESH


def _tick_valid(offset, sign, count):
    slot = offset + sign * lax.axis_index("section")
    return jnp.logical_and(slot >= 0, slot < count)


def _enter(barrier, h, n):
    @pl.when(h > 0)
    def _():
        pl.semaphore_signal(barrier, 1, device_id={"head": h - 1}, device_id_type=MESH)

    @pl.when(h < n - 1)
    def _():
        pl.semaphore_signal(barrier, 1, device_id={"head": h + 1}, device_id_type=MESH)

    @pl.when(jnp.logical_and(h > 0, h < n - 1))
    def _():
        pl.semaphore_wait(barrier, 2)

    @pl.when(jnp.logical_or(h == 0, h == n - 1))
    def _():
        pl.semaphore_wait(barrier, 1)


def gather_body(n, tick, x_ref, o_ref, land, send_r, send_l, recv):
    h = lax.axis_index("head")
    valid = _tick_valid(*tick)

    @pl.when(valid)
    def _():
        _enter(pltpu.get_barrier_semaphore(), h, n)

        def copy_right(s, k):
            src = x_ref if s == 0 else land.at[k]
            return pltpu.make_async_remote_copy(
                src_ref=src, dst_ref=land.at[k], send_sem=send_r.at[s], recv_sem=recv.at[k],
                device_id={"head": h + 1}, device_id_type=MESH)

        def copy_left(s, k):
            src = x_ref if s == 0 else land.at[k]
            return pltpu.make_async_remote_copy(
                src_ref=src, dst_ref=land.at[k], send_sem=send_l.at[s], recv_sem=recv.at[k],
                device_id={"head": h - 1}, device_id_type=MESH)

        for s in range(n):
            k_r = h - s
            k_l = h + s
            if s >= 1:
                @pl.when(k_r >= 0)
                def _():
                    pltpu.make_async_remote_copy(
                        src_ref=land.at[k_r], dst_ref=land.at[k_r], send_sem=send_r.at[0],
                        recv_sem=recv.at[k_r], device_id={"head": h}, device_id_type=MESH
                    ).wait_recv()

                @pl.when(k_l <= n - 1)
                def _():
                    pltpu.make_async_remote_copy(
                        src_ref=land.at[k_l], dst_ref=land.at[k_l], send_sem=send_l.at[0],
                        recv_sem=recv.at[k_l], device_id={"head": h}, device_id_type=MESH
                    ).wait_recv()
            if s <= n - 2:
                @pl.when(jnp.logical_and(k_r >= 0, h < n - 1))
                def _():
                    copy_right(s, k_r).start()

                @pl.when(jnp.logical_and(k_l <= n - 1, h > 0))
                def _():
                    copy_left(s, k_l).start()
        land[h] = x_ref[...]
        for s in range(n - 1):
            k_r = h - s
            k_l = h + s

            @pl.when(jnp.logical_and(k_r >= 0, h < n - 1))
            def _():
                copy_right(s, k_r).wait_send()

            @pl.when(jnp.logical_and(k_l <= n - 1, h > 0))
            def _():
                copy_left(s, k_l).wait_send()
        o_ref[...] = land[...]

    @pl.when(jnp.logical_not(valid))
    def _():
        o_ref[...] = jnp.zeros(o_ref.shape, o_ref.dtype)


def head_gather(x, tick, cid):
    n = lax.axis_size("head")
    rows, cols = x.shape
    return pl.pallas_call(
        functools.partial(gather_body, n, tick),
        out_shape=jax.ShapeDtypeStruct((n, rows, cols), x.dtype),
        in_specs=[pl.BlockSpec(memory_space=pltpu.VMEM)],
        out_specs=pl.BlockSpec(memory_space=pltpu.VMEM),
        scratch_shapes=[
            pltpu.VMEM((n, rows, cols), x.dtype),
            pltpu.SemaphoreType.DMA((n,)),
            pltpu.SemaphoreType.DMA((n,)),
            pltpu.SemaphoreType.DMA((n,)),
        ],
        compiler_params=pltpu.CompilerParams(collective_id=cid, has_side_effects=True),
    )(x)


def scatter_body(n, tick, p_ref, o_ref, recv_l, recv_r, send_l, send_r, ssem_l, ssem_r, rsem_l, rsem_r):
    h = lax.axis_index("head")
    valid = _tick_valid(*tick)
    link = send_r.dtype

    @pl.when(valid)
    def _():
        _enter(pltpu.get_barrier_semaphore(), h, n)

        def to_right(k):
            return pltpu.make_async_remote_copy(
                src_ref=send_r.at[k], dst_ref=recv_l.at[k], send_sem=ssem_r.at[k],
                recv_sem=rsem_l.at[k], device_id={"head": h + 1}, device_id_type=MESH)

        def to_left(k):
            return pltpu.make_async_remote_copy(
                src_ref=send_l.at[k], dst_ref=recv_r.at[k], send_sem=ssem_l.at[k],
                recv_sem=rsem_r.at[k], device_id={"head": h - 1}, device_id_type=MESH)

        for s in range(n - 1):
            k_r = n - 1 - s
            k_l = s

            @pl.when(k_r > h)
            def _():
                @pl.when(h > 0)
                def _():
                    to_right(k_r).wait_recv()
                    send_r[k_r] = (p_ref[k_r] + recv_l[k_r].astype(jnp.float32)).astype(link)

                @pl.when(h == 0)
                def _():
                    send_r[k_r] = p_ref[k_r].astype(link)

                to_right(k_r).start()

            @pl.when(k_l < h)
            def _():
                @pl.when(h < n - 1)
                def _():
                    to_left(k_l).wait_recv()
                    send_l[k_l] = (p_ref[k_l] + recv_r[k_l].astype(jnp.float32)).astype(link)

                @pl.when(h == n - 1)
                def _():
                    send_l[k_l] = p_ref[k_l].astype(link)

                to_left(k_l).start()
        total = p_ref[h]

        @pl.when(h > 0)
        def _():
            to_right(h).wait_recv()

        @pl.when(h < n - 1)
        def _():
            to_left(h).wait_recv()

        left_part = jnp.where(h > 0, recv_l[h].astype(jnp.float32), 0.0)
        right_part = jnp.where(h < n - 1, recv_r[h].astype(jnp.float32), 0.0)
        o_ref[...] = (total + left_part + right_part).astype(o_ref.dtype)
        for s in range(n - 1):
            k_r = n - 1 - s
            k_l = s

            @pl.when(k_r > h)
            def _():
                to_right(k_r).wait_send()

            @pl.when(k_l < h)
            def _():
                to_left(k_l).wait_send()

    @pl.when(jnp.logical_not(valid))
    def _():
        o_ref[...] = jnp.zeros(o_ref.shape, o_ref.dtype)


def head_scatter(parts, tick, cid, link=jnp.bfloat16):
    n = lax.axis_size("head")
    _, rows, cols = parts.shape
    return pl.pallas_call(
        functools.partial(scatter_body, n, tick),
        out_shape=jax.ShapeDtypeStruct((rows, cols), jnp.float32),
        in_specs=[pl.BlockSpec(memory_space=pltpu.VMEM)],
        out_specs=pl.BlockSpec(memory_space=pltpu.VMEM),
        scratch_shapes=[
            pltpu.VMEM((n, rows, cols), link),
            pltpu.VMEM((n, rows, cols), link),
            pltpu.VMEM((n, rows, cols), link),
            pltpu.VMEM((n, rows, cols), link),
            pltpu.SemaphoreType.DMA((n,)),
            pltpu.SemaphoreType.DMA((n,)),
            pltpu.SemaphoreType.DMA((n,)),
            pltpu.SemaphoreType.DMA((n,)),
        ],
        compiler_params=pltpu.CompilerParams(collective_id=cid, has_side_effects=True),
    )(parts)


norm_eps = 1e-05
far_below = -1e30
highest = lax.Precision.HIGHEST


def shifted(value, axis, by):
    count = lax.axis_size(axis)
    pairs = [(i, i + by) for i in range(count) if 0 <= i + by < count]
    return lax.ppermute(value, axis, pairs)


def entering(value, axis, combine, identity):
    count, mine = (lax.axis_size(axis), lax.axis_index(axis))
    everything = jax.tree.map(lambda part: lax.all_gather(part, axis), value)
    before = jax.tree.map(
        lambda part, zero: jnp.broadcast_to(jnp.asarray(zero, part.dtype), part.shape),
        value,
        identity,
    )
    for k in range(count - 1):
        reached = k < mine
        new = combine(before, jax.tree.map(lambda part: part[k], everything))
        before = jax.tree.map(lambda a, b: jnp.where(reached, a, b), new, before)
    return before


def entering_2(value, axis, join, neutral):
    count = lax.axis_size(axis)
    place = lax.axis_index(axis)
    ahead = count - 1 - place
    gathered = jax.tree.map(
        lambda a, kind: lax.all_gather(a.astype(kind), axis),
        value,
        jax.tree.map(lambda a: jnp.bfloat16 if a.dtype == jnp.float32 else a.dtype, value),
    )
    state = jax.tree.map(lambda a, e: jnp.zeros_like(a) + jnp.asarray(e, a.dtype), value, neutral)
    for lap in range(count - 1):
        source = count - 1 - lap
        new = join(
            state,
            jax.tree.map(lambda a, own: a[source].astype(own.dtype), gathered, value),
        )
        active = lap < ahead
        state = jax.tree.map(lambda a, b: jnp.where(active, a, b), new, state)
    return state


def rms_scale(values):
    return lax.rsqrt(jnp.mean(values * values, axis=-1, keepdims=True) + norm_eps)


def silu_slope(values):
    logistic = jax.nn.sigmoid(values)
    return logistic * (1.0 + values * (1.0 - logistic))


def causal_conv(extended, marks_ext, weight, conv_bias):
    tap_count = weight.shape[0]
    length = extended.shape[0] - tap_count + 1
    counts = jnp.cumsum(marks_ext)
    conv_sum = jnp.zeros((length, extended.shape[1]), jnp.float32) + conv_bias
    for tap_index in range(tap_count):
        linked = (counts[tap_count - 1 :] == counts[tap_index : tap_index + length]).astype(
            jnp.float32
        )
        conv_sum = (
            conv_sum
            + linked[:, None] * weight[tap_index] * extended[tap_index : tap_index + length]
        )
    return conv_sum


def prepare(extended, dt_pre, marks_ext, alive_mask, conv_weight, conv_bias, dt_bias, a_log):
    inner_width = dt_pre.shape[1] * P_SIZE
    activated = jax.nn.silu(causal_conv(extended, marks_ext, conv_weight, conv_bias))
    inner_act = activated[:, :inner_width] * alive_mask[:, None]
    b_mat = activated[:, inner_width : inner_width + N]
    c_mat = activated[:, inner_width + N :]
    step_size = jax.nn.softplus(dt_pre + dt_bias) * alive_mask[:, None]
    log_decay = -step_size * jnp.exp(a_log)
    return (inner_act, step_size, log_decay, b_mat, c_mat)


def block_terms(inner_act, step_size, log_decay, b_mat, start_marks):
    blocks = inner_act.shape[0] // SCAN_BLOCK
    head_count = step_size.shape[1]
    x_blocks = inner_act.reshape(blocks, SCAN_BLOCK, head_count, P_SIZE)
    dt_blocks = step_size.reshape(blocks, SCAN_BLOCK, head_count)
    cum_decay = jnp.cumsum(log_decay.reshape(blocks, SCAN_BLOCK, head_count), axis=1)
    mark_count = jnp.cumsum(start_marks.reshape(blocks, SCAN_BLOCK), axis=1)
    b_blocks = b_mat.reshape(blocks, SCAN_BLOCK, N)
    last_cum = cum_decay[:, -1]
    last_mark = mark_count[:, -1]
    same_end = (mark_count == last_mark[:, None]).astype(jnp.float32)
    end_weight = jnp.exp(last_cum[:, None, :] - cum_decay) * same_end[:, :, None] * dt_blocks
    block_states = jnp.einsum(
        "cjh,cjhp,cjn->chpn", end_weight, x_blocks, b_blocks, precision=highest
    )
    block_decay = jnp.exp(last_cum) * (last_mark == 0).astype(jnp.float32)[:, None]
    return (block_decay, block_states, cum_decay, mark_count, x_blocks, dt_blocks)


def compose_blocks(block_decay, block_states, start_state):
    chain_state = start_state
    incoming = []
    for block_index in range(block_decay.shape[0]):
        incoming.append(chain_state)
        chain_state = (
            block_decay[block_index][:, None, None] * chain_state + block_states[block_index]
        )
    return (chain_state, jnp.stack(incoming))


def block_output(block_parts, b_mat, c_mat, skip, incoming):
    block_decay, block_states, cum_decay, mark_count, x_blocks, dt_blocks = block_parts
    blocks = cum_decay.shape[0]
    head_count = cum_decay.shape[2]
    b_blocks = b_mat.reshape(blocks, SCAN_BLOCK, N)
    c_blocks = c_mat.reshape(blocks, SCAN_BLOCK, N)
    inner_prod = jnp.einsum("cin,cjn->cij", c_blocks, b_blocks, precision=highest)
    arange_pos = jnp.arange(SCAN_BLOCK)
    linked = (arange_pos[:, None] >= arange_pos[None, :])[None] & (
        mark_count[:, :, None] == mark_count[:, None, :]
    )
    spread = jnp.where(
        linked[..., None], cum_decay[:, :, None, :] - cum_decay[:, None, :, :], far_below
    )
    weights = jnp.exp(spread) * inner_prod[..., None] * dt_blocks[:, None, :, :]
    y_intra = jnp.einsum("cijh,cjhp->cihp", weights, x_blocks, precision=highest)
    carry_in = jnp.exp(cum_decay) * (mark_count == 0).astype(jnp.float32)[:, :, None]
    y_inter = (
        jnp.einsum("cin,chpn->cihp", c_blocks, incoming, precision=highest) * carry_in[..., None]
    )
    mixed_out = y_intra + y_inter + skip[None, None, :, None] * x_blocks
    return mixed_out.reshape(blocks * SCAN_BLOCK, head_count * P_SIZE)


def local_front(marks_ext, alive_mask, extended, dt_pre, conv_weight, conv_bias, dt_bias, a_log):
    inner_act, step_size, log_decay, b_mat, c_mat = prepare(
        extended, dt_pre, marks_ext, alive_mask, conv_weight, conv_bias, dt_bias, a_log
    )
    block_parts = block_terms(inner_act, step_size, log_decay, b_mat, marks_ext[KW - 1 :])
    zero_state = jnp.zeros(block_parts[1].shape[1:], jnp.float32)
    total_state, _ = compose_blocks(block_parts[0], block_parts[1], zero_state)
    total_decay = jnp.prod(block_parts[0], axis=0)
    return (block_parts, b_mat, c_mat, total_decay, total_state)


def local_rear(block_parts, b_mat, c_mat, skip, start_state):
    _, incoming = compose_blocks(block_parts[0], block_parts[1], start_state)
    return block_output(block_parts, b_mat, c_mat, skip, incoming)


def local_pass(
    marks_ext,
    alive_mask,
    extended,
    dt_pre,
    conv_weight,
    conv_bias,
    dt_bias,
    a_log,
    skip,
    start_state,
):
    block_parts, b_mat, c_mat, total_decay, total_state = local_front(
        marks_ext, alive_mask, extended, dt_pre, conv_weight, conv_bias, dt_bias, a_log
    )
    return (local_rear(block_parts, b_mat, c_mat, skip, start_state), total_decay, total_state)


def chain_combine(earlier, later):
    return (earlier[0] * later[0], later[0][:, None, None] * earlier[1] + later[1])


def extend(pre_conv, start_marks, edge_rows, edge_marks):
    extended = jnp.concatenate([edge_rows, pre_conv], axis=0)
    marks_ext = jnp.concatenate([edge_marks.astype(jnp.int32), start_marks], axis=0)
    return (extended, marks_ext)


def mixer_forward(stream, start_marks, alive_mask, layer_weights, tick, ids):
    (
        norm_gain,
        w_main,
        w_low,
        w_bc,
        conv_weight,
        conv_bias,
        dt_bias,
        a_log,
        skip,
        gate_gain,
        w_out,
    ) = layer_weights
    inner_width = w_out.shape[0]
    normed = (stream * rms_scale(stream) * norm_gain).astype(jnp.bfloat16)
    gathered = head_gather(normed, tick, ids[0])
    gathered = gathered.reshape(-1, gathered.shape[-1])
    projected = jnp.dot(gathered, w_main, preferred_element_type=jnp.float32)
    gate_pre = projected[:, :inner_width]
    pre_conv = projected[:, inner_width : 2 * inner_width + 2 * N]
    dt_pre = projected[:, 2 * inner_width + 2 * N :]
    marks_float = start_marks.astype(jnp.float32)
    tail_from = pre_conv.shape[0] - KW + 1
    edge_parts = shifted((pre_conv[tail_from:], marks_float[tail_from:]), "seq", 1)
    extended, marks_ext = extend(pre_conv, start_marks, edge_parts[0], edge_parts[1])
    front_fn = partial(local_front, marks_ext, alive_mask)
    front_out, front_pull = jax.vjp(
        front_fn, extended, dt_pre, conv_weight, conv_bias, dt_bias, a_log
    )
    block_parts, b_mat, c_mat, total_decay, total_state = front_out
    neutral = (jnp.ones_like(total_decay), jnp.zeros_like(total_state))
    prefix = entering((total_decay, total_state), "seq", chain_combine, neutral)
    start_state = prefix[1]
    mixed_out, rear_pull = jax.vjp(local_rear, block_parts, b_mat, c_mat, skip, start_state)
    silu_gate = jax.nn.silu(gate_pre)
    gated_mix = mixed_out * silu_gate
    square_total = lax.psum(jnp.sum(gated_mix * gated_mix, axis=-1), "head")
    scale_out = lax.rsqrt(square_total / DI + norm_eps)
    normed_out = (gated_mix * scale_out[:, None] * gate_gain).astype(jnp.bfloat16)
    head_count = lax.axis_size("head")
    branch = head_scatter(
        jnp.dot(normed_out, w_out, preferred_element_type=jnp.float32).reshape(
            head_count, -1, w_out.shape[1]
        ),
        tick,
        ids[1],
    )
    saved = (
        stream,
        gathered,
        gate_pre,
        mixed_out,
        silu_gate,
        gated_mix,
        scale_out,
        normed_out,
        total_decay,
        start_state,
        front_pull,
        rear_pull,
    )
    return stream + branch, saved


def mixer_backward(grad_next, layer_weights, saved, mask_value, tick, ids, hook=None):
    (
        norm_gain,
        w_main,
        w_low,
        w_bc,
        conv_weight,
        conv_bias,
        dt_bias,
        a_log,
        skip,
        gate_gain,
        w_out,
    ) = layer_weights
    (
        stream,
        gathered,
        gate_pre,
        mixed_out,
        silu_gate,
        gated_mix,
        scale_out,
        normed_out,
        total_decay,
        start_state,
        front_pull,
        rear_pull,
    ) = saved
    inner_width = w_out.shape[0]
    grad_branch = grad_next.astype(jnp.bfloat16)
    shard_rows = head_gather(grad_branch, tick, ids[0])
    shard_rows = shard_rows.reshape(-1, shard_rows.shape[-1])
    g_w_out = lax.dot_general(
        normed_out, shard_rows, (((0,), (0,)), ((), ())), preferred_element_type=jnp.float32
    ) * mask_value
    grad_normed = lax.dot_general(
        shard_rows, w_out, (((1,), (1,)), ((), ())), preferred_element_type=jnp.float32
    )
    weighted = grad_normed * gate_gain
    g_gate_gain = jnp.sum(grad_normed * gated_mix * scale_out[:, None], axis=0)
    cross_sum = lax.psum(jnp.sum(weighted * gated_mix, axis=-1), "head")
    grad_gated = (
        scale_out[:, None] * weighted - gated_mix * (scale_out**3 * cross_sum / DI)[:, None]
    )
    grad_mixed = grad_gated * silu_gate
    grad_gate = (grad_gated * mixed_out * silu_slope(gate_pre)).astype(jnp.bfloat16)
    g_parts, g_b_mat, g_c_mat, g_skip, g_start = rear_pull(grad_mixed)
    neutral = (jnp.ones_like(total_decay), jnp.zeros_like(g_start))
    suffix = entering_2((total_decay, g_start), "seq", chain_combine, neutral)
    after_state = suffix[1]
    grad_decay = jnp.sum(after_state * start_state, axis=(1, 2))
    grad_ext, grad_dt_pre, g_conv_w, g_conv_b, g_dt_bias, g_a_log = front_pull(
        (g_parts, g_b_mat, g_c_mat, grad_decay, after_state)
    )
    returned = shifted(grad_ext[: KW - 1], "seq", -1)
    grad_pre = grad_ext[KW - 1 :]
    tail_from = grad_pre.shape[0] - KW + 1
    grad_pre = jnp.concatenate([grad_pre[:tail_from], grad_pre[tail_from:] + returned], axis=0)
    grad_inner = grad_pre[:, :inner_width].astype(jnp.bfloat16)
    grad_bc = grad_pre[:, inner_width:]
    grad_low = jnp.concatenate([grad_gate, grad_inner, grad_dt_pre.astype(jnp.bfloat16)], axis=1)
    w_bc_float = w_bc.astype(jnp.float32)
    g_low = lax.dot_general(
        gathered, grad_low, (((0,), (0,)), ((), ())), preferred_element_type=jnp.float32
    )
    g_w_bc = lax.dot_general(
        gathered.astype(jnp.float32),
        grad_bc,
        (((0,), (0,)), ((), ())),
        precision=highest,
        preferred_element_type=jnp.float32,
    )
    main_term = lax.dot_general(
        grad_low, w_low, (((1,), (1,)), ((), ())), preferred_element_type=jnp.float32
    )
    side_term = lax.dot_general(
        grad_bc,
        w_bc_float,
        (((1,), (1,)), ((), ())),
        precision=highest,
        preferred_element_type=jnp.float32,
    )
    head_count = lax.axis_size("head")
    lead = 0.0
    if hook is not None:
        lead = hook((g_w_bc, g_conv_w[:, inner_width:], g_conv_b[inner_width:]))
    grad_normed_in = head_scatter(
        (main_term + side_term + lead).reshape(head_count, -1, main_term.shape[1]), tick, ids[1]
    )
    scale_in = rms_scale(stream)
    g_norm_gain = jnp.sum(grad_normed_in * stream * scale_in, axis=0)
    weighted_in = grad_normed_in * norm_gain
    grad_stream = (
        grad_next
        + scale_in * weighted_in
        - stream * scale_in**3 * jnp.mean(weighted_in * stream, axis=-1, keepdims=True)
    )
    head_part = (
        g_low[:, :inner_width],
        g_low[:, inner_width : 2 * inner_width],
        g_low[:, 2 * inner_width :],
        g_conv_w[:, :inner_width],
        g_conv_b[:inner_width],
        g_dt_bias,
        g_a_log,
        g_skip,
        g_gate_gain,
    )
    shared_part = (g_norm_gain, g_w_bc, g_conv_w[:, inner_width:], g_conv_b[inner_width:])
    return (grad_stream, head_part, shared_part, g_w_out)


def pack_rows(members, width, multiple):
    rows = jnp.concatenate([member.reshape(-1, width) for member in members], axis=0)
    return jnp.pad(rows, ((0, -rows.shape[0] % multiple), (0, 0)))


def unpack_rows(rows, shapes, width):
    pieces = []
    start = 0
    for shape in shapes:
        count = math.prod(shape) // width
        pieces.append(rows[start : start + count].reshape(shape))
        start += count
    return tuple(pieces)


def reduce_grads(head_part, norm_part, bc_part, tick_count):
    head_count = lax.axis_size("head")
    host = head_part[0]
    width = host.shape[-1]
    joined = jnp.concatenate([host, bc_part.reshape(-1, width)], axis=0)
    summed = tuple(
        lax.psum(member.astype(jnp.bfloat16), "seq").astype(jnp.float32)
        for member in (joined,) + tuple(head_part[1:])
    )
    head_sum = (summed[0][: host.shape[0]],) + summed[1:]
    bc_sum = summed[0][host.shape[0] :].reshape(bc_part.shape)
    bc_rows = head_gather(bc_sum, (0, 0, 1), 4 * tick_count + 1)
    norm_sum = lax.psum(norm_part, ("seq", "head"))
    return (head_sum, norm_sum, bc_rows.reshape(-1, bc_rows.shape[-1]))


def store_slot(buffer, value, slot_index, is_valid):
    current = lax.dynamic_index_in_dim(buffer, slot_index, 0, False)
    return lax.dynamic_update_index_in_dim(
        buffer, jnp.where(is_valid, value, current), slot_index, 0
    )


def on_device(
    inputs,
    cotangent,
    starts,
    live,
    norm_gain,
    w_gate,
    w_in,
    w_bc,
    w_dt,
    conv_x,
    conv_x_bias,
    conv_bc,
    conv_bc_bias,
    dt_bias,
    a_log,
    skip,
    gate_gain,
    w_out,
):
    section_count = lax.axis_size("section")
    section_index = lax.axis_index("section")
    micro_count = inputs.shape[0]
    tick_count = micro_count + section_count - 1
    w_main = jnp.concatenate([w_gate[0], w_in[0], w_bc[0], w_dt[0]], axis=1)
    w_low = jnp.concatenate([w_gate[0], w_in[0], w_dt[0]], axis=1)
    conv_weight = jnp.concatenate([conv_x[0], conv_bc[0]], axis=1).astype(jnp.float32)
    conv_bias = jnp.concatenate([conv_x_bias[0], conv_bc_bias[0]], axis=0)
    layer_weights = (
        norm_gain[0],
        w_main,
        w_low,
        w_bc[0],
        conv_weight,
        conv_bias,
        dt_bias[0],
        a_log[0],
        skip[0],
        gate_gain[0],
        w_out[0],
    )
    row_shape = inputs.shape[1:]
    outputs_all = jnp.zeros((micro_count,) + row_shape, jnp.float32)
    arrived = jnp.zeros(row_shape, jnp.float32)
    ticks = []
    for tick_index in range(tick_count):
        slot_index = tick_index - section_index
        is_valid = (slot_index >= 0) & (slot_index < micro_count)
        clipped = jnp.clip(slot_index, 0, micro_count - 1)
        fresh_rows = lax.dynamic_index_in_dim(inputs, clipped, 0, False).astype(jnp.float32)
        stream = jnp.where(section_index == 0, fresh_rows, arrived)
        start_marks = lax.dynamic_index_in_dim(starts, clipped, 0, False)
        alive_mask = lax.dynamic_index_in_dim(live, clipped, 0, False).astype(jnp.float32)
        result, saved = mixer_forward(
            stream,
            start_marks,
            alive_mask,
            layer_weights,
            (tick_index, -1, micro_count),
            (tick_index, tick_count + tick_index),
        )
        outputs_all = store_slot(outputs_all, result, clipped, is_valid)
        ticks.append((clipped, is_valid, saved))
        if tick_index + 1 < tick_count:
            arrived = shifted(result, "section", 1)
    back_arrived = jnp.zeros(row_shape, jnp.float32)
    input_grads = jnp.zeros((micro_count,) + row_shape, jnp.float32)
    head_count = lax.axis_size("head")
    bc_box = []
    head_total = ()
    shared_total = ()
    for tick_index in range(tick_count):
        clipped, is_valid, saved = ticks[tick_count - 1 - tick_index]
        outer_grad = lax.dynamic_index_in_dim(cotangent, clipped, 0, False).astype(jnp.float32)
        grad_next = jnp.where(section_index == section_count - 1, outer_grad, back_arrived)
        mask_value = is_valid.astype(jnp.float32)
        hook = None
        if tick_index + 1 == tick_count:

            def hook(bc_local, mask_value=mask_value, earlier=shared_total):
                totals = tuple(
                    (prev + member * mask_value) if earlier else member * mask_value
                    for prev, member in zip(earlier[1:] or bc_local, bc_local)
                )
                rows = pack_rows(totals, totals[0].shape[-1], 8 * head_count)
                part = head_scatter(
                    rows.reshape(head_count, -1, rows.shape[-1]), (0, 0, 1), 4 * tick_count
                )
                bc_box.append((part, [member.shape for member in totals]))
                return part[0, 0] * 0.0

        grad_stream, head_part, shared_part, out_part = mixer_backward(
            grad_next,
            layer_weights,
            saved,
            mask_value,
            (tick_count - 1 - tick_index, -1, micro_count),
            (2 * tick_count + tick_index, 3 * tick_count + tick_index),
            hook,
        )
        if tick_index == 0:
            out_total = out_part
        else:
            out_total = out_total + out_part
        if tick_index + 1 == tick_count:
            out_total = lax.psum(out_total.astype(jnp.bfloat16), "seq")
        head_part = tuple((member * mask_value for member in head_part))
        shared_part = tuple((member * mask_value for member in shared_part))
        if tick_index == 0:
            head_total = head_part
            shared_total = shared_part
        else:
            head_total = tuple((former + latter for former, latter in zip(head_total, head_part)))
            shared_total = tuple(
                (former + latter for former, latter in zip(shared_total, shared_part))
            )
        input_grads = store_slot(input_grads, grad_stream, clipped, is_valid)
        if tick_index + 1 < tick_count:
            back_arrived = shifted(grad_stream.astype(jnp.bfloat16), "section", -1).astype(
                grad_stream.dtype
            )
    anchor = out_total[0, 0].astype(jnp.float32) * 0.0
    head_total = (head_total[0] + anchor,) + head_total[1:]
    bc_part, bc_shapes = bc_box[0]
    head_total, norm_sum, bc_rows = reduce_grads(head_total, shared_total[0], bc_part, tick_count)
    shared_total = (norm_sum,) + unpack_rows(bc_rows, bc_shapes, bc_rows.shape[-1])
    head_total = head_total[:3] + (out_total.astype(jnp.float32),) + head_total[3:]
    return (
        outputs_all[None],
        input_grads[None],
        shared_total[0][None],
        head_total[0][None],
        head_total[1][None],
        shared_total[1][None],
        head_total[2][None],
        head_total[4][None],
        head_total[5][None],
        shared_total[2][None],
        shared_total[3][None],
        head_total[6][None],
        head_total[7][None],
        head_total[8][None],
        head_total[9][None],
        head_total[3][None],
    )


def solution(mesh):
    return jax.shard_map(
        on_device,
        mesh=mesh,
        in_specs=(
            P(None, ("seq", "head"), None),
            P(None, ("seq", "head"), None),
            P(None, "seq"),
            P(None, "seq"),
            P("section", None),
            P("section", None, "head"),
            P("section", None, "head"),
            P("section", None, None),
            P("section", None, "head"),
            P("section", None, "head"),
            P("section", "head"),
            P("section", None, None),
            P("section", None),
            P("section", "head"),
            P("section", "head"),
            P("section", "head"),
            P("section", "head"),
            P("section", "head", None),
        ),
        out_specs=(
            P("section", None, ("seq", "head"), None),
            P("section", None, ("seq", "head"), None),
            P("section", None),
            P("section", None, "head"),
            P("section", None, "head"),
            P("section", None, None),
            P("section", None, "head"),
            P("section", None, "head"),
            P("section", "head"),
            P("section", None, None),
            P("section", None),
            P("section", "head"),
            P("section", "head"),
            P("section", "head"),
            P("section", "head"),
            P("section", "head", None),
        ),
        check_vma=False,
    )
```

```python
from functools import partial

import functools
import math

import jax
import jax.numpy as jnp
from jax import lax
from jax.experimental import pallas as pl
from jax.experimental.pallas import tpu as pltpu
from jax.sharding import PartitionSpec as P

DI = 4096
P_SIZE = 64
N = 128
KW = 4
SCAN_BLOCK = 256


MESH = pl.DeviceIdType.MESH


def _tick_valid(offset, sign, count):
    slot = offset + sign * lax.axis_index("section")
    return jnp.logical_and(slot >= 0, slot < count)


def _enter(barrier, h, n):
    @pl.when(h > 0)
    def _():
        pl.semaphore_signal(barrier, 1, device_id={"head": h - 1}, device_id_type=MESH)

    @pl.when(h < n - 1)
    def _():
        pl.semaphore_signal(barrier, 1, device_id={"head": h + 1}, device_id_type=MESH)

    @pl.when(jnp.logical_and(h > 0, h < n - 1))
    def _():
        pl.semaphore_wait(barrier, 2)

    @pl.when(jnp.logical_or(h == 0, h == n - 1))
    def _():
        pl.semaphore_wait(barrier, 1)


def gather_body(n, tick, x_ref, o_ref, land, send_r, send_l, recv):
    h = lax.axis_index("head")
    valid = _tick_valid(*tick)

    @pl.when(valid)
    def _():
        _enter(pltpu.get_barrier_semaphore(), h, n)

        def copy_right(s, k):
            src = x_ref if s == 0 else land.at[k]
            return pltpu.make_async_remote_copy(
                src_ref=src, dst_ref=land.at[k], send_sem=send_r.at[s], recv_sem=recv.at[k],
                device_id={"head": h + 1}, device_id_type=MESH)

        def copy_left(s, k):
            src = x_ref if s == 0 else land.at[k]
            return pltpu.make_async_remote_copy(
                src_ref=src, dst_ref=land.at[k], send_sem=send_l.at[s], recv_sem=recv.at[k],
                device_id={"head": h - 1}, device_id_type=MESH)

        for s in range(n):
            k_r = h - s
            k_l = h + s
            if s >= 1:
                @pl.when(k_r >= 0)
                def _():
                    pltpu.make_async_remote_copy(
                        src_ref=land.at[k_r], dst_ref=land.at[k_r], send_sem=send_r.at[0],
                        recv_sem=recv.at[k_r], device_id={"head": h}, device_id_type=MESH
                    ).wait_recv()

                @pl.when(k_l <= n - 1)
                def _():
                    pltpu.make_async_remote_copy(
                        src_ref=land.at[k_l], dst_ref=land.at[k_l], send_sem=send_l.at[0],
                        recv_sem=recv.at[k_l], device_id={"head": h}, device_id_type=MESH
                    ).wait_recv()
            if s <= n - 2:
                @pl.when(jnp.logical_and(k_r >= 0, h < n - 1))
                def _():
                    copy_right(s, k_r).start()

                @pl.when(jnp.logical_and(k_l <= n - 1, h > 0))
                def _():
                    copy_left(s, k_l).start()
        land[h] = x_ref[...]
        for s in range(n - 1):
            k_r = h - s
            k_l = h + s

            @pl.when(jnp.logical_and(k_r >= 0, h < n - 1))
            def _():
                copy_right(s, k_r).wait_send()

            @pl.when(jnp.logical_and(k_l <= n - 1, h > 0))
            def _():
                copy_left(s, k_l).wait_send()
        o_ref[...] = land[...]

    @pl.when(jnp.logical_not(valid))
    def _():
        o_ref[...] = jnp.zeros(o_ref.shape, o_ref.dtype)


def head_gather(x, tick, cid):
    n = lax.axis_size("head")
    rows, cols = x.shape
    return pl.pallas_call(
        functools.partial(gather_body, n, tick),
        out_shape=jax.ShapeDtypeStruct((n, rows, cols), x.dtype),
        in_specs=[pl.BlockSpec(memory_space=pltpu.VMEM)],
        out_specs=pl.BlockSpec(memory_space=pltpu.VMEM),
        scratch_shapes=[
            pltpu.VMEM((n, rows, cols), x.dtype),
            pltpu.SemaphoreType.DMA((n,)),
            pltpu.SemaphoreType.DMA((n,)),
            pltpu.SemaphoreType.DMA((n,)),
        ],
        compiler_params=pltpu.CompilerParams(collective_id=cid, has_side_effects=True),
    )(x)


def scatter_body(n, tick, p_ref, o_ref, recv_l, recv_r, send_l, send_r, ssem_l, ssem_r, rsem_l, rsem_r):
    h = lax.axis_index("head")
    valid = _tick_valid(*tick)
    link = send_r.dtype

    @pl.when(valid)
    def _():
        _enter(pltpu.get_barrier_semaphore(), h, n)

        def to_right(k):
            return pltpu.make_async_remote_copy(
                src_ref=send_r.at[k], dst_ref=recv_l.at[k], send_sem=ssem_r.at[k],
                recv_sem=rsem_l.at[k], device_id={"head": h + 1}, device_id_type=MESH)

        def to_left(k):
            return pltpu.make_async_remote_copy(
                src_ref=send_l.at[k], dst_ref=recv_r.at[k], send_sem=ssem_l.at[k],
                recv_sem=rsem_r.at[k], device_id={"head": h - 1}, device_id_type=MESH)

        for s in range(n - 1):
            k_r = n - 1 - s
            k_l = s

            @pl.when(k_r > h)
            def _():
                @pl.when(h > 0)
                def _():
                    to_right(k_r).wait_recv()
                    send_r[k_r] = (p_ref[k_r] + recv_l[k_r].astype(jnp.float32)).astype(link)

                @pl.when(h == 0)
                def _():
                    send_r[k_r] = p_ref[k_r].astype(link)

                to_right(k_r).start()

            @pl.when(k_l < h)
            def _():
                @pl.when(h < n - 1)
                def _():
                    to_left(k_l).wait_recv()
                    send_l[k_l] = (p_ref[k_l] + recv_r[k_l].astype(jnp.float32)).astype(link)

                @pl.when(h == n - 1)
                def _():
                    send_l[k_l] = p_ref[k_l].astype(link)

                to_left(k_l).start()
        total = p_ref[h]

        @pl.when(h > 0)
        def _():
            to_right(h).wait_recv()

        @pl.when(h < n - 1)
        def _():
            to_left(h).wait_recv()

        left_part = jnp.where(h > 0, recv_l[h].astype(jnp.float32), 0.0)
        right_part = jnp.where(h < n - 1, recv_r[h].astype(jnp.float32), 0.0)
        o_ref[...] = (total + left_part + right_part).astype(o_ref.dtype)
        for s in range(n - 1):
            k_r = n - 1 - s
            k_l = s

            @pl.when(k_r > h)
            def _():
                to_right(k_r).wait_send()

            @pl.when(k_l < h)
            def _():
                to_left(k_l).wait_send()

    @pl.when(jnp.logical_not(valid))
    def _():
        o_ref[...] = jnp.zeros(o_ref.shape, o_ref.dtype)


def head_scatter(parts, tick, cid, link=jnp.bfloat16):
    n = lax.axis_size("head")
    _, rows, cols = parts.shape
    return pl.pallas_call(
        functools.partial(scatter_body, n, tick),
        out_shape=jax.ShapeDtypeStruct((rows, cols), jnp.float32),
        in_specs=[pl.BlockSpec(memory_space=pltpu.VMEM)],
        out_specs=pl.BlockSpec(memory_space=pltpu.VMEM),
        scratch_shapes=[
            pltpu.VMEM((n, rows, cols), link),
            pltpu.VMEM((n, rows, cols), link),
            pltpu.VMEM((n, rows, cols), link),
            pltpu.VMEM((n, rows, cols), link),
            pltpu.SemaphoreType.DMA((n,)),
            pltpu.SemaphoreType.DMA((n,)),
            pltpu.SemaphoreType.DMA((n,)),
            pltpu.SemaphoreType.DMA((n,)),
        ],
        compiler_params=pltpu.CompilerParams(collective_id=cid, has_side_effects=True),
    )(parts)


norm_eps = 1e-05
far_below = -1e30
highest = lax.Precision.HIGHEST


def shifted(value, axis, by):
    count = lax.axis_size(axis)
    pairs = [(i, i + by) for i in range(count) if 0 <= i + by < count]
    return lax.ppermute(value, axis, pairs)


def entering(value, axis, combine, identity):
    count, mine = (lax.axis_size(axis), lax.axis_index(axis))
    everything = jax.tree.map(lambda part: lax.all_gather(part, axis), value)
    before = jax.tree.map(
        lambda part, zero: jnp.broadcast_to(jnp.asarray(zero, part.dtype), part.shape),
        value,
        identity,
    )
    for k in range(count - 1):
        reached = k < mine
        new = combine(before, jax.tree.map(lambda part: part[k], everything))
        before = jax.tree.map(lambda a, b: jnp.where(reached, a, b), new, before)
    return before


def entering_2(value, axis, join, neutral):
    count = lax.axis_size(axis)
    place = lax.axis_index(axis)
    ahead = count - 1 - place
    gathered = jax.tree.map(
        lambda a, kind: lax.all_gather(a.astype(kind), axis),
        value,
        jax.tree.map(lambda a: jnp.bfloat16 if a.dtype == jnp.float32 else a.dtype, value),
    )
    state = jax.tree.map(lambda a, e: jnp.zeros_like(a) + jnp.asarray(e, a.dtype), value, neutral)
    for lap in range(count - 1):
        source = count - 1 - lap
        new = join(
            state,
            jax.tree.map(lambda a, own: a[source].astype(own.dtype), gathered, value),
        )
        active = lap < ahead
        state = jax.tree.map(lambda a, b: jnp.where(active, a, b), new, state)
    return state


def rms_scale(values):
    return lax.rsqrt(jnp.mean(values * values, axis=-1, keepdims=True) + norm_eps)


def silu_slope(values):
    logistic = jax.nn.sigmoid(values)
    return logistic * (1.0 + values * (1.0 - logistic))


def causal_conv(extended, marks_ext, weight, conv_bias):
    tap_count = weight.shape[0]
    length = extended.shape[0] - tap_count + 1
    counts = jnp.cumsum(marks_ext)
    conv_sum = jnp.zeros((length, extended.shape[1]), jnp.float32) + conv_bias
    for tap_index in range(tap_count):
        linked = (counts[tap_count - 1 :] == counts[tap_index : tap_index + length]).astype(
            jnp.float32
        )
        conv_sum = (
            conv_sum
            + linked[:, None] * weight[tap_index] * extended[tap_index : tap_index + length]
        )
    return conv_sum


def prepare(extended, dt_pre, marks_ext, alive_mask, conv_weight, conv_bias, dt_bias, a_log):
    inner_width = dt_pre.shape[1] * P_SIZE
    activated = jax.nn.silu(causal_conv(extended, marks_ext, conv_weight, conv_bias))
    inner_act = activated[:, :inner_width] * alive_mask[:, None]
    b_mat = activated[:, inner_width : inner_width + N]
    c_mat = activated[:, inner_width + N :]
    step_size = jax.nn.softplus(dt_pre + dt_bias) * alive_mask[:, None]
    log_decay = -step_size * jnp.exp(a_log)
    return (inner_act, step_size, log_decay, b_mat, c_mat)


def block_terms(inner_act, step_size, log_decay, b_mat, start_marks):
    blocks = inner_act.shape[0] // SCAN_BLOCK
    head_count = step_size.shape[1]
    x_blocks = inner_act.reshape(blocks, SCAN_BLOCK, head_count, P_SIZE)
    dt_blocks = step_size.reshape(blocks, SCAN_BLOCK, head_count)
    cum_decay = jnp.cumsum(log_decay.reshape(blocks, SCAN_BLOCK, head_count), axis=1)
    mark_count = jnp.cumsum(start_marks.reshape(blocks, SCAN_BLOCK), axis=1)
    b_blocks = b_mat.reshape(blocks, SCAN_BLOCK, N)
    last_cum = cum_decay[:, -1]
    last_mark = mark_count[:, -1]
    same_end = (mark_count == last_mark[:, None]).astype(jnp.float32)
    end_weight = jnp.exp(last_cum[:, None, :] - cum_decay) * same_end[:, :, None] * dt_blocks
    block_states = jnp.einsum(
        "cjh,cjhp,cjn->chpn", end_weight, x_blocks, b_blocks, precision=highest
    )
    block_decay = jnp.exp(last_cum) * (last_mark == 0).astype(jnp.float32)[:, None]
    return (block_decay, block_states, cum_decay, mark_count, x_blocks, dt_blocks)


def compose_blocks(block_decay, block_states, start_state):
    chain_state = start_state
    incoming = []
    for block_index in range(block_decay.shape[0]):
        incoming.append(chain_state)
        chain_state = (
            block_decay[block_index][:, None, None] * chain_state + block_states[block_index]
        )
    return (chain_state, jnp.stack(incoming))


def block_output(block_parts, b_mat, c_mat, skip, incoming):
    block_decay, block_states, cum_decay, mark_count, x_blocks, dt_blocks = block_parts
    blocks = cum_decay.shape[0]
    head_count = cum_decay.shape[2]
    b_blocks = b_mat.reshape(blocks, SCAN_BLOCK, N)
    c_blocks = c_mat.reshape(blocks, SCAN_BLOCK, N)
    inner_prod = jnp.einsum("cin,cjn->cij", c_blocks, b_blocks, precision=highest)
    arange_pos = jnp.arange(SCAN_BLOCK)
    linked = (arange_pos[:, None] >= arange_pos[None, :])[None] & (
        mark_count[:, :, None] == mark_count[:, None, :]
    )
    spread = jnp.where(
        linked[..., None], cum_decay[:, :, None, :] - cum_decay[:, None, :, :], far_below
    )
    weights = jnp.exp(spread) * inner_prod[..., None] * dt_blocks[:, None, :, :]
    y_intra = jnp.einsum("cijh,cjhp->cihp", weights, x_blocks, precision=highest)
    carry_in = jnp.exp(cum_decay) * (mark_count == 0).astype(jnp.float32)[:, :, None]
    y_inter = (
        jnp.einsum("cin,chpn->cihp", c_blocks, incoming, precision=highest) * carry_in[..., None]
    )
    mixed_out = y_intra + y_inter + skip[None, None, :, None] * x_blocks
    return mixed_out.reshape(blocks * SCAN_BLOCK, head_count * P_SIZE)


def local_front(marks_ext, alive_mask, extended, dt_pre, conv_weight, conv_bias, dt_bias, a_log):
    inner_act, step_size, log_decay, b_mat, c_mat = prepare(
        extended, dt_pre, marks_ext, alive_mask, conv_weight, conv_bias, dt_bias, a_log
    )
    block_parts = block_terms(inner_act, step_size, log_decay, b_mat, marks_ext[KW - 1 :])
    zero_state = jnp.zeros(block_parts[1].shape[1:], jnp.float32)
    total_state, _ = compose_blocks(block_parts[0], block_parts[1], zero_state)
    total_decay = jnp.prod(block_parts[0], axis=0)
    return (block_parts, b_mat, c_mat, total_decay, total_state)


def local_rear(block_parts, b_mat, c_mat, skip, start_state):
    _, incoming = compose_blocks(block_parts[0], block_parts[1], start_state)
    return block_output(block_parts, b_mat, c_mat, skip, incoming)


def local_pass(
    marks_ext,
    alive_mask,
    extended,
    dt_pre,
    conv_weight,
    conv_bias,
    dt_bias,
    a_log,
    skip,
    start_state,
):
    block_parts, b_mat, c_mat, total_decay, total_state = local_front(
        marks_ext, alive_mask, extended, dt_pre, conv_weight, conv_bias, dt_bias, a_log
    )
    return (local_rear(block_parts, b_mat, c_mat, skip, start_state), total_decay, total_state)


def chain_combine(earlier, later):
    return (earlier[0] * later[0], later[0][:, None, None] * earlier[1] + later[1])


def extend(pre_conv, start_marks, edge_rows, edge_marks):
    extended = jnp.concatenate([edge_rows, pre_conv], axis=0)
    marks_ext = jnp.concatenate([edge_marks.astype(jnp.int32), start_marks], axis=0)
    return (extended, marks_ext)


def mixer_forward(stream, start_marks, alive_mask, layer_weights, tick, ids):
    (
        norm_gain,
        w_main,
        w_low,
        w_bc,
        conv_weight,
        conv_bias,
        dt_bias,
        a_log,
        skip,
        gate_gain,
        w_out,
    ) = layer_weights
    inner_width = w_out.shape[0]
    normed = (stream * rms_scale(stream) * norm_gain).astype(jnp.bfloat16)
    gathered = head_gather(normed, tick, ids[0])
    gathered = gathered.reshape(-1, gathered.shape[-1])
    projected = jnp.dot(gathered, w_main, preferred_element_type=jnp.float32)
    gate_pre = projected[:, :inner_width]
    pre_conv = projected[:, inner_width : 2 * inner_width + 2 * N]
    dt_pre = projected[:, 2 * inner_width + 2 * N :]
    marks_float = start_marks.astype(jnp.float32)
    tail_from = pre_conv.shape[0] - KW + 1
    edge_parts = shifted((pre_conv[tail_from:], marks_float[tail_from:]), "seq", 1)
    extended, marks_ext = extend(pre_conv, start_marks, edge_parts[0], edge_parts[1])
    front_fn = partial(local_front, marks_ext, alive_mask)
    front_out, front_pull = jax.vjp(
        front_fn, extended, dt_pre, conv_weight, conv_bias, dt_bias, a_log
    )
    block_parts, b_mat, c_mat, total_decay, total_state = front_out
    neutral = (jnp.ones_like(total_decay), jnp.zeros_like(total_state))
    prefix = entering((total_decay, total_state), "seq", chain_combine, neutral)
    start_state = prefix[1]
    mixed_out, rear_pull = jax.vjp(local_rear, block_parts, b_mat, c_mat, skip, start_state)
    silu_gate = jax.nn.silu(gate_pre)
    gated_mix = mixed_out * silu_gate
    square_total = lax.psum(jnp.sum(gated_mix * gated_mix, axis=-1), "head")
    scale_out = lax.rsqrt(square_total / DI + norm_eps)
    normed_out = (gated_mix * scale_out[:, None] * gate_gain).astype(jnp.bfloat16)
    head_count = lax.axis_size("head")
    branch = head_scatter(
        jnp.dot(normed_out, w_out, preferred_element_type=jnp.float32).reshape(
            head_count, -1, w_out.shape[1]
        ),
        tick,
        ids[1],
    )
    saved = (
        stream,
        gathered,
        gate_pre,
        mixed_out,
        silu_gate,
        gated_mix,
        scale_out,
        normed_out,
        total_decay,
        start_state,
        front_pull,
        rear_pull,
    )
    return stream + branch, saved


def mixer_backward(grad_next, layer_weights, saved, mask_value, tick, ids, hook=None):
    (
        norm_gain,
        w_main,
        w_low,
        w_bc,
        conv_weight,
        conv_bias,
        dt_bias,
        a_log,
        skip,
        gate_gain,
        w_out,
    ) = layer_weights
    (
        stream,
        gathered,
        gate_pre,
        mixed_out,
        silu_gate,
        gated_mix,
        scale_out,
        normed_out,
        total_decay,
        start_state,
        front_pull,
        rear_pull,
    ) = saved
    inner_width = w_out.shape[0]
    grad_branch = grad_next.astype(jnp.bfloat16)
    shard_rows = head_gather(grad_branch, tick, ids[0])
    shard_rows = shard_rows.reshape(-1, shard_rows.shape[-1])
    g_w_out = lax.dot_general(
        normed_out, shard_rows, (((0,), (0,)), ((), ())), preferred_element_type=jnp.float32
    ) * mask_value
    grad_normed = lax.dot_general(
        shard_rows, w_out, (((1,), (1,)), ((), ())), preferred_element_type=jnp.float32
    )
    weighted = grad_normed * gate_gain
    g_gate_gain = jnp.sum(grad_normed * gated_mix * scale_out[:, None], axis=0)
    cross_sum = lax.psum(jnp.sum(weighted * gated_mix, axis=-1), "head")
    grad_gated = (
        scale_out[:, None] * weighted - gated_mix * (scale_out**3 * cross_sum / DI)[:, None]
    )
    grad_mixed = grad_gated * silu_gate
    grad_gate = (grad_gated * mixed_out * silu_slope(gate_pre)).astype(jnp.bfloat16)
    g_parts, g_b_mat, g_c_mat, g_skip, g_start = rear_pull(grad_mixed)
    neutral = (jnp.ones_like(total_decay), jnp.zeros_like(g_start))
    suffix = entering_2((total_decay, g_start), "seq", chain_combine, neutral)
    after_state = suffix[1]
    grad_decay = jnp.sum(after_state * start_state, axis=(1, 2))
    grad_ext, grad_dt_pre, g_conv_w, g_conv_b, g_dt_bias, g_a_log = front_pull(
        (g_parts, g_b_mat, g_c_mat, grad_decay, after_state)
    )
    returned = shifted(grad_ext[: KW - 1], "seq", -1)
    grad_pre = grad_ext[KW - 1 :]
    tail_from = grad_pre.shape[0] - KW + 1
    grad_pre = jnp.concatenate([grad_pre[:tail_from], grad_pre[tail_from:] + returned], axis=0)
    grad_inner = grad_pre[:, :inner_width].astype(jnp.bfloat16)
    grad_bc = grad_pre[:, inner_width:]
    grad_low = jnp.concatenate([grad_gate, grad_inner, grad_dt_pre.astype(jnp.bfloat16)], axis=1)
    w_bc_float = w_bc.astype(jnp.float32)
    g_low = lax.dot_general(
        gathered, grad_low, (((0,), (0,)), ((), ())), preferred_element_type=jnp.float32
    )
    g_w_bc = lax.dot_general(
        gathered.astype(jnp.float32),
        grad_bc,
        (((0,), (0,)), ((), ())),
        precision=highest,
        preferred_element_type=jnp.float32,
    )
    main_term = lax.dot_general(
        grad_low, w_low, (((1,), (1,)), ((), ())), preferred_element_type=jnp.float32
    )
    side_term = lax.dot_general(
        grad_bc,
        w_bc_float,
        (((1,), (1,)), ((), ())),
        precision=highest,
        preferred_element_type=jnp.float32,
    )
    head_count = lax.axis_size("head")
    lead = 0.0
    if hook is not None:
        lead = hook((g_w_bc, g_conv_w[:, inner_width:], g_conv_b[inner_width:]))
    grad_normed_in = head_scatter(
        (main_term + side_term + lead).reshape(head_count, -1, main_term.shape[1]), tick, ids[1]
    )
    scale_in = rms_scale(stream)
    g_norm_gain = jnp.sum(grad_normed_in * stream * scale_in, axis=0)
    weighted_in = grad_normed_in * norm_gain
    grad_stream = (
        grad_next
        + scale_in * weighted_in
        - stream * scale_in**3 * jnp.mean(weighted_in * stream, axis=-1, keepdims=True)
    )
    head_part = (
        g_low[:, :inner_width],
        g_low[:, inner_width : 2 * inner_width],
        g_low[:, 2 * inner_width :],
        g_conv_w[:, :inner_width],
        g_conv_b[:inner_width],
        g_dt_bias,
        g_a_log,
        g_skip,
        g_gate_gain,
    )
    shared_part = (g_norm_gain, g_w_bc, g_conv_w[:, inner_width:], g_conv_b[inner_width:])
    return (grad_stream, head_part, shared_part, g_w_out)


def pack_rows(members, width, multiple):
    rows = jnp.concatenate([member.reshape(-1, width) for member in members], axis=0)
    return jnp.pad(rows, ((0, -rows.shape[0] % multiple), (0, 0)))


def unpack_rows(rows, shapes, width):
    pieces = []
    start = 0
    for shape in shapes:
        count = math.prod(shape) // width
        pieces.append(rows[start : start + count].reshape(shape))
        start += count
    return tuple(pieces)


def reduce_grads(head_part, norm_part, bc_part, tick_count):
    summed = lax.psum(
        tuple(member.astype(jnp.bfloat16) for member in head_part[:3] + (bc_part,)), "seq"
    )
    head_sum = tuple(member.astype(jnp.float32) for member in summed[:3]) + tuple(
        lax.psum(member.astype(jnp.bfloat16), "seq").astype(jnp.float32)
        for member in head_part[3:]
    )
    bc_rows = head_gather(summed[3], (0, 0, 1), 4 * tick_count + 1).astype(jnp.float32)
    norm_sum = lax.psum(norm_part, ("seq", "head"))
    return (head_sum, norm_sum, bc_rows.reshape(-1, bc_rows.shape[-1]))


def store_slot(buffer, value, slot_index, is_valid):
    current = lax.dynamic_index_in_dim(buffer, slot_index, 0, False)
    return lax.dynamic_update_index_in_dim(
        buffer, jnp.where(is_valid, value, current), slot_index, 0
    )


def on_device(
    inputs,
    cotangent,
    starts,
    live,
    norm_gain,
    w_gate,
    w_in,
    w_bc,
    w_dt,
    conv_x,
    conv_x_bias,
    conv_bc,
    conv_bc_bias,
    dt_bias,
    a_log,
    skip,
    gate_gain,
    w_out,
):
    section_count = lax.axis_size("section")
    section_index = lax.axis_index("section")
    micro_count = inputs.shape[0]
    tick_count = micro_count + section_count - 1
    w_main = jnp.concatenate([w_gate[0], w_in[0], w_bc[0], w_dt[0]], axis=1)
    w_low = jnp.concatenate([w_gate[0], w_in[0], w_dt[0]], axis=1)
    conv_weight = jnp.concatenate([conv_x[0], conv_bc[0]], axis=1).astype(jnp.float32)
    conv_bias = jnp.concatenate([conv_x_bias[0], conv_bc_bias[0]], axis=0)
    layer_weights = (
        norm_gain[0],
        w_main,
        w_low,
        w_bc[0],
        conv_weight,
        conv_bias,
        dt_bias[0],
        a_log[0],
        skip[0],
        gate_gain[0],
        w_out[0],
    )
    row_shape = inputs.shape[1:]
    outputs_all = jnp.zeros((micro_count,) + row_shape, jnp.float32)
    arrived = jnp.zeros(row_shape, jnp.float32)
    ticks = []
    for tick_index in range(tick_count):
        slot_index = tick_index - section_index
        is_valid = (slot_index >= 0) & (slot_index < micro_count)
        clipped = jnp.clip(slot_index, 0, micro_count - 1)
        fresh_rows = lax.dynamic_index_in_dim(inputs, clipped, 0, False).astype(jnp.float32)
        stream = jnp.where(section_index == 0, fresh_rows, arrived)
        start_marks = lax.dynamic_index_in_dim(starts, clipped, 0, False)
        alive_mask = lax.dynamic_index_in_dim(live, clipped, 0, False).astype(jnp.float32)
        result, saved = mixer_forward(
            stream,
            start_marks,
            alive_mask,
            layer_weights,
            (tick_index, -1, micro_count),
            (tick_index, tick_count + tick_index),
        )
        outputs_all = store_slot(outputs_all, result, clipped, is_valid)
        ticks.append((clipped, is_valid, saved))
        if tick_index + 1 < tick_count:
            arrived = shifted(result, "section", 1)
    back_arrived = jnp.zeros(row_shape, jnp.float32)
    input_grads = jnp.zeros((micro_count,) + row_shape, jnp.float32)
    head_count = lax.axis_size("head")
    bc_box = []
    head_total = ()
    shared_total = ()
    for tick_index in range(tick_count):
        clipped, is_valid, saved = ticks[tick_count - 1 - tick_index]
        outer_grad = lax.dynamic_index_in_dim(cotangent, clipped, 0, False).astype(jnp.float32)
        grad_next = jnp.where(section_index == section_count - 1, outer_grad, back_arrived)
        mask_value = is_valid.astype(jnp.float32)
        hook = None
        if tick_index + 1 == tick_count:

            def hook(bc_local, mask_value=mask_value, earlier=shared_total):
                totals = tuple(
                    (prev + member * mask_value) if earlier else member * mask_value
                    for prev, member in zip(earlier[1:] or bc_local, bc_local)
                )
                rows = pack_rows(totals, totals[0].shape[-1], 8 * head_count)
                part = head_scatter(
                    rows.reshape(head_count, -1, rows.shape[-1]), (0, 0, 1), 4 * tick_count
                )
                bc_box.append((part, [member.shape for member in totals]))
                return part[0, 0] * 0.0

        grad_stream, head_part, shared_part, out_part = mixer_backward(
            grad_next,
            layer_weights,
            saved,
            mask_value,
            (tick_count - 1 - tick_index, -1, micro_count),
            (2 * tick_count + tick_index, 3 * tick_count + tick_index),
            hook,
        )
        if tick_index == 0:
            out_total = out_part
        else:
            out_total = out_total + out_part
        if tick_index + 1 == tick_count:
            out_total = lax.psum(out_total.astype(jnp.bfloat16), "seq")
        head_part = tuple((member * mask_value for member in head_part))
        shared_part = tuple((member * mask_value for member in shared_part))
        if tick_index == 0:
            head_total = head_part
            shared_total = shared_part
        else:
            head_total = tuple((former + latter for former, latter in zip(head_total, head_part)))
            shared_total = tuple(
                (former + latter for former, latter in zip(shared_total, shared_part))
            )
        input_grads = store_slot(input_grads, grad_stream, clipped, is_valid)
        if tick_index + 1 < tick_count:
            back_arrived = shifted(grad_stream.astype(jnp.bfloat16), "section", -1).astype(
                grad_stream.dtype
            )
    anchor = out_total[0, 0].astype(jnp.float32) * 0.0
    head_total = (head_total[0] + anchor,) + head_total[1:]
    bc_part, bc_shapes = bc_box[0]
    head_total, norm_sum, bc_rows = reduce_grads(head_total, shared_total[0], bc_part, tick_count)
    shared_total = (norm_sum,) + unpack_rows(bc_rows, bc_shapes, bc_rows.shape[-1])
    head_total = head_total[:3] + (out_total.astype(jnp.float32),) + head_total[3:]
    return (
        outputs_all[None],
        input_grads[None],
        shared_total[0][None],
        head_total[0][None],
        head_total[1][None],
        shared_total[1][None],
        head_total[2][None],
        head_total[4][None],
        head_total[5][None],
        shared_total[2][None],
        shared_total[3][None],
        head_total[6][None],
        head_total[7][None],
        head_total[8][None],
        head_total[9][None],
        head_total[3][None],
    )


def solution(mesh):
    return jax.shard_map(
        on_device,
        mesh=mesh,
        in_specs=(
            P(None, ("seq", "head"), None),
            P(None, ("seq", "head"), None),
            P(None, "seq"),
            P(None, "seq"),
            P("section", None),
            P("section", None, "head"),
            P("section", None, "head"),
            P("section", None, None),
            P("section", None, "head"),
            P("section", None, "head"),
            P("section", "head"),
            P("section", None, None),
            P("section", None),
            P("section", "head"),
            P("section", "head"),
            P("section", "head"),
            P("section", "head"),
            P("section", "head", None),
        ),
        out_specs=(
            P("section", None, ("seq", "head"), None),
            P("section", None, ("seq", "head"), None),
            P("section", None),
            P("section", None, "head"),
            P("section", None, "head"),
            P("section", None, None),
            P("section", None, "head"),
            P("section", None, "head"),
            P("section", "head"),
            P("section", None, None),
            P("section", None),
            P("section", "head"),
            P("section", "head"),
            P("section", "head"),
            P("section", "head"),
            P("section", "head", None),
        ),
        check_vma=False,
    )
```

```python
from functools import partial

import functools
import math

import jax
import jax.numpy as jnp
from jax import lax
from jax.experimental import pallas as pl
from jax.experimental.pallas import tpu as pltpu
from jax.sharding import PartitionSpec as P

DI = 4096
P_SIZE = 64
N = 128
KW = 4
SCAN_BLOCK = 256


MESH = pl.DeviceIdType.MESH


def _tick_valid(offset, sign, count):
    slot = offset + sign * lax.axis_index("section")
    return jnp.logical_and(slot >= 0, slot < count)


def _enter(barrier, h, n):
    @pl.when(h > 0)
    def _():
        pl.semaphore_signal(barrier, 1, device_id={"head": h - 1}, device_id_type=MESH)

    @pl.when(h < n - 1)
    def _():
        pl.semaphore_signal(barrier, 1, device_id={"head": h + 1}, device_id_type=MESH)

    @pl.when(jnp.logical_and(h > 0, h < n - 1))
    def _():
        pl.semaphore_wait(barrier, 2)

    @pl.when(jnp.logical_or(h == 0, h == n - 1))
    def _():
        pl.semaphore_wait(barrier, 1)


def gather_body(n, tick, x_ref, o_ref, land, send_r, send_l, recv):
    h = lax.axis_index("head")
    valid = _tick_valid(*tick)

    @pl.when(valid)
    def _():
        _enter(pltpu.get_barrier_semaphore(), h, n)

        def copy_right(s, k):
            src = x_ref if s == 0 else land.at[k]
            return pltpu.make_async_remote_copy(
                src_ref=src, dst_ref=land.at[k], send_sem=send_r.at[s], recv_sem=recv.at[k],
                device_id={"head": h + 1}, device_id_type=MESH)

        def copy_left(s, k):
            src = x_ref if s == 0 else land.at[k]
            return pltpu.make_async_remote_copy(
                src_ref=src, dst_ref=land.at[k], send_sem=send_l.at[s], recv_sem=recv.at[k],
                device_id={"head": h - 1}, device_id_type=MESH)

        for s in range(n):
            k_r = h - s
            k_l = h + s
            if s >= 1:
                @pl.when(k_r >= 0)
                def _():
                    pltpu.make_async_remote_copy(
                        src_ref=land.at[k_r], dst_ref=land.at[k_r], send_sem=send_r.at[0],
                        recv_sem=recv.at[k_r], device_id={"head": h}, device_id_type=MESH
                    ).wait_recv()

                @pl.when(k_l <= n - 1)
                def _():
                    pltpu.make_async_remote_copy(
                        src_ref=land.at[k_l], dst_ref=land.at[k_l], send_sem=send_l.at[0],
                        recv_sem=recv.at[k_l], device_id={"head": h}, device_id_type=MESH
                    ).wait_recv()
            if s <= n - 2:
                @pl.when(jnp.logical_and(k_r >= 0, h < n - 1))
                def _():
                    copy_right(s, k_r).start()

                @pl.when(jnp.logical_and(k_l <= n - 1, h > 0))
                def _():
                    copy_left(s, k_l).start()
        land[h] = x_ref[...]
        for s in range(n - 1):
            k_r = h - s
            k_l = h + s

            @pl.when(jnp.logical_and(k_r >= 0, h < n - 1))
            def _():
                copy_right(s, k_r).wait_send()

            @pl.when(jnp.logical_and(k_l <= n - 1, h > 0))
            def _():
                copy_left(s, k_l).wait_send()
        o_ref[...] = land[...]

    @pl.when(jnp.logical_not(valid))
    def _():
        o_ref[...] = jnp.zeros(o_ref.shape, o_ref.dtype)


def head_gather(x, tick, cid):
    n = lax.axis_size("head")
    rows, cols = x.shape
    return pl.pallas_call(
        functools.partial(gather_body, n, tick),
        out_shape=jax.ShapeDtypeStruct((n, rows, cols), x.dtype),
        in_specs=[pl.BlockSpec(memory_space=pltpu.VMEM)],
        out_specs=pl.BlockSpec(memory_space=pltpu.VMEM),
        scratch_shapes=[
            pltpu.VMEM((n, rows, cols), x.dtype),
            pltpu.SemaphoreType.DMA((n,)),
            pltpu.SemaphoreType.DMA((n,)),
            pltpu.SemaphoreType.DMA((n,)),
        ],
        compiler_params=pltpu.CompilerParams(collective_id=cid, has_side_effects=True),
    )(x)


def scatter_body(n, tick, p_ref, o_ref, recv_l, recv_r, send_l, send_r, ssem_l, ssem_r, rsem_l, rsem_r):
    h = lax.axis_index("head")
    valid = _tick_valid(*tick)
    link = send_r.dtype

    @pl.when(valid)
    def _():
        _enter(pltpu.get_barrier_semaphore(), h, n)

        def to_right(k):
            return pltpu.make_async_remote_copy(
                src_ref=send_r.at[k], dst_ref=recv_l.at[k], send_sem=ssem_r.at[k],
                recv_sem=rsem_l.at[k], device_id={"head": h + 1}, device_id_type=MESH)

        def to_left(k):
            return pltpu.make_async_remote_copy(
                src_ref=send_l.at[k], dst_ref=recv_r.at[k], send_sem=ssem_l.at[k],
                recv_sem=rsem_r.at[k], device_id={"head": h - 1}, device_id_type=MESH)

        for s in range(n - 1):
            k_r = n - 1 - s
            k_l = s

            @pl.when(k_r > h)
            def _():
                @pl.when(h > 0)
                def _():
                    to_right(k_r).wait_recv()
                    send_r[k_r] = (p_ref[k_r] + recv_l[k_r].astype(jnp.float32)).astype(link)

                @pl.when(h == 0)
                def _():
                    send_r[k_r] = p_ref[k_r].astype(link)

                to_right(k_r).start()

            @pl.when(k_l < h)
            def _():
                @pl.when(h < n - 1)
                def _():
                    to_left(k_l).wait_recv()
                    send_l[k_l] = (p_ref[k_l] + recv_r[k_l].astype(jnp.float32)).astype(link)

                @pl.when(h == n - 1)
                def _():
                    send_l[k_l] = p_ref[k_l].astype(link)

                to_left(k_l).start()
        total = p_ref[h]

        @pl.when(h > 0)
        def _():
            to_right(h).wait_recv()

        @pl.when(h < n - 1)
        def _():
            to_left(h).wait_recv()

        left_part = jnp.where(h > 0, recv_l[h].astype(jnp.float32), 0.0)
        right_part = jnp.where(h < n - 1, recv_r[h].astype(jnp.float32), 0.0)
        o_ref[...] = (total + left_part + right_part).astype(o_ref.dtype)
        for s in range(n - 1):
            k_r = n - 1 - s
            k_l = s

            @pl.when(k_r > h)
            def _():
                to_right(k_r).wait_send()

            @pl.when(k_l < h)
            def _():
                to_left(k_l).wait_send()

    @pl.when(jnp.logical_not(valid))
    def _():
        o_ref[...] = jnp.zeros(o_ref.shape, o_ref.dtype)


def head_sum_rows(values, tick, cid):
    blocks = head_gather(values.reshape(-1, 128), tick, cid)
    total = blocks[0]
    for index in range(1, blocks.shape[0]):
        total = total + blocks[index]
    return total.reshape(values.shape)


def head_scatter(parts, tick, cid, link=jnp.bfloat16):
    n = lax.axis_size("head")
    _, rows, cols = parts.shape
    return pl.pallas_call(
        functools.partial(scatter_body, n, tick),
        out_shape=jax.ShapeDtypeStruct((rows, cols), jnp.float32),
        in_specs=[pl.BlockSpec(memory_space=pltpu.VMEM)],
        out_specs=pl.BlockSpec(memory_space=pltpu.VMEM),
        scratch_shapes=[
            pltpu.VMEM((n, rows, cols), link),
            pltpu.VMEM((n, rows, cols), link),
            pltpu.VMEM((n, rows, cols), link),
            pltpu.VMEM((n, rows, cols), link),
            pltpu.SemaphoreType.DMA((n,)),
            pltpu.SemaphoreType.DMA((n,)),
            pltpu.SemaphoreType.DMA((n,)),
            pltpu.SemaphoreType.DMA((n,)),
        ],
        compiler_params=pltpu.CompilerParams(collective_id=cid, has_side_effects=True),
    )(parts)


norm_eps = 1e-05
far_below = -1e30
highest = lax.Precision.HIGHEST


def shifted(value, axis, by):
    count = lax.axis_size(axis)
    pairs = [(i, i + by) for i in range(count) if 0 <= i + by < count]
    return lax.ppermute(value, axis, pairs)


def entering(value, axis, combine, identity):
    count, mine = (lax.axis_size(axis), lax.axis_index(axis))
    everything = jax.tree.map(lambda part: lax.all_gather(part, axis), value)
    before = jax.tree.map(
        lambda part, zero: jnp.broadcast_to(jnp.asarray(zero, part.dtype), part.shape),
        value,
        identity,
    )
    for k in range(count - 1):
        reached = k < mine
        new = combine(before, jax.tree.map(lambda part: part[k], everything))
        before = jax.tree.map(lambda a, b: jnp.where(reached, a, b), new, before)
    return before


def entering_2(value, axis, join, neutral):
    count = lax.axis_size(axis)
    place = lax.axis_index(axis)
    ahead = count - 1 - place
    gathered = jax.tree.map(
        lambda a, kind: lax.all_gather(a.astype(kind), axis),
        value,
        jax.tree.map(lambda a: jnp.bfloat16 if a.dtype == jnp.float32 else a.dtype, value),
    )
    state = jax.tree.map(lambda a, e: jnp.zeros_like(a) + jnp.asarray(e, a.dtype), value, neutral)
    for lap in range(count - 1):
        source = count - 1 - lap
        new = join(
            state,
            jax.tree.map(lambda a, own: a[source].astype(own.dtype), gathered, value),
        )
        active = lap < ahead
        state = jax.tree.map(lambda a, b: jnp.where(active, a, b), new, state)
    return state


def rms_scale(values):
    return lax.rsqrt(jnp.mean(values * values, axis=-1, keepdims=True) + norm_eps)


def silu_slope(values):
    logistic = jax.nn.sigmoid(values)
    return logistic * (1.0 + values * (1.0 - logistic))


def causal_conv(extended, marks_ext, weight, conv_bias):
    tap_count = weight.shape[0]
    length = extended.shape[0] - tap_count + 1
    counts = jnp.cumsum(marks_ext)
    conv_sum = jnp.zeros((length, extended.shape[1]), jnp.float32) + conv_bias
    for tap_index in range(tap_count):
        linked = (counts[tap_count - 1 :] == counts[tap_index : tap_index + length]).astype(
            jnp.float32
        )
        conv_sum = (
            conv_sum
            + linked[:, None] * weight[tap_index] * extended[tap_index : tap_index + length]
        )
    return conv_sum


def prepare(extended, dt_pre, marks_ext, alive_mask, conv_weight, conv_bias, dt_bias, a_log):
    inner_width = dt_pre.shape[1] * P_SIZE
    activated = jax.nn.silu(causal_conv(extended, marks_ext, conv_weight, conv_bias))
    inner_act = activated[:, :inner_width] * alive_mask[:, None]
    b_mat = activated[:, inner_width : inner_width + N]
    c_mat = activated[:, inner_width + N :]
    step_size = jax.nn.softplus(dt_pre + dt_bias) * alive_mask[:, None]
    log_decay = -step_size * jnp.exp(a_log)
    return (inner_act, step_size, log_decay, b_mat, c_mat)


def block_terms(inner_act, step_size, log_decay, b_mat, start_marks):
    blocks = inner_act.shape[0] // SCAN_BLOCK
    head_count = step_size.shape[1]
    x_blocks = inner_act.reshape(blocks, SCAN_BLOCK, head_count, P_SIZE)
    dt_blocks = step_size.reshape(blocks, SCAN_BLOCK, head_count)
    cum_decay = jnp.cumsum(log_decay.reshape(blocks, SCAN_BLOCK, head_count), axis=1)
    mark_count = jnp.cumsum(start_marks.reshape(blocks, SCAN_BLOCK), axis=1)
    b_blocks = b_mat.reshape(blocks, SCAN_BLOCK, N)
    last_cum = cum_decay[:, -1]
    last_mark = mark_count[:, -1]
    same_end = (mark_count == last_mark[:, None]).astype(jnp.float32)
    end_weight = jnp.exp(last_cum[:, None, :] - cum_decay) * same_end[:, :, None] * dt_blocks
    block_states = jnp.einsum(
        "cjh,cjhp,cjn->chpn", end_weight, x_blocks, b_blocks, precision=highest
    )
    block_decay = jnp.exp(last_cum) * (last_mark == 0).astype(jnp.float32)[:, None]
    return (block_decay, block_states, cum_decay, mark_count, x_blocks, dt_blocks)


def compose_blocks(block_decay, block_states, start_state):
    chain_state = start_state
    incoming = []
    for block_index in range(block_decay.shape[0]):
        incoming.append(chain_state)
        chain_state = (
            block_decay[block_index][:, None, None] * chain_state + block_states[block_index]
        )
    return (chain_state, jnp.stack(incoming))


def block_output(block_parts, b_mat, c_mat, skip, incoming):
    block_decay, block_states, cum_decay, mark_count, x_blocks, dt_blocks = block_parts
    blocks = cum_decay.shape[0]
    head_count = cum_decay.shape[2]
    b_blocks = b_mat.reshape(blocks, SCAN_BLOCK, N)
    c_blocks = c_mat.reshape(blocks, SCAN_BLOCK, N)
    inner_prod = jnp.einsum("cin,cjn->cij", c_blocks, b_blocks, precision=highest)
    arange_pos = jnp.arange(SCAN_BLOCK)
    linked = (arange_pos[:, None] >= arange_pos[None, :])[None] & (
        mark_count[:, :, None] == mark_count[:, None, :]
    )
    spread = jnp.where(
        linked[..., None], cum_decay[:, :, None, :] - cum_decay[:, None, :, :], far_below
    )
    weights = jnp.exp(spread) * inner_prod[..., None] * dt_blocks[:, None, :, :]
    y_intra = jnp.einsum("cijh,cjhp->cihp", weights, x_blocks, precision=highest)
    carry_in = jnp.exp(cum_decay) * (mark_count == 0).astype(jnp.float32)[:, :, None]
    y_inter = (
        jnp.einsum("cin,chpn->cihp", c_blocks, incoming, precision=highest) * carry_in[..., None]
    )
    mixed_out = y_intra + y_inter + skip[None, None, :, None] * x_blocks
    return mixed_out.reshape(blocks * SCAN_BLOCK, head_count * P_SIZE)


def local_front(marks_ext, alive_mask, extended, dt_pre, conv_weight, conv_bias, dt_bias, a_log):
    inner_act, step_size, log_decay, b_mat, c_mat = prepare(
        extended, dt_pre, marks_ext, alive_mask, conv_weight, conv_bias, dt_bias, a_log
    )
    block_parts = block_terms(inner_act, step_size, log_decay, b_mat, marks_ext[KW - 1 :])
    zero_state = jnp.zeros(block_parts[1].shape[1:], jnp.float32)
    total_state, _ = compose_blocks(block_parts[0], block_parts[1], zero_state)
    total_decay = jnp.prod(block_parts[0], axis=0)
    return (block_parts, b_mat, c_mat, total_decay, total_state)


def local_rear(block_parts, b_mat, c_mat, skip, start_state):
    _, incoming = compose_blocks(block_parts[0], block_parts[1], start_state)
    return block_output(block_parts, b_mat, c_mat, skip, incoming)


def local_pass(
    marks_ext,
    alive_mask,
    extended,
    dt_pre,
    conv_weight,
    conv_bias,
    dt_bias,
    a_log,
    skip,
    start_state,
):
    block_parts, b_mat, c_mat, total_decay, total_state = local_front(
        marks_ext, alive_mask, extended, dt_pre, conv_weight, conv_bias, dt_bias, a_log
    )
    return (local_rear(block_parts, b_mat, c_mat, skip, start_state), total_decay, total_state)


def chain_combine(earlier, later):
    return (earlier[0] * later[0], later[0][:, None, None] * earlier[1] + later[1])


def extend(pre_conv, start_marks, edge_rows, edge_marks):
    extended = jnp.concatenate([edge_rows, pre_conv], axis=0)
    marks_ext = jnp.concatenate([edge_marks.astype(jnp.int32), start_marks], axis=0)
    return (extended, marks_ext)


def mixer_forward(stream, start_marks, alive_mask, layer_weights, tick, ids):
    (
        norm_gain,
        w_main,
        w_low,
        w_bc,
        conv_weight,
        conv_bias,
        dt_bias,
        a_log,
        skip,
        gate_gain,
        w_out,
    ) = layer_weights
    inner_width = w_out.shape[0]
    normed = (stream * rms_scale(stream) * norm_gain).astype(jnp.bfloat16)
    gathered = head_gather(normed, tick, ids[0])
    gathered = gathered.reshape(-1, gathered.shape[-1])
    projected = jnp.dot(gathered, w_main, preferred_element_type=jnp.float32)
    gate_pre = projected[:, :inner_width]
    pre_conv = projected[:, inner_width : 2 * inner_width + 2 * N]
    dt_pre = projected[:, 2 * inner_width + 2 * N :]
    marks_float = start_marks.astype(jnp.float32)
    tail_from = pre_conv.shape[0] - KW + 1
    edge_parts = shifted((pre_conv[tail_from:], marks_float[tail_from:]), "seq", 1)
    extended, marks_ext = extend(pre_conv, start_marks, edge_parts[0], edge_parts[1])
    front_fn = partial(local_front, marks_ext, alive_mask)
    front_out, front_pull = jax.vjp(
        front_fn, extended, dt_pre, conv_weight, conv_bias, dt_bias, a_log
    )
    block_parts, b_mat, c_mat, total_decay, total_state = front_out
    neutral = (jnp.ones_like(total_decay), jnp.zeros_like(total_state))
    prefix = entering((total_decay, total_state), "seq", chain_combine, neutral)
    start_state = prefix[1]
    mixed_out, rear_pull = jax.vjp(local_rear, block_parts, b_mat, c_mat, skip, start_state)
    silu_gate = jax.nn.silu(gate_pre)
    gated_mix = mixed_out * silu_gate
    square_total = head_sum_rows(jnp.sum(gated_mix * gated_mix, axis=-1), tick, ids[2])
    scale_out = lax.rsqrt(square_total / DI + norm_eps)
    normed_out = (gated_mix * scale_out[:, None] * gate_gain).astype(jnp.bfloat16)
    head_count = lax.axis_size("head")
    branch = head_scatter(
        jnp.dot(normed_out, w_out, preferred_element_type=jnp.float32).reshape(
            head_count, -1, w_out.shape[1]
        ),
        tick,
        ids[1],
    )
    saved = (
        stream,
        gathered,
        gate_pre,
        mixed_out,
        silu_gate,
        gated_mix,
        scale_out,
        normed_out,
        total_decay,
        start_state,
        front_pull,
        rear_pull,
    )
    return stream + branch, saved


def mixer_backward(grad_next, layer_weights, saved, mask_value, tick, ids, hook=None):
    (
        norm_gain,
        w_main,
        w_low,
        w_bc,
        conv_weight,
        conv_bias,
        dt_bias,
        a_log,
        skip,
        gate_gain,
        w_out,
    ) = layer_weights
    (
        stream,
        gathered,
        gate_pre,
        mixed_out,
        silu_gate,
        gated_mix,
        scale_out,
        normed_out,
        total_decay,
        start_state,
        front_pull,
        rear_pull,
    ) = saved
    inner_width = w_out.shape[0]
    grad_branch = grad_next.astype(jnp.bfloat16)
    shard_rows = head_gather(grad_branch, tick, ids[0])
    shard_rows = shard_rows.reshape(-1, shard_rows.shape[-1])
    g_w_out = lax.dot_general(
        normed_out, shard_rows, (((0,), (0,)), ((), ())), preferred_element_type=jnp.float32
    ) * mask_value
    grad_normed = lax.dot_general(
        shard_rows, w_out, (((1,), (1,)), ((), ())), preferred_element_type=jnp.float32
    )
    weighted = grad_normed * gate_gain
    g_gate_gain = jnp.sum(grad_normed * gated_mix * scale_out[:, None], axis=0)
    cross_sum = head_sum_rows(jnp.sum(weighted * gated_mix, axis=-1), tick, ids[2])
    grad_gated = (
        scale_out[:, None] * weighted - gated_mix * (scale_out**3 * cross_sum / DI)[:, None]
    )
    grad_mixed = grad_gated * silu_gate
    grad_gate = (grad_gated * mixed_out * silu_slope(gate_pre)).astype(jnp.bfloat16)
    g_parts, g_b_mat, g_c_mat, g_skip, g_start = rear_pull(grad_mixed)
    neutral = (jnp.ones_like(total_decay), jnp.zeros_like(g_start))
    suffix = entering_2((total_decay, g_start), "seq", chain_combine, neutral)
    after_state = suffix[1]
    grad_decay = jnp.sum(after_state * start_state, axis=(1, 2))
    grad_ext, grad_dt_pre, g_conv_w, g_conv_b, g_dt_bias, g_a_log = front_pull(
        (g_parts, g_b_mat, g_c_mat, grad_decay, after_state)
    )
    returned = shifted(grad_ext[: KW - 1], "seq", -1)
    grad_pre = grad_ext[KW - 1 :]
    tail_from = grad_pre.shape[0] - KW + 1
    grad_pre = jnp.concatenate([grad_pre[:tail_from], grad_pre[tail_from:] + returned], axis=0)
    grad_inner = grad_pre[:, :inner_width].astype(jnp.bfloat16)
    grad_bc = grad_pre[:, inner_width:]
    grad_low = jnp.concatenate([grad_gate, grad_inner, grad_dt_pre.astype(jnp.bfloat16)], axis=1)
    w_bc_float = w_bc.astype(jnp.float32)
    g_low = lax.dot_general(
        gathered, grad_low, (((0,), (0,)), ((), ())), preferred_element_type=jnp.float32
    )
    g_w_bc = lax.dot_general(
        gathered.astype(jnp.float32),
        grad_bc,
        (((0,), (0,)), ((), ())),
        precision=highest,
        preferred_element_type=jnp.float32,
    )
    main_term = lax.dot_general(
        grad_low, w_low, (((1,), (1,)), ((), ())), preferred_element_type=jnp.float32
    )
    side_term = lax.dot_general(
        grad_bc,
        w_bc_float,
        (((1,), (1,)), ((), ())),
        precision=highest,
        preferred_element_type=jnp.float32,
    )
    head_count = lax.axis_size("head")
    lead = 0.0
    if hook is not None:
        lead = hook((g_w_bc, g_conv_w[:, inner_width:], g_conv_b[inner_width:]))
    grad_normed_in = head_scatter(
        (main_term + side_term + lead).reshape(head_count, -1, main_term.shape[1]), tick, ids[1]
    )
    scale_in = rms_scale(stream)
    g_norm_gain = jnp.sum(grad_normed_in * stream * scale_in, axis=0)
    weighted_in = grad_normed_in * norm_gain
    grad_stream = (
        grad_next
        + scale_in * weighted_in
        - stream * scale_in**3 * jnp.mean(weighted_in * stream, axis=-1, keepdims=True)
    )
    head_part = (
        g_low[:, :inner_width],
        g_low[:, inner_width : 2 * inner_width],
        g_low[:, 2 * inner_width :],
        g_conv_w[:, :inner_width],
        g_conv_b[:inner_width],
        g_dt_bias,
        g_a_log,
        g_skip,
        g_gate_gain,
    )
    shared_part = (g_norm_gain, g_w_bc, g_conv_w[:, inner_width:], g_conv_b[inner_width:])
    return (grad_stream, head_part, shared_part, g_w_out)


def pack_rows(members, width, multiple):
    rows = jnp.concatenate([member.reshape(-1, width) for member in members], axis=0)
    return jnp.pad(rows, ((0, -rows.shape[0] % multiple), (0, 0)))


def unpack_rows(rows, shapes, width):
    pieces = []
    start = 0
    for shape in shapes:
        count = math.prod(shape) // width
        pieces.append(rows[start : start + count].reshape(shape))
        start += count
    return tuple(pieces)


def reduce_grads(head_part, norm_part, bc_part, tick_count):
    summed = lax.psum(
        tuple(member.astype(jnp.bfloat16) for member in head_part[:3] + (bc_part,)), "seq"
    )
    head_sum = tuple(member.astype(jnp.float32) for member in summed[:3]) + tuple(
        lax.psum(member.astype(jnp.bfloat16), "seq").astype(jnp.float32)
        for member in head_part[3:]
    )
    bc_rows = head_gather(summed[3], (0, 0, 1), 4 * tick_count + 1).astype(jnp.float32)
    norm_sum = lax.psum(norm_part, ("seq", "head"))
    return (head_sum, norm_sum, bc_rows.reshape(-1, bc_rows.shape[-1]))


def store_slot(buffer, value, slot_index, is_valid):
    current = lax.dynamic_index_in_dim(buffer, slot_index, 0, False)
    return lax.dynamic_update_index_in_dim(
        buffer, jnp.where(is_valid, value, current), slot_index, 0
    )


def on_device(
    inputs,
    cotangent,
    starts,
    live,
    norm_gain,
    w_gate,
    w_in,
    w_bc,
    w_dt,
    conv_x,
    conv_x_bias,
    conv_bc,
    conv_bc_bias,
    dt_bias,
    a_log,
    skip,
    gate_gain,
    w_out,
):
    section_count = lax.axis_size("section")
    section_index = lax.axis_index("section")
    micro_count = inputs.shape[0]
    tick_count = micro_count + section_count - 1
    w_main = jnp.concatenate([w_gate[0], w_in[0], w_bc[0], w_dt[0]], axis=1)
    w_low = jnp.concatenate([w_gate[0], w_in[0], w_dt[0]], axis=1)
    conv_weight = jnp.concatenate([conv_x[0], conv_bc[0]], axis=1).astype(jnp.float32)
    conv_bias = jnp.concatenate([conv_x_bias[0], conv_bc_bias[0]], axis=0)
    layer_weights = (
        norm_gain[0],
        w_main,
        w_low,
        w_bc[0],
        conv_weight,
        conv_bias,
        dt_bias[0],
        a_log[0],
        skip[0],
        gate_gain[0],
        w_out[0],
    )
    row_shape = inputs.shape[1:]
    outputs_all = jnp.zeros((micro_count,) + row_shape, jnp.float32)
    arrived = jnp.zeros(row_shape, jnp.float32)
    ticks = []
    for tick_index in range(tick_count):
        slot_index = tick_index - section_index
        is_valid = (slot_index >= 0) & (slot_index < micro_count)
        clipped = jnp.clip(slot_index, 0, micro_count - 1)
        fresh_rows = lax.dynamic_index_in_dim(inputs, clipped, 0, False).astype(jnp.float32)
        stream = jnp.where(section_index == 0, fresh_rows, arrived)
        start_marks = lax.dynamic_index_in_dim(starts, clipped, 0, False)
        alive_mask = lax.dynamic_index_in_dim(live, clipped, 0, False).astype(jnp.float32)
        result, saved = mixer_forward(
            stream,
            start_marks,
            alive_mask,
            layer_weights,
            (tick_index, -1, micro_count),
            (tick_index, tick_count + tick_index, 4 * tick_count + 2 + tick_index),
        )
        outputs_all = store_slot(outputs_all, result, clipped, is_valid)
        ticks.append((clipped, is_valid, saved))
        if tick_index + 1 < tick_count:
            arrived = shifted(result, "section", 1)
    back_arrived = jnp.zeros(row_shape, jnp.float32)
    input_grads = jnp.zeros((micro_count,) + row_shape, jnp.float32)
    head_count = lax.axis_size("head")
    bc_box = []
    head_total = ()
    shared_total = ()
    for tick_index in range(tick_count):
        clipped, is_valid, saved = ticks[tick_count - 1 - tick_index]
        outer_grad = lax.dynamic_index_in_dim(cotangent, clipped, 0, False).astype(jnp.float32)
        grad_next = jnp.where(section_index == section_count - 1, outer_grad, back_arrived)
        mask_value = is_valid.astype(jnp.float32)
        hook = None
        if tick_index + 1 == tick_count:

            def hook(bc_local, mask_value=mask_value, earlier=shared_total):
                totals = tuple(
                    (prev + member * mask_value) if earlier else member * mask_value
                    for prev, member in zip(earlier[1:] or bc_local, bc_local)
                )
                rows = pack_rows(totals, totals[0].shape[-1], 8 * head_count)
                part = head_scatter(
                    rows.reshape(head_count, -1, rows.shape[-1]), (0, 0, 1), 4 * tick_count
                )
                bc_box.append((part, [member.shape for member in totals]))
                return part[0, 0] * 0.0

        grad_stream, head_part, shared_part, out_part = mixer_backward(
            grad_next,
            layer_weights,
            saved,
            mask_value,
            (tick_count - 1 - tick_index, -1, micro_count),
            (
                2 * tick_count + tick_index,
                3 * tick_count + tick_index,
                5 * tick_count + 2 + tick_index,
            ),
            hook,
        )
        if tick_index == 0:
            out_total = out_part
        else:
            out_total = out_total + out_part
        if tick_index + 1 == tick_count:
            out_total = lax.psum(out_total.astype(jnp.bfloat16), "seq")
        head_part = tuple((member * mask_value for member in head_part))
        shared_part = tuple((member * mask_value for member in shared_part))
        if tick_index == 0:
            head_total = head_part
            shared_total = shared_part
        else:
            head_total = tuple((former + latter for former, latter in zip(head_total, head_part)))
            shared_total = tuple(
                (former + latter for former, latter in zip(shared_total, shared_part))
            )
        input_grads = store_slot(input_grads, grad_stream, clipped, is_valid)
        if tick_index + 1 < tick_count:
            back_arrived = shifted(grad_stream.astype(jnp.bfloat16), "section", -1).astype(
                grad_stream.dtype
            )
    anchor = out_total[0, 0].astype(jnp.float32) * 0.0
    head_total = (head_total[0] + anchor,) + head_total[1:]
    bc_part, bc_shapes = bc_box[0]
    head_total, norm_sum, bc_rows = reduce_grads(head_total, shared_total[0], bc_part, tick_count)
    shared_total = (norm_sum,) + unpack_rows(bc_rows, bc_shapes, bc_rows.shape[-1])
    head_total = head_total[:3] + (out_total.astype(jnp.float32),) + head_total[3:]
    return (
        outputs_all[None],
        input_grads[None],
        shared_total[0][None],
        head_total[0][None],
        head_total[1][None],
        shared_total[1][None],
        head_total[2][None],
        head_total[4][None],
        head_total[5][None],
        shared_total[2][None],
        shared_total[3][None],
        head_total[6][None],
        head_total[7][None],
        head_total[8][None],
        head_total[9][None],
        head_total[3][None],
    )


def solution(mesh):
    return jax.shard_map(
        on_device,
        mesh=mesh,
        in_specs=(
            P(None, ("seq", "head"), None),
            P(None, ("seq", "head"), None),
            P(None, "seq"),
            P(None, "seq"),
            P("section", None),
            P("section", None, "head"),
            P("section", None, "head"),
            P("section", None, None),
            P("section", None, "head"),
            P("section", None, "head"),
            P("section", "head"),
            P("section", None, None),
            P("section", None),
            P("section", "head"),
            P("section", "head"),
            P("section", "head"),
            P("section", "head"),
            P("section", "head", None),
        ),
        out_specs=(
            P("section", None, ("seq", "head"), None),
            P("section", None, ("seq", "head"), None),
            P("section", None),
            P("section", None, "head"),
            P("section", None, "head"),
            P("section", None, None),
            P("section", None, "head"),
            P("section", None, "head"),
            P("section", "head"),
            P("section", None, None),
            P("section", None),
            P("section", "head"),
            P("section", "head"),
            P("section", "head"),
            P("section", "head"),
            P("section", "head", None),
        ),
        check_vma=False,
    )
```

```python
from functools import partial

import functools
import math

import jax
import jax.numpy as jnp
from jax import lax
from jax.experimental import pallas as pl
from jax.experimental.pallas import tpu as pltpu
from jax.sharding import PartitionSpec as P

DI = 4096
P_SIZE = 64
N = 128
KW = 4
SCAN_BLOCK = 256


MESH = pl.DeviceIdType.MESH


def _tick_valid(offset, sign, count):
    slot = offset + sign * lax.axis_index("section")
    return jnp.logical_and(slot >= 0, slot < count)


def _enter(barrier, h, n):
    @pl.when(h > 0)
    def _():
        pl.semaphore_signal(barrier, 1, device_id={"head": h - 1}, device_id_type=MESH)

    @pl.when(h < n - 1)
    def _():
        pl.semaphore_signal(barrier, 1, device_id={"head": h + 1}, device_id_type=MESH)

    @pl.when(jnp.logical_and(h > 0, h < n - 1))
    def _():
        pl.semaphore_wait(barrier, 2)

    @pl.when(jnp.logical_or(h == 0, h == n - 1))
    def _():
        pl.semaphore_wait(barrier, 1)


def gather_body(n, tick, x_ref, o_ref, land, send_r, send_l, recv):
    h = lax.axis_index("head")
    valid = _tick_valid(*tick)

    @pl.when(valid)
    def _():
        _enter(pltpu.get_barrier_semaphore(), h, n)

        def copy_right(s, k):
            src = x_ref if s == 0 else land.at[k]
            return pltpu.make_async_remote_copy(
                src_ref=src, dst_ref=land.at[k], send_sem=send_r.at[s], recv_sem=recv.at[k],
                device_id={"head": h + 1}, device_id_type=MESH)

        def copy_left(s, k):
            src = x_ref if s == 0 else land.at[k]
            return pltpu.make_async_remote_copy(
                src_ref=src, dst_ref=land.at[k], send_sem=send_l.at[s], recv_sem=recv.at[k],
                device_id={"head": h - 1}, device_id_type=MESH)

        for s in range(n):
            k_r = h - s
            k_l = h + s
            if s >= 1:
                @pl.when(k_r >= 0)
                def _():
                    pltpu.make_async_remote_copy(
                        src_ref=land.at[k_r], dst_ref=land.at[k_r], send_sem=send_r.at[0],
                        recv_sem=recv.at[k_r], device_id={"head": h}, device_id_type=MESH
                    ).wait_recv()

                @pl.when(k_l <= n - 1)
                def _():
                    pltpu.make_async_remote_copy(
                        src_ref=land.at[k_l], dst_ref=land.at[k_l], send_sem=send_l.at[0],
                        recv_sem=recv.at[k_l], device_id={"head": h}, device_id_type=MESH
                    ).wait_recv()
            if s <= n - 2:
                @pl.when(jnp.logical_and(k_r >= 0, h < n - 1))
                def _():
                    copy_right(s, k_r).start()

                @pl.when(jnp.logical_and(k_l <= n - 1, h > 0))
                def _():
                    copy_left(s, k_l).start()
        land[h] = x_ref[...]
        for s in range(n - 1):
            k_r = h - s
            k_l = h + s

            @pl.when(jnp.logical_and(k_r >= 0, h < n - 1))
            def _():
                copy_right(s, k_r).wait_send()

            @pl.when(jnp.logical_and(k_l <= n - 1, h > 0))
            def _():
                copy_left(s, k_l).wait_send()
        o_ref[...] = land[...]

    @pl.when(jnp.logical_not(valid))
    def _():
        o_ref[...] = jnp.zeros(o_ref.shape, o_ref.dtype)


def head_gather(x, tick, cid):
    n = lax.axis_size("head")
    rows, cols = x.shape
    return pl.pallas_call(
        functools.partial(gather_body, n, tick),
        out_shape=jax.ShapeDtypeStruct((n, rows, cols), x.dtype),
        in_specs=[pl.BlockSpec(memory_space=pltpu.VMEM)],
        out_specs=pl.BlockSpec(memory_space=pltpu.VMEM),
        scratch_shapes=[
            pltpu.VMEM((n, rows, cols), x.dtype),
            pltpu.SemaphoreType.DMA((n,)),
            pltpu.SemaphoreType.DMA((n,)),
            pltpu.SemaphoreType.DMA((n,)),
        ],
        compiler_params=pltpu.CompilerParams(collective_id=cid, has_side_effects=True),
    )(x)


def scatter_body(n, tick, p_ref, o_ref, recv_l, recv_r, send_l, send_r, ssem_l, ssem_r, rsem_l, rsem_r):
    h = lax.axis_index("head")
    valid = _tick_valid(*tick)
    link = send_r.dtype

    @pl.when(valid)
    def _():
        _enter(pltpu.get_barrier_semaphore(), h, n)

        def to_right(k):
            return pltpu.make_async_remote_copy(
                src_ref=send_r.at[k], dst_ref=recv_l.at[k], send_sem=ssem_r.at[k],
                recv_sem=rsem_l.at[k], device_id={"head": h + 1}, device_id_type=MESH)

        def to_left(k):
            return pltpu.make_async_remote_copy(
                src_ref=send_l.at[k], dst_ref=recv_r.at[k], send_sem=ssem_l.at[k],
                recv_sem=rsem_r.at[k], device_id={"head": h - 1}, device_id_type=MESH)

        for s in range(n - 1):
            k_r = n - 1 - s
            k_l = s

            @pl.when(k_r > h)
            def _():
                @pl.when(h > 0)
                def _():
                    to_right(k_r).wait_recv()
                    send_r[k_r] = (p_ref[k_r] + recv_l[k_r].astype(jnp.float32)).astype(link)

                @pl.when(h == 0)
                def _():
                    send_r[k_r] = p_ref[k_r].astype(link)

                to_right(k_r).start()

            @pl.when(k_l < h)
            def _():
                @pl.when(h < n - 1)
                def _():
                    to_left(k_l).wait_recv()
                    send_l[k_l] = (p_ref[k_l] + recv_r[k_l].astype(jnp.float32)).astype(link)

                @pl.when(h == n - 1)
                def _():
                    send_l[k_l] = p_ref[k_l].astype(link)

                to_left(k_l).start()
        total = p_ref[h]

        @pl.when(h > 0)
        def _():
            to_right(h).wait_recv()

        @pl.when(h < n - 1)
        def _():
            to_left(h).wait_recv()

        left_part = jnp.where(h > 0, recv_l[h].astype(jnp.float32), 0.0)
        right_part = jnp.where(h < n - 1, recv_r[h].astype(jnp.float32), 0.0)
        o_ref[...] = (total + left_part + right_part).astype(o_ref.dtype)
        for s in range(n - 1):
            k_r = n - 1 - s
            k_l = s

            @pl.when(k_r > h)
            def _():
                to_right(k_r).wait_send()

            @pl.when(k_l < h)
            def _():
                to_left(k_l).wait_send()

    @pl.when(jnp.logical_not(valid))
    def _():
        o_ref[...] = jnp.zeros(o_ref.shape, o_ref.dtype)


def head_scatter(parts, tick, cid, link=jnp.bfloat16):
    n = lax.axis_size("head")
    _, rows, cols = parts.shape
    return pl.pallas_call(
        functools.partial(scatter_body, n, tick),
        out_shape=jax.ShapeDtypeStruct((rows, cols), jnp.float32),
        in_specs=[pl.BlockSpec(memory_space=pltpu.VMEM)],
        out_specs=pl.BlockSpec(memory_space=pltpu.VMEM),
        scratch_shapes=[
            pltpu.VMEM((n, rows, cols), link),
            pltpu.VMEM((n, rows, cols), link),
            pltpu.VMEM((n, rows, cols), link),
            pltpu.VMEM((n, rows, cols), link),
            pltpu.SemaphoreType.DMA((n,)),
            pltpu.SemaphoreType.DMA((n,)),
            pltpu.SemaphoreType.DMA((n,)),
            pltpu.SemaphoreType.DMA((n,)),
        ],
        compiler_params=pltpu.CompilerParams(collective_id=cid, has_side_effects=True),
    )(parts)


norm_eps = 1e-05
far_below = -1e30
highest = lax.Precision.HIGH


def shifted(value, axis, by):
    count = lax.axis_size(axis)
    pairs = [(i, i + by) for i in range(count) if 0 <= i + by < count]
    return lax.ppermute(value, axis, pairs)


def entering(value, axis, combine, identity):
    count, mine = (lax.axis_size(axis), lax.axis_index(axis))
    everything = jax.tree.map(lambda part: lax.all_gather(part, axis), value)
    before = jax.tree.map(
        lambda part, zero: jnp.broadcast_to(jnp.asarray(zero, part.dtype), part.shape),
        value,
        identity,
    )
    for k in range(count - 1):
        reached = k < mine
        new = combine(before, jax.tree.map(lambda part: part[k], everything))
        before = jax.tree.map(lambda a, b: jnp.where(reached, a, b), new, before)
    return before


def entering_2(value, axis, join, neutral):
    count = lax.axis_size(axis)
    place = lax.axis_index(axis)
    ahead = count - 1 - place
    gathered = jax.tree.map(
        lambda a, kind: lax.all_gather(a.astype(kind), axis),
        value,
        jax.tree.map(lambda a: jnp.bfloat16 if a.dtype == jnp.float32 else a.dtype, value),
    )
    state = jax.tree.map(lambda a, e: jnp.zeros_like(a) + jnp.asarray(e, a.dtype), value, neutral)
    for lap in range(count - 1):
        source = count - 1 - lap
        new = join(
            state,
            jax.tree.map(lambda a, own: a[source].astype(own.dtype), gathered, value),
        )
        active = lap < ahead
        state = jax.tree.map(lambda a, b: jnp.where(active, a, b), new, state)
    return state


def rms_scale(values):
    return lax.rsqrt(jnp.mean(values * values, axis=-1, keepdims=True) + norm_eps)


def silu_slope(values):
    logistic = jax.nn.sigmoid(values)
    return logistic * (1.0 + values * (1.0 - logistic))


def causal_conv(extended, marks_ext, weight, conv_bias):
    tap_count = weight.shape[0]
    length = extended.shape[0] - tap_count + 1
    counts = jnp.cumsum(marks_ext)
    conv_sum = jnp.zeros((length, extended.shape[1]), jnp.float32) + conv_bias
    for tap_index in range(tap_count):
        linked = (counts[tap_count - 1 :] == counts[tap_index : tap_index + length]).astype(
            jnp.float32
        )
        conv_sum = (
            conv_sum
            + linked[:, None] * weight[tap_index] * extended[tap_index : tap_index + length]
        )
    return conv_sum


def prepare(extended, dt_pre, marks_ext, alive_mask, conv_weight, conv_bias, dt_bias, a_log):
    inner_width = dt_pre.shape[1] * P_SIZE
    activated = jax.nn.silu(causal_conv(extended, marks_ext, conv_weight, conv_bias))
    inner_act = activated[:, :inner_width] * alive_mask[:, None]
    b_mat = activated[:, inner_width : inner_width + N]
    c_mat = activated[:, inner_width + N :]
    step_size = jax.nn.softplus(dt_pre + dt_bias) * alive_mask[:, None]
    log_decay = -step_size * jnp.exp(a_log)
    return (inner_act, step_size, log_decay, b_mat, c_mat)


def block_terms(inner_act, step_size, log_decay, b_mat, start_marks):
    blocks = inner_act.shape[0] // SCAN_BLOCK
    head_count = step_size.shape[1]
    x_blocks = inner_act.reshape(blocks, SCAN_BLOCK, head_count, P_SIZE)
    dt_blocks = step_size.reshape(blocks, SCAN_BLOCK, head_count)
    cum_decay = jnp.cumsum(log_decay.reshape(blocks, SCAN_BLOCK, head_count), axis=1)
    mark_count = jnp.cumsum(start_marks.reshape(blocks, SCAN_BLOCK), axis=1)
    b_blocks = b_mat.reshape(blocks, SCAN_BLOCK, N)
    last_cum = cum_decay[:, -1]
    last_mark = mark_count[:, -1]
    same_end = (mark_count == last_mark[:, None]).astype(jnp.float32)
    end_weight = jnp.exp(last_cum[:, None, :] - cum_decay) * same_end[:, :, None] * dt_blocks
    block_states = jnp.einsum(
        "cjh,cjhp,cjn->chpn", end_weight, x_blocks, b_blocks, precision=highest
    )
    block_decay = jnp.exp(last_cum) * (last_mark == 0).astype(jnp.float32)[:, None]
    return (block_decay, block_states, cum_decay, mark_count, x_blocks, dt_blocks)


def compose_blocks(block_decay, block_states, start_state):
    chain_state = start_state
    incoming = []
    for block_index in range(block_decay.shape[0]):
        incoming.append(chain_state)
        chain_state = (
            block_decay[block_index][:, None, None] * chain_state + block_states[block_index]
        )
    return (chain_state, jnp.stack(incoming))


def block_output(block_parts, b_mat, c_mat, skip, incoming):
    block_decay, block_states, cum_decay, mark_count, x_blocks, dt_blocks = block_parts
    blocks = cum_decay.shape[0]
    head_count = cum_decay.shape[2]
    b_blocks = b_mat.reshape(blocks, SCAN_BLOCK, N)
    c_blocks = c_mat.reshape(blocks, SCAN_BLOCK, N)
    inner_prod = jnp.einsum("cin,cjn->cij", c_blocks, b_blocks, precision=highest)
    arange_pos = jnp.arange(SCAN_BLOCK)
    linked = (arange_pos[:, None] >= arange_pos[None, :])[None] & (
        mark_count[:, :, None] == mark_count[:, None, :]
    )
    spread = jnp.where(
        linked[..., None], cum_decay[:, :, None, :] - cum_decay[:, None, :, :], far_below
    )
    weights = jnp.exp(spread) * inner_prod[..., None] * dt_blocks[:, None, :, :]
    y_intra = jnp.einsum("cijh,cjhp->cihp", weights, x_blocks, precision=highest)
    carry_in = jnp.exp(cum_decay) * (mark_count == 0).astype(jnp.float32)[:, :, None]
    y_inter = (
        jnp.einsum("cin,chpn->cihp", c_blocks, incoming, precision=highest) * carry_in[..., None]
    )
    mixed_out = y_intra + y_inter + skip[None, None, :, None] * x_blocks
    return mixed_out.reshape(blocks * SCAN_BLOCK, head_count * P_SIZE)


def local_front(marks_ext, alive_mask, extended, dt_pre, conv_weight, conv_bias, dt_bias, a_log):
    inner_act, step_size, log_decay, b_mat, c_mat = prepare(
        extended, dt_pre, marks_ext, alive_mask, conv_weight, conv_bias, dt_bias, a_log
    )
    block_parts = block_terms(inner_act, step_size, log_decay, b_mat, marks_ext[KW - 1 :])
    zero_state = jnp.zeros(block_parts[1].shape[1:], jnp.float32)
    total_state, _ = compose_blocks(block_parts[0], block_parts[1], zero_state)
    total_decay = jnp.prod(block_parts[0], axis=0)
    return (block_parts, b_mat, c_mat, total_decay, total_state)


def local_rear(block_parts, b_mat, c_mat, skip, start_state):
    _, incoming = compose_blocks(block_parts[0], block_parts[1], start_state)
    return block_output(block_parts, b_mat, c_mat, skip, incoming)


def local_pass(
    marks_ext,
    alive_mask,
    extended,
    dt_pre,
    conv_weight,
    conv_bias,
    dt_bias,
    a_log,
    skip,
    start_state,
):
    block_parts, b_mat, c_mat, total_decay, total_state = local_front(
        marks_ext, alive_mask, extended, dt_pre, conv_weight, conv_bias, dt_bias, a_log
    )
    return (local_rear(block_parts, b_mat, c_mat, skip, start_state), total_decay, total_state)


def chain_combine(earlier, later):
    return (earlier[0] * later[0], later[0][:, None, None] * earlier[1] + later[1])


def extend(pre_conv, start_marks, edge_rows, edge_marks):
    extended = jnp.concatenate([edge_rows, pre_conv], axis=0)
    marks_ext = jnp.concatenate([edge_marks.astype(jnp.int32), start_marks], axis=0)
    return (extended, marks_ext)


def mixer_forward(stream, start_marks, alive_mask, layer_weights, tick, ids):
    (
        norm_gain,
        w_main,
        w_low,
        w_bc,
        conv_weight,
        conv_bias,
        dt_bias,
        a_log,
        skip,
        gate_gain,
        w_out,
    ) = layer_weights
    inner_width = w_out.shape[0]
    normed = (stream * rms_scale(stream) * norm_gain).astype(jnp.bfloat16)
    gathered = head_gather(normed, tick, ids[0])
    gathered = gathered.reshape(-1, gathered.shape[-1])
    projected = jnp.dot(gathered, w_main, preferred_element_type=jnp.float32)
    gate_pre = projected[:, :inner_width]
    pre_conv = projected[:, inner_width : 2 * inner_width + 2 * N]
    dt_pre = projected[:, 2 * inner_width + 2 * N :]
    marks_float = start_marks.astype(jnp.float32)
    tail_from = pre_conv.shape[0] - KW + 1
    edge_parts = shifted((pre_conv[tail_from:], marks_float[tail_from:]), "seq", 1)
    extended, marks_ext = extend(pre_conv, start_marks, edge_parts[0], edge_parts[1])
    front_fn = partial(local_front, marks_ext, alive_mask)
    front_out, front_pull = jax.vjp(
        front_fn, extended, dt_pre, conv_weight, conv_bias, dt_bias, a_log
    )
    block_parts, b_mat, c_mat, total_decay, total_state = front_out
    neutral = (jnp.ones_like(total_decay), jnp.zeros_like(total_state))
    prefix = entering((total_decay, total_state), "seq", chain_combine, neutral)
    start_state = prefix[1]
    mixed_out, rear_pull = jax.vjp(local_rear, block_parts, b_mat, c_mat, skip, start_state)
    silu_gate = jax.nn.silu(gate_pre)
    gated_mix = mixed_out * silu_gate
    square_total = lax.psum(jnp.sum(gated_mix * gated_mix, axis=-1), "head")
    scale_out = lax.rsqrt(square_total / DI + norm_eps)
    normed_out = (gated_mix * scale_out[:, None] * gate_gain).astype(jnp.bfloat16)
    head_count = lax.axis_size("head")
    branch = head_scatter(
        jnp.dot(normed_out, w_out, preferred_element_type=jnp.float32).reshape(
            head_count, -1, w_out.shape[1]
        ),
        tick,
        ids[1],
    )
    saved = (
        stream,
        gathered,
        gate_pre,
        mixed_out,
        silu_gate,
        gated_mix,
        scale_out,
        normed_out,
        total_decay,
        start_state,
        front_pull,
        rear_pull,
    )
    return stream + branch, saved


def mixer_backward(grad_next, layer_weights, saved, mask_value, tick, ids, hook=None):
    (
        norm_gain,
        w_main,
        w_low,
        w_bc,
        conv_weight,
        conv_bias,
        dt_bias,
        a_log,
        skip,
        gate_gain,
        w_out,
    ) = layer_weights
    (
        stream,
        gathered,
        gate_pre,
        mixed_out,
        silu_gate,
        gated_mix,
        scale_out,
        normed_out,
        total_decay,
        start_state,
        front_pull,
        rear_pull,
    ) = saved
    inner_width = w_out.shape[0]
    grad_branch = grad_next.astype(jnp.bfloat16)
    shard_rows = head_gather(grad_branch, tick, ids[0])
    shard_rows = shard_rows.reshape(-1, shard_rows.shape[-1])
    g_w_out = lax.dot_general(
        normed_out, shard_rows, (((0,), (0,)), ((), ())), preferred_element_type=jnp.float32
    ) * mask_value
    grad_normed = lax.dot_general(
        shard_rows, w_out, (((1,), (1,)), ((), ())), preferred_element_type=jnp.float32
    )
    weighted = grad_normed * gate_gain
    g_gate_gain = jnp.sum(grad_normed * gated_mix * scale_out[:, None], axis=0)
    cross_sum = lax.psum(jnp.sum(weighted * gated_mix, axis=-1), "head")
    grad_gated = (
        scale_out[:, None] * weighted - gated_mix * (scale_out**3 * cross_sum / DI)[:, None]
    )
    grad_mixed = grad_gated * silu_gate
    grad_gate = (grad_gated * mixed_out * silu_slope(gate_pre)).astype(jnp.bfloat16)
    g_parts, g_b_mat, g_c_mat, g_skip, g_start = rear_pull(grad_mixed)
    neutral = (jnp.ones_like(total_decay), jnp.zeros_like(g_start))
    suffix = entering_2((total_decay, g_start), "seq", chain_combine, neutral)
    after_state = suffix[1]
    grad_decay = jnp.sum(after_state * start_state, axis=(1, 2))
    grad_ext, grad_dt_pre, g_conv_w, g_conv_b, g_dt_bias, g_a_log = front_pull(
        (g_parts, g_b_mat, g_c_mat, grad_decay, after_state)
    )
    returned = shifted(grad_ext[: KW - 1], "seq", -1)
    grad_pre = grad_ext[KW - 1 :]
    tail_from = grad_pre.shape[0] - KW + 1
    grad_pre = jnp.concatenate([grad_pre[:tail_from], grad_pre[tail_from:] + returned], axis=0)
    grad_inner = grad_pre[:, :inner_width].astype(jnp.bfloat16)
    grad_bc = grad_pre[:, inner_width:]
    grad_low = jnp.concatenate([grad_gate, grad_inner, grad_dt_pre.astype(jnp.bfloat16)], axis=1)
    w_bc_float = w_bc.astype(jnp.float32)
    g_low = lax.dot_general(
        gathered, grad_low, (((0,), (0,)), ((), ())), preferred_element_type=jnp.float32
    )
    g_w_bc = lax.dot_general(
        gathered.astype(jnp.float32),
        grad_bc,
        (((0,), (0,)), ((), ())),
        precision=highest,
        preferred_element_type=jnp.float32,
    )
    main_term = lax.dot_general(
        grad_low, w_low, (((1,), (1,)), ((), ())), preferred_element_type=jnp.float32
    )
    side_term = lax.dot_general(
        grad_bc,
        w_bc_float,
        (((1,), (1,)), ((), ())),
        precision=highest,
        preferred_element_type=jnp.float32,
    )
    head_count = lax.axis_size("head")
    lead = 0.0
    if hook is not None:
        lead = hook((g_w_bc, g_conv_w[:, inner_width:], g_conv_b[inner_width:]))
    grad_normed_in = head_scatter(
        (main_term + side_term + lead).reshape(head_count, -1, main_term.shape[1]), tick, ids[1]
    )
    scale_in = rms_scale(stream)
    g_norm_gain = jnp.sum(grad_normed_in * stream * scale_in, axis=0)
    weighted_in = grad_normed_in * norm_gain
    grad_stream = (
        grad_next
        + scale_in * weighted_in
        - stream * scale_in**3 * jnp.mean(weighted_in * stream, axis=-1, keepdims=True)
    )
    head_part = (
        g_low[:, :inner_width],
        g_low[:, inner_width : 2 * inner_width],
        g_low[:, 2 * inner_width :],
        g_conv_w[:, :inner_width],
        g_conv_b[:inner_width],
        g_dt_bias,
        g_a_log,
        g_skip,
        g_gate_gain,
    )
    shared_part = (g_norm_gain, g_w_bc, g_conv_w[:, inner_width:], g_conv_b[inner_width:])
    return (grad_stream, head_part, shared_part, g_w_out)


def pack_rows(members, width, multiple):
    rows = jnp.concatenate([member.reshape(-1, width) for member in members], axis=0)
    return jnp.pad(rows, ((0, -rows.shape[0] % multiple), (0, 0)))


def unpack_rows(rows, shapes, width):
    pieces = []
    start = 0
    for shape in shapes:
        count = math.prod(shape) // width
        pieces.append(rows[start : start + count].reshape(shape))
        start += count
    return tuple(pieces)


def reduce_grads(head_part, norm_part, bc_part, tick_count):
    summed = lax.psum(
        tuple(member.astype(jnp.bfloat16) for member in head_part[:3] + (bc_part,)), "seq"
    )
    head_sum = tuple(member.astype(jnp.float32) for member in summed[:3]) + tuple(
        lax.psum(member.astype(jnp.bfloat16), "seq").astype(jnp.float32)
        for member in head_part[3:]
    )
    bc_rows = head_gather(summed[3], (0, 0, 1), 4 * tick_count + 1).astype(jnp.float32)
    norm_sum = lax.psum(norm_part, ("seq", "head"))
    return (head_sum, norm_sum, bc_rows.reshape(-1, bc_rows.shape[-1]))


def store_slot(buffer, value, slot_index, is_valid):
    current = lax.dynamic_index_in_dim(buffer, slot_index, 0, False)
    return lax.dynamic_update_index_in_dim(
        buffer, jnp.where(is_valid, value, current), slot_index, 0
    )


def on_device(
    inputs,
    cotangent,
    starts,
    live,
    norm_gain,
    w_gate,
    w_in,
    w_bc,
    w_dt,
    conv_x,
    conv_x_bias,
    conv_bc,
    conv_bc_bias,
    dt_bias,
    a_log,
    skip,
    gate_gain,
    w_out,
):
    section_count = lax.axis_size("section")
    section_index = lax.axis_index("section")
    micro_count = inputs.shape[0]
    tick_count = micro_count + section_count - 1
    w_main = jnp.concatenate([w_gate[0], w_in[0], w_bc[0], w_dt[0]], axis=1)
    w_low = jnp.concatenate([w_gate[0], w_in[0], w_dt[0]], axis=1)
    conv_weight = jnp.concatenate([conv_x[0], conv_bc[0]], axis=1).astype(jnp.float32)
    conv_bias = jnp.concatenate([conv_x_bias[0], conv_bc_bias[0]], axis=0)
    layer_weights = (
        norm_gain[0],
        w_main,
        w_low,
        w_bc[0],
        conv_weight,
        conv_bias,
        dt_bias[0],
        a_log[0],
        skip[0],
        gate_gain[0],
        w_out[0],
    )
    row_shape = inputs.shape[1:]
    outputs_all = jnp.zeros((micro_count,) + row_shape, jnp.float32)
    arrived = jnp.zeros(row_shape, jnp.float32)
    ticks = []
    for tick_index in range(tick_count):
        slot_index = tick_index - section_index
        is_valid = (slot_index >= 0) & (slot_index < micro_count)
        clipped = jnp.clip(slot_index, 0, micro_count - 1)
        fresh_rows = lax.dynamic_index_in_dim(inputs, clipped, 0, False).astype(jnp.float32)
        stream = jnp.where(section_index == 0, fresh_rows, arrived)
        start_marks = lax.dynamic_index_in_dim(starts, clipped, 0, False)
        alive_mask = lax.dynamic_index_in_dim(live, clipped, 0, False).astype(jnp.float32)
        result, saved = mixer_forward(
            stream,
            start_marks,
            alive_mask,
            layer_weights,
            (tick_index, -1, micro_count),
            (tick_index, tick_count + tick_index),
        )
        outputs_all = store_slot(outputs_all, result, clipped, is_valid)
        ticks.append((clipped, is_valid, saved))
        if tick_index + 1 < tick_count:
            arrived = shifted(result, "section", 1)
    back_arrived = jnp.zeros(row_shape, jnp.float32)
    input_grads = jnp.zeros((micro_count,) + row_shape, jnp.float32)
    head_count = lax.axis_size("head")
    bc_box = []
    head_total = ()
    shared_total = ()
    for tick_index in range(tick_count):
        clipped, is_valid, saved = ticks[tick_count - 1 - tick_index]
        outer_grad = lax.dynamic_index_in_dim(cotangent, clipped, 0, False).astype(jnp.float32)
        grad_next = jnp.where(section_index == section_count - 1, outer_grad, back_arrived)
        mask_value = is_valid.astype(jnp.float32)
        hook = None
        if tick_index + 1 == tick_count:

            def hook(bc_local, mask_value=mask_value, earlier=shared_total):
                totals = tuple(
                    (prev + member * mask_value) if earlier else member * mask_value
                    for prev, member in zip(earlier[1:] or bc_local, bc_local)
                )
                rows = pack_rows(totals, totals[0].shape[-1], 8 * head_count)
                part = head_scatter(
                    rows.reshape(head_count, -1, rows.shape[-1]), (0, 0, 1), 4 * tick_count
                )
                bc_box.append((part, [member.shape for member in totals]))
                return part[0, 0] * 0.0

        grad_stream, head_part, shared_part, out_part = mixer_backward(
            grad_next,
            layer_weights,
            saved,
            mask_value,
            (tick_count - 1 - tick_index, -1, micro_count),
            (2 * tick_count + tick_index, 3 * tick_count + tick_index),
            hook,
        )
        if tick_index == 0:
            out_total = out_part
        else:
            out_total = out_total + out_part
        if tick_index + 1 == tick_count:
            out_total = lax.psum(out_total.astype(jnp.bfloat16), "seq")
        head_part = tuple((member * mask_value for member in head_part))
        shared_part = tuple((member * mask_value for member in shared_part))
        if tick_index == 0:
            head_total = head_part
            shared_total = shared_part
        else:
            head_total = tuple((former + latter for former, latter in zip(head_total, head_part)))
            shared_total = tuple(
                (former + latter for former, latter in zip(shared_total, shared_part))
            )
        input_grads = store_slot(input_grads, grad_stream, clipped, is_valid)
        if tick_index + 1 < tick_count:
            back_arrived = shifted(grad_stream.astype(jnp.bfloat16), "section", -1).astype(
                grad_stream.dtype
            )
    anchor = out_total[0, 0].astype(jnp.float32) * 0.0
    head_total = (head_total[0] + anchor,) + head_total[1:]
    bc_part, bc_shapes = bc_box[0]
    head_total, norm_sum, bc_rows = reduce_grads(head_total, shared_total[0], bc_part, tick_count)
    shared_total = (norm_sum,) + unpack_rows(bc_rows, bc_shapes, bc_rows.shape[-1])
    head_total = head_total[:3] + (out_total.astype(jnp.float32),) + head_total[3:]
    return (
        outputs_all[None],
        input_grads[None],
        shared_total[0][None],
        head_total[0][None],
        head_total[1][None],
        shared_total[1][None],
        head_total[2][None],
        head_total[4][None],
        head_total[5][None],
        shared_total[2][None],
        shared_total[3][None],
        head_total[6][None],
        head_total[7][None],
        head_total[8][None],
        head_total[9][None],
        head_total[3][None],
    )


def solution(mesh):
    return jax.shard_map(
        on_device,
        mesh=mesh,
        in_specs=(
            P(None, ("seq", "head"), None),
            P(None, ("seq", "head"), None),
            P(None, "seq"),
            P(None, "seq"),
            P("section", None),
            P("section", None, "head"),
            P("section", None, "head"),
            P("section", None, None),
            P("section", None, "head"),
            P("section", None, "head"),
            P("section", "head"),
            P("section", None, None),
            P("section", None),
            P("section", "head"),
            P("section", "head"),
            P("section", "head"),
            P("section", "head"),
            P("section", "head", None),
        ),
        out_specs=(
            P("section", None, ("seq", "head"), None),
            P("section", None, ("seq", "head"), None),
            P("section", None),
            P("section", None, "head"),
            P("section", None, "head"),
            P("section", None, None),
            P("section", None, "head"),
            P("section", None, "head"),
            P("section", "head"),
            P("section", None, None),
            P("section", None),
            P("section", "head"),
            P("section", "head"),
            P("section", "head"),
            P("section", "head"),
            P("section", "head", None),
        ),
        check_vma=False,
    )
```

```python
from functools import partial

import functools
import math

import jax
import jax.numpy as jnp
from jax import lax
from jax.experimental import pallas as pl
from jax.experimental.pallas import tpu as pltpu
from jax.sharding import PartitionSpec as P

DI = 4096
P_SIZE = 64
N = 128
KW = 4
SCAN_BLOCK = 256


MESH = pl.DeviceIdType.MESH


def _tick_valid(offset, sign, count):
    slot = offset + sign * lax.axis_index("section")
    return jnp.logical_and(slot >= 0, slot < count)


def _enter(barrier, h, n):
    @pl.when(h > 0)
    def _():
        pl.semaphore_signal(barrier, 1, device_id={"head": h - 1}, device_id_type=MESH)

    @pl.when(h < n - 1)
    def _():
        pl.semaphore_signal(barrier, 1, device_id={"head": h + 1}, device_id_type=MESH)

    @pl.when(jnp.logical_and(h > 0, h < n - 1))
    def _():
        pl.semaphore_wait(barrier, 2)

    @pl.when(jnp.logical_or(h == 0, h == n - 1))
    def _():
        pl.semaphore_wait(barrier, 1)


def gather_body(n, tick, x_ref, o_ref, land, send_r, send_l, recv):
    h = lax.axis_index("head")
    valid = _tick_valid(*tick)

    @pl.when(valid)
    def _():
        _enter(pltpu.get_barrier_semaphore(), h, n)

        def copy_right(s, k):
            src = x_ref if s == 0 else land.at[k]
            return pltpu.make_async_remote_copy(
                src_ref=src, dst_ref=land.at[k], send_sem=send_r.at[s], recv_sem=recv.at[k],
                device_id={"head": h + 1}, device_id_type=MESH)

        def copy_left(s, k):
            src = x_ref if s == 0 else land.at[k]
            return pltpu.make_async_remote_copy(
                src_ref=src, dst_ref=land.at[k], send_sem=send_l.at[s], recv_sem=recv.at[k],
                device_id={"head": h - 1}, device_id_type=MESH)

        for s in range(n):
            k_r = h - s
            k_l = h + s
            if s >= 1:
                @pl.when(k_r >= 0)
                def _():
                    pltpu.make_async_remote_copy(
                        src_ref=land.at[k_r], dst_ref=land.at[k_r], send_sem=send_r.at[0],
                        recv_sem=recv.at[k_r], device_id={"head": h}, device_id_type=MESH
                    ).wait_recv()

                @pl.when(k_l <= n - 1)
                def _():
                    pltpu.make_async_remote_copy(
                        src_ref=land.at[k_l], dst_ref=land.at[k_l], send_sem=send_l.at[0],
                        recv_sem=recv.at[k_l], device_id={"head": h}, device_id_type=MESH
                    ).wait_recv()
            if s <= n - 2:
                @pl.when(jnp.logical_and(k_r >= 0, h < n - 1))
                def _():
                    copy_right(s, k_r).start()

                @pl.when(jnp.logical_and(k_l <= n - 1, h > 0))
                def _():
                    copy_left(s, k_l).start()
        land[h] = x_ref[...]
        for s in range(n - 1):
            k_r = h - s
            k_l = h + s

            @pl.when(jnp.logical_and(k_r >= 0, h < n - 1))
            def _():
                copy_right(s, k_r).wait_send()

            @pl.when(jnp.logical_and(k_l <= n - 1, h > 0))
            def _():
                copy_left(s, k_l).wait_send()
        o_ref[...] = land[...]

    @pl.when(jnp.logical_not(valid))
    def _():
        o_ref[...] = jnp.zeros(o_ref.shape, o_ref.dtype)


def head_gather(x, tick, cid):
    n = lax.axis_size("head")
    rows, cols = x.shape
    return pl.pallas_call(
        functools.partial(gather_body, n, tick),
        out_shape=jax.ShapeDtypeStruct((n, rows, cols), x.dtype),
        in_specs=[pl.BlockSpec(memory_space=pltpu.VMEM)],
        out_specs=pl.BlockSpec(memory_space=pltpu.VMEM),
        scratch_shapes=[
            pltpu.VMEM((n, rows, cols), x.dtype),
            pltpu.SemaphoreType.DMA((n,)),
            pltpu.SemaphoreType.DMA((n,)),
            pltpu.SemaphoreType.DMA((n,)),
        ],
        compiler_params=pltpu.CompilerParams(collective_id=cid, has_side_effects=True),
    )(x)


def scatter_body(n, tick, p_ref, o_ref, recv_l, recv_r, send_l, send_r, ssem_l, ssem_r, rsem_l, rsem_r):
    h = lax.axis_index("head")
    valid = _tick_valid(*tick)
    link = send_r.dtype

    @pl.when(valid)
    def _():
        _enter(pltpu.get_barrier_semaphore(), h, n)

        def to_right(k):
            return pltpu.make_async_remote_copy(
                src_ref=send_r.at[k], dst_ref=recv_l.at[k], send_sem=ssem_r.at[k],
                recv_sem=rsem_l.at[k], device_id={"head": h + 1}, device_id_type=MESH)

        def to_left(k):
            return pltpu.make_async_remote_copy(
                src_ref=send_l.at[k], dst_ref=recv_r.at[k], send_sem=ssem_l.at[k],
                recv_sem=rsem_r.at[k], device_id={"head": h - 1}, device_id_type=MESH)

        def rightward(s):
            k_r = n - 1 - s

            @pl.when(k_r > h)
            def _():
                @pl.when(h > 0)
                def _():
                    to_right(k_r).wait_recv()
                    send_r[k_r] = (p_ref[k_r] + recv_l[k_r].astype(jnp.float32)).astype(link)

                @pl.when(h == 0)
                def _():
                    send_r[k_r] = p_ref[k_r].astype(link)

                to_right(k_r).start()

        def leftward(s):
            k_l = s

            @pl.when(k_l < h)
            def _():
                @pl.when(h < n - 1)
                def _():
                    to_left(k_l).wait_recv()
                    send_l[k_l] = (p_ref[k_l] + recv_r[k_l].astype(jnp.float32)).astype(link)

                @pl.when(h == n - 1)
                def _():
                    send_l[k_l] = p_ref[k_l].astype(link)

                to_left(k_l).start()

        for s in range(n - 1):

            @pl.when(2 * h < n)
            def _():
                rightward(s)
                leftward(s)

            @pl.when(2 * h >= n)
            def _():
                leftward(s)
                rightward(s)

        total = p_ref[h]

        @pl.when(h > 0)
        def _():
            to_right(h).wait_recv()

        @pl.when(h < n - 1)
        def _():
            to_left(h).wait_recv()

        left_part = jnp.where(h > 0, recv_l[h].astype(jnp.float32), 0.0)
        right_part = jnp.where(h < n - 1, recv_r[h].astype(jnp.float32), 0.0)
        o_ref[...] = (total + left_part + right_part).astype(o_ref.dtype)
        for s in range(n - 1):
            k_r = n - 1 - s
            k_l = s

            @pl.when(k_r > h)
            def _():
                to_right(k_r).wait_send()

            @pl.when(k_l < h)
            def _():
                to_left(k_l).wait_send()

    @pl.when(jnp.logical_not(valid))
    def _():
        o_ref[...] = jnp.zeros(o_ref.shape, o_ref.dtype)


def head_scatter(parts, tick, cid, link=jnp.bfloat16):
    n = lax.axis_size("head")
    _, rows, cols = parts.shape
    return pl.pallas_call(
        functools.partial(scatter_body, n, tick),
        out_shape=jax.ShapeDtypeStruct((rows, cols), jnp.float32),
        in_specs=[pl.BlockSpec(memory_space=pltpu.VMEM)],
        out_specs=pl.BlockSpec(memory_space=pltpu.VMEM),
        scratch_shapes=[
            pltpu.VMEM((n, rows, cols), link),
            pltpu.VMEM((n, rows, cols), link),
            pltpu.VMEM((n, rows, cols), link),
            pltpu.VMEM((n, rows, cols), link),
            pltpu.SemaphoreType.DMA((n,)),
            pltpu.SemaphoreType.DMA((n,)),
            pltpu.SemaphoreType.DMA((n,)),
            pltpu.SemaphoreType.DMA((n,)),
        ],
        compiler_params=pltpu.CompilerParams(collective_id=cid, has_side_effects=True),
    )(parts)


norm_eps = 1e-05
far_below = -1e30
highest = lax.Precision.HIGH


def shifted(value, axis, by):
    count = lax.axis_size(axis)
    pairs = [(i, i + by) for i in range(count) if 0 <= i + by < count]
    return lax.ppermute(value, axis, pairs)


def entering(value, axis, combine, identity):
    count, mine = (lax.axis_size(axis), lax.axis_index(axis))
    everything = jax.tree.map(lambda part: lax.all_gather(part, axis), value)
    before = jax.tree.map(
        lambda part, zero: jnp.broadcast_to(jnp.asarray(zero, part.dtype), part.shape),
        value,
        identity,
    )
    for k in range(count - 1):
        reached = k < mine
        new = combine(before, jax.tree.map(lambda part: part[k], everything))
        before = jax.tree.map(lambda a, b: jnp.where(reached, a, b), new, before)
    return before


def entering_2(value, axis, join, neutral):
    count = lax.axis_size(axis)
    place = lax.axis_index(axis)
    ahead = count - 1 - place
    gathered = jax.tree.map(
        lambda a, kind: lax.all_gather(a.astype(kind), axis),
        value,
        jax.tree.map(lambda a: jnp.bfloat16 if a.dtype == jnp.float32 else a.dtype, value),
    )
    state = jax.tree.map(lambda a, e: jnp.zeros_like(a) + jnp.asarray(e, a.dtype), value, neutral)
    for lap in range(count - 1):
        source = count - 1 - lap
        new = join(
            state,
            jax.tree.map(lambda a, own: a[source].astype(own.dtype), gathered, value),
        )
        active = lap < ahead
        state = jax.tree.map(lambda a, b: jnp.where(active, a, b), new, state)
    return state


def rms_scale(values):
    return lax.rsqrt(jnp.mean(values * values, axis=-1, keepdims=True) + norm_eps)


def silu_slope(values):
    logistic = jax.nn.sigmoid(values)
    return logistic * (1.0 + values * (1.0 - logistic))


def causal_conv(extended, marks_ext, weight, conv_bias):
    tap_count = weight.shape[0]
    length = extended.shape[0] - tap_count + 1
    counts = jnp.cumsum(marks_ext)
    conv_sum = jnp.zeros((length, extended.shape[1]), jnp.float32) + conv_bias
    for tap_index in range(tap_count):
        linked = (counts[tap_count - 1 :] == counts[tap_index : tap_index + length]).astype(
            jnp.float32
        )
        conv_sum = (
            conv_sum
            + linked[:, None] * weight[tap_index] * extended[tap_index : tap_index + length]
        )
    return conv_sum


def prepare(extended, dt_pre, marks_ext, alive_mask, conv_weight, conv_bias, dt_bias, a_log):
    inner_width = dt_pre.shape[1] * P_SIZE
    activated = jax.nn.silu(causal_conv(extended, marks_ext, conv_weight, conv_bias))
    inner_act = activated[:, :inner_width] * alive_mask[:, None]
    b_mat = activated[:, inner_width : inner_width + N]
    c_mat = activated[:, inner_width + N :]
    step_size = jax.nn.softplus(dt_pre + dt_bias) * alive_mask[:, None]
    log_decay = -step_size * jnp.exp(a_log)
    return (inner_act, step_size, log_decay, b_mat, c_mat)


def block_terms(inner_act, step_size, log_decay, b_mat, start_marks):
    blocks = inner_act.shape[0] // SCAN_BLOCK
    head_count = step_size.shape[1]
    x_blocks = inner_act.reshape(blocks, SCAN_BLOCK, head_count, P_SIZE)
    dt_blocks = step_size.reshape(blocks, SCAN_BLOCK, head_count)
    cum_decay = jnp.cumsum(log_decay.reshape(blocks, SCAN_BLOCK, head_count), axis=1)
    mark_count = jnp.cumsum(start_marks.reshape(blocks, SCAN_BLOCK), axis=1)
    b_blocks = b_mat.reshape(blocks, SCAN_BLOCK, N)
    last_cum = cum_decay[:, -1]
    last_mark = mark_count[:, -1]
    same_end = (mark_count == last_mark[:, None]).astype(jnp.float32)
    end_weight = jnp.exp(last_cum[:, None, :] - cum_decay) * same_end[:, :, None] * dt_blocks
    block_states = jnp.einsum(
        "cjh,cjhp,cjn->chpn", end_weight, x_blocks, b_blocks, precision=highest
    )
    block_decay = jnp.exp(last_cum) * (last_mark == 0).astype(jnp.float32)[:, None]
    return (block_decay, block_states, cum_decay, mark_count, x_blocks, dt_blocks)


def compose_blocks(block_decay, block_states, start_state):
    chain_state = start_state
    incoming = []
    for block_index in range(block_decay.shape[0]):
        incoming.append(chain_state)
        chain_state = (
            block_decay[block_index][:, None, None] * chain_state + block_states[block_index]
        )
    return (chain_state, jnp.stack(incoming))


def block_output(block_parts, b_mat, c_mat, skip, incoming):
    block_decay, block_states, cum_decay, mark_count, x_blocks, dt_blocks = block_parts
    blocks = cum_decay.shape[0]
    head_count = cum_decay.shape[2]
    b_blocks = b_mat.reshape(blocks, SCAN_BLOCK, N)
    c_blocks = c_mat.reshape(blocks, SCAN_BLOCK, N)
    inner_prod = jnp.einsum("cin,cjn->cij", c_blocks, b_blocks, precision=highest)
    arange_pos = jnp.arange(SCAN_BLOCK)
    linked = (arange_pos[:, None] >= arange_pos[None, :])[None] & (
        mark_count[:, :, None] == mark_count[:, None, :]
    )
    spread = jnp.where(
        linked[..., None], cum_decay[:, :, None, :] - cum_decay[:, None, :, :], far_below
    )
    weights = jnp.exp(spread) * inner_prod[..., None] * dt_blocks[:, None, :, :]
    y_intra = jnp.einsum("cijh,cjhp->cihp", weights, x_blocks, precision=highest)
    carry_in = jnp.exp(cum_decay) * (mark_count == 0).astype(jnp.float32)[:, :, None]
    y_inter = (
        jnp.einsum("cin,chpn->cihp", c_blocks, incoming, precision=highest) * carry_in[..., None]
    )
    mixed_out = y_intra + y_inter + skip[None, None, :, None] * x_blocks
    return mixed_out.reshape(blocks * SCAN_BLOCK, head_count * P_SIZE)


def local_front(marks_ext, alive_mask, extended, dt_pre, conv_weight, conv_bias, dt_bias, a_log):
    inner_act, step_size, log_decay, b_mat, c_mat = prepare(
        extended, dt_pre, marks_ext, alive_mask, conv_weight, conv_bias, dt_bias, a_log
    )
    block_parts = block_terms(inner_act, step_size, log_decay, b_mat, marks_ext[KW - 1 :])
    zero_state = jnp.zeros(block_parts[1].shape[1:], jnp.float32)
    total_state, _ = compose_blocks(block_parts[0], block_parts[1], zero_state)
    total_decay = jnp.prod(block_parts[0], axis=0)
    return (block_parts, b_mat, c_mat, total_decay, total_state)


def local_rear(block_parts, b_mat, c_mat, skip, start_state):
    _, incoming = compose_blocks(block_parts[0], block_parts[1], start_state)
    return block_output(block_parts, b_mat, c_mat, skip, incoming)


def local_pass(
    marks_ext,
    alive_mask,
    extended,
    dt_pre,
    conv_weight,
    conv_bias,
    dt_bias,
    a_log,
    skip,
    start_state,
):
    block_parts, b_mat, c_mat, total_decay, total_state = local_front(
        marks_ext, alive_mask, extended, dt_pre, conv_weight, conv_bias, dt_bias, a_log
    )
    return (local_rear(block_parts, b_mat, c_mat, skip, start_state), total_decay, total_state)


def chain_combine(earlier, later):
    return (earlier[0] * later[0], later[0][:, None, None] * earlier[1] + later[1])


def extend(pre_conv, start_marks, edge_rows, edge_marks):
    extended = jnp.concatenate([edge_rows, pre_conv], axis=0)
    marks_ext = jnp.concatenate([edge_marks.astype(jnp.int32), start_marks], axis=0)
    return (extended, marks_ext)


def mixer_forward(stream, start_marks, alive_mask, layer_weights, tick, ids):
    (
        norm_gain,
        w_main,
        w_low,
        w_bc,
        conv_weight,
        conv_bias,
        dt_bias,
        a_log,
        skip,
        gate_gain,
        w_out,
    ) = layer_weights
    inner_width = w_out.shape[0]
    normed = (stream * rms_scale(stream) * norm_gain).astype(jnp.bfloat16)
    gathered = head_gather(normed, tick, ids[0])
    gathered = gathered.reshape(-1, gathered.shape[-1])
    projected = jnp.dot(gathered, w_main, preferred_element_type=jnp.float32)
    gate_pre = projected[:, :inner_width]
    pre_conv = projected[:, inner_width : 2 * inner_width + 2 * N]
    dt_pre = projected[:, 2 * inner_width + 2 * N :]
    marks_float = start_marks.astype(jnp.float32)
    tail_from = pre_conv.shape[0] - KW + 1
    edge_parts = shifted((pre_conv[tail_from:], marks_float[tail_from:]), "seq", 1)
    extended, marks_ext = extend(pre_conv, start_marks, edge_parts[0], edge_parts[1])
    front_fn = partial(local_front, marks_ext, alive_mask)
    front_out, front_pull = jax.vjp(
        front_fn, extended, dt_pre, conv_weight, conv_bias, dt_bias, a_log
    )
    block_parts, b_mat, c_mat, total_decay, total_state = front_out
    neutral = (jnp.ones_like(total_decay), jnp.zeros_like(total_state))
    prefix = entering((total_decay, total_state), "seq", chain_combine, neutral)
    start_state = prefix[1]
    mixed_out, rear_pull = jax.vjp(local_rear, block_parts, b_mat, c_mat, skip, start_state)
    silu_gate = jax.nn.silu(gate_pre)
    gated_mix = mixed_out * silu_gate
    square_total = lax.psum(jnp.sum(gated_mix * gated_mix, axis=-1), "head")
    scale_out = lax.rsqrt(square_total / DI + norm_eps)
    normed_out = (gated_mix * scale_out[:, None] * gate_gain).astype(jnp.bfloat16)
    head_count = lax.axis_size("head")
    branch = head_scatter(
        jnp.dot(normed_out, w_out, preferred_element_type=jnp.float32).reshape(
            head_count, -1, w_out.shape[1]
        ),
        tick,
        ids[1],
    )
    saved = (
        stream,
        gathered,
        gate_pre,
        mixed_out,
        silu_gate,
        gated_mix,
        scale_out,
        normed_out,
        total_decay,
        start_state,
        front_pull,
        rear_pull,
    )
    return stream + branch, saved


def mixer_backward(grad_next, layer_weights, saved, mask_value, tick, ids, hook=None):
    (
        norm_gain,
        w_main,
        w_low,
        w_bc,
        conv_weight,
        conv_bias,
        dt_bias,
        a_log,
        skip,
        gate_gain,
        w_out,
    ) = layer_weights
    (
        stream,
        gathered,
        gate_pre,
        mixed_out,
        silu_gate,
        gated_mix,
        scale_out,
        normed_out,
        total_decay,
        start_state,
        front_pull,
        rear_pull,
    ) = saved
    inner_width = w_out.shape[0]
    grad_branch = grad_next.astype(jnp.bfloat16)
    shard_rows = head_gather(grad_branch, tick, ids[0])
    shard_rows = shard_rows.reshape(-1, shard_rows.shape[-1])
    g_w_out = lax.dot_general(
        normed_out, shard_rows, (((0,), (0,)), ((), ())), preferred_element_type=jnp.float32
    ) * mask_value
    grad_normed = lax.dot_general(
        shard_rows, w_out, (((1,), (1,)), ((), ())), preferred_element_type=jnp.float32
    )
    weighted = grad_normed * gate_gain
    g_gate_gain = jnp.sum(grad_normed * gated_mix * scale_out[:, None], axis=0)
    cross_sum = lax.psum(jnp.sum(weighted * gated_mix, axis=-1), "head")
    grad_gated = (
        scale_out[:, None] * weighted - gated_mix * (scale_out**3 * cross_sum / DI)[:, None]
    )
    grad_mixed = grad_gated * silu_gate
    grad_gate = (grad_gated * mixed_out * silu_slope(gate_pre)).astype(jnp.bfloat16)
    g_parts, g_b_mat, g_c_mat, g_skip, g_start = rear_pull(grad_mixed)
    neutral = (jnp.ones_like(total_decay), jnp.zeros_like(g_start))
    suffix = entering_2((total_decay, g_start), "seq", chain_combine, neutral)
    after_state = suffix[1]
    grad_decay = jnp.sum(after_state * start_state, axis=(1, 2))
    grad_ext, grad_dt_pre, g_conv_w, g_conv_b, g_dt_bias, g_a_log = front_pull(
        (g_parts, g_b_mat, g_c_mat, grad_decay, after_state)
    )
    returned = shifted(grad_ext[: KW - 1], "seq", -1)
    grad_pre = grad_ext[KW - 1 :]
    tail_from = grad_pre.shape[0] - KW + 1
    grad_pre = jnp.concatenate([grad_pre[:tail_from], grad_pre[tail_from:] + returned], axis=0)
    grad_inner = grad_pre[:, :inner_width].astype(jnp.bfloat16)
    grad_bc = grad_pre[:, inner_width:]
    grad_low = jnp.concatenate([grad_gate, grad_inner, grad_dt_pre.astype(jnp.bfloat16)], axis=1)
    w_bc_float = w_bc.astype(jnp.float32)
    g_low = lax.dot_general(
        gathered, grad_low, (((0,), (0,)), ((), ())), preferred_element_type=jnp.float32
    )
    g_w_bc = lax.dot_general(
        gathered.astype(jnp.float32),
        grad_bc,
        (((0,), (0,)), ((), ())),
        precision=highest,
        preferred_element_type=jnp.float32,
    )
    main_term = lax.dot_general(
        grad_low, w_low, (((1,), (1,)), ((), ())), preferred_element_type=jnp.float32
    )
    side_term = lax.dot_general(
        grad_bc,
        w_bc_float,
        (((1,), (1,)), ((), ())),
        precision=highest,
        preferred_element_type=jnp.float32,
    )
    head_count = lax.axis_size("head")
    lead = 0.0
    if hook is not None:
        lead = hook((g_w_bc, g_conv_w[:, inner_width:], g_conv_b[inner_width:]))
    grad_normed_in = head_scatter(
        (main_term + side_term + lead).reshape(head_count, -1, main_term.shape[1]), tick, ids[1]
    )
    scale_in = rms_scale(stream)
    g_norm_gain = jnp.sum(grad_normed_in * stream * scale_in, axis=0)
    weighted_in = grad_normed_in * norm_gain
    grad_stream = (
        grad_next
        + scale_in * weighted_in
        - stream * scale_in**3 * jnp.mean(weighted_in * stream, axis=-1, keepdims=True)
    )
    head_part = (
        g_low[:, :inner_width],
        g_low[:, inner_width : 2 * inner_width],
        g_low[:, 2 * inner_width :],
        g_conv_w[:, :inner_width],
        g_conv_b[:inner_width],
        g_dt_bias,
        g_a_log,
        g_skip,
        g_gate_gain,
    )
    shared_part = (g_norm_gain, g_w_bc, g_conv_w[:, inner_width:], g_conv_b[inner_width:])
    return (grad_stream, head_part, shared_part, g_w_out)


def pack_rows(members, width, multiple):
    rows = jnp.concatenate([member.reshape(-1, width) for member in members], axis=0)
    return jnp.pad(rows, ((0, -rows.shape[0] % multiple), (0, 0)))


def unpack_rows(rows, shapes, width):
    pieces = []
    start = 0
    for shape in shapes:
        count = math.prod(shape) // width
        pieces.append(rows[start : start + count].reshape(shape))
        start += count
    return tuple(pieces)


def reduce_grads(head_part, norm_part, bc_part, tick_count):
    summed = lax.psum(
        tuple(member.astype(jnp.bfloat16) for member in head_part[:3] + (bc_part,)), "seq"
    )
    head_sum = tuple(member.astype(jnp.float32) for member in summed[:3]) + tuple(
        lax.psum(member.astype(jnp.bfloat16), "seq").astype(jnp.float32)
        for member in head_part[3:]
    )
    bc_rows = head_gather(summed[3], (0, 0, 1), 4 * tick_count + 1).astype(jnp.float32)
    norm_sum = lax.psum(norm_part, ("seq", "head"))
    return (head_sum, norm_sum, bc_rows.reshape(-1, bc_rows.shape[-1]))


def store_slot(buffer, value, slot_index, is_valid):
    current = lax.dynamic_index_in_dim(buffer, slot_index, 0, False)
    return lax.dynamic_update_index_in_dim(
        buffer, jnp.where(is_valid, value, current), slot_index, 0
    )


def on_device(
    inputs,
    cotangent,
    starts,
    live,
    norm_gain,
    w_gate,
    w_in,
    w_bc,
    w_dt,
    conv_x,
    conv_x_bias,
    conv_bc,
    conv_bc_bias,
    dt_bias,
    a_log,
    skip,
    gate_gain,
    w_out,
):
    section_count = lax.axis_size("section")
    section_index = lax.axis_index("section")
    micro_count = inputs.shape[0]
    tick_count = micro_count + section_count - 1
    w_main = jnp.concatenate([w_gate[0], w_in[0], w_bc[0], w_dt[0]], axis=1)
    w_low = jnp.concatenate([w_gate[0], w_in[0], w_dt[0]], axis=1)
    conv_weight = jnp.concatenate([conv_x[0], conv_bc[0]], axis=1).astype(jnp.float32)
    conv_bias = jnp.concatenate([conv_x_bias[0], conv_bc_bias[0]], axis=0)
    layer_weights = (
        norm_gain[0],
        w_main,
        w_low,
        w_bc[0],
        conv_weight,
        conv_bias,
        dt_bias[0],
        a_log[0],
        skip[0],
        gate_gain[0],
        w_out[0],
    )
    row_shape = inputs.shape[1:]
    outputs_all = jnp.zeros((micro_count,) + row_shape, jnp.float32)
    arrived = jnp.zeros(row_shape, jnp.float32)
    ticks = []
    for tick_index in range(tick_count):
        slot_index = tick_index - section_index
        is_valid = (slot_index >= 0) & (slot_index < micro_count)
        clipped = jnp.clip(slot_index, 0, micro_count - 1)
        fresh_rows = lax.dynamic_index_in_dim(inputs, clipped, 0, False).astype(jnp.float32)
        stream = jnp.where(section_index == 0, fresh_rows, arrived)
        start_marks = lax.dynamic_index_in_dim(starts, clipped, 0, False)
        alive_mask = lax.dynamic_index_in_dim(live, clipped, 0, False).astype(jnp.float32)
        result, saved = mixer_forward(
            stream,
            start_marks,
            alive_mask,
            layer_weights,
            (tick_index, -1, micro_count),
            (tick_index, tick_count + tick_index),
        )
        outputs_all = store_slot(outputs_all, result, clipped, is_valid)
        ticks.append((clipped, is_valid, saved))
        if tick_index + 1 < tick_count:
            arrived = shifted(result, "section", 1)
    back_arrived = jnp.zeros(row_shape, jnp.float32)
    input_grads = jnp.zeros((micro_count,) + row_shape, jnp.float32)
    head_count = lax.axis_size("head")
    bc_box = []
    head_total = ()
    shared_total = ()
    for tick_index in range(tick_count):
        clipped, is_valid, saved = ticks[tick_count - 1 - tick_index]
        outer_grad = lax.dynamic_index_in_dim(cotangent, clipped, 0, False).astype(jnp.float32)
        grad_next = jnp.where(section_index == section_count - 1, outer_grad, back_arrived)
        mask_value = is_valid.astype(jnp.float32)
        hook = None
        if tick_index + 1 == tick_count:

            def hook(bc_local, mask_value=mask_value, earlier=shared_total):
                totals = tuple(
                    (prev + member * mask_value) if earlier else member * mask_value
                    for prev, member in zip(earlier[1:] or bc_local, bc_local)
                )
                rows = pack_rows(totals, totals[0].shape[-1], 8 * head_count)
                part = head_scatter(
                    rows.reshape(head_count, -1, rows.shape[-1]), (0, 0, 1), 4 * tick_count
                )
                bc_box.append((part, [member.shape for member in totals]))
                return part[0, 0] * 0.0

        grad_stream, head_part, shared_part, out_part = mixer_backward(
            grad_next,
            layer_weights,
            saved,
            mask_value,
            (tick_count - 1 - tick_index, -1, micro_count),
            (2 * tick_count + tick_index, 3 * tick_count + tick_index),
            hook,
        )
        if tick_index == 0:
            out_total = out_part
        else:
            out_total = out_total + out_part
        if tick_index + 1 == tick_count:
            out_total = lax.psum(out_total.astype(jnp.bfloat16), "seq")
        head_part = tuple((member * mask_value for member in head_part))
        shared_part = tuple((member * mask_value for member in shared_part))
        if tick_index == 0:
            head_total = head_part
            shared_total = shared_part
        else:
            head_total = tuple((former + latter for former, latter in zip(head_total, head_part)))
            shared_total = tuple(
                (former + latter for former, latter in zip(shared_total, shared_part))
            )
        input_grads = store_slot(input_grads, grad_stream, clipped, is_valid)
        if tick_index + 1 < tick_count:
            back_arrived = shifted(grad_stream.astype(jnp.bfloat16), "section", -1).astype(
                grad_stream.dtype
            )
    anchor = out_total[0, 0].astype(jnp.float32) * 0.0
    head_total = (head_total[0] + anchor,) + head_total[1:]
    bc_part, bc_shapes = bc_box[0]
    head_total, norm_sum, bc_rows = reduce_grads(head_total, shared_total[0], bc_part, tick_count)
    shared_total = (norm_sum,) + unpack_rows(bc_rows, bc_shapes, bc_rows.shape[-1])
    head_total = head_total[:3] + (out_total.astype(jnp.float32),) + head_total[3:]
    return (
        outputs_all[None],
        input_grads[None],
        shared_total[0][None],
        head_total[0][None],
        head_total[1][None],
        shared_total[1][None],
        head_total[2][None],
        head_total[4][None],
        head_total[5][None],
        shared_total[2][None],
        shared_total[3][None],
        head_total[6][None],
        head_total[7][None],
        head_total[8][None],
        head_total[9][None],
        head_total[3][None],
    )


def solution(mesh):
    return jax.shard_map(
        on_device,
        mesh=mesh,
        in_specs=(
            P(None, ("seq", "head"), None),
            P(None, ("seq", "head"), None),
            P(None, "seq"),
            P(None, "seq"),
            P("section", None),
            P("section", None, "head"),
            P("section", None, "head"),
            P("section", None, None),
            P("section", None, "head"),
            P("section", None, "head"),
            P("section", "head"),
            P("section", None, None),
            P("section", None),
            P("section", "head"),
            P("section", "head"),
            P("section", "head"),
            P("section", "head"),
            P("section", "head", None),
        ),
        out_specs=(
            P("section", None, ("seq", "head"), None),
            P("section", None, ("seq", "head"), None),
            P("section", None),
            P("section", None, "head"),
            P("section", None, "head"),
            P("section", None, None),
            P("section", None, "head"),
            P("section", None, "head"),
            P("section", "head"),
            P("section", None, None),
            P("section", None),
            P("section", "head"),
            P("section", "head"),
            P("section", "head"),
            P("section", "head"),
            P("section", "head", None),
        ),
        check_vma=False,
    )
```

```python
from functools import partial

import functools
import math

import jax
import jax.numpy as jnp
from jax import lax
from jax.experimental import pallas as pl
from jax.experimental.pallas import tpu as pltpu
from jax.sharding import PartitionSpec as P

DI = 4096
P_SIZE = 64
N = 128
KW = 4
SCAN_BLOCK = 256


MESH = pl.DeviceIdType.MESH


def _tick_valid(offset, sign, count):
    slot = offset + sign * lax.axis_index("section")
    return jnp.logical_and(slot >= 0, slot < count)


def _enter(barrier, h, n):
    @pl.when(h > 0)
    def _():
        pl.semaphore_signal(barrier, 1, device_id={"head": h - 1}, device_id_type=MESH)

    @pl.when(h < n - 1)
    def _():
        pl.semaphore_signal(barrier, 1, device_id={"head": h + 1}, device_id_type=MESH)

    @pl.when(jnp.logical_and(h > 0, h < n - 1))
    def _():
        pl.semaphore_wait(barrier, 2)

    @pl.when(jnp.logical_or(h == 0, h == n - 1))
    def _():
        pl.semaphore_wait(barrier, 1)


def gather_body(n, tick, x_ref, o_ref, land, send_r, send_l, recv):
    h = lax.axis_index("head")
    valid = _tick_valid(*tick)

    @pl.when(valid)
    def _():
        _enter(pltpu.get_barrier_semaphore(), h, n)

        rows = x_ref.shape[0]
        pieces = 2 if rows % 32 == 0 else 1
        size = rows // pieces

        def chunked(s, k, sems, peer):
            copies = []
            for c in range(pieces):
                part = pl.ds(c * size, size)
                src = x_ref.at[part] if s == 0 else land.at[k, part]
                copies.append(pltpu.make_async_remote_copy(
                    src_ref=src, dst_ref=land.at[k, part], send_sem=sems.at[s * pieces + c],
                    recv_sem=recv.at[k], device_id={"head": peer}, device_id_type=MESH))
            return copies

        class Group:
            def __init__(self, copies):
                self.copies = copies

            def start(self):
                for copy in self.copies:
                    copy.start()

            def wait_send(self):
                for copy in self.copies:
                    copy.wait_send()

        def copy_right(s, k):
            return Group(chunked(s, k, send_r, h + 1))

        def copy_left(s, k):
            return Group(chunked(s, k, send_l, h - 1))

        for s in range(n):
            k_r = h - s
            k_l = h + s
            if s >= 1:
                @pl.when(k_r >= 0)
                def _():
                    pltpu.make_async_remote_copy(
                        src_ref=land.at[k_r], dst_ref=land.at[k_r], send_sem=send_r.at[0],
                        recv_sem=recv.at[k_r], device_id={"head": h}, device_id_type=MESH
                    ).wait_recv()

                @pl.when(k_l <= n - 1)
                def _():
                    pltpu.make_async_remote_copy(
                        src_ref=land.at[k_l], dst_ref=land.at[k_l], send_sem=send_l.at[0],
                        recv_sem=recv.at[k_l], device_id={"head": h}, device_id_type=MESH
                    ).wait_recv()
            if s <= n - 2:
                @pl.when(jnp.logical_and(k_r >= 0, h < n - 1))
                def _():
                    copy_right(s, k_r).start()

                @pl.when(jnp.logical_and(k_l <= n - 1, h > 0))
                def _():
                    copy_left(s, k_l).start()
        land[h] = x_ref[...]
        for s in range(n - 1):
            k_r = h - s
            k_l = h + s

            @pl.when(jnp.logical_and(k_r >= 0, h < n - 1))
            def _():
                copy_right(s, k_r).wait_send()

            @pl.when(jnp.logical_and(k_l <= n - 1, h > 0))
            def _():
                copy_left(s, k_l).wait_send()
        o_ref[...] = land[...]

    @pl.when(jnp.logical_not(valid))
    def _():
        o_ref[...] = jnp.zeros(o_ref.shape, o_ref.dtype)


def head_gather(x, tick, cid):
    n = lax.axis_size("head")
    rows, cols = x.shape
    return pl.pallas_call(
        functools.partial(gather_body, n, tick),
        out_shape=jax.ShapeDtypeStruct((n, rows, cols), x.dtype),
        in_specs=[pl.BlockSpec(memory_space=pltpu.VMEM)],
        out_specs=pl.BlockSpec(memory_space=pltpu.VMEM),
        scratch_shapes=[
            pltpu.VMEM((n, rows, cols), x.dtype),
            pltpu.SemaphoreType.DMA((2 * n,)),
            pltpu.SemaphoreType.DMA((2 * n,)),
            pltpu.SemaphoreType.DMA((n,)),
        ],
        compiler_params=pltpu.CompilerParams(collective_id=cid, has_side_effects=True),
    )(x)


def scatter_body(n, tick, p_ref, o_ref, recv_l, recv_r, send_l, send_r, ssem_l, ssem_r, rsem_l, rsem_r):
    h = lax.axis_index("head")
    valid = _tick_valid(*tick)
    link = send_r.dtype

    @pl.when(valid)
    def _():
        _enter(pltpu.get_barrier_semaphore(), h, n)

        rows = p_ref.shape[1]
        pieces = 2 if rows % 32 == 0 else 1
        size = rows // pieces

        def to_right(k, c=None):
            part = slice(None) if c is None else pl.ds(c * size, size)
            return pltpu.make_async_remote_copy(
                src_ref=send_r.at[k, part], dst_ref=recv_l.at[k, part],
                send_sem=ssem_r.at[k * pieces + (c or 0)], recv_sem=rsem_l.at[k],
                device_id={"head": h + 1}, device_id_type=MESH)

        def to_left(k, c=None):
            part = slice(None) if c is None else pl.ds(c * size, size)
            return pltpu.make_async_remote_copy(
                src_ref=send_l.at[k, part], dst_ref=recv_r.at[k, part],
                send_sem=ssem_l.at[k * pieces + (c or 0)], recv_sem=rsem_r.at[k],
                device_id={"head": h - 1}, device_id_type=MESH)

        def rightward(s):
            k_r = n - 1 - s

            @pl.when(k_r > h)
            def _():
                @pl.when(h > 0)
                def _():
                    to_right(k_r).wait_recv()

                for c in range(pieces):
                    part = pl.ds(c * size, size)

                    @pl.when(h > 0)
                    def _():
                        send_r[k_r, part] = (
                            p_ref[k_r, part] + recv_l[k_r, part].astype(jnp.float32)
                        ).astype(link)

                    @pl.when(h == 0)
                    def _():
                        send_r[k_r, part] = p_ref[k_r, part].astype(link)

                    to_right(k_r, c).start()

        def leftward(s):
            k_l = s

            @pl.when(k_l < h)
            def _():
                @pl.when(h < n - 1)
                def _():
                    to_left(k_l).wait_recv()

                for c in range(pieces):
                    part = pl.ds(c * size, size)

                    @pl.when(h < n - 1)
                    def _():
                        send_l[k_l, part] = (
                            p_ref[k_l, part] + recv_r[k_l, part].astype(jnp.float32)
                        ).astype(link)

                    @pl.when(h == n - 1)
                    def _():
                        send_l[k_l, part] = p_ref[k_l, part].astype(link)

                    to_left(k_l, c).start()

        for s in range(n - 1):

            @pl.when(2 * h < n)
            def _():
                rightward(s)
                leftward(s)

            @pl.when(2 * h >= n)
            def _():
                leftward(s)
                rightward(s)

        total = p_ref[h]

        @pl.when(h > 0)
        def _():
            to_right(h).wait_recv()

        @pl.when(h < n - 1)
        def _():
            to_left(h).wait_recv()

        left_part = jnp.where(h > 0, recv_l[h].astype(jnp.float32), 0.0)
        right_part = jnp.where(h < n - 1, recv_r[h].astype(jnp.float32), 0.0)
        o_ref[...] = (total + left_part + right_part).astype(o_ref.dtype)
        for s in range(n - 1):
            k_r = n - 1 - s
            k_l = s

            @pl.when(k_r > h)
            def _():
                for c in range(pieces):
                    to_right(k_r, c).wait_send()

            @pl.when(k_l < h)
            def _():
                for c in range(pieces):
                    to_left(k_l, c).wait_send()

    @pl.when(jnp.logical_not(valid))
    def _():
        o_ref[...] = jnp.zeros(o_ref.shape, o_ref.dtype)


def head_scatter(parts, tick, cid, link=jnp.bfloat16):
    n = lax.axis_size("head")
    _, rows, cols = parts.shape
    return pl.pallas_call(
        functools.partial(scatter_body, n, tick),
        out_shape=jax.ShapeDtypeStruct((rows, cols), jnp.float32),
        in_specs=[pl.BlockSpec(memory_space=pltpu.VMEM)],
        out_specs=pl.BlockSpec(memory_space=pltpu.VMEM),
        scratch_shapes=[
            pltpu.VMEM((n, rows, cols), link),
            pltpu.VMEM((n, rows, cols), link),
            pltpu.VMEM((n, rows, cols), link),
            pltpu.VMEM((n, rows, cols), link),
            pltpu.SemaphoreType.DMA((2 * n,)),
            pltpu.SemaphoreType.DMA((2 * n,)),
            pltpu.SemaphoreType.DMA((n,)),
            pltpu.SemaphoreType.DMA((n,)),
        ],
        compiler_params=pltpu.CompilerParams(collective_id=cid, has_side_effects=True),
    )(parts)


norm_eps = 1e-05
far_below = -1e30
highest = lax.Precision.HIGH


def shifted(value, axis, by):
    count = lax.axis_size(axis)
    pairs = [(i, i + by) for i in range(count) if 0 <= i + by < count]
    return lax.ppermute(value, axis, pairs)


def entering(value, axis, combine, identity):
    count, mine = (lax.axis_size(axis), lax.axis_index(axis))
    everything = jax.tree.map(lambda part: lax.all_gather(part, axis), value)
    before = jax.tree.map(
        lambda part, zero: jnp.broadcast_to(jnp.asarray(zero, part.dtype), part.shape),
        value,
        identity,
    )
    for k in range(count - 1):
        reached = k < mine
        new = combine(before, jax.tree.map(lambda part: part[k], everything))
        before = jax.tree.map(lambda a, b: jnp.where(reached, a, b), new, before)
    return before


def entering_2(value, axis, join, neutral):
    count = lax.axis_size(axis)
    place = lax.axis_index(axis)
    ahead = count - 1 - place
    gathered = jax.tree.map(
        lambda a, kind: lax.all_gather(a.astype(kind), axis),
        value,
        jax.tree.map(lambda a: jnp.bfloat16 if a.dtype == jnp.float32 else a.dtype, value),
    )
    state = jax.tree.map(lambda a, e: jnp.zeros_like(a) + jnp.asarray(e, a.dtype), value, neutral)
    for lap in range(count - 1):
        source = count - 1 - lap
        new = join(
            state,
            jax.tree.map(lambda a, own: a[source].astype(own.dtype), gathered, value),
        )
        active = lap < ahead
        state = jax.tree.map(lambda a, b: jnp.where(active, a, b), new, state)
    return state


def rms_scale(values):
    return lax.rsqrt(jnp.mean(values * values, axis=-1, keepdims=True) + norm_eps)


def silu_slope(values):
    logistic = jax.nn.sigmoid(values)
    return logistic * (1.0 + values * (1.0 - logistic))


def causal_conv(extended, marks_ext, weight, conv_bias):
    tap_count = weight.shape[0]
    length = extended.shape[0] - tap_count + 1
    counts = jnp.cumsum(marks_ext)
    conv_sum = jnp.zeros((length, extended.shape[1]), jnp.float32) + conv_bias
    for tap_index in range(tap_count):
        linked = (counts[tap_count - 1 :] == counts[tap_index : tap_index + length]).astype(
            jnp.float32
        )
        conv_sum = (
            conv_sum
            + linked[:, None] * weight[tap_index] * extended[tap_index : tap_index + length]
        )
    return conv_sum


def prepare(extended, dt_pre, marks_ext, alive_mask, conv_weight, conv_bias, dt_bias, a_log):
    inner_width = dt_pre.shape[1] * P_SIZE
    activated = jax.nn.silu(causal_conv(extended, marks_ext, conv_weight, conv_bias))
    inner_act = activated[:, :inner_width] * alive_mask[:, None]
    b_mat = activated[:, inner_width : inner_width + N]
    c_mat = activated[:, inner_width + N :]
    step_size = jax.nn.softplus(dt_pre + dt_bias) * alive_mask[:, None]
    log_decay = -step_size * jnp.exp(a_log)
    return (inner_act, step_size, log_decay, b_mat, c_mat)


def block_terms(inner_act, step_size, log_decay, b_mat, start_marks):
    blocks = inner_act.shape[0] // SCAN_BLOCK
    head_count = step_size.shape[1]
    x_blocks = inner_act.reshape(blocks, SCAN_BLOCK, head_count, P_SIZE)
    dt_blocks = step_size.reshape(blocks, SCAN_BLOCK, head_count)
    cum_decay = jnp.cumsum(log_decay.reshape(blocks, SCAN_BLOCK, head_count), axis=1)
    mark_count = jnp.cumsum(start_marks.reshape(blocks, SCAN_BLOCK), axis=1)
    b_blocks = b_mat.reshape(blocks, SCAN_BLOCK, N)
    last_cum = cum_decay[:, -1]
    last_mark = mark_count[:, -1]
    same_end = (mark_count == last_mark[:, None]).astype(jnp.float32)
    end_weight = jnp.exp(last_cum[:, None, :] - cum_decay) * same_end[:, :, None] * dt_blocks
    block_states = jnp.einsum(
        "cjh,cjhp,cjn->chpn", end_weight, x_blocks, b_blocks, precision=highest
    )
    block_decay = jnp.exp(last_cum) * (last_mark == 0).astype(jnp.float32)[:, None]
    return (block_decay, block_states, cum_decay, mark_count, x_blocks, dt_blocks)


def compose_blocks(block_decay, block_states, start_state):
    chain_state = start_state
    incoming = []
    for block_index in range(block_decay.shape[0]):
        incoming.append(chain_state)
        chain_state = (
            block_decay[block_index][:, None, None] * chain_state + block_states[block_index]
        )
    return (chain_state, jnp.stack(incoming))


def block_output(block_parts, b_mat, c_mat, skip, incoming):
    block_decay, block_states, cum_decay, mark_count, x_blocks, dt_blocks = block_parts
    blocks = cum_decay.shape[0]
    head_count = cum_decay.shape[2]
    b_blocks = b_mat.reshape(blocks, SCAN_BLOCK, N)
    c_blocks = c_mat.reshape(blocks, SCAN_BLOCK, N)
    inner_prod = jnp.einsum("cin,cjn->cij", c_blocks, b_blocks, precision=highest)
    arange_pos = jnp.arange(SCAN_BLOCK)
    linked = (arange_pos[:, None] >= arange_pos[None, :])[None] & (
        mark_count[:, :, None] == mark_count[:, None, :]
    )
    spread = jnp.where(
        linked[..., None], cum_decay[:, :, None, :] - cum_decay[:, None, :, :], far_below
    )
    weights = jnp.exp(spread) * inner_prod[..., None] * dt_blocks[:, None, :, :]
    y_intra = jnp.einsum("cijh,cjhp->cihp", weights, x_blocks, precision=highest)
    carry_in = jnp.exp(cum_decay) * (mark_count == 0).astype(jnp.float32)[:, :, None]
    y_inter = (
        jnp.einsum("cin,chpn->cihp", c_blocks, incoming, precision=highest) * carry_in[..., None]
    )
    mixed_out = y_intra + y_inter + skip[None, None, :, None] * x_blocks
    return mixed_out.reshape(blocks * SCAN_BLOCK, head_count * P_SIZE)


def local_front(marks_ext, alive_mask, extended, dt_pre, conv_weight, conv_bias, dt_bias, a_log):
    inner_act, step_size, log_decay, b_mat, c_mat = prepare(
        extended, dt_pre, marks_ext, alive_mask, conv_weight, conv_bias, dt_bias, a_log
    )
    block_parts = block_terms(inner_act, step_size, log_decay, b_mat, marks_ext[KW - 1 :])
    zero_state = jnp.zeros(block_parts[1].shape[1:], jnp.float32)
    total_state, _ = compose_blocks(block_parts[0], block_parts[1], zero_state)
    total_decay = jnp.prod(block_parts[0], axis=0)
    return (block_parts, b_mat, c_mat, total_decay, total_state)


def local_rear(block_parts, b_mat, c_mat, skip, start_state):
    _, incoming = compose_blocks(block_parts[0], block_parts[1], start_state)
    return block_output(block_parts, b_mat, c_mat, skip, incoming)


def local_pass(
    marks_ext,
    alive_mask,
    extended,
    dt_pre,
    conv_weight,
    conv_bias,
    dt_bias,
    a_log,
    skip,
    start_state,
):
    block_parts, b_mat, c_mat, total_decay, total_state = local_front(
        marks_ext, alive_mask, extended, dt_pre, conv_weight, conv_bias, dt_bias, a_log
    )
    return (local_rear(block_parts, b_mat, c_mat, skip, start_state), total_decay, total_state)


def chain_combine(earlier, later):
    return (earlier[0] * later[0], later[0][:, None, None] * earlier[1] + later[1])


def extend(pre_conv, start_marks, edge_rows, edge_marks):
    extended = jnp.concatenate([edge_rows, pre_conv], axis=0)
    marks_ext = jnp.concatenate([edge_marks.astype(jnp.int32), start_marks], axis=0)
    return (extended, marks_ext)


def mixer_forward(stream, start_marks, alive_mask, layer_weights, tick, ids):
    (
        norm_gain,
        w_main,
        w_low,
        w_bc,
        conv_weight,
        conv_bias,
        dt_bias,
        a_log,
        skip,
        gate_gain,
        w_out,
    ) = layer_weights
    inner_width = w_out.shape[0]
    normed = (stream * rms_scale(stream) * norm_gain).astype(jnp.bfloat16)
    gathered = head_gather(normed, tick, ids[0])
    gathered = gathered.reshape(-1, gathered.shape[-1])
    projected = jnp.dot(gathered, w_main, preferred_element_type=jnp.float32)
    gate_pre = projected[:, :inner_width]
    pre_conv = projected[:, inner_width : 2 * inner_width + 2 * N]
    dt_pre = projected[:, 2 * inner_width + 2 * N :]
    marks_float = start_marks.astype(jnp.float32)
    tail_from = pre_conv.shape[0] - KW + 1
    edge_parts = shifted((pre_conv[tail_from:], marks_float[tail_from:]), "seq", 1)
    extended, marks_ext = extend(pre_conv, start_marks, edge_parts[0], edge_parts[1])
    front_fn = partial(local_front, marks_ext, alive_mask)
    front_out, front_pull = jax.vjp(
        front_fn, extended, dt_pre, conv_weight, conv_bias, dt_bias, a_log
    )
    block_parts, b_mat, c_mat, total_decay, total_state = front_out
    neutral = (jnp.ones_like(total_decay), jnp.zeros_like(total_state))
    prefix = entering((total_decay, total_state), "seq", chain_combine, neutral)
    start_state = prefix[1]
    mixed_out, rear_pull = jax.vjp(local_rear, block_parts, b_mat, c_mat, skip, start_state)
    silu_gate = jax.nn.silu(gate_pre)
    gated_mix = mixed_out * silu_gate
    square_total = lax.psum(jnp.sum(gated_mix * gated_mix, axis=-1), "head")
    scale_out = lax.rsqrt(square_total / DI + norm_eps)
    normed_out = (gated_mix * scale_out[:, None] * gate_gain).astype(jnp.bfloat16)
    head_count = lax.axis_size("head")
    branch = head_scatter(
        jnp.dot(normed_out, w_out, preferred_element_type=jnp.float32).reshape(
            head_count, -1, w_out.shape[1]
        ),
        tick,
        ids[1],
    )
    saved = (
        stream,
        gathered,
        gate_pre,
        mixed_out,
        silu_gate,
        gated_mix,
        scale_out,
        normed_out,
        total_decay,
        start_state,
        front_pull,
        rear_pull,
    )
    return stream + branch, saved


def mixer_backward(grad_next, layer_weights, saved, mask_value, tick, ids, hook=None):
    (
        norm_gain,
        w_main,
        w_low,
        w_bc,
        conv_weight,
        conv_bias,
        dt_bias,
        a_log,
        skip,
        gate_gain,
        w_out,
    ) = layer_weights
    (
        stream,
        gathered,
        gate_pre,
        mixed_out,
        silu_gate,
        gated_mix,
        scale_out,
        normed_out,
        total_decay,
        start_state,
        front_pull,
        rear_pull,
    ) = saved
    inner_width = w_out.shape[0]
    grad_branch = grad_next.astype(jnp.bfloat16)
    shard_rows = head_gather(grad_branch, tick, ids[0])
    shard_rows = shard_rows.reshape(-1, shard_rows.shape[-1])
    g_w_out = lax.dot_general(
        normed_out, shard_rows, (((0,), (0,)), ((), ())), preferred_element_type=jnp.float32
    ) * mask_value
    grad_normed = lax.dot_general(
        shard_rows, w_out, (((1,), (1,)), ((), ())), preferred_element_type=jnp.float32
    )
    weighted = grad_normed * gate_gain
    g_gate_gain = jnp.sum(grad_normed * gated_mix * scale_out[:, None], axis=0)
    cross_sum = lax.psum(jnp.sum(weighted * gated_mix, axis=-1), "head")
    grad_gated = (
        scale_out[:, None] * weighted - gated_mix * (scale_out**3 * cross_sum / DI)[:, None]
    )
    grad_mixed = grad_gated * silu_gate
    grad_gate = (grad_gated * mixed_out * silu_slope(gate_pre)).astype(jnp.bfloat16)
    g_parts, g_b_mat, g_c_mat, g_skip, g_start = rear_pull(grad_mixed)
    neutral = (jnp.ones_like(total_decay), jnp.zeros_like(g_start))
    suffix = entering_2((total_decay, g_start), "seq", chain_combine, neutral)
    after_state = suffix[1]
    grad_decay = jnp.sum(after_state * start_state, axis=(1, 2))
    grad_ext, grad_dt_pre, g_conv_w, g_conv_b, g_dt_bias, g_a_log = front_pull(
        (g_parts, g_b_mat, g_c_mat, grad_decay, after_state)
    )
    returned = shifted(grad_ext[: KW - 1], "seq", -1)
    grad_pre = grad_ext[KW - 1 :]
    tail_from = grad_pre.shape[0] - KW + 1
    grad_pre = jnp.concatenate([grad_pre[:tail_from], grad_pre[tail_from:] + returned], axis=0)
    grad_inner = grad_pre[:, :inner_width].astype(jnp.bfloat16)
    grad_bc = grad_pre[:, inner_width:]
    grad_low = jnp.concatenate([grad_gate, grad_inner, grad_dt_pre.astype(jnp.bfloat16)], axis=1)
    w_bc_float = w_bc.astype(jnp.float32)
    g_low = lax.dot_general(
        gathered, grad_low, (((0,), (0,)), ((), ())), preferred_element_type=jnp.float32
    )
    g_w_bc = lax.dot_general(
        gathered.astype(jnp.float32),
        grad_bc,
        (((0,), (0,)), ((), ())),
        precision=highest,
        preferred_element_type=jnp.float32,
    )
    main_term = lax.dot_general(
        grad_low, w_low, (((1,), (1,)), ((), ())), preferred_element_type=jnp.float32
    )
    side_term = lax.dot_general(
        grad_bc,
        w_bc_float,
        (((1,), (1,)), ((), ())),
        precision=highest,
        preferred_element_type=jnp.float32,
    )
    head_count = lax.axis_size("head")
    lead = 0.0
    if hook is not None:
        lead = hook((g_w_bc, g_conv_w[:, inner_width:], g_conv_b[inner_width:]))
    grad_normed_in = head_scatter(
        (main_term + side_term + lead).reshape(head_count, -1, main_term.shape[1]), tick, ids[1]
    )
    scale_in = rms_scale(stream)
    g_norm_gain = jnp.sum(grad_normed_in * stream * scale_in, axis=0)
    weighted_in = grad_normed_in * norm_gain
    grad_stream = (
        grad_next
        + scale_in * weighted_in
        - stream * scale_in**3 * jnp.mean(weighted_in * stream, axis=-1, keepdims=True)
    )
    head_part = (
        g_low[:, :inner_width],
        g_low[:, inner_width : 2 * inner_width],
        g_low[:, 2 * inner_width :],
        g_conv_w[:, :inner_width],
        g_conv_b[:inner_width],
        g_dt_bias,
        g_a_log,
        g_skip,
        g_gate_gain,
    )
    shared_part = (g_norm_gain, g_w_bc, g_conv_w[:, inner_width:], g_conv_b[inner_width:])
    return (grad_stream, head_part, shared_part, g_w_out)


def pack_rows(members, width, multiple):
    rows = jnp.concatenate([member.reshape(-1, width) for member in members], axis=0)
    return jnp.pad(rows, ((0, -rows.shape[0] % multiple), (0, 0)))


def unpack_rows(rows, shapes, width):
    pieces = []
    start = 0
    for shape in shapes:
        count = math.prod(shape) // width
        pieces.append(rows[start : start + count].reshape(shape))
        start += count
    return tuple(pieces)


def reduce_grads(head_part, norm_part, bc_part, tick_count):
    summed = lax.psum(
        tuple(member.astype(jnp.bfloat16) for member in head_part[:3] + (bc_part,)), "seq"
    )
    head_sum = tuple(member.astype(jnp.float32) for member in summed[:3]) + tuple(
        lax.psum(member.astype(jnp.bfloat16), "seq").astype(jnp.float32)
        for member in head_part[3:]
    )
    bc_rows = head_gather(summed[3], (0, 0, 1), 4 * tick_count + 1).astype(jnp.float32)
    norm_sum = lax.psum(norm_part, ("seq", "head"))
    return (head_sum, norm_sum, bc_rows.reshape(-1, bc_rows.shape[-1]))


def store_slot(buffer, value, slot_index, is_valid):
    current = lax.dynamic_index_in_dim(buffer, slot_index, 0, False)
    return lax.dynamic_update_index_in_dim(
        buffer, jnp.where(is_valid, value, current), slot_index, 0
    )


def on_device(
    inputs,
    cotangent,
    starts,
    live,
    norm_gain,
    w_gate,
    w_in,
    w_bc,
    w_dt,
    conv_x,
    conv_x_bias,
    conv_bc,
    conv_bc_bias,
    dt_bias,
    a_log,
    skip,
    gate_gain,
    w_out,
):
    section_count = lax.axis_size("section")
    section_index = lax.axis_index("section")
    micro_count = inputs.shape[0]
    tick_count = micro_count + section_count - 1
    w_main = jnp.concatenate([w_gate[0], w_in[0], w_bc[0], w_dt[0]], axis=1)
    w_low = jnp.concatenate([w_gate[0], w_in[0], w_dt[0]], axis=1)
    conv_weight = jnp.concatenate([conv_x[0], conv_bc[0]], axis=1).astype(jnp.float32)
    conv_bias = jnp.concatenate([conv_x_bias[0], conv_bc_bias[0]], axis=0)
    layer_weights = (
        norm_gain[0],
        w_main,
        w_low,
        w_bc[0],
        conv_weight,
        conv_bias,
        dt_bias[0],
        a_log[0],
        skip[0],
        gate_gain[0],
        w_out[0],
    )
    row_shape = inputs.shape[1:]
    outputs_all = jnp.zeros((micro_count,) + row_shape, jnp.float32)
    arrived = jnp.zeros(row_shape, jnp.float32)
    ticks = []
    for tick_index in range(tick_count):
        slot_index = tick_index - section_index
        is_valid = (slot_index >= 0) & (slot_index < micro_count)
        clipped = jnp.clip(slot_index, 0, micro_count - 1)
        fresh_rows = lax.dynamic_index_in_dim(inputs, clipped, 0, False).astype(jnp.float32)
        stream = jnp.where(section_index == 0, fresh_rows, arrived)
        start_marks = lax.dynamic_index_in_dim(starts, clipped, 0, False)
        alive_mask = lax.dynamic_index_in_dim(live, clipped, 0, False).astype(jnp.float32)
        result, saved = mixer_forward(
            stream,
            start_marks,
            alive_mask,
            layer_weights,
            (tick_index, -1, micro_count),
            (tick_index, tick_count + tick_index),
        )
        outputs_all = store_slot(outputs_all, result, clipped, is_valid)
        ticks.append((clipped, is_valid, saved))
        if tick_index + 1 < tick_count:
            arrived = shifted(result, "section", 1)
    back_arrived = jnp.zeros(row_shape, jnp.float32)
    input_grads = jnp.zeros((micro_count,) + row_shape, jnp.float32)
    head_count = lax.axis_size("head")
    bc_box = []
    head_total = ()
    shared_total = ()
    for tick_index in range(tick_count):
        clipped, is_valid, saved = ticks[tick_count - 1 - tick_index]
        outer_grad = lax.dynamic_index_in_dim(cotangent, clipped, 0, False).astype(jnp.float32)
        grad_next = jnp.where(section_index == section_count - 1, outer_grad, back_arrived)
        mask_value = is_valid.astype(jnp.float32)
        hook = None
        if tick_index + 1 == tick_count:

            def hook(bc_local, mask_value=mask_value, earlier=shared_total):
                totals = tuple(
                    (prev + member * mask_value) if earlier else member * mask_value
                    for prev, member in zip(earlier[1:] or bc_local, bc_local)
                )
                rows = pack_rows(totals, totals[0].shape[-1], 8 * head_count)
                part = head_scatter(
                    rows.reshape(head_count, -1, rows.shape[-1]), (0, 0, 1), 4 * tick_count
                )
                bc_box.append((part, [member.shape for member in totals]))
                return part[0, 0] * 0.0

        grad_stream, head_part, shared_part, out_part = mixer_backward(
            grad_next,
            layer_weights,
            saved,
            mask_value,
            (tick_count - 1 - tick_index, -1, micro_count),
            (2 * tick_count + tick_index, 3 * tick_count + tick_index),
            hook,
        )
        if tick_index == 0:
            out_total = out_part
        else:
            out_total = out_total + out_part
        if tick_index + 1 == tick_count:
            out_total = lax.psum(out_total.astype(jnp.bfloat16), "seq")
        head_part = tuple((member * mask_value for member in head_part))
        shared_part = tuple((member * mask_value for member in shared_part))
        if tick_index == 0:
            head_total = head_part
            shared_total = shared_part
        else:
            head_total = tuple((former + latter for former, latter in zip(head_total, head_part)))
            shared_total = tuple(
                (former + latter for former, latter in zip(shared_total, shared_part))
            )
        input_grads = store_slot(input_grads, grad_stream, clipped, is_valid)
        if tick_index + 1 < tick_count:
            back_arrived = shifted(grad_stream.astype(jnp.bfloat16), "section", -1).astype(
                grad_stream.dtype
            )
    anchor = out_total[0, 0].astype(jnp.float32) * 0.0
    head_total = (head_total[0] + anchor,) + head_total[1:]
    bc_part, bc_shapes = bc_box[0]
    head_total, norm_sum, bc_rows = reduce_grads(head_total, shared_total[0], bc_part, tick_count)
    shared_total = (norm_sum,) + unpack_rows(bc_rows, bc_shapes, bc_rows.shape[-1])
    head_total = head_total[:3] + (out_total.astype(jnp.float32),) + head_total[3:]
    return (
        outputs_all[None],
        input_grads[None],
        shared_total[0][None],
        head_total[0][None],
        head_total[1][None],
        shared_total[1][None],
        head_total[2][None],
        head_total[4][None],
        head_total[5][None],
        shared_total[2][None],
        shared_total[3][None],
        head_total[6][None],
        head_total[7][None],
        head_total[8][None],
        head_total[9][None],
        head_total[3][None],
    )


def solution(mesh):
    return jax.shard_map(
        on_device,
        mesh=mesh,
        in_specs=(
            P(None, ("seq", "head"), None),
            P(None, ("seq", "head"), None),
            P(None, "seq"),
            P(None, "seq"),
            P("section", None),
            P("section", None, "head"),
            P("section", None, "head"),
            P("section", None, None),
            P("section", None, "head"),
            P("section", None, "head"),
            P("section", "head"),
            P("section", None, None),
            P("section", None),
            P("section", "head"),
            P("section", "head"),
            P("section", "head"),
            P("section", "head"),
            P("section", "head", None),
        ),
        out_specs=(
            P("section", None, ("seq", "head"), None),
            P("section", None, ("seq", "head"), None),
            P("section", None),
            P("section", None, "head"),
            P("section", None, "head"),
            P("section", None, None),
            P("section", None, "head"),
            P("section", None, "head"),
            P("section", "head"),
            P("section", None, None),
            P("section", None),
            P("section", "head"),
            P("section", "head"),
            P("section", "head"),
            P("section", "head"),
            P("section", "head", None),
        ),
        check_vma=False,
    )
```

```python
from functools import partial

import functools
import math

import jax
import jax.numpy as jnp
from jax import lax
from jax.experimental import pallas as pl
from jax.experimental.pallas import tpu as pltpu
from jax.sharding import PartitionSpec as P

DI = 4096
P_SIZE = 64
N = 128
KW = 4
SCAN_BLOCK = 256


MESH = pl.DeviceIdType.MESH


def _tick_valid(offset, sign, count):
    slot = offset + sign * lax.axis_index("section")
    return jnp.logical_and(slot >= 0, slot < count)


def _enter(barrier, h, n):
    @pl.when(h > 0)
    def _():
        pl.semaphore_signal(barrier, 1, device_id={"head": h - 1}, device_id_type=MESH)

    @pl.when(h < n - 1)
    def _():
        pl.semaphore_signal(barrier, 1, device_id={"head": h + 1}, device_id_type=MESH)

    @pl.when(jnp.logical_and(h > 0, h < n - 1))
    def _():
        pl.semaphore_wait(barrier, 2)

    @pl.when(jnp.logical_or(h == 0, h == n - 1))
    def _():
        pl.semaphore_wait(barrier, 1)


def gather_body(n, tick, x_ref, o_ref, land, send_r, send_l, recv):
    h = lax.axis_index("head")
    valid = _tick_valid(*tick)

    @pl.when(valid)
    def _():
        _enter(pltpu.get_barrier_semaphore(), h, n)

        def copy_right(s, k):
            src = x_ref if s == 0 else land.at[k]
            return pltpu.make_async_remote_copy(
                src_ref=src, dst_ref=land.at[k], send_sem=send_r.at[s], recv_sem=recv.at[k],
                device_id={"head": h + 1}, device_id_type=MESH)

        def copy_left(s, k):
            src = x_ref if s == 0 else land.at[k]
            return pltpu.make_async_remote_copy(
                src_ref=src, dst_ref=land.at[k], send_sem=send_l.at[s], recv_sem=recv.at[k],
                device_id={"head": h - 1}, device_id_type=MESH)

        for s in range(n):
            k_r = h - s
            k_l = h + s
            if s >= 1:
                @pl.when(k_r >= 0)
                def _():
                    pltpu.make_async_remote_copy(
                        src_ref=land.at[k_r], dst_ref=land.at[k_r], send_sem=send_r.at[0],
                        recv_sem=recv.at[k_r], device_id={"head": h}, device_id_type=MESH
                    ).wait_recv()

                @pl.when(k_l <= n - 1)
                def _():
                    pltpu.make_async_remote_copy(
                        src_ref=land.at[k_l], dst_ref=land.at[k_l], send_sem=send_l.at[0],
                        recv_sem=recv.at[k_l], device_id={"head": h}, device_id_type=MESH
                    ).wait_recv()
            if s <= n - 2:
                @pl.when(jnp.logical_and(k_r >= 0, h < n - 1))
                def _():
                    copy_right(s, k_r).start()

                @pl.when(jnp.logical_and(k_l <= n - 1, h > 0))
                def _():
                    copy_left(s, k_l).start()
        land[h] = x_ref[...]
        for s in range(n - 1):
            k_r = h - s
            k_l = h + s

            @pl.when(jnp.logical_and(k_r >= 0, h < n - 1))
            def _():
                copy_right(s, k_r).wait_send()

            @pl.when(jnp.logical_and(k_l <= n - 1, h > 0))
            def _():
                copy_left(s, k_l).wait_send()
        o_ref[...] = land[...]

    @pl.when(jnp.logical_not(valid))
    def _():
        o_ref[...] = jnp.zeros(o_ref.shape, o_ref.dtype)


def head_gather(x, tick, cid):
    n = lax.axis_size("head")
    rows, cols = x.shape
    return pl.pallas_call(
        functools.partial(gather_body, n, tick),
        out_shape=jax.ShapeDtypeStruct((n, rows, cols), x.dtype),
        in_specs=[pl.BlockSpec(memory_space=pltpu.VMEM)],
        out_specs=pl.BlockSpec(memory_space=pltpu.VMEM),
        scratch_shapes=[
            pltpu.VMEM((n, rows, cols), x.dtype),
            pltpu.SemaphoreType.DMA((n,)),
            pltpu.SemaphoreType.DMA((n,)),
            pltpu.SemaphoreType.DMA((n,)),
        ],
        compiler_params=pltpu.CompilerParams(collective_id=cid, has_side_effects=True),
    )(x)


def scatter_body(n, tick, p_ref, o_ref, recv_l, recv_r, send_l, send_r, ssem_l, ssem_r, rsem_l, rsem_r):
    h = lax.axis_index("head")
    valid = _tick_valid(*tick)
    link = send_r.dtype

    @pl.when(valid)
    def _():
        _enter(pltpu.get_barrier_semaphore(), h, n)

        def to_right(k):
            return pltpu.make_async_remote_copy(
                src_ref=send_r.at[k], dst_ref=recv_l.at[k], send_sem=ssem_r.at[k],
                recv_sem=rsem_l.at[k], device_id={"head": h + 1}, device_id_type=MESH)

        def to_left(k):
            return pltpu.make_async_remote_copy(
                src_ref=send_l.at[k], dst_ref=recv_r.at[k], send_sem=ssem_l.at[k],
                recv_sem=rsem_r.at[k], device_id={"head": h - 1}, device_id_type=MESH)

        def rightward(s):
            k_r = n - 1 - s

            @pl.when(k_r > h)
            def _():
                @pl.when(h > 0)
                def _():
                    to_right(k_r).wait_recv()
                    send_r[k_r] = (p_ref[k_r] + recv_l[k_r].astype(jnp.float32)).astype(link)

                @pl.when(h == 0)
                def _():
                    send_r[k_r] = p_ref[k_r].astype(link)

                to_right(k_r).start()

        def leftward(s):
            k_l = s

            @pl.when(k_l < h)
            def _():
                @pl.when(h < n - 1)
                def _():
                    to_left(k_l).wait_recv()
                    send_l[k_l] = (p_ref[k_l] + recv_r[k_l].astype(jnp.float32)).astype(link)

                @pl.when(h == n - 1)
                def _():
                    send_l[k_l] = p_ref[k_l].astype(link)

                to_left(k_l).start()

        for s in range(n - 1):

            @pl.when(2 * h < n)
            def _():
                rightward(s)
                leftward(s)

            @pl.when(2 * h >= n)
            def _():
                leftward(s)
                rightward(s)

        total = p_ref[h]

        @pl.when(h > 0)
        def _():
            to_right(h).wait_recv()

        @pl.when(h < n - 1)
        def _():
            to_left(h).wait_recv()

        left_part = jnp.where(h > 0, recv_l[h].astype(jnp.float32), 0.0)
        right_part = jnp.where(h < n - 1, recv_r[h].astype(jnp.float32), 0.0)
        o_ref[...] = (total + left_part + right_part).astype(o_ref.dtype)
        for s in range(n - 1):
            k_r = n - 1 - s
            k_l = s

            @pl.when(k_r > h)
            def _():
                to_right(k_r).wait_send()

            @pl.when(k_l < h)
            def _():
                to_left(k_l).wait_send()

    @pl.when(jnp.logical_not(valid))
    def _():
        o_ref[...] = jnp.zeros(o_ref.shape, o_ref.dtype)


def head_scatter(parts, tick, cid, link=jnp.bfloat16):
    n = lax.axis_size("head")
    _, rows, cols = parts.shape
    return pl.pallas_call(
        functools.partial(scatter_body, n, tick),
        out_shape=jax.ShapeDtypeStruct((rows, cols), jnp.float32),
        in_specs=[pl.BlockSpec(memory_space=pltpu.VMEM)],
        out_specs=pl.BlockSpec(memory_space=pltpu.VMEM),
        scratch_shapes=[
            pltpu.VMEM((n, rows, cols), link),
            pltpu.VMEM((n, rows, cols), link),
            pltpu.VMEM((n, rows, cols), link),
            pltpu.VMEM((n, rows, cols), link),
            pltpu.SemaphoreType.DMA((n,)),
            pltpu.SemaphoreType.DMA((n,)),
            pltpu.SemaphoreType.DMA((n,)),
            pltpu.SemaphoreType.DMA((n,)),
        ],
        compiler_params=pltpu.CompilerParams(collective_id=cid, has_side_effects=True),
    )(parts)


norm_eps = 1e-05
far_below = -1e30
highest = lax.Precision.HIGH


def shifted(value, axis, by):
    count = lax.axis_size(axis)
    pairs = [(i, i + by) for i in range(count) if 0 <= i + by < count]
    return lax.ppermute(value, axis, pairs)


def entering(value, axis, combine, identity):
    count, mine = (lax.axis_size(axis), lax.axis_index(axis))
    everything = jax.tree.map(lambda part: lax.all_gather(part, axis), value)
    before = jax.tree.map(
        lambda part, zero: jnp.broadcast_to(jnp.asarray(zero, part.dtype), part.shape),
        value,
        identity,
    )
    for k in range(count - 1):
        reached = k < mine
        new = combine(before, jax.tree.map(lambda part: part[k], everything))
        before = jax.tree.map(lambda a, b: jnp.where(reached, a, b), new, before)
    return before


def entering_2(value, axis, join, neutral):
    count = lax.axis_size(axis)
    place = lax.axis_index(axis)
    ahead = count - 1 - place
    gathered = jax.tree.map(
        lambda a, kind: lax.all_gather(a.astype(kind), axis),
        value,
        jax.tree.map(lambda a: jnp.bfloat16 if a.dtype == jnp.float32 else a.dtype, value),
    )
    state = jax.tree.map(lambda a, e: jnp.zeros_like(a) + jnp.asarray(e, a.dtype), value, neutral)
    for lap in range(count - 1):
        source = count - 1 - lap
        new = join(
            state,
            jax.tree.map(lambda a, own: a[source].astype(own.dtype), gathered, value),
        )
        active = lap < ahead
        state = jax.tree.map(lambda a, b: jnp.where(active, a, b), new, state)
    return state


def rms_scale(values):
    return lax.rsqrt(jnp.mean(values * values, axis=-1, keepdims=True) + norm_eps)


def silu_slope(values):
    logistic = jax.nn.sigmoid(values)
    return logistic * (1.0 + values * (1.0 - logistic))


def causal_conv(extended, marks_ext, weight, conv_bias):
    tap_count = weight.shape[0]
    length = extended.shape[0] - tap_count + 1
    counts = jnp.cumsum(marks_ext)
    conv_sum = jnp.zeros((length, extended.shape[1]), jnp.float32) + conv_bias
    for tap_index in range(tap_count):
        linked = (counts[tap_count - 1 :] == counts[tap_index : tap_index + length]).astype(
            jnp.float32
        )
        conv_sum = (
            conv_sum
            + linked[:, None] * weight[tap_index] * extended[tap_index : tap_index + length]
        )
    return conv_sum


def prepare(extended, dt_pre, marks_ext, alive_mask, conv_weight, conv_bias, dt_bias, a_log):
    inner_width = dt_pre.shape[1] * P_SIZE
    activated = jax.nn.silu(causal_conv(extended, marks_ext, conv_weight, conv_bias))
    inner_act = activated[:, :inner_width] * alive_mask[:, None]
    b_mat = activated[:, inner_width : inner_width + N]
    c_mat = activated[:, inner_width + N :]
    step_size = jax.nn.softplus(dt_pre + dt_bias) * alive_mask[:, None]
    log_decay = -step_size * jnp.exp(a_log)
    return (inner_act, step_size, log_decay, b_mat, c_mat)


def block_terms(inner_act, step_size, log_decay, b_mat, start_marks):
    blocks = inner_act.shape[0] // SCAN_BLOCK
    head_count = step_size.shape[1]
    x_blocks = inner_act.reshape(blocks, SCAN_BLOCK, head_count, P_SIZE)
    dt_blocks = step_size.reshape(blocks, SCAN_BLOCK, head_count)
    cum_decay = jnp.cumsum(log_decay.reshape(blocks, SCAN_BLOCK, head_count), axis=1)
    mark_count = jnp.cumsum(start_marks.reshape(blocks, SCAN_BLOCK), axis=1)
    b_blocks = b_mat.reshape(blocks, SCAN_BLOCK, N)
    last_cum = cum_decay[:, -1]
    last_mark = mark_count[:, -1]
    same_end = (mark_count == last_mark[:, None]).astype(jnp.float32)
    end_weight = jnp.exp(last_cum[:, None, :] - cum_decay) * same_end[:, :, None] * dt_blocks
    block_states = jnp.einsum(
        "cjh,cjhp,cjn->chpn", end_weight, x_blocks, b_blocks, precision=highest
    )
    block_decay = jnp.exp(last_cum) * (last_mark == 0).astype(jnp.float32)[:, None]
    return (block_decay, block_states, cum_decay, mark_count, x_blocks, dt_blocks)


def compose_blocks(block_decay, block_states, start_state):
    chain_state = start_state
    incoming = []
    for block_index in range(block_decay.shape[0]):
        incoming.append(chain_state)
        chain_state = (
            block_decay[block_index][:, None, None] * chain_state + block_states[block_index]
        )
    return (chain_state, jnp.stack(incoming))


def block_output(block_parts, b_mat, c_mat, skip, incoming):
    block_decay, block_states, cum_decay, mark_count, x_blocks, dt_blocks = block_parts
    blocks = cum_decay.shape[0]
    head_count = cum_decay.shape[2]
    b_blocks = b_mat.reshape(blocks, SCAN_BLOCK, N)
    c_blocks = c_mat.reshape(blocks, SCAN_BLOCK, N)
    inner_prod = jnp.einsum("cin,cjn->cij", c_blocks, b_blocks, precision=highest)
    arange_pos = jnp.arange(SCAN_BLOCK)
    linked = (arange_pos[:, None] >= arange_pos[None, :])[None] & (
        mark_count[:, :, None] == mark_count[:, None, :]
    )
    spread = jnp.where(
        linked[..., None], cum_decay[:, :, None, :] - cum_decay[:, None, :, :], far_below
    )
    weights = jnp.exp(spread) * inner_prod[..., None] * dt_blocks[:, None, :, :]
    y_intra = jnp.einsum("cijh,cjhp->cihp", weights, x_blocks, precision=highest)
    carry_in = jnp.exp(cum_decay) * (mark_count == 0).astype(jnp.float32)[:, :, None]
    y_inter = (
        jnp.einsum("cin,chpn->cihp", c_blocks, incoming, precision=highest) * carry_in[..., None]
    )
    mixed_out = y_intra + y_inter + skip[None, None, :, None] * x_blocks
    return mixed_out.reshape(blocks * SCAN_BLOCK, head_count * P_SIZE)


def local_front(marks_ext, alive_mask, extended, dt_pre, conv_weight, conv_bias, dt_bias, a_log):
    inner_act, step_size, log_decay, b_mat, c_mat = prepare(
        extended, dt_pre, marks_ext, alive_mask, conv_weight, conv_bias, dt_bias, a_log
    )
    block_parts = block_terms(inner_act, step_size, log_decay, b_mat, marks_ext[KW - 1 :])
    zero_state = jnp.zeros(block_parts[1].shape[1:], jnp.float32)
    total_state, _ = compose_blocks(block_parts[0], block_parts[1], zero_state)
    total_decay = jnp.prod(block_parts[0], axis=0)
    return (block_parts, b_mat, c_mat, total_decay, total_state)


def local_rear(block_parts, b_mat, c_mat, skip, start_state):
    _, incoming = compose_blocks(block_parts[0], block_parts[1], start_state)
    return block_output(block_parts, b_mat, c_mat, skip, incoming)


def local_pass(
    marks_ext,
    alive_mask,
    extended,
    dt_pre,
    conv_weight,
    conv_bias,
    dt_bias,
    a_log,
    skip,
    start_state,
):
    block_parts, b_mat, c_mat, total_decay, total_state = local_front(
        marks_ext, alive_mask, extended, dt_pre, conv_weight, conv_bias, dt_bias, a_log
    )
    return (local_rear(block_parts, b_mat, c_mat, skip, start_state), total_decay, total_state)


def chain_combine(earlier, later):
    return (earlier[0] * later[0], later[0][:, None, None] * earlier[1] + later[1])


def extend(pre_conv, start_marks, edge_rows, edge_marks):
    extended = jnp.concatenate([edge_rows, pre_conv], axis=0)
    marks_ext = jnp.concatenate([edge_marks.astype(jnp.int32), start_marks], axis=0)
    return (extended, marks_ext)


def mixer_forward(stream, start_marks, alive_mask, layer_weights, tick, ids):
    (
        norm_gain,
        w_main,
        w_low,
        w_bc,
        conv_weight,
        conv_bias,
        dt_bias,
        a_log,
        skip,
        gate_gain,
        w_out,
    ) = layer_weights
    inner_width = w_out.shape[0]
    normed = (stream * rms_scale(stream) * norm_gain).astype(jnp.bfloat16)
    gathered = head_gather(normed, tick, ids[0])
    gathered = gathered.reshape(-1, gathered.shape[-1])
    projected = jnp.dot(gathered, w_main, preferred_element_type=jnp.float32)
    gate_pre = projected[:, :inner_width]
    pre_conv = projected[:, inner_width : 2 * inner_width + 2 * N]
    dt_pre = projected[:, 2 * inner_width + 2 * N :]
    marks_float = start_marks.astype(jnp.float32)
    tail_from = pre_conv.shape[0] - KW + 1
    edge_parts = shifted((pre_conv[tail_from:], marks_float[tail_from:]), "seq", 1)
    extended, marks_ext = extend(pre_conv, start_marks, edge_parts[0], edge_parts[1])
    front_fn = partial(local_front, marks_ext, alive_mask)
    front_out, front_pull = jax.vjp(
        front_fn, extended, dt_pre, conv_weight, conv_bias, dt_bias, a_log
    )
    block_parts, b_mat, c_mat, total_decay, total_state = front_out
    neutral = (jnp.ones_like(total_decay), jnp.zeros_like(total_state))
    prefix = entering((total_decay, total_state), "seq", chain_combine, neutral)
    start_state = prefix[1]
    mixed_out, rear_pull = jax.vjp(local_rear, block_parts, b_mat, c_mat, skip, start_state)
    silu_gate = jax.nn.silu(gate_pre)
    gated_mix = mixed_out * silu_gate
    square_total = lax.psum(jnp.sum(gated_mix * gated_mix, axis=-1), "head")
    scale_out = lax.rsqrt(square_total / DI + norm_eps)
    normed_out = (gated_mix * scale_out[:, None] * gate_gain).astype(jnp.bfloat16)
    head_count = lax.axis_size("head")
    branch = head_scatter(
        jnp.dot(normed_out, w_out, preferred_element_type=jnp.float32).reshape(
            head_count, -1, w_out.shape[1]
        ),
        tick,
        ids[1],
    )
    saved = (
        stream,
        gathered,
        gate_pre,
        mixed_out,
        silu_gate,
        gated_mix,
        scale_out,
        normed_out,
        total_decay,
        start_state,
        front_pull,
        rear_pull,
    )
    return stream + branch, saved


def mixer_backward(grad_next, layer_weights, saved, mask_value, tick, ids, hook=None):
    (
        norm_gain,
        w_main,
        w_low,
        w_bc,
        conv_weight,
        conv_bias,
        dt_bias,
        a_log,
        skip,
        gate_gain,
        w_out,
    ) = layer_weights
    (
        stream,
        gathered,
        gate_pre,
        mixed_out,
        silu_gate,
        gated_mix,
        scale_out,
        normed_out,
        total_decay,
        start_state,
        front_pull,
        rear_pull,
    ) = saved
    inner_width = w_out.shape[0]
    grad_branch = grad_next.astype(jnp.bfloat16)
    shard_rows = head_gather(grad_branch, tick, ids[0])
    shard_rows = shard_rows.reshape(-1, shard_rows.shape[-1])
    g_w_out = lax.dot_general(
        normed_out, shard_rows, (((0,), (0,)), ((), ())), preferred_element_type=jnp.float32
    ) * mask_value
    grad_normed = lax.dot_general(
        shard_rows, w_out, (((1,), (1,)), ((), ())), preferred_element_type=jnp.float32
    )
    weighted = grad_normed * gate_gain
    g_gate_gain = jnp.sum(grad_normed * gated_mix * scale_out[:, None], axis=0)
    cross_sum = lax.psum(jnp.sum(weighted * gated_mix, axis=-1), "head")
    grad_gated = (
        scale_out[:, None] * weighted - gated_mix * (scale_out**3 * cross_sum / DI)[:, None]
    )
    grad_mixed = grad_gated * silu_gate
    grad_gate = (grad_gated * mixed_out * silu_slope(gate_pre)).astype(jnp.bfloat16)
    g_parts, g_b_mat, g_c_mat, g_skip, g_start = rear_pull(grad_mixed)
    neutral = (jnp.ones_like(total_decay), jnp.zeros_like(g_start))
    suffix = entering_2((total_decay, g_start), "seq", chain_combine, neutral)
    after_state = suffix[1]
    grad_decay = jnp.sum(after_state * start_state, axis=(1, 2))
    grad_ext, grad_dt_pre, g_conv_w, g_conv_b, g_dt_bias, g_a_log = front_pull(
        (g_parts, g_b_mat, g_c_mat, grad_decay, after_state)
    )
    returned = shifted(grad_ext[: KW - 1], "seq", -1)
    grad_pre = grad_ext[KW - 1 :]
    tail_from = grad_pre.shape[0] - KW + 1
    grad_pre = jnp.concatenate([grad_pre[:tail_from], grad_pre[tail_from:] + returned], axis=0)
    grad_inner = grad_pre[:, :inner_width].astype(jnp.bfloat16)
    grad_bc = grad_pre[:, inner_width:]
    grad_low = jnp.concatenate([grad_gate, grad_inner, grad_dt_pre.astype(jnp.bfloat16)], axis=1)
    w_bc_float = w_bc.astype(jnp.float32)
    g_low = lax.dot_general(
        gathered, grad_low, (((0,), (0,)), ((), ())), preferred_element_type=jnp.float32
    )
    g_w_bc = lax.dot_general(
        gathered.astype(jnp.float32),
        grad_bc,
        (((0,), (0,)), ((), ())),
        precision=highest,
        preferred_element_type=jnp.float32,
    )
    main_term = lax.dot_general(
        grad_low, w_low, (((1,), (1,)), ((), ())), preferred_element_type=jnp.float32
    )
    side_term = lax.dot_general(
        grad_bc,
        w_bc_float,
        (((1,), (1,)), ((), ())),
        precision=highest,
        preferred_element_type=jnp.float32,
    )
    head_count = lax.axis_size("head")
    lead = 0.0
    if hook is not None:
        lead = hook((g_w_bc, g_conv_w[:, inner_width:], g_conv_b[inner_width:]))
    grad_normed_in = head_scatter(
        (main_term + side_term + lead).reshape(head_count, -1, main_term.shape[1]), tick, ids[1]
    )
    scale_in = rms_scale(stream)
    g_norm_gain = jnp.sum(grad_normed_in * stream * scale_in, axis=0)
    weighted_in = grad_normed_in * norm_gain
    grad_stream = (
        grad_next
        + scale_in * weighted_in
        - stream * scale_in**3 * jnp.mean(weighted_in * stream, axis=-1, keepdims=True)
    )
    head_part = (
        g_low[:, :inner_width],
        g_low[:, inner_width : 2 * inner_width],
        g_low[:, 2 * inner_width :],
        g_conv_w[:, :inner_width],
        g_conv_b[:inner_width],
        g_dt_bias,
        g_a_log,
        g_skip,
        g_gate_gain,
    )
    shared_part = (g_norm_gain, g_w_bc, g_conv_w[:, inner_width:], g_conv_b[inner_width:])
    return (grad_stream, head_part, shared_part, g_w_out)


def pack_rows(members, width, multiple):
    rows = jnp.concatenate([member.reshape(-1, width) for member in members], axis=0)
    return jnp.pad(rows, ((0, -rows.shape[0] % multiple), (0, 0)))


def unpack_rows(rows, shapes, width):
    pieces = []
    start = 0
    for shape in shapes:
        count = math.prod(shape) // width
        pieces.append(rows[start : start + count].reshape(shape))
        start += count
    return tuple(pieces)


def reduce_grads(head_part, norm_part, bc_part, tick_count):
    bc_all = lax.all_gather(bc_part.astype(jnp.bfloat16), "seq")
    bc_sum = bc_all[0].astype(jnp.float32)
    for index in range(1, bc_all.shape[0]):
        bc_sum = bc_sum + bc_all[index].astype(jnp.float32)
    anchor = bc_all[0, 0, 0].astype(jnp.float32) * 0.0
    summed = lax.psum(
        tuple(member.astype(jnp.bfloat16) for member in (head_part[0] + anchor,) + head_part[1:3]),
        "seq",
    )
    head_sum = tuple(member.astype(jnp.float32) for member in summed) + tuple(
        lax.psum(member.astype(jnp.bfloat16), "seq").astype(jnp.float32)
        for member in head_part[3:]
    )
    bc_rows = head_gather(bc_sum, (0, 0, 1), 4 * tick_count + 1)
    norm_sum = lax.psum(norm_part, ("seq", "head"))
    return (head_sum, norm_sum, bc_rows.reshape(-1, bc_rows.shape[-1]))


def store_slot(buffer, value, slot_index, is_valid):
    current = lax.dynamic_index_in_dim(buffer, slot_index, 0, False)
    return lax.dynamic_update_index_in_dim(
        buffer, jnp.where(is_valid, value, current), slot_index, 0
    )


def on_device(
    inputs,
    cotangent,
    starts,
    live,
    norm_gain,
    w_gate,
    w_in,
    w_bc,
    w_dt,
    conv_x,
    conv_x_bias,
    conv_bc,
    conv_bc_bias,
    dt_bias,
    a_log,
    skip,
    gate_gain,
    w_out,
):
    section_count = lax.axis_size("section")
    section_index = lax.axis_index("section")
    micro_count = inputs.shape[0]
    tick_count = micro_count + section_count - 1
    w_main = jnp.concatenate([w_gate[0], w_in[0], w_bc[0], w_dt[0]], axis=1)
    w_low = jnp.concatenate([w_gate[0], w_in[0], w_dt[0]], axis=1)
    conv_weight = jnp.concatenate([conv_x[0], conv_bc[0]], axis=1).astype(jnp.float32)
    conv_bias = jnp.concatenate([conv_x_bias[0], conv_bc_bias[0]], axis=0)
    layer_weights = (
        norm_gain[0],
        w_main,
        w_low,
        w_bc[0],
        conv_weight,
        conv_bias,
        dt_bias[0],
        a_log[0],
        skip[0],
        gate_gain[0],
        w_out[0],
    )
    row_shape = inputs.shape[1:]
    outputs_all = jnp.zeros((micro_count,) + row_shape, jnp.float32)
    arrived = jnp.zeros(row_shape, jnp.float32)
    ticks = []
    for tick_index in range(tick_count):
        slot_index = tick_index - section_index
        is_valid = (slot_index >= 0) & (slot_index < micro_count)
        clipped = jnp.clip(slot_index, 0, micro_count - 1)
        fresh_rows = lax.dynamic_index_in_dim(inputs, clipped, 0, False).astype(jnp.float32)
        stream = jnp.where(section_index == 0, fresh_rows, arrived)
        start_marks = lax.dynamic_index_in_dim(starts, clipped, 0, False)
        alive_mask = lax.dynamic_index_in_dim(live, clipped, 0, False).astype(jnp.float32)
        result, saved = mixer_forward(
            stream,
            start_marks,
            alive_mask,
            layer_weights,
            (tick_index, -1, micro_count),
            (tick_index, tick_count + tick_index),
        )
        outputs_all = store_slot(outputs_all, result, clipped, is_valid)
        ticks.append((clipped, is_valid, saved))
        if tick_index + 1 < tick_count:
            arrived = shifted(result, "section", 1)
    back_arrived = jnp.zeros(row_shape, jnp.float32)
    input_grads = jnp.zeros((micro_count,) + row_shape, jnp.float32)
    head_count = lax.axis_size("head")
    bc_box = []
    head_total = ()
    shared_total = ()
    for tick_index in range(tick_count):
        clipped, is_valid, saved = ticks[tick_count - 1 - tick_index]
        outer_grad = lax.dynamic_index_in_dim(cotangent, clipped, 0, False).astype(jnp.float32)
        grad_next = jnp.where(section_index == section_count - 1, outer_grad, back_arrived)
        mask_value = is_valid.astype(jnp.float32)
        hook = None
        if tick_index + 1 == tick_count:

            def hook(bc_local, mask_value=mask_value, earlier=shared_total):
                totals = tuple(
                    (prev + member * mask_value) if earlier else member * mask_value
                    for prev, member in zip(earlier[1:] or bc_local, bc_local)
                )
                rows = pack_rows(totals, totals[0].shape[-1], 8 * head_count)
                part = head_scatter(
                    rows.reshape(head_count, -1, rows.shape[-1]), (0, 0, 1), 4 * tick_count
                )
                bc_box.append((part, [member.shape for member in totals]))
                return part[0, 0] * 0.0

        grad_stream, head_part, shared_part, out_part = mixer_backward(
            grad_next,
            layer_weights,
            saved,
            mask_value,
            (tick_count - 1 - tick_index, -1, micro_count),
            (2 * tick_count + tick_index, 3 * tick_count + tick_index),
            hook,
        )
        if tick_index == 0:
            out_total = out_part
        else:
            out_total = out_total + out_part
        if tick_index + 1 == tick_count:
            out_total = lax.psum(out_total.astype(jnp.bfloat16), "seq")
        head_part = tuple((member * mask_value for member in head_part))
        shared_part = tuple((member * mask_value for member in shared_part))
        if tick_index == 0:
            head_total = head_part
            shared_total = shared_part
        else:
            head_total = tuple((former + latter for former, latter in zip(head_total, head_part)))
            shared_total = tuple(
                (former + latter for former, latter in zip(shared_total, shared_part))
            )
        input_grads = store_slot(input_grads, grad_stream, clipped, is_valid)
        if tick_index + 1 < tick_count:
            back_arrived = shifted(grad_stream.astype(jnp.bfloat16), "section", -1).astype(
                grad_stream.dtype
            )
    anchor = out_total[0, 0].astype(jnp.float32) * 0.0
    head_total = (head_total[0] + anchor,) + head_total[1:]
    bc_part, bc_shapes = bc_box[0]
    head_total, norm_sum, bc_rows = reduce_grads(head_total, shared_total[0], bc_part, tick_count)
    shared_total = (norm_sum,) + unpack_rows(bc_rows, bc_shapes, bc_rows.shape[-1])
    head_total = head_total[:3] + (out_total.astype(jnp.float32),) + head_total[3:]
    return (
        outputs_all[None],
        input_grads[None],
        shared_total[0][None],
        head_total[0][None],
        head_total[1][None],
        shared_total[1][None],
        head_total[2][None],
        head_total[4][None],
        head_total[5][None],
        shared_total[2][None],
        shared_total[3][None],
        head_total[6][None],
        head_total[7][None],
        head_total[8][None],
        head_total[9][None],
        head_total[3][None],
    )


def solution(mesh):
    return jax.shard_map(
        on_device,
        mesh=mesh,
        in_specs=(
            P(None, ("seq", "head"), None),
            P(None, ("seq", "head"), None),
            P(None, "seq"),
            P(None, "seq"),
            P("section", None),
            P("section", None, "head"),
            P("section", None, "head"),
            P("section", None, None),
            P("section", None, "head"),
            P("section", None, "head"),
            P("section", "head"),
            P("section", None, None),
            P("section", None),
            P("section", "head"),
            P("section", "head"),
            P("section", "head"),
            P("section", "head"),
            P("section", "head", None),
        ),
        out_specs=(
            P("section", None, ("seq", "head"), None),
            P("section", None, ("seq", "head"), None),
            P("section", None),
            P("section", None, "head"),
            P("section", None, "head"),
            P("section", None, None),
            P("section", None, "head"),
            P("section", None, "head"),
            P("section", "head"),
            P("section", None, None),
            P("section", None),
            P("section", "head"),
            P("section", "head"),
            P("section", "head"),
            P("section", "head"),
            P("section", "head", None),
        ),
        check_vma=False,
    )
```

```python
from functools import partial

import functools
import math

import jax
import jax.numpy as jnp
from jax import lax
from jax.experimental import pallas as pl
from jax.experimental.pallas import tpu as pltpu
from jax.sharding import PartitionSpec as P

DI = 4096
P_SIZE = 64
N = 128
KW = 4
SCAN_BLOCK = 256


MESH = pl.DeviceIdType.MESH


def _tick_valid(offset, sign, count):
    slot = offset + sign * lax.axis_index("section")
    return jnp.logical_and(slot >= 0, slot < count)


def _enter(barrier, h, n):
    @pl.when(h > 0)
    def _():
        pl.semaphore_signal(barrier, 1, device_id={"head": h - 1}, device_id_type=MESH)

    @pl.when(h < n - 1)
    def _():
        pl.semaphore_signal(barrier, 1, device_id={"head": h + 1}, device_id_type=MESH)

    @pl.when(jnp.logical_and(h > 0, h < n - 1))
    def _():
        pl.semaphore_wait(barrier, 2)

    @pl.when(jnp.logical_or(h == 0, h == n - 1))
    def _():
        pl.semaphore_wait(barrier, 1)


def gather_body(n, tick, x_ref, o_ref, land, send_r, send_l, recv):
    h = lax.axis_index("head")
    valid = _tick_valid(*tick)

    @pl.when(valid)
    def _():
        _enter(pltpu.get_barrier_semaphore(), h, n)

        def copy_right(s, k):
            src = x_ref if s == 0 else land.at[k]
            return pltpu.make_async_remote_copy(
                src_ref=src, dst_ref=land.at[k], send_sem=send_r.at[s], recv_sem=recv.at[k],
                device_id={"head": h + 1}, device_id_type=MESH)

        def copy_left(s, k):
            src = x_ref if s == 0 else land.at[k]
            return pltpu.make_async_remote_copy(
                src_ref=src, dst_ref=land.at[k], send_sem=send_l.at[s], recv_sem=recv.at[k],
                device_id={"head": h - 1}, device_id_type=MESH)

        for s in range(n):
            k_r = h - s
            k_l = h + s
            if s >= 1:
                @pl.when(k_r >= 0)
                def _():
                    pltpu.make_async_remote_copy(
                        src_ref=land.at[k_r], dst_ref=land.at[k_r], send_sem=send_r.at[0],
                        recv_sem=recv.at[k_r], device_id={"head": h}, device_id_type=MESH
                    ).wait_recv()

                @pl.when(k_l <= n - 1)
                def _():
                    pltpu.make_async_remote_copy(
                        src_ref=land.at[k_l], dst_ref=land.at[k_l], send_sem=send_l.at[0],
                        recv_sem=recv.at[k_l], device_id={"head": h}, device_id_type=MESH
                    ).wait_recv()
            if s <= n - 2:
                @pl.when(jnp.logical_and(k_r >= 0, h < n - 1))
                def _():
                    copy_right(s, k_r).start()

                @pl.when(jnp.logical_and(k_l <= n - 1, h > 0))
                def _():
                    copy_left(s, k_l).start()
        land[h] = x_ref[...]
        for s in range(n - 1):
            k_r = h - s
            k_l = h + s

            @pl.when(jnp.logical_and(k_r >= 0, h < n - 1))
            def _():
                copy_right(s, k_r).wait_send()

            @pl.when(jnp.logical_and(k_l <= n - 1, h > 0))
            def _():
                copy_left(s, k_l).wait_send()
        o_ref[...] = land[...]

    @pl.when(jnp.logical_not(valid))
    def _():
        o_ref[...] = jnp.zeros(o_ref.shape, o_ref.dtype)


def head_gather(x, tick, cid):
    n = lax.axis_size("head")
    rows, cols = x.shape
    return pl.pallas_call(
        functools.partial(gather_body, n, tick),
        out_shape=jax.ShapeDtypeStruct((n, rows, cols), x.dtype),
        in_specs=[pl.BlockSpec(memory_space=pltpu.VMEM)],
        out_specs=pl.BlockSpec(memory_space=pltpu.VMEM),
        scratch_shapes=[
            pltpu.VMEM((n, rows, cols), x.dtype),
            pltpu.SemaphoreType.DMA((n,)),
            pltpu.SemaphoreType.DMA((n,)),
            pltpu.SemaphoreType.DMA((n,)),
        ],
        compiler_params=pltpu.CompilerParams(collective_id=cid, has_side_effects=True),
    )(x)


def scatter_body(n, tick, p_ref, o_ref, recv_l, recv_r, send_l, send_r, ssem_l, ssem_r, rsem_l, rsem_r):
    h = lax.axis_index("head")
    valid = _tick_valid(*tick)
    link = send_r.dtype

    @pl.when(valid)
    def _():
        _enter(pltpu.get_barrier_semaphore(), h, n)

        def to_right(k):
            return pltpu.make_async_remote_copy(
                src_ref=send_r.at[k], dst_ref=recv_l.at[k], send_sem=ssem_r.at[k],
                recv_sem=rsem_l.at[k], device_id={"head": h + 1}, device_id_type=MESH)

        def to_left(k):
            return pltpu.make_async_remote_copy(
                src_ref=send_l.at[k], dst_ref=recv_r.at[k], send_sem=ssem_l.at[k],
                recv_sem=rsem_r.at[k], device_id={"head": h - 1}, device_id_type=MESH)

        def rightward(s):
            k_r = n - 1 - s

            @pl.when(k_r > h)
            def _():
                @pl.when(h > 0)
                def _():
                    to_right(k_r).wait_recv()
                    send_r[k_r] = (p_ref[k_r] + recv_l[k_r].astype(jnp.float32)).astype(link)

                @pl.when(h == 0)
                def _():
                    send_r[k_r] = p_ref[k_r].astype(link)

                to_right(k_r).start()

        def leftward(s):
            k_l = s

            @pl.when(k_l < h)
            def _():
                @pl.when(h < n - 1)
                def _():
                    to_left(k_l).wait_recv()
                    send_l[k_l] = (p_ref[k_l] + recv_r[k_l].astype(jnp.float32)).astype(link)

                @pl.when(h == n - 1)
                def _():
                    send_l[k_l] = p_ref[k_l].astype(link)

                to_left(k_l).start()

        for s in range(n - 1):

            @pl.when(2 * h < n)
            def _():
                rightward(s)
                leftward(s)

            @pl.when(2 * h >= n)
            def _():
                leftward(s)
                rightward(s)

        total = p_ref[h]

        @pl.when(h > 0)
        def _():
            to_right(h).wait_recv()

        @pl.when(h < n - 1)
        def _():
            to_left(h).wait_recv()

        left_part = jnp.where(h > 0, recv_l[h].astype(jnp.float32), 0.0)
        right_part = jnp.where(h < n - 1, recv_r[h].astype(jnp.float32), 0.0)
        o_ref[...] = (total + left_part + right_part).astype(o_ref.dtype)
        for s in range(n - 1):
            k_r = n - 1 - s
            k_l = s

            @pl.when(k_r > h)
            def _():
                to_right(k_r).wait_send()

            @pl.when(k_l < h)
            def _():
                to_left(k_l).wait_send()

    @pl.when(jnp.logical_not(valid))
    def _():
        o_ref[...] = jnp.zeros(o_ref.shape, o_ref.dtype)


def head_scatter(parts, tick, cid, link=jnp.bfloat16):
    n = lax.axis_size("head")
    _, rows, cols = parts.shape
    return pl.pallas_call(
        functools.partial(scatter_body, n, tick),
        out_shape=jax.ShapeDtypeStruct((rows, cols), jnp.float32),
        in_specs=[pl.BlockSpec(memory_space=pltpu.VMEM)],
        out_specs=pl.BlockSpec(memory_space=pltpu.VMEM),
        scratch_shapes=[
            pltpu.VMEM((n, rows, cols), link),
            pltpu.VMEM((n, rows, cols), link),
            pltpu.VMEM((n, rows, cols), link),
            pltpu.VMEM((n, rows, cols), link),
            pltpu.SemaphoreType.DMA((n,)),
            pltpu.SemaphoreType.DMA((n,)),
            pltpu.SemaphoreType.DMA((n,)),
            pltpu.SemaphoreType.DMA((n,)),
        ],
        compiler_params=pltpu.CompilerParams(collective_id=cid, has_side_effects=True),
    )(parts)


norm_eps = 1e-05
far_below = -1e30
highest = lax.Precision.HIGH


def shifted(value, axis, by):
    count = lax.axis_size(axis)
    pairs = [(i, i + by) for i in range(count) if 0 <= i + by < count]
    return lax.ppermute(value, axis, pairs)


def entering(value, axis, combine, identity):
    count, mine = (lax.axis_size(axis), lax.axis_index(axis))
    everything = jax.tree.map(lambda part: lax.all_gather(part, axis), value)
    before = jax.tree.map(
        lambda part, zero: jnp.broadcast_to(jnp.asarray(zero, part.dtype), part.shape),
        value,
        identity,
    )
    for k in range(count - 1):
        reached = k < mine
        new = combine(before, jax.tree.map(lambda part: part[k], everything))
        before = jax.tree.map(lambda a, b: jnp.where(reached, a, b), new, before)
    return before


def entering_2(value, axis, join, neutral):
    count = lax.axis_size(axis)
    place = lax.axis_index(axis)
    ahead = count - 1 - place
    gathered = jax.tree.map(
        lambda a, kind: lax.all_gather(a.astype(kind), axis),
        value,
        jax.tree.map(lambda a: jnp.bfloat16 if a.dtype == jnp.float32 else a.dtype, value),
    )
    state = jax.tree.map(lambda a, e: jnp.zeros_like(a) + jnp.asarray(e, a.dtype), value, neutral)
    for lap in range(count - 1):
        source = count - 1 - lap
        new = join(
            state,
            jax.tree.map(lambda a, own: a[source].astype(own.dtype), gathered, value),
        )
        active = lap < ahead
        state = jax.tree.map(lambda a, b: jnp.where(active, a, b), new, state)
    return state


def rms_scale(values):
    return lax.rsqrt(jnp.mean(values * values, axis=-1, keepdims=True) + norm_eps)


def silu_slope(values):
    logistic = jax.nn.sigmoid(values)
    return logistic * (1.0 + values * (1.0 - logistic))


def causal_conv(extended, marks_ext, weight, conv_bias):
    tap_count = weight.shape[0]
    length = extended.shape[0] - tap_count + 1
    counts = jnp.cumsum(marks_ext)
    conv_sum = jnp.zeros((length, extended.shape[1]), jnp.float32) + conv_bias
    for tap_index in range(tap_count):
        linked = (counts[tap_count - 1 :] == counts[tap_index : tap_index + length]).astype(
            jnp.float32
        )
        conv_sum = (
            conv_sum
            + linked[:, None] * weight[tap_index] * extended[tap_index : tap_index + length]
        )
    return conv_sum


def prepare(extended, dt_pre, marks_ext, alive_mask, conv_weight, conv_bias, dt_bias, a_log):
    inner_width = dt_pre.shape[1] * P_SIZE
    activated = jax.nn.silu(causal_conv(extended, marks_ext, conv_weight, conv_bias))
    inner_act = activated[:, :inner_width] * alive_mask[:, None]
    b_mat = activated[:, inner_width : inner_width + N]
    c_mat = activated[:, inner_width + N :]
    step_size = jax.nn.softplus(dt_pre + dt_bias) * alive_mask[:, None]
    log_decay = -step_size * jnp.exp(a_log)
    return (inner_act, step_size, log_decay, b_mat, c_mat)


def block_terms(inner_act, step_size, log_decay, b_mat, start_marks):
    blocks = inner_act.shape[0] // SCAN_BLOCK
    head_count = step_size.shape[1]
    x_blocks = inner_act.reshape(blocks, SCAN_BLOCK, head_count, P_SIZE)
    dt_blocks = step_size.reshape(blocks, SCAN_BLOCK, head_count)
    cum_decay = jnp.cumsum(log_decay.reshape(blocks, SCAN_BLOCK, head_count), axis=1)
    mark_count = jnp.cumsum(start_marks.reshape(blocks, SCAN_BLOCK), axis=1)
    b_blocks = b_mat.reshape(blocks, SCAN_BLOCK, N)
    last_cum = cum_decay[:, -1]
    last_mark = mark_count[:, -1]
    same_end = (mark_count == last_mark[:, None]).astype(jnp.float32)
    end_weight = jnp.exp(last_cum[:, None, :] - cum_decay) * same_end[:, :, None] * dt_blocks
    block_states = jnp.einsum(
        "cjh,cjhp,cjn->chpn", end_weight, x_blocks, b_blocks, precision=highest
    )
    block_decay = jnp.exp(last_cum) * (last_mark == 0).astype(jnp.float32)[:, None]
    return (block_decay, block_states, cum_decay, mark_count, x_blocks, dt_blocks)


def compose_blocks(block_decay, block_states, start_state):
    chain_state = start_state
    incoming = []
    for block_index in range(block_decay.shape[0]):
        incoming.append(chain_state)
        chain_state = (
            block_decay[block_index][:, None, None] * chain_state + block_states[block_index]
        )
    return (chain_state, jnp.stack(incoming))


def block_output(block_parts, b_mat, c_mat, skip, incoming):
    block_decay, block_states, cum_decay, mark_count, x_blocks, dt_blocks = block_parts
    blocks = cum_decay.shape[0]
    head_count = cum_decay.shape[2]
    b_blocks = b_mat.reshape(blocks, SCAN_BLOCK, N)
    c_blocks = c_mat.reshape(blocks, SCAN_BLOCK, N)
    inner_prod = jnp.einsum("cin,cjn->cij", c_blocks, b_blocks, precision=highest)
    arange_pos = jnp.arange(SCAN_BLOCK)
    linked = (arange_pos[:, None] >= arange_pos[None, :])[None] & (
        mark_count[:, :, None] == mark_count[:, None, :]
    )
    spread = jnp.where(
        linked[..., None], cum_decay[:, :, None, :] - cum_decay[:, None, :, :], far_below
    )
    weights = jnp.exp(spread) * inner_prod[..., None] * dt_blocks[:, None, :, :]
    y_intra = jnp.einsum("cijh,cjhp->cihp", weights, x_blocks, precision=highest)
    carry_in = jnp.exp(cum_decay) * (mark_count == 0).astype(jnp.float32)[:, :, None]
    y_inter = (
        jnp.einsum("cin,chpn->cihp", c_blocks, incoming, precision=highest) * carry_in[..., None]
    )
    mixed_out = y_intra + y_inter + skip[None, None, :, None] * x_blocks
    return mixed_out.reshape(blocks * SCAN_BLOCK, head_count * P_SIZE)


def local_front(marks_ext, alive_mask, extended, dt_pre, conv_weight, conv_bias, dt_bias, a_log):
    inner_act, step_size, log_decay, b_mat, c_mat = prepare(
        extended, dt_pre, marks_ext, alive_mask, conv_weight, conv_bias, dt_bias, a_log
    )
    block_parts = block_terms(inner_act, step_size, log_decay, b_mat, marks_ext[KW - 1 :])
    zero_state = jnp.zeros(block_parts[1].shape[1:], jnp.float32)
    total_state, _ = compose_blocks(block_parts[0], block_parts[1], zero_state)
    total_decay = jnp.prod(block_parts[0], axis=0)
    return (block_parts, b_mat, c_mat, total_decay, total_state)


def local_rear(block_parts, b_mat, c_mat, skip, start_state):
    _, incoming = compose_blocks(block_parts[0], block_parts[1], start_state)
    return block_output(block_parts, b_mat, c_mat, skip, incoming)


def local_pass(
    marks_ext,
    alive_mask,
    extended,
    dt_pre,
    conv_weight,
    conv_bias,
    dt_bias,
    a_log,
    skip,
    start_state,
):
    block_parts, b_mat, c_mat, total_decay, total_state = local_front(
        marks_ext, alive_mask, extended, dt_pre, conv_weight, conv_bias, dt_bias, a_log
    )
    return (local_rear(block_parts, b_mat, c_mat, skip, start_state), total_decay, total_state)


def chain_combine(earlier, later):
    return (earlier[0] * later[0], later[0][:, None, None] * earlier[1] + later[1])


def extend(pre_conv, start_marks, edge_rows, edge_marks):
    extended = jnp.concatenate([edge_rows, pre_conv], axis=0)
    marks_ext = jnp.concatenate([edge_marks.astype(jnp.int32), start_marks], axis=0)
    return (extended, marks_ext)


def mixer_forward(stream, start_marks, alive_mask, layer_weights, tick, ids):
    (
        norm_gain,
        w_main,
        w_low,
        w_bc,
        conv_weight,
        conv_bias,
        dt_bias,
        a_log,
        skip,
        gate_gain,
        w_out,
    ) = layer_weights
    inner_width = w_out.shape[0]
    normed = (stream * rms_scale(stream) * norm_gain).astype(jnp.bfloat16)
    gathered = head_gather(normed, tick, ids[0])
    gathered = gathered.reshape(-1, gathered.shape[-1])
    projected = jnp.dot(gathered, w_main, preferred_element_type=jnp.float32)
    gate_pre = projected[:, :inner_width]
    pre_conv = projected[:, inner_width : 2 * inner_width + 2 * N]
    dt_pre = projected[:, 2 * inner_width + 2 * N :]
    marks_float = start_marks.astype(jnp.float32)
    tail_from = pre_conv.shape[0] - KW + 1
    edge_parts = shifted((pre_conv[tail_from:], marks_float[tail_from:]), "seq", 1)
    extended, marks_ext = extend(pre_conv, start_marks, edge_parts[0], edge_parts[1])
    front_fn = partial(local_front, marks_ext, alive_mask)
    front_out, front_pull = jax.vjp(
        front_fn, extended, dt_pre, conv_weight, conv_bias, dt_bias, a_log
    )
    block_parts, b_mat, c_mat, total_decay, total_state = front_out
    neutral = (jnp.ones_like(total_decay), jnp.zeros_like(total_state))
    prefix = entering((total_decay, total_state), "seq", chain_combine, neutral)
    start_state = prefix[1]
    mixed_out, rear_pull = jax.vjp(local_rear, block_parts, b_mat, c_mat, skip, start_state)
    silu_gate = jax.nn.silu(gate_pre)
    gated_mix = mixed_out * silu_gate
    square_total = lax.psum(jnp.sum(gated_mix * gated_mix, axis=-1), "head")
    scale_out = lax.rsqrt(square_total / DI + norm_eps)
    normed_out = (gated_mix * scale_out[:, None] * gate_gain).astype(jnp.bfloat16)
    head_count = lax.axis_size("head")
    branch = head_scatter(
        jnp.dot(normed_out, w_out, preferred_element_type=jnp.float32).reshape(
            head_count, -1, w_out.shape[1]
        ),
        tick,
        ids[1],
    )
    saved = (
        stream,
        gathered,
        gate_pre,
        mixed_out,
        silu_gate,
        gated_mix,
        scale_out,
        normed_out,
        total_decay,
        start_state,
        front_pull,
        rear_pull,
    )
    return stream + branch, saved


def mixer_backward(grad_next, layer_weights, saved, mask_value, tick, ids, hook=None):
    (
        norm_gain,
        w_main,
        w_low,
        w_bc,
        conv_weight,
        conv_bias,
        dt_bias,
        a_log,
        skip,
        gate_gain,
        w_out,
    ) = layer_weights
    (
        stream,
        gathered,
        gate_pre,
        mixed_out,
        silu_gate,
        gated_mix,
        scale_out,
        normed_out,
        total_decay,
        start_state,
        front_pull,
        rear_pull,
    ) = saved
    inner_width = w_out.shape[0]
    grad_branch = grad_next.astype(jnp.bfloat16)
    shard_rows = head_gather(grad_branch, tick, ids[0])
    shard_rows = shard_rows.reshape(-1, shard_rows.shape[-1])
    g_w_out = lax.dot_general(
        normed_out, shard_rows, (((0,), (0,)), ((), ())), preferred_element_type=jnp.float32
    ) * mask_value
    grad_normed = lax.dot_general(
        shard_rows, w_out, (((1,), (1,)), ((), ())), preferred_element_type=jnp.float32
    )
    weighted = grad_normed * gate_gain
    g_gate_gain = jnp.sum(grad_normed * gated_mix * scale_out[:, None], axis=0)
    cross_sum = lax.psum(jnp.sum(weighted * gated_mix, axis=-1), "head")
    grad_gated = (
        scale_out[:, None] * weighted - gated_mix * (scale_out**3 * cross_sum / DI)[:, None]
    )
    grad_mixed = grad_gated * silu_gate
    grad_gate = (grad_gated * mixed_out * silu_slope(gate_pre)).astype(jnp.bfloat16)
    g_parts, g_b_mat, g_c_mat, g_skip, g_start = rear_pull(grad_mixed)
    neutral = (jnp.ones_like(total_decay), jnp.zeros_like(g_start))
    suffix = entering_2((total_decay, g_start), "seq", chain_combine, neutral)
    after_state = suffix[1]
    grad_decay = jnp.sum(after_state * start_state, axis=(1, 2))
    grad_ext, grad_dt_pre, g_conv_w, g_conv_b, g_dt_bias, g_a_log = front_pull(
        (g_parts, g_b_mat, g_c_mat, grad_decay, after_state)
    )
    returned = shifted(grad_ext[: KW - 1], "seq", -1)
    grad_pre = grad_ext[KW - 1 :]
    tail_from = grad_pre.shape[0] - KW + 1
    grad_pre = jnp.concatenate([grad_pre[:tail_from], grad_pre[tail_from:] + returned], axis=0)
    grad_inner = grad_pre[:, :inner_width].astype(jnp.bfloat16)
    grad_bc = grad_pre[:, inner_width:]
    grad_low = jnp.concatenate([grad_gate, grad_inner, grad_dt_pre.astype(jnp.bfloat16)], axis=1)
    w_bc_float = w_bc.astype(jnp.float32)
    g_low = lax.dot_general(
        gathered, grad_low, (((0,), (0,)), ((), ())), preferred_element_type=jnp.float32
    )
    g_w_bc = lax.dot_general(
        gathered.astype(jnp.float32),
        grad_bc,
        (((0,), (0,)), ((), ())),
        precision=highest,
        preferred_element_type=jnp.float32,
    )
    main_term = lax.dot_general(
        grad_low, w_low, (((1,), (1,)), ((), ())), preferred_element_type=jnp.float32
    )
    side_term = lax.dot_general(
        grad_bc,
        w_bc_float,
        (((1,), (1,)), ((), ())),
        precision=highest,
        preferred_element_type=jnp.float32,
    )
    head_count = lax.axis_size("head")
    lead = 0.0
    if hook is not None:
        lead = hook((g_w_bc, g_conv_w[:, inner_width:], g_conv_b[inner_width:]))
    grad_normed_in = head_scatter(
        (main_term + side_term + lead).reshape(head_count, -1, main_term.shape[1]), tick, ids[1]
    )
    scale_in = rms_scale(stream)
    g_norm_gain = jnp.sum(grad_normed_in * stream * scale_in, axis=0)
    weighted_in = grad_normed_in * norm_gain
    grad_stream = (
        grad_next
        + scale_in * weighted_in
        - stream * scale_in**3 * jnp.mean(weighted_in * stream, axis=-1, keepdims=True)
    )
    head_part = (
        g_low[:, :inner_width],
        g_low[:, inner_width : 2 * inner_width],
        g_low[:, 2 * inner_width :],
        g_conv_w[:, :inner_width],
        g_conv_b[:inner_width],
        g_dt_bias,
        g_a_log,
        g_skip,
        g_gate_gain,
    )
    shared_part = (g_norm_gain, g_w_bc, g_conv_w[:, inner_width:], g_conv_b[inner_width:])
    return (grad_stream, head_part, shared_part, g_w_out)


def pack_rows(members, width, multiple):
    rows = jnp.concatenate([member.reshape(-1, width) for member in members], axis=0)
    return jnp.pad(rows, ((0, -rows.shape[0] % multiple), (0, 0)))


def unpack_rows(rows, shapes, width):
    pieces = []
    start = 0
    for shape in shapes:
        count = math.prod(shape) // width
        pieces.append(rows[start : start + count].reshape(shape))
        start += count
    return tuple(pieces)


def reduce_grads(head_part, norm_part, bc_part, tick_count):
    bc_all = lax.all_gather(bc_part.astype(jnp.bfloat16), "seq")
    bc_sum = bc_all[0].astype(jnp.float32)
    for index in range(1, bc_all.shape[0]):
        bc_sum = bc_sum + bc_all[index].astype(jnp.float32)
    anchor = bc_all[0, 0, 0].astype(jnp.float32) * 0.0
    summed = lax.psum(
        tuple(member.astype(jnp.bfloat16) for member in (head_part[0] + anchor,) + head_part[1:3]),
        "seq",
    )
    head_sum = tuple(member.astype(jnp.float32) for member in summed) + tuple(
        lax.psum(member.astype(jnp.bfloat16), "seq").astype(jnp.float32)
        for member in head_part[3:]
    )
    bc_rows = head_gather(bc_sum, (0, 0, 1), 4 * tick_count + 1)
    norm_sum = lax.psum(norm_part, ("seq", "head"))
    return (head_sum, norm_sum, bc_rows.reshape(-1, bc_rows.shape[-1]))


def store_slot(buffer, value, slot_index, is_valid):
    current = lax.dynamic_index_in_dim(buffer, slot_index, 0, False)
    return lax.dynamic_update_index_in_dim(
        buffer, jnp.where(is_valid, value, current), slot_index, 0
    )


def on_device(
    inputs,
    cotangent,
    starts,
    live,
    norm_gain,
    w_gate,
    w_in,
    w_bc,
    w_dt,
    conv_x,
    conv_x_bias,
    conv_bc,
    conv_bc_bias,
    dt_bias,
    a_log,
    skip,
    gate_gain,
    w_out,
):
    section_count = lax.axis_size("section")
    section_index = lax.axis_index("section")
    micro_count = inputs.shape[0]
    tick_count = micro_count + section_count - 1
    w_main = jnp.concatenate([w_gate[0], w_in[0], w_bc[0], w_dt[0]], axis=1)
    w_low = jnp.concatenate([w_gate[0], w_in[0], w_dt[0]], axis=1)
    conv_weight = jnp.concatenate([conv_x[0], conv_bc[0]], axis=1).astype(jnp.float32)
    conv_bias = jnp.concatenate([conv_x_bias[0], conv_bc_bias[0]], axis=0)
    layer_weights = (
        norm_gain[0],
        w_main,
        w_low,
        w_bc[0],
        conv_weight,
        conv_bias,
        dt_bias[0],
        a_log[0],
        skip[0],
        gate_gain[0],
        w_out[0],
    )
    row_shape = inputs.shape[1:]
    outputs_all = jnp.zeros((micro_count,) + row_shape, jnp.float32)
    arrived = jnp.zeros(row_shape, jnp.float32)
    ticks = []
    for tick_index in range(tick_count):
        slot_index = tick_index - section_index
        is_valid = (slot_index >= 0) & (slot_index < micro_count)
        clipped = jnp.clip(slot_index, 0, micro_count - 1)
        fresh_rows = lax.dynamic_index_in_dim(inputs, clipped, 0, False).astype(jnp.float32)
        stream = jnp.where(section_index == 0, fresh_rows, arrived)
        start_marks = lax.dynamic_index_in_dim(starts, clipped, 0, False)
        alive_mask = lax.dynamic_index_in_dim(live, clipped, 0, False).astype(jnp.float32)
        result, saved = mixer_forward(
            stream,
            start_marks,
            alive_mask,
            layer_weights,
            (tick_index, -1, micro_count),
            (tick_index, tick_count + tick_index),
        )
        outputs_all = store_slot(outputs_all, result, clipped, is_valid)
        ticks.append((clipped, is_valid, saved))
        if tick_index + 1 < tick_count:
            arrived = shifted(result, "section", 1)
    back_arrived = jnp.zeros(row_shape, jnp.float32)
    input_grads = jnp.zeros((micro_count,) + row_shape, jnp.float32)
    head_count = lax.axis_size("head")
    bc_box = []
    head_total = ()
    shared_total = ()
    for tick_index in range(tick_count):
        clipped, is_valid, saved = ticks[tick_count - 1 - tick_index]
        outer_grad = lax.dynamic_index_in_dim(cotangent, clipped, 0, False).astype(jnp.float32)
        grad_next = jnp.where(section_index == section_count - 1, outer_grad, back_arrived)
        mask_value = is_valid.astype(jnp.float32)
        hook = None
        if tick_index + 1 == tick_count:

            def hook(bc_local, mask_value=mask_value, earlier=shared_total):
                totals = tuple(
                    (prev + member * mask_value) if earlier else member * mask_value
                    for prev, member in zip(earlier[1:] or bc_local, bc_local)
                )
                rows = pack_rows(totals, totals[0].shape[-1], 8 * head_count)
                part = head_scatter(
                    rows.reshape(head_count, -1, rows.shape[-1]), (0, 0, 1), 4 * tick_count
                )
                bc_box.append((part, [member.shape for member in totals]))
                return part[0, 0] * 0.0

        grad_stream, head_part, shared_part, out_part = mixer_backward(
            grad_next,
            layer_weights,
            saved,
            mask_value,
            (tick_count - 1 - tick_index, -1, micro_count),
            (2 * tick_count + tick_index, 3 * tick_count + tick_index),
            hook,
        )
        if tick_index == 0:
            out_total = out_part
        else:
            out_total = out_total + out_part
        if tick_index + 1 == tick_count:
            out_total = lax.psum(out_total.astype(jnp.bfloat16), "seq")
        head_part = tuple((member * mask_value for member in head_part))
        shared_part = tuple((member * mask_value for member in shared_part))
        if tick_index == 0:
            head_total = head_part
            shared_total = shared_part
        else:
            head_total = tuple((former + latter for former, latter in zip(head_total, head_part)))
            shared_total = tuple(
                (former + latter for former, latter in zip(shared_total, shared_part))
            )
        input_grads = store_slot(input_grads, grad_stream, clipped, is_valid)
        if tick_index + 1 < tick_count:
            back_arrived = shifted(grad_stream.astype(jnp.bfloat16), "section", -1).astype(
                grad_stream.dtype
            )
    anchor = out_total[0, 0].astype(jnp.float32) * 0.0
    head_total = (head_total[0] + anchor,) + head_total[1:]
    bc_part, bc_shapes = bc_box[0]
    bc_part = bc_part + anchor
    head_total, norm_sum, bc_rows = reduce_grads(head_total, shared_total[0], bc_part, tick_count)
    shared_total = (norm_sum,) + unpack_rows(bc_rows, bc_shapes, bc_rows.shape[-1])
    head_total = head_total[:3] + (out_total.astype(jnp.float32),) + head_total[3:]
    return (
        outputs_all[None],
        input_grads[None],
        shared_total[0][None],
        head_total[0][None],
        head_total[1][None],
        shared_total[1][None],
        head_total[2][None],
        head_total[4][None],
        head_total[5][None],
        shared_total[2][None],
        shared_total[3][None],
        head_total[6][None],
        head_total[7][None],
        head_total[8][None],
        head_total[9][None],
        head_total[3][None],
    )


def solution(mesh):
    return jax.shard_map(
        on_device,
        mesh=mesh,
        in_specs=(
            P(None, ("seq", "head"), None),
            P(None, ("seq", "head"), None),
            P(None, "seq"),
            P(None, "seq"),
            P("section", None),
            P("section", None, "head"),
            P("section", None, "head"),
            P("section", None, None),
            P("section", None, "head"),
            P("section", None, "head"),
            P("section", "head"),
            P("section", None, None),
            P("section", None),
            P("section", "head"),
            P("section", "head"),
            P("section", "head"),
            P("section", "head"),
            P("section", "head", None),
        ),
        out_specs=(
            P("section", None, ("seq", "head"), None),
            P("section", None, ("seq", "head"), None),
            P("section", None),
            P("section", None, "head"),
            P("section", None, "head"),
            P("section", None, None),
            P("section", None, "head"),
            P("section", None, "head"),
            P("section", "head"),
            P("section", None, None),
            P("section", None),
            P("section", "head"),
            P("section", "head"),
            P("section", "head"),
            P("section", "head"),
            P("section", "head", None),
        ),
        check_vma=False,
    )
```

```python
from functools import partial

import functools
import math

import jax
import jax.numpy as jnp
from jax import lax
from jax.experimental import pallas as pl
from jax.experimental.pallas import tpu as pltpu
from jax.sharding import PartitionSpec as P

DI = 4096
P_SIZE = 64
N = 128
KW = 4
SCAN_BLOCK = 256


MESH = pl.DeviceIdType.MESH


def _tick_valid(offset, sign, count):
    slot = offset + sign * lax.axis_index("section")
    return jnp.logical_and(slot >= 0, slot < count)


def _enter(barrier, h, n):
    @pl.when(h > 0)
    def _():
        pl.semaphore_signal(barrier, 1, device_id={"head": h - 1}, device_id_type=MESH)

    @pl.when(h < n - 1)
    def _():
        pl.semaphore_signal(barrier, 1, device_id={"head": h + 1}, device_id_type=MESH)

    @pl.when(jnp.logical_and(h > 0, h < n - 1))
    def _():
        pl.semaphore_wait(barrier, 2)

    @pl.when(jnp.logical_or(h == 0, h == n - 1))
    def _():
        pl.semaphore_wait(barrier, 1)


def gather_body(n, tick, x_ref, o_ref, land, send_r, send_l, recv):
    h = lax.axis_index("head")
    valid = _tick_valid(*tick)

    @pl.when(valid)
    def _():
        _enter(pltpu.get_barrier_semaphore(), h, n)

        def copy_right(s, k):
            src = x_ref if s == 0 else land.at[k]
            return pltpu.make_async_remote_copy(
                src_ref=src, dst_ref=land.at[k], send_sem=send_r.at[s], recv_sem=recv.at[k],
                device_id={"head": h + 1}, device_id_type=MESH)

        def copy_left(s, k):
            src = x_ref if s == 0 else land.at[k]
            return pltpu.make_async_remote_copy(
                src_ref=src, dst_ref=land.at[k], send_sem=send_l.at[s], recv_sem=recv.at[k],
                device_id={"head": h - 1}, device_id_type=MESH)

        for s in range(n):
            k_r = h - s
            k_l = h + s
            if s >= 1:
                @pl.when(k_r >= 0)
                def _():
                    pltpu.make_async_remote_copy(
                        src_ref=land.at[k_r], dst_ref=land.at[k_r], send_sem=send_r.at[0],
                        recv_sem=recv.at[k_r], device_id={"head": h}, device_id_type=MESH
                    ).wait_recv()

                @pl.when(k_l <= n - 1)
                def _():
                    pltpu.make_async_remote_copy(
                        src_ref=land.at[k_l], dst_ref=land.at[k_l], send_sem=send_l.at[0],
                        recv_sem=recv.at[k_l], device_id={"head": h}, device_id_type=MESH
                    ).wait_recv()
            if s <= n - 2:
                @pl.when(jnp.logical_and(k_r >= 0, h < n - 1))
                def _():
                    copy_right(s, k_r).start()

                @pl.when(jnp.logical_and(k_l <= n - 1, h > 0))
                def _():
                    copy_left(s, k_l).start()
        land[h] = x_ref[...]
        for s in range(n - 1):
            k_r = h - s
            k_l = h + s

            @pl.when(jnp.logical_and(k_r >= 0, h < n - 1))
            def _():
                copy_right(s, k_r).wait_send()

            @pl.when(jnp.logical_and(k_l <= n - 1, h > 0))
            def _():
                copy_left(s, k_l).wait_send()
        o_ref[...] = land[...]

    @pl.when(jnp.logical_not(valid))
    def _():
        o_ref[...] = jnp.zeros(o_ref.shape, o_ref.dtype)


def head_gather(x, tick, cid):
    n = lax.axis_size("head")
    rows, cols = x.shape
    return pl.pallas_call(
        functools.partial(gather_body, n, tick),
        out_shape=jax.ShapeDtypeStruct((n, rows, cols), x.dtype),
        in_specs=[pl.BlockSpec(memory_space=pltpu.VMEM)],
        out_specs=pl.BlockSpec(memory_space=pltpu.VMEM),
        scratch_shapes=[
            pltpu.VMEM((n, rows, cols), x.dtype),
            pltpu.SemaphoreType.DMA((n,)),
            pltpu.SemaphoreType.DMA((n,)),
            pltpu.SemaphoreType.DMA((n,)),
        ],
        compiler_params=pltpu.CompilerParams(collective_id=cid, has_side_effects=True),
    )(x)


def scatter_body(n, tick, p_ref, o_ref, recv_l, recv_r, send_l, send_r, ssem_l, ssem_r, rsem_l, rsem_r):
    h = lax.axis_index("head")
    valid = _tick_valid(*tick)
    link = send_r.dtype

    @pl.when(valid)
    def _():
        _enter(pltpu.get_barrier_semaphore(), h, n)

        def to_right(k):
            return pltpu.make_async_remote_copy(
                src_ref=send_r.at[k], dst_ref=recv_l.at[k], send_sem=ssem_r.at[k],
                recv_sem=rsem_l.at[k], device_id={"head": h + 1}, device_id_type=MESH)

        def to_left(k):
            return pltpu.make_async_remote_copy(
                src_ref=send_l.at[k], dst_ref=recv_r.at[k], send_sem=ssem_l.at[k],
                recv_sem=rsem_r.at[k], device_id={"head": h - 1}, device_id_type=MESH)

        def rightward(s):
            k_r = n - 1 - s

            @pl.when(k_r > h)
            def _():
                @pl.when(h > 0)
                def _():
                    to_right(k_r).wait_recv()
                    send_r[k_r] = (p_ref[k_r] + recv_l[k_r].astype(jnp.float32)).astype(link)

                @pl.when(h == 0)
                def _():
                    send_r[k_r] = p_ref[k_r].astype(link)

                to_right(k_r).start()

        def leftward(s):
            k_l = s

            @pl.when(k_l < h)
            def _():
                @pl.when(h < n - 1)
                def _():
                    to_left(k_l).wait_recv()
                    send_l[k_l] = (p_ref[k_l] + recv_r[k_l].astype(jnp.float32)).astype(link)

                @pl.when(h == n - 1)
                def _():
                    send_l[k_l] = p_ref[k_l].astype(link)

                to_left(k_l).start()

        for s in range(n - 1):

            @pl.when(2 * h < n)
            def _():
                rightward(s)
                leftward(s)

            @pl.when(2 * h >= n)
            def _():
                leftward(s)
                rightward(s)

        total = p_ref[h]

        @pl.when(h > 0)
        def _():
            to_right(h).wait_recv()

        @pl.when(h < n - 1)
        def _():
            to_left(h).wait_recv()

        left_part = jnp.where(h > 0, recv_l[h].astype(jnp.float32), 0.0)
        right_part = jnp.where(h < n - 1, recv_r[h].astype(jnp.float32), 0.0)
        o_ref[...] = (total + left_part + right_part).astype(o_ref.dtype)
        for s in range(n - 1):
            k_r = n - 1 - s
            k_l = s

            @pl.when(k_r > h)
            def _():
                to_right(k_r).wait_send()

            @pl.when(k_l < h)
            def _():
                to_left(k_l).wait_send()

    @pl.when(jnp.logical_not(valid))
    def _():
        o_ref[...] = jnp.zeros(o_ref.shape, o_ref.dtype)


def head_scatter(parts, tick, cid, link=jnp.bfloat16):
    n = lax.axis_size("head")
    _, rows, cols = parts.shape
    return pl.pallas_call(
        functools.partial(scatter_body, n, tick),
        out_shape=jax.ShapeDtypeStruct((rows, cols), jnp.float32),
        in_specs=[pl.BlockSpec(memory_space=pltpu.VMEM)],
        out_specs=pl.BlockSpec(memory_space=pltpu.VMEM),
        scratch_shapes=[
            pltpu.VMEM((n, rows, cols), link),
            pltpu.VMEM((n, rows, cols), link),
            pltpu.VMEM((n, rows, cols), link),
            pltpu.VMEM((n, rows, cols), link),
            pltpu.SemaphoreType.DMA((n,)),
            pltpu.SemaphoreType.DMA((n,)),
            pltpu.SemaphoreType.DMA((n,)),
            pltpu.SemaphoreType.DMA((n,)),
        ],
        compiler_params=pltpu.CompilerParams(collective_id=cid, has_side_effects=True),
    )(parts)


norm_eps = 1e-05
far_below = -1e30
highest = lax.Precision.HIGH


def shifted(value, axis, by):
    count = lax.axis_size(axis)
    pairs = [(i, i + by) for i in range(count) if 0 <= i + by < count]
    return lax.ppermute(value, axis, pairs)


def entering(value, axis, combine, identity):
    count, mine = (lax.axis_size(axis), lax.axis_index(axis))
    everything = jax.tree.map(lambda part: lax.all_gather(part, axis), value)
    before = jax.tree.map(
        lambda part, zero: jnp.broadcast_to(jnp.asarray(zero, part.dtype), part.shape),
        value,
        identity,
    )
    for k in range(count - 1):
        reached = k < mine
        new = combine(before, jax.tree.map(lambda part: part[k], everything))
        before = jax.tree.map(lambda a, b: jnp.where(reached, a, b), new, before)
    return before


def entering_2(value, axis, join, neutral):
    count = lax.axis_size(axis)
    place = lax.axis_index(axis)
    ahead = count - 1 - place
    gathered = jax.tree.map(
        lambda a, kind: lax.all_gather(a.astype(kind), axis),
        value,
        jax.tree.map(lambda a: jnp.bfloat16 if a.dtype == jnp.float32 else a.dtype, value),
    )
    state = jax.tree.map(lambda a, e: jnp.zeros_like(a) + jnp.asarray(e, a.dtype), value, neutral)
    for lap in range(count - 1):
        source = count - 1 - lap
        new = join(
            state,
            jax.tree.map(lambda a, own: a[source].astype(own.dtype), gathered, value),
        )
        active = lap < ahead
        state = jax.tree.map(lambda a, b: jnp.where(active, a, b), new, state)
    return state


def rms_scale(values):
    return lax.rsqrt(jnp.mean(values * values, axis=-1, keepdims=True) + norm_eps)


def silu_slope(values):
    logistic = jax.nn.sigmoid(values)
    return logistic * (1.0 + values * (1.0 - logistic))


def causal_conv(extended, marks_ext, weight, conv_bias):
    tap_count = weight.shape[0]
    length = extended.shape[0] - tap_count + 1
    counts = jnp.cumsum(marks_ext)
    conv_sum = jnp.zeros((length, extended.shape[1]), jnp.float32) + conv_bias
    for tap_index in range(tap_count):
        linked = (counts[tap_count - 1 :] == counts[tap_index : tap_index + length]).astype(
            jnp.float32
        )
        conv_sum = (
            conv_sum
            + linked[:, None] * weight[tap_index] * extended[tap_index : tap_index + length]
        )
    return conv_sum


def prepare(extended, dt_pre, marks_ext, alive_mask, conv_weight, conv_bias, dt_bias, a_log):
    inner_width = dt_pre.shape[1] * P_SIZE
    activated = jax.nn.silu(causal_conv(extended, marks_ext, conv_weight, conv_bias))
    inner_act = activated[:, :inner_width] * alive_mask[:, None]
    b_mat = activated[:, inner_width : inner_width + N]
    c_mat = activated[:, inner_width + N :]
    step_size = jax.nn.softplus(dt_pre + dt_bias) * alive_mask[:, None]
    log_decay = -step_size * jnp.exp(a_log)
    return (inner_act, step_size, log_decay, b_mat, c_mat)


def block_terms(inner_act, step_size, log_decay, b_mat, start_marks):
    blocks = inner_act.shape[0] // SCAN_BLOCK
    head_count = step_size.shape[1]
    x_blocks = inner_act.reshape(blocks, SCAN_BLOCK, head_count, P_SIZE)
    dt_blocks = step_size.reshape(blocks, SCAN_BLOCK, head_count)
    cum_decay = jnp.cumsum(log_decay.reshape(blocks, SCAN_BLOCK, head_count), axis=1)
    mark_count = jnp.cumsum(start_marks.reshape(blocks, SCAN_BLOCK), axis=1)
    b_blocks = b_mat.reshape(blocks, SCAN_BLOCK, N)
    last_cum = cum_decay[:, -1]
    last_mark = mark_count[:, -1]
    same_end = (mark_count == last_mark[:, None]).astype(jnp.float32)
    end_weight = jnp.exp(last_cum[:, None, :] - cum_decay) * same_end[:, :, None] * dt_blocks
    block_states = jnp.einsum(
        "cjh,cjhp,cjn->chpn", end_weight, x_blocks, b_blocks, precision=highest
    )
    block_decay = jnp.exp(last_cum) * (last_mark == 0).astype(jnp.float32)[:, None]
    return (block_decay, block_states, cum_decay, mark_count, x_blocks, dt_blocks)


def compose_blocks(block_decay, block_states, start_state):
    chain_state = start_state
    incoming = []
    for block_index in range(block_decay.shape[0]):
        incoming.append(chain_state)
        chain_state = (
            block_decay[block_index][:, None, None] * chain_state + block_states[block_index]
        )
    return (chain_state, jnp.stack(incoming))


def block_output(block_parts, b_mat, c_mat, skip, incoming):
    block_decay, block_states, cum_decay, mark_count, x_blocks, dt_blocks = block_parts
    blocks = cum_decay.shape[0]
    head_count = cum_decay.shape[2]
    b_blocks = b_mat.reshape(blocks, SCAN_BLOCK, N)
    c_blocks = c_mat.reshape(blocks, SCAN_BLOCK, N)
    inner_prod = jnp.einsum("cin,cjn->cij", c_blocks, b_blocks, precision=highest)
    arange_pos = jnp.arange(SCAN_BLOCK)
    linked = (arange_pos[:, None] >= arange_pos[None, :])[None] & (
        mark_count[:, :, None] == mark_count[:, None, :]
    )
    spread = jnp.where(
        linked[..., None], cum_decay[:, :, None, :] - cum_decay[:, None, :, :], far_below
    )
    weights = jnp.exp(spread) * inner_prod[..., None] * dt_blocks[:, None, :, :]
    y_intra = jnp.einsum(
        "cijh,cjhp->cihp", weights, x_blocks, precision=lax.Precision.DEFAULT
    )
    carry_in = jnp.exp(cum_decay) * (mark_count == 0).astype(jnp.float32)[:, :, None]
    y_inter = (
        jnp.einsum("cin,chpn->cihp", c_blocks, incoming, precision=highest) * carry_in[..., None]
    )
    mixed_out = y_intra + y_inter + skip[None, None, :, None] * x_blocks
    return mixed_out.reshape(blocks * SCAN_BLOCK, head_count * P_SIZE)


def local_front(marks_ext, alive_mask, extended, dt_pre, conv_weight, conv_bias, dt_bias, a_log):
    inner_act, step_size, log_decay, b_mat, c_mat = prepare(
        extended, dt_pre, marks_ext, alive_mask, conv_weight, conv_bias, dt_bias, a_log
    )
    block_parts = block_terms(inner_act, step_size, log_decay, b_mat, marks_ext[KW - 1 :])
    zero_state = jnp.zeros(block_parts[1].shape[1:], jnp.float32)
    total_state, _ = compose_blocks(block_parts[0], block_parts[1], zero_state)
    total_decay = jnp.prod(block_parts[0], axis=0)
    return (block_parts, b_mat, c_mat, total_decay, total_state)


def local_rear(block_parts, b_mat, c_mat, skip, start_state):
    _, incoming = compose_blocks(block_parts[0], block_parts[1], start_state)
    return block_output(block_parts, b_mat, c_mat, skip, incoming)


def local_pass(
    marks_ext,
    alive_mask,
    extended,
    dt_pre,
    conv_weight,
    conv_bias,
    dt_bias,
    a_log,
    skip,
    start_state,
):
    block_parts, b_mat, c_mat, total_decay, total_state = local_front(
        marks_ext, alive_mask, extended, dt_pre, conv_weight, conv_bias, dt_bias, a_log
    )
    return (local_rear(block_parts, b_mat, c_mat, skip, start_state), total_decay, total_state)


def chain_combine(earlier, later):
    return (earlier[0] * later[0], later[0][:, None, None] * earlier[1] + later[1])


def extend(pre_conv, start_marks, edge_rows, edge_marks):
    extended = jnp.concatenate([edge_rows, pre_conv], axis=0)
    marks_ext = jnp.concatenate([edge_marks.astype(jnp.int32), start_marks], axis=0)
    return (extended, marks_ext)


def mixer_forward(stream, start_marks, alive_mask, layer_weights, tick, ids):
    (
        norm_gain,
        w_main,
        w_low,
        w_bc,
        conv_weight,
        conv_bias,
        dt_bias,
        a_log,
        skip,
        gate_gain,
        w_out,
    ) = layer_weights
    inner_width = w_out.shape[0]
    normed = (stream * rms_scale(stream) * norm_gain).astype(jnp.bfloat16)
    gathered = head_gather(normed, tick, ids[0])
    gathered = gathered.reshape(-1, gathered.shape[-1])
    projected = jnp.dot(gathered, w_main, preferred_element_type=jnp.float32)
    gate_pre = projected[:, :inner_width]
    pre_conv = projected[:, inner_width : 2 * inner_width + 2 * N]
    dt_pre = projected[:, 2 * inner_width + 2 * N :]
    marks_float = start_marks.astype(jnp.float32)
    tail_from = pre_conv.shape[0] - KW + 1
    edge_parts = shifted((pre_conv[tail_from:], marks_float[tail_from:]), "seq", 1)
    extended, marks_ext = extend(pre_conv, start_marks, edge_parts[0], edge_parts[1])
    front_fn = partial(local_front, marks_ext, alive_mask)
    front_out, front_pull = jax.vjp(
        front_fn, extended, dt_pre, conv_weight, conv_bias, dt_bias, a_log
    )
    block_parts, b_mat, c_mat, total_decay, total_state = front_out
    neutral = (jnp.ones_like(total_decay), jnp.zeros_like(total_state))
    prefix = entering((total_decay, total_state), "seq", chain_combine, neutral)
    start_state = prefix[1]
    mixed_out, rear_pull = jax.vjp(local_rear, block_parts, b_mat, c_mat, skip, start_state)
    silu_gate = jax.nn.silu(gate_pre)
    gated_mix = mixed_out * silu_gate
    square_total = lax.psum(jnp.sum(gated_mix * gated_mix, axis=-1), "head")
    scale_out = lax.rsqrt(square_total / DI + norm_eps)
    normed_out = (gated_mix * scale_out[:, None] * gate_gain).astype(jnp.bfloat16)
    head_count = lax.axis_size("head")
    branch = head_scatter(
        jnp.dot(normed_out, w_out, preferred_element_type=jnp.float32).reshape(
            head_count, -1, w_out.shape[1]
        ),
        tick,
        ids[1],
    )
    saved = (
        stream,
        gathered,
        gate_pre,
        mixed_out,
        silu_gate,
        gated_mix,
        scale_out,
        normed_out,
        total_decay,
        start_state,
        front_pull,
        rear_pull,
    )
    return stream + branch, saved


def mixer_backward(grad_next, layer_weights, saved, mask_value, tick, ids, hook=None):
    (
        norm_gain,
        w_main,
        w_low,
        w_bc,
        conv_weight,
        conv_bias,
        dt_bias,
        a_log,
        skip,
        gate_gain,
        w_out,
    ) = layer_weights
    (
        stream,
        gathered,
        gate_pre,
        mixed_out,
        silu_gate,
        gated_mix,
        scale_out,
        normed_out,
        total_decay,
        start_state,
        front_pull,
        rear_pull,
    ) = saved
    inner_width = w_out.shape[0]
    grad_branch = grad_next.astype(jnp.bfloat16)
    shard_rows = head_gather(grad_branch, tick, ids[0])
    shard_rows = shard_rows.reshape(-1, shard_rows.shape[-1])
    g_w_out = lax.dot_general(
        normed_out, shard_rows, (((0,), (0,)), ((), ())), preferred_element_type=jnp.float32
    ) * mask_value
    grad_normed = lax.dot_general(
        shard_rows, w_out, (((1,), (1,)), ((), ())), preferred_element_type=jnp.float32
    )
    weighted = grad_normed * gate_gain
    g_gate_gain = jnp.sum(grad_normed * gated_mix * scale_out[:, None], axis=0)
    cross_sum = lax.psum(jnp.sum(weighted * gated_mix, axis=-1), "head")
    grad_gated = (
        scale_out[:, None] * weighted - gated_mix * (scale_out**3 * cross_sum / DI)[:, None]
    )
    grad_mixed = grad_gated * silu_gate
    grad_gate = (grad_gated * mixed_out * silu_slope(gate_pre)).astype(jnp.bfloat16)
    g_parts, g_b_mat, g_c_mat, g_skip, g_start = rear_pull(grad_mixed)
    neutral = (jnp.ones_like(total_decay), jnp.zeros_like(g_start))
    suffix = entering_2((total_decay, g_start), "seq", chain_combine, neutral)
    after_state = suffix[1]
    grad_decay = jnp.sum(after_state * start_state, axis=(1, 2))
    grad_ext, grad_dt_pre, g_conv_w, g_conv_b, g_dt_bias, g_a_log = front_pull(
        (g_parts, g_b_mat, g_c_mat, grad_decay, after_state)
    )
    returned = shifted(grad_ext[: KW - 1], "seq", -1)
    grad_pre = grad_ext[KW - 1 :]
    tail_from = grad_pre.shape[0] - KW + 1
    grad_pre = jnp.concatenate([grad_pre[:tail_from], grad_pre[tail_from:] + returned], axis=0)
    grad_inner = grad_pre[:, :inner_width].astype(jnp.bfloat16)
    grad_bc = grad_pre[:, inner_width:]
    grad_low = jnp.concatenate([grad_gate, grad_inner, grad_dt_pre.astype(jnp.bfloat16)], axis=1)
    w_bc_float = w_bc.astype(jnp.float32)
    g_low = lax.dot_general(
        gathered, grad_low, (((0,), (0,)), ((), ())), preferred_element_type=jnp.float32
    )
    g_w_bc = lax.dot_general(
        gathered,
        grad_bc.astype(jnp.bfloat16),
        (((0,), (0,)), ((), ())),
        preferred_element_type=jnp.float32,
    )
    main_term = lax.dot_general(
        grad_low, w_low, (((1,), (1,)), ((), ())), preferred_element_type=jnp.float32
    )
    side_term = lax.dot_general(
        grad_bc.astype(jnp.bfloat16),
        w_bc,
        (((1,), (1,)), ((), ())),
        preferred_element_type=jnp.float32,
    )
    head_count = lax.axis_size("head")
    lead = 0.0
    if hook is not None:
        lead = hook((g_w_bc, g_conv_w[:, inner_width:], g_conv_b[inner_width:]))
    grad_normed_in = head_scatter(
        (main_term + side_term + lead).reshape(head_count, -1, main_term.shape[1]), tick, ids[1]
    )
    scale_in = rms_scale(stream)
    g_norm_gain = jnp.sum(grad_normed_in * stream * scale_in, axis=0)
    weighted_in = grad_normed_in * norm_gain
    grad_stream = (
        grad_next
        + scale_in * weighted_in
        - stream * scale_in**3 * jnp.mean(weighted_in * stream, axis=-1, keepdims=True)
    )
    head_part = (
        g_low[:, :inner_width],
        g_low[:, inner_width : 2 * inner_width],
        g_low[:, 2 * inner_width :],
        g_conv_w[:, :inner_width],
        g_conv_b[:inner_width],
        g_dt_bias,
        g_a_log,
        g_skip,
        g_gate_gain,
    )
    shared_part = (g_norm_gain, g_w_bc, g_conv_w[:, inner_width:], g_conv_b[inner_width:])
    return (grad_stream, head_part, shared_part, g_w_out)


def pack_rows(members, width, multiple):
    rows = jnp.concatenate([member.reshape(-1, width) for member in members], axis=0)
    return jnp.pad(rows, ((0, -rows.shape[0] % multiple), (0, 0)))


def unpack_rows(rows, shapes, width):
    pieces = []
    start = 0
    for shape in shapes:
        count = math.prod(shape) // width
        pieces.append(rows[start : start + count].reshape(shape))
        start += count
    return tuple(pieces)


def reduce_grads(head_part, norm_part, bc_part, tick_count):
    bc_all = lax.all_gather(bc_part.astype(jnp.bfloat16), "seq")
    bc_sum = bc_all[0].astype(jnp.float32)
    for index in range(1, bc_all.shape[0]):
        bc_sum = bc_sum + bc_all[index].astype(jnp.float32)
    anchor = bc_all[0, 0, 0].astype(jnp.float32) * 0.0
    summed = lax.psum(
        tuple(member.astype(jnp.bfloat16) for member in (head_part[0] + anchor,) + head_part[1:3]),
        "seq",
    )
    head_sum = tuple(member.astype(jnp.float32) for member in summed) + tuple(
        lax.psum(member.astype(jnp.bfloat16), "seq").astype(jnp.float32)
        for member in head_part[3:]
    )
    bc_rows = head_gather(bc_sum, (0, 0, 1), 4 * tick_count + 1)
    norm_sum = lax.psum(norm_part, ("seq", "head"))
    return (head_sum, norm_sum, bc_rows.reshape(-1, bc_rows.shape[-1]))


def store_slot(buffer, value, slot_index, is_valid):
    current = lax.dynamic_index_in_dim(buffer, slot_index, 0, False)
    return lax.dynamic_update_index_in_dim(
        buffer, jnp.where(is_valid, value, current), slot_index, 0
    )


def on_device(
    inputs,
    cotangent,
    starts,
    live,
    norm_gain,
    w_gate,
    w_in,
    w_bc,
    w_dt,
    conv_x,
    conv_x_bias,
    conv_bc,
    conv_bc_bias,
    dt_bias,
    a_log,
    skip,
    gate_gain,
    w_out,
):
    section_count = lax.axis_size("section")
    section_index = lax.axis_index("section")
    micro_count = inputs.shape[0]
    tick_count = micro_count + section_count - 1
    w_main = jnp.concatenate([w_gate[0], w_in[0], w_bc[0], w_dt[0]], axis=1)
    w_low = jnp.concatenate([w_gate[0], w_in[0], w_dt[0]], axis=1)
    conv_weight = jnp.concatenate([conv_x[0], conv_bc[0]], axis=1).astype(jnp.float32)
    conv_bias = jnp.concatenate([conv_x_bias[0], conv_bc_bias[0]], axis=0)
    layer_weights = (
        norm_gain[0],
        w_main,
        w_low,
        w_bc[0],
        conv_weight,
        conv_bias,
        dt_bias[0],
        a_log[0],
        skip[0],
        gate_gain[0],
        w_out[0],
    )
    row_shape = inputs.shape[1:]
    outputs_all = jnp.zeros((micro_count,) + row_shape, jnp.float32)
    arrived = jnp.zeros(row_shape, jnp.float32)
    ticks = []
    for tick_index in range(tick_count):
        slot_index = tick_index - section_index
        is_valid = (slot_index >= 0) & (slot_index < micro_count)
        clipped = jnp.clip(slot_index, 0, micro_count - 1)
        fresh_rows = lax.dynamic_index_in_dim(inputs, clipped, 0, False).astype(jnp.float32)
        stream = jnp.where(section_index == 0, fresh_rows, arrived)
        start_marks = lax.dynamic_index_in_dim(starts, clipped, 0, False)
        alive_mask = lax.dynamic_index_in_dim(live, clipped, 0, False).astype(jnp.float32)
        result, saved = mixer_forward(
            stream,
            start_marks,
            alive_mask,
            layer_weights,
            (tick_index, -1, micro_count),
            (tick_index, tick_count + tick_index),
        )
        outputs_all = store_slot(outputs_all, result, clipped, is_valid)
        ticks.append((clipped, is_valid, saved))
        if tick_index + 1 < tick_count:
            arrived = shifted(result, "section", 1)
    back_arrived = jnp.zeros(row_shape, jnp.float32)
    input_grads = jnp.zeros((micro_count,) + row_shape, jnp.float32)
    head_count = lax.axis_size("head")
    bc_box = []
    head_total = ()
    shared_total = ()
    for tick_index in range(tick_count):
        clipped, is_valid, saved = ticks[tick_count - 1 - tick_index]
        outer_grad = lax.dynamic_index_in_dim(cotangent, clipped, 0, False).astype(jnp.float32)
        grad_next = jnp.where(section_index == section_count - 1, outer_grad, back_arrived)
        mask_value = is_valid.astype(jnp.float32)
        hook = None
        if tick_index + 1 == tick_count:

            def hook(bc_local, mask_value=mask_value, earlier=shared_total):
                totals = tuple(
                    (prev + member * mask_value) if earlier else member * mask_value
                    for prev, member in zip(earlier[1:] or bc_local, bc_local)
                )
                rows = pack_rows(totals, totals[0].shape[-1], 8 * head_count)
                part = head_scatter(
                    rows.reshape(head_count, -1, rows.shape[-1]), (0, 0, 1), 4 * tick_count
                )
                bc_box.append((part, [member.shape for member in totals]))
                return part[0, 0] * 0.0

        grad_stream, head_part, shared_part, out_part = mixer_backward(
            grad_next,
            layer_weights,
            saved,
            mask_value,
            (tick_count - 1 - tick_index, -1, micro_count),
            (2 * tick_count + tick_index, 3 * tick_count + tick_index),
            hook,
        )
        if tick_index == 0:
            out_total = out_part
        else:
            out_total = out_total + out_part
        if tick_index + 1 == tick_count:
            out_total = lax.psum(out_total.astype(jnp.bfloat16), "seq")
        head_part = tuple((member * mask_value for member in head_part))
        shared_part = tuple((member * mask_value for member in shared_part))
        if tick_index == 0:
            head_total = head_part
            shared_total = shared_part
        else:
            head_total = tuple((former + latter for former, latter in zip(head_total, head_part)))
            shared_total = tuple(
                (former + latter for former, latter in zip(shared_total, shared_part))
            )
        input_grads = store_slot(input_grads, grad_stream, clipped, is_valid)
        if tick_index + 1 < tick_count:
            back_arrived = shifted(grad_stream.astype(jnp.bfloat16), "section", -1).astype(
                grad_stream.dtype
            )
    anchor = out_total[0, 0].astype(jnp.float32) * 0.0
    head_total = (head_total[0] + anchor,) + head_total[1:]
    bc_part, bc_shapes = bc_box[0]
    bc_part = bc_part + anchor
    head_total, norm_sum, bc_rows = reduce_grads(head_total, shared_total[0], bc_part, tick_count)
    shared_total = (norm_sum,) + unpack_rows(bc_rows, bc_shapes, bc_rows.shape[-1])
    head_total = head_total[:3] + (out_total.astype(jnp.float32),) + head_total[3:]
    return (
        outputs_all[None],
        input_grads[None],
        shared_total[0][None],
        head_total[0][None],
        head_total[1][None],
        shared_total[1][None],
        head_total[2][None],
        head_total[4][None],
        head_total[5][None],
        shared_total[2][None],
        shared_total[3][None],
        head_total[6][None],
        head_total[7][None],
        head_total[8][None],
        head_total[9][None],
        head_total[3][None],
    )


def solution(mesh):
    return jax.shard_map(
        on_device,
        mesh=mesh,
        in_specs=(
            P(None, ("seq", "head"), None),
            P(None, ("seq", "head"), None),
            P(None, "seq"),
            P(None, "seq"),
            P("section", None),
            P("section", None, "head"),
            P("section", None, "head"),
            P("section", None, None),
            P("section", None, "head"),
            P("section", None, "head"),
            P("section", "head"),
            P("section", None, None),
            P("section", None),
            P("section", "head"),
            P("section", "head"),
            P("section", "head"),
            P("section", "head"),
            P("section", "head", None),
        ),
        out_specs=(
            P("section", None, ("seq", "head"), None),
            P("section", None, ("seq", "head"), None),
            P("section", None),
            P("section", None, "head"),
            P("section", None, "head"),
            P("section", None, None),
            P("section", None, "head"),
            P("section", None, "head"),
            P("section", "head"),
            P("section", None, None),
            P("section", None),
            P("section", "head"),
            P("section", "head"),
            P("section", "head"),
            P("section", "head"),
            P("section", "head", None),
        ),
        check_vma=False,
    )
```

```python
from functools import partial

import functools
import math

import jax
import jax.numpy as jnp
from jax import lax
from jax.experimental import pallas as pl
from jax.experimental.pallas import tpu as pltpu
from jax.sharding import PartitionSpec as P

DI = 4096
P_SIZE = 64
N = 128
KW = 4
SCAN_BLOCK = 256


MESH = pl.DeviceIdType.MESH


def _tick_valid(offset, sign, count):
    slot = offset + sign * lax.axis_index("section")
    return jnp.logical_and(slot >= 0, slot < count)


def _enter(barrier, h, n):
    @pl.when(h > 0)
    def _():
        pl.semaphore_signal(barrier, 1, device_id={"head": h - 1}, device_id_type=MESH)

    @pl.when(h < n - 1)
    def _():
        pl.semaphore_signal(barrier, 1, device_id={"head": h + 1}, device_id_type=MESH)

    @pl.when(jnp.logical_and(h > 0, h < n - 1))
    def _():
        pl.semaphore_wait(barrier, 2)

    @pl.when(jnp.logical_or(h == 0, h == n - 1))
    def _():
        pl.semaphore_wait(barrier, 1)


def gather_body(n, tick, x_ref, o_ref, land, send_r, send_l, recv):
    h = lax.axis_index("head")
    valid = _tick_valid(*tick)

    @pl.when(valid)
    def _():
        _enter(pltpu.get_barrier_semaphore(), h, n)

        def copy_right(s, k):
            src = x_ref if s == 0 else land.at[k]
            return pltpu.make_async_remote_copy(
                src_ref=src, dst_ref=land.at[k], send_sem=send_r.at[s], recv_sem=recv.at[k],
                device_id={"head": h + 1}, device_id_type=MESH)

        def copy_left(s, k):
            src = x_ref if s == 0 else land.at[k]
            return pltpu.make_async_remote_copy(
                src_ref=src, dst_ref=land.at[k], send_sem=send_l.at[s], recv_sem=recv.at[k],
                device_id={"head": h - 1}, device_id_type=MESH)

        for s in range(n):
            k_r = h - s
            k_l = h + s
            if s >= 1:
                @pl.when(k_r >= 0)
                def _():
                    pltpu.make_async_remote_copy(
                        src_ref=land.at[k_r], dst_ref=land.at[k_r], send_sem=send_r.at[0],
                        recv_sem=recv.at[k_r], device_id={"head": h}, device_id_type=MESH
                    ).wait_recv()

                @pl.when(k_l <= n - 1)
                def _():
                    pltpu.make_async_remote_copy(
                        src_ref=land.at[k_l], dst_ref=land.at[k_l], send_sem=send_l.at[0],
                        recv_sem=recv.at[k_l], device_id={"head": h}, device_id_type=MESH
                    ).wait_recv()
            if s <= n - 2:
                @pl.when(jnp.logical_and(k_r >= 0, h < n - 1))
                def _():
                    copy_right(s, k_r).start()

                @pl.when(jnp.logical_and(k_l <= n - 1, h > 0))
                def _():
                    copy_left(s, k_l).start()
        land[h] = x_ref[...]
        for s in range(n - 1):
            k_r = h - s
            k_l = h + s

            @pl.when(jnp.logical_and(k_r >= 0, h < n - 1))
            def _():
                copy_right(s, k_r).wait_send()

            @pl.when(jnp.logical_and(k_l <= n - 1, h > 0))
            def _():
                copy_left(s, k_l).wait_send()
        o_ref[...] = land[...]

    @pl.when(jnp.logical_not(valid))
    def _():
        o_ref[...] = jnp.zeros(o_ref.shape, o_ref.dtype)


def head_gather(x, tick, cid):
    n = lax.axis_size("head")
    rows, cols = x.shape
    return pl.pallas_call(
        functools.partial(gather_body, n, tick),
        out_shape=jax.ShapeDtypeStruct((n, rows, cols), x.dtype),
        in_specs=[pl.BlockSpec(memory_space=pltpu.VMEM)],
        out_specs=pl.BlockSpec(memory_space=pltpu.VMEM),
        scratch_shapes=[
            pltpu.VMEM((n, rows, cols), x.dtype),
            pltpu.SemaphoreType.DMA((n,)),
            pltpu.SemaphoreType.DMA((n,)),
            pltpu.SemaphoreType.DMA((n,)),
        ],
        compiler_params=pltpu.CompilerParams(collective_id=cid, has_side_effects=True),
    )(x)


def scatter_body(n, tick, p_ref, o_ref, recv_l, recv_r, send_l, send_r, ssem_l, ssem_r, rsem_l, rsem_r):
    h = lax.axis_index("head")
    valid = _tick_valid(*tick)
    link = send_r.dtype

    @pl.when(valid)
    def _():
        _enter(pltpu.get_barrier_semaphore(), h, n)

        def to_right(k):
            return pltpu.make_async_remote_copy(
                src_ref=send_r.at[k], dst_ref=recv_l.at[k], send_sem=ssem_r.at[k],
                recv_sem=rsem_l.at[k], device_id={"head": h + 1}, device_id_type=MESH)

        def to_left(k):
            return pltpu.make_async_remote_copy(
                src_ref=send_l.at[k], dst_ref=recv_r.at[k], send_sem=ssem_l.at[k],
                recv_sem=rsem_r.at[k], device_id={"head": h - 1}, device_id_type=MESH)

        def rightward(s):
            k_r = n - 1 - s

            @pl.when(k_r > h)
            def _():
                @pl.when(h > 0)
                def _():
                    to_right(k_r).wait_recv()
                    send_r[k_r] = (p_ref[k_r] + recv_l[k_r].astype(jnp.float32)).astype(link)

                @pl.when(h == 0)
                def _():
                    send_r[k_r] = p_ref[k_r].astype(link)

                to_right(k_r).start()

        def leftward(s):
            k_l = s

            @pl.when(k_l < h)
            def _():
                @pl.when(h < n - 1)
                def _():
                    to_left(k_l).wait_recv()
                    send_l[k_l] = (p_ref[k_l] + recv_r[k_l].astype(jnp.float32)).astype(link)

                @pl.when(h == n - 1)
                def _():
                    send_l[k_l] = p_ref[k_l].astype(link)

                to_left(k_l).start()

        for s in range(n - 1):

            @pl.when(2 * h < n)
            def _():
                rightward(s)
                leftward(s)

            @pl.when(2 * h >= n)
            def _():
                leftward(s)
                rightward(s)

        total = p_ref[h]

        @pl.when(h > 0)
        def _():
            to_right(h).wait_recv()

        @pl.when(h < n - 1)
        def _():
            to_left(h).wait_recv()

        left_part = jnp.where(h > 0, recv_l[h].astype(jnp.float32), 0.0)
        right_part = jnp.where(h < n - 1, recv_r[h].astype(jnp.float32), 0.0)
        o_ref[...] = (total + left_part + right_part).astype(o_ref.dtype)
        for s in range(n - 1):
            k_r = n - 1 - s
            k_l = s

            @pl.when(k_r > h)
            def _():
                to_right(k_r).wait_send()

            @pl.when(k_l < h)
            def _():
                to_left(k_l).wait_send()

    @pl.when(jnp.logical_not(valid))
    def _():
        o_ref[...] = jnp.zeros(o_ref.shape, o_ref.dtype)


def head_scatter(parts, tick, cid, link=jnp.bfloat16):
    n = lax.axis_size("head")
    _, rows, cols = parts.shape
    return pl.pallas_call(
        functools.partial(scatter_body, n, tick),
        out_shape=jax.ShapeDtypeStruct((rows, cols), jnp.float32),
        in_specs=[pl.BlockSpec(memory_space=pltpu.VMEM)],
        out_specs=pl.BlockSpec(memory_space=pltpu.VMEM),
        scratch_shapes=[
            pltpu.VMEM((n, rows, cols), link),
            pltpu.VMEM((n, rows, cols), link),
            pltpu.VMEM((n, rows, cols), link),
            pltpu.VMEM((n, rows, cols), link),
            pltpu.SemaphoreType.DMA((n,)),
            pltpu.SemaphoreType.DMA((n,)),
            pltpu.SemaphoreType.DMA((n,)),
            pltpu.SemaphoreType.DMA((n,)),
        ],
        compiler_params=pltpu.CompilerParams(collective_id=cid, has_side_effects=True),
    )(parts)


norm_eps = 1e-05
far_below = -1e30
highest = lax.Precision.DEFAULT


def shifted(value, axis, by):
    count = lax.axis_size(axis)
    pairs = [(i, i + by) for i in range(count) if 0 <= i + by < count]
    return lax.ppermute(value, axis, pairs)


def entering(value, axis, combine, identity):
    count, mine = (lax.axis_size(axis), lax.axis_index(axis))
    everything = jax.tree.map(lambda part: lax.all_gather(part, axis), value)
    before = jax.tree.map(
        lambda part, zero: jnp.broadcast_to(jnp.asarray(zero, part.dtype), part.shape),
        value,
        identity,
    )
    for k in range(count - 1):
        reached = k < mine
        new = combine(before, jax.tree.map(lambda part: part[k], everything))
        before = jax.tree.map(lambda a, b: jnp.where(reached, a, b), new, before)
    return before


def entering_2(value, axis, join, neutral):
    count = lax.axis_size(axis)
    place = lax.axis_index(axis)
    ahead = count - 1 - place
    gathered = jax.tree.map(
        lambda a, kind: lax.all_gather(a.astype(kind), axis),
        value,
        jax.tree.map(lambda a: jnp.bfloat16 if a.dtype == jnp.float32 else a.dtype, value),
    )
    state = jax.tree.map(lambda a, e: jnp.zeros_like(a) + jnp.asarray(e, a.dtype), value, neutral)
    for lap in range(count - 1):
        source = count - 1 - lap
        new = join(
            state,
            jax.tree.map(lambda a, own: a[source].astype(own.dtype), gathered, value),
        )
        active = lap < ahead
        state = jax.tree.map(lambda a, b: jnp.where(active, a, b), new, state)
    return state


def rms_scale(values):
    return lax.rsqrt(jnp.mean(values * values, axis=-1, keepdims=True) + norm_eps)


def silu_slope(values):
    logistic = jax.nn.sigmoid(values)
    return logistic * (1.0 + values * (1.0 - logistic))


def causal_conv(extended, marks_ext, weight, conv_bias):
    tap_count = weight.shape[0]
    length = extended.shape[0] - tap_count + 1
    counts = jnp.cumsum(marks_ext)
    conv_sum = jnp.zeros((length, extended.shape[1]), jnp.float32) + conv_bias
    for tap_index in range(tap_count):
        linked = (counts[tap_count - 1 :] == counts[tap_index : tap_index + length]).astype(
            jnp.float32
        )
        conv_sum = (
            conv_sum
            + linked[:, None] * weight[tap_index] * extended[tap_index : tap_index + length]
        )
    return conv_sum


def prepare(extended, dt_pre, marks_ext, alive_mask, conv_weight, conv_bias, dt_bias, a_log):
    inner_width = dt_pre.shape[1] * P_SIZE
    activated = jax.nn.silu(causal_conv(extended, marks_ext, conv_weight, conv_bias))
    inner_act = activated[:, :inner_width] * alive_mask[:, None]
    b_mat = activated[:, inner_width : inner_width + N]
    c_mat = activated[:, inner_width + N :]
    step_size = jax.nn.softplus(dt_pre + dt_bias) * alive_mask[:, None]
    log_decay = -step_size * jnp.exp(a_log)
    return (inner_act, step_size, log_decay, b_mat, c_mat)


def block_terms(inner_act, step_size, log_decay, b_mat, start_marks):
    blocks = inner_act.shape[0] // SCAN_BLOCK
    head_count = step_size.shape[1]
    x_blocks = inner_act.reshape(blocks, SCAN_BLOCK, head_count, P_SIZE)
    dt_blocks = step_size.reshape(blocks, SCAN_BLOCK, head_count)
    cum_decay = jnp.cumsum(log_decay.reshape(blocks, SCAN_BLOCK, head_count), axis=1)
    mark_count = jnp.cumsum(start_marks.reshape(blocks, SCAN_BLOCK), axis=1)
    b_blocks = b_mat.reshape(blocks, SCAN_BLOCK, N)
    last_cum = cum_decay[:, -1]
    last_mark = mark_count[:, -1]
    same_end = (mark_count == last_mark[:, None]).astype(jnp.float32)
    end_weight = jnp.exp(last_cum[:, None, :] - cum_decay) * same_end[:, :, None] * dt_blocks
    block_states = jnp.einsum(
        "cjh,cjhp,cjn->chpn", end_weight, x_blocks, b_blocks, precision=highest
    )
    block_decay = jnp.exp(last_cum) * (last_mark == 0).astype(jnp.float32)[:, None]
    return (block_decay, block_states, cum_decay, mark_count, x_blocks, dt_blocks)


def compose_blocks(block_decay, block_states, start_state):
    chain_state = start_state
    incoming = []
    for block_index in range(block_decay.shape[0]):
        incoming.append(chain_state)
        chain_state = (
            block_decay[block_index][:, None, None] * chain_state + block_states[block_index]
        )
    return (chain_state, jnp.stack(incoming))


def block_output(block_parts, b_mat, c_mat, skip, incoming):
    block_decay, block_states, cum_decay, mark_count, x_blocks, dt_blocks = block_parts
    blocks = cum_decay.shape[0]
    head_count = cum_decay.shape[2]
    b_blocks = b_mat.reshape(blocks, SCAN_BLOCK, N)
    c_blocks = c_mat.reshape(blocks, SCAN_BLOCK, N)
    inner_prod = jnp.einsum("cin,cjn->cij", c_blocks, b_blocks, precision=highest)
    arange_pos = jnp.arange(SCAN_BLOCK)
    linked = (arange_pos[:, None] >= arange_pos[None, :])[None] & (
        mark_count[:, :, None] == mark_count[:, None, :]
    )
    spread = jnp.where(
        linked[..., None], cum_decay[:, :, None, :] - cum_decay[:, None, :, :], far_below
    )
    weights = jnp.exp(spread) * inner_prod[..., None] * dt_blocks[:, None, :, :]
    y_intra = jnp.einsum(
        "cijh,cjhp->cihp", weights, x_blocks, precision=lax.Precision.DEFAULT
    )
    carry_in = jnp.exp(cum_decay) * (mark_count == 0).astype(jnp.float32)[:, :, None]
    y_inter = (
        jnp.einsum("cin,chpn->cihp", c_blocks, incoming, precision=highest) * carry_in[..., None]
    )
    mixed_out = y_intra + y_inter + skip[None, None, :, None] * x_blocks
    return mixed_out.reshape(blocks * SCAN_BLOCK, head_count * P_SIZE)


def local_front(marks_ext, alive_mask, extended, dt_pre, conv_weight, conv_bias, dt_bias, a_log):
    inner_act, step_size, log_decay, b_mat, c_mat = prepare(
        extended, dt_pre, marks_ext, alive_mask, conv_weight, conv_bias, dt_bias, a_log
    )
    block_parts = block_terms(inner_act, step_size, log_decay, b_mat, marks_ext[KW - 1 :])
    zero_state = jnp.zeros(block_parts[1].shape[1:], jnp.float32)
    total_state, _ = compose_blocks(block_parts[0], block_parts[1], zero_state)
    total_decay = jnp.prod(block_parts[0], axis=0)
    return (block_parts, b_mat, c_mat, total_decay, total_state)


def local_rear(block_parts, b_mat, c_mat, skip, start_state):
    _, incoming = compose_blocks(block_parts[0], block_parts[1], start_state)
    return block_output(block_parts, b_mat, c_mat, skip, incoming)


def local_pass(
    marks_ext,
    alive_mask,
    extended,
    dt_pre,
    conv_weight,
    conv_bias,
    dt_bias,
    a_log,
    skip,
    start_state,
):
    block_parts, b_mat, c_mat, total_decay, total_state = local_front(
        marks_ext, alive_mask, extended, dt_pre, conv_weight, conv_bias, dt_bias, a_log
    )
    return (local_rear(block_parts, b_mat, c_mat, skip, start_state), total_decay, total_state)


def chain_combine(earlier, later):
    return (earlier[0] * later[0], later[0][:, None, None] * earlier[1] + later[1])


def extend(pre_conv, start_marks, edge_rows, edge_marks):
    extended = jnp.concatenate([edge_rows, pre_conv], axis=0)
    marks_ext = jnp.concatenate([edge_marks.astype(jnp.int32), start_marks], axis=0)
    return (extended, marks_ext)


def mixer_forward(stream, start_marks, alive_mask, layer_weights, tick, ids):
    (
        norm_gain,
        w_main,
        w_low,
        w_bc,
        conv_weight,
        conv_bias,
        dt_bias,
        a_log,
        skip,
        gate_gain,
        w_out,
    ) = layer_weights
    inner_width = w_out.shape[0]
    normed = (stream * rms_scale(stream) * norm_gain).astype(jnp.bfloat16)
    gathered = head_gather(normed, tick, ids[0])
    gathered = gathered.reshape(-1, gathered.shape[-1])
    projected = jnp.dot(gathered, w_main, preferred_element_type=jnp.float32)
    gate_pre = projected[:, :inner_width]
    pre_conv = projected[:, inner_width : 2 * inner_width + 2 * N]
    dt_pre = projected[:, 2 * inner_width + 2 * N :]
    marks_float = start_marks.astype(jnp.float32)
    tail_from = pre_conv.shape[0] - KW + 1
    edge_parts = shifted((pre_conv[tail_from:], marks_float[tail_from:]), "seq", 1)
    extended, marks_ext = extend(pre_conv, start_marks, edge_parts[0], edge_parts[1])
    front_fn = partial(local_front, marks_ext, alive_mask)
    front_out, front_pull = jax.vjp(
        front_fn, extended, dt_pre, conv_weight, conv_bias, dt_bias, a_log
    )
    block_parts, b_mat, c_mat, total_decay, total_state = front_out
    neutral = (jnp.ones_like(total_decay), jnp.zeros_like(total_state))
    prefix = entering((total_decay, total_state), "seq", chain_combine, neutral)
    start_state = prefix[1]
    mixed_out, rear_pull = jax.vjp(local_rear, block_parts, b_mat, c_mat, skip, start_state)
    silu_gate = jax.nn.silu(gate_pre)
    gated_mix = mixed_out * silu_gate
    square_total = lax.psum(jnp.sum(gated_mix * gated_mix, axis=-1), "head")
    scale_out = lax.rsqrt(square_total / DI + norm_eps)
    normed_out = (gated_mix * scale_out[:, None] * gate_gain).astype(jnp.bfloat16)
    head_count = lax.axis_size("head")
    branch = head_scatter(
        jnp.dot(normed_out, w_out, preferred_element_type=jnp.float32).reshape(
            head_count, -1, w_out.shape[1]
        ),
        tick,
        ids[1],
    )
    saved = (
        stream,
        gathered,
        gate_pre,
        mixed_out,
        silu_gate,
        gated_mix,
        scale_out,
        normed_out,
        total_decay,
        start_state,
        front_pull,
        rear_pull,
    )
    return stream + branch, saved


def mixer_backward(grad_next, layer_weights, saved, mask_value, tick, ids, hook=None):
    (
        norm_gain,
        w_main,
        w_low,
        w_bc,
        conv_weight,
        conv_bias,
        dt_bias,
        a_log,
        skip,
        gate_gain,
        w_out,
    ) = layer_weights
    (
        stream,
        gathered,
        gate_pre,
        mixed_out,
        silu_gate,
        gated_mix,
        scale_out,
        normed_out,
        total_decay,
        start_state,
        front_pull,
        rear_pull,
    ) = saved
    inner_width = w_out.shape[0]
    grad_branch = grad_next.astype(jnp.bfloat16)
    shard_rows = head_gather(grad_branch, tick, ids[0])
    shard_rows = shard_rows.reshape(-1, shard_rows.shape[-1])
    g_w_out = lax.dot_general(
        normed_out, shard_rows, (((0,), (0,)), ((), ())), preferred_element_type=jnp.float32
    ) * mask_value
    grad_normed = lax.dot_general(
        shard_rows, w_out, (((1,), (1,)), ((), ())), preferred_element_type=jnp.float32
    )
    weighted = grad_normed * gate_gain
    g_gate_gain = jnp.sum(grad_normed * gated_mix * scale_out[:, None], axis=0)
    cross_sum = lax.psum(jnp.sum(weighted * gated_mix, axis=-1), "head")
    grad_gated = (
        scale_out[:, None] * weighted - gated_mix * (scale_out**3 * cross_sum / DI)[:, None]
    )
    grad_mixed = grad_gated * silu_gate
    grad_gate = (grad_gated * mixed_out * silu_slope(gate_pre)).astype(jnp.bfloat16)
    g_parts, g_b_mat, g_c_mat, g_skip, g_start = rear_pull(grad_mixed)
    neutral = (jnp.ones_like(total_decay), jnp.zeros_like(g_start))
    suffix = entering_2((total_decay, g_start), "seq", chain_combine, neutral)
    after_state = suffix[1]
    grad_decay = jnp.sum(after_state * start_state, axis=(1, 2))
    grad_ext, grad_dt_pre, g_conv_w, g_conv_b, g_dt_bias, g_a_log = front_pull(
        (g_parts, g_b_mat, g_c_mat, grad_decay, after_state)
    )
    returned = shifted(grad_ext[: KW - 1], "seq", -1)
    grad_pre = grad_ext[KW - 1 :]
    tail_from = grad_pre.shape[0] - KW + 1
    grad_pre = jnp.concatenate([grad_pre[:tail_from], grad_pre[tail_from:] + returned], axis=0)
    grad_inner = grad_pre[:, :inner_width].astype(jnp.bfloat16)
    grad_bc = grad_pre[:, inner_width:]
    grad_low = jnp.concatenate([grad_gate, grad_inner, grad_dt_pre.astype(jnp.bfloat16)], axis=1)
    w_bc_float = w_bc.astype(jnp.float32)
    g_low = lax.dot_general(
        gathered, grad_low, (((0,), (0,)), ((), ())), preferred_element_type=jnp.float32
    )
    g_w_bc = lax.dot_general(
        gathered,
        grad_bc.astype(jnp.bfloat16),
        (((0,), (0,)), ((), ())),
        preferred_element_type=jnp.float32,
    )
    main_term = lax.dot_general(
        grad_low, w_low, (((1,), (1,)), ((), ())), preferred_element_type=jnp.float32
    )
    side_term = lax.dot_general(
        grad_bc.astype(jnp.bfloat16),
        w_bc,
        (((1,), (1,)), ((), ())),
        preferred_element_type=jnp.float32,
    )
    head_count = lax.axis_size("head")
    lead = 0.0
    if hook is not None:
        lead = hook((g_w_bc, g_conv_w[:, inner_width:], g_conv_b[inner_width:]))
    grad_normed_in = head_scatter(
        (main_term + side_term + lead).reshape(head_count, -1, main_term.shape[1]), tick, ids[1]
    )
    scale_in = rms_scale(stream)
    g_norm_gain = jnp.sum(grad_normed_in * stream * scale_in, axis=0)
    weighted_in = grad_normed_in * norm_gain
    grad_stream = (
        grad_next
        + scale_in * weighted_in
        - stream * scale_in**3 * jnp.mean(weighted_in * stream, axis=-1, keepdims=True)
    )
    head_part = (
        g_low[:, :inner_width],
        g_low[:, inner_width : 2 * inner_width],
        g_low[:, 2 * inner_width :],
        g_conv_w[:, :inner_width],
        g_conv_b[:inner_width],
        g_dt_bias,
        g_a_log,
        g_skip,
        g_gate_gain,
    )
    shared_part = (g_norm_gain, g_w_bc, g_conv_w[:, inner_width:], g_conv_b[inner_width:])
    return (grad_stream, head_part, shared_part, g_w_out)


def pack_rows(members, width, multiple):
    rows = jnp.concatenate([member.reshape(-1, width) for member in members], axis=0)
    return jnp.pad(rows, ((0, -rows.shape[0] % multiple), (0, 0)))


def unpack_rows(rows, shapes, width):
    pieces = []
    start = 0
    for shape in shapes:
        count = math.prod(shape) // width
        pieces.append(rows[start : start + count].reshape(shape))
        start += count
    return tuple(pieces)


def reduce_grads(head_part, norm_part, bc_part, tick_count):
    bc_all = lax.all_gather(bc_part.astype(jnp.bfloat16), "seq")
    bc_sum = bc_all[0].astype(jnp.float32)
    for index in range(1, bc_all.shape[0]):
        bc_sum = bc_sum + bc_all[index].astype(jnp.float32)
    anchor = bc_all[0, 0, 0].astype(jnp.float32) * 0.0
    summed = lax.psum(
        tuple(member.astype(jnp.bfloat16) for member in (head_part[0] + anchor,) + head_part[1:3]),
        "seq",
    )
    head_sum = tuple(member.astype(jnp.float32) for member in summed) + tuple(
        lax.psum(member.astype(jnp.bfloat16), "seq").astype(jnp.float32)
        for member in head_part[3:]
    )
    bc_rows = head_gather(bc_sum, (0, 0, 1), 4 * tick_count + 1)
    norm_sum = lax.psum(norm_part, ("seq", "head"))
    return (head_sum, norm_sum, bc_rows.reshape(-1, bc_rows.shape[-1]))


def store_slot(buffer, value, slot_index, is_valid):
    current = lax.dynamic_index_in_dim(buffer, slot_index, 0, False)
    return lax.dynamic_update_index_in_dim(
        buffer, jnp.where(is_valid, value, current), slot_index, 0
    )


def on_device(
    inputs,
    cotangent,
    starts,
    live,
    norm_gain,
    w_gate,
    w_in,
    w_bc,
    w_dt,
    conv_x,
    conv_x_bias,
    conv_bc,
    conv_bc_bias,
    dt_bias,
    a_log,
    skip,
    gate_gain,
    w_out,
):
    section_count = lax.axis_size("section")
    section_index = lax.axis_index("section")
    micro_count = inputs.shape[0]
    tick_count = micro_count + section_count - 1
    w_main = jnp.concatenate([w_gate[0], w_in[0], w_bc[0], w_dt[0]], axis=1)
    w_low = jnp.concatenate([w_gate[0], w_in[0], w_dt[0]], axis=1)
    conv_weight = jnp.concatenate([conv_x[0], conv_bc[0]], axis=1).astype(jnp.float32)
    conv_bias = jnp.concatenate([conv_x_bias[0], conv_bc_bias[0]], axis=0)
    layer_weights = (
        norm_gain[0],
        w_main,
        w_low,
        w_bc[0],
        conv_weight,
        conv_bias,
        dt_bias[0],
        a_log[0],
        skip[0],
        gate_gain[0],
        w_out[0],
    )
    row_shape = inputs.shape[1:]
    outputs_all = jnp.zeros((micro_count,) + row_shape, jnp.float32)
    arrived = jnp.zeros(row_shape, jnp.float32)
    ticks = []
    for tick_index in range(tick_count):
        slot_index = tick_index - section_index
        is_valid = (slot_index >= 0) & (slot_index < micro_count)
        clipped = jnp.clip(slot_index, 0, micro_count - 1)
        fresh_rows = lax.dynamic_index_in_dim(inputs, clipped, 0, False).astype(jnp.float32)
        stream = jnp.where(section_index == 0, fresh_rows, arrived)
        start_marks = lax.dynamic_index_in_dim(starts, clipped, 0, False)
        alive_mask = lax.dynamic_index_in_dim(live, clipped, 0, False).astype(jnp.float32)
        result, saved = mixer_forward(
            stream,
            start_marks,
            alive_mask,
            layer_weights,
            (tick_index, -1, micro_count),
            (tick_index, tick_count + tick_index),
        )
        outputs_all = store_slot(outputs_all, result, clipped, is_valid)
        ticks.append((clipped, is_valid, saved))
        if tick_index + 1 < tick_count:
            arrived = shifted(result, "section", 1)
    back_arrived = jnp.zeros(row_shape, jnp.float32)
    input_grads = jnp.zeros((micro_count,) + row_shape, jnp.float32)
    head_count = lax.axis_size("head")
    bc_box = []
    head_total = ()
    shared_total = ()
    for tick_index in range(tick_count):
        clipped, is_valid, saved = ticks[tick_count - 1 - tick_index]
        outer_grad = lax.dynamic_index_in_dim(cotangent, clipped, 0, False).astype(jnp.float32)
        grad_next = jnp.where(section_index == section_count - 1, outer_grad, back_arrived)
        mask_value = is_valid.astype(jnp.float32)
        hook = None
        if tick_index + 1 == tick_count:

            def hook(bc_local, mask_value=mask_value, earlier=shared_total):
                totals = tuple(
                    (prev + member * mask_value) if earlier else member * mask_value
                    for prev, member in zip(earlier[1:] or bc_local, bc_local)
                )
                rows = pack_rows(totals, totals[0].shape[-1], 8 * head_count)
                part = head_scatter(
                    rows.reshape(head_count, -1, rows.shape[-1]), (0, 0, 1), 4 * tick_count
                )
                bc_box.append((part, [member.shape for member in totals]))
                return part[0, 0] * 0.0

        grad_stream, head_part, shared_part, out_part = mixer_backward(
            grad_next,
            layer_weights,
            saved,
            mask_value,
            (tick_count - 1 - tick_index, -1, micro_count),
            (2 * tick_count + tick_index, 3 * tick_count + tick_index),
            hook,
        )
        if tick_index == 0:
            out_total = out_part
        else:
            out_total = out_total + out_part
        if tick_index + 1 == tick_count:
            out_total = lax.psum(out_total.astype(jnp.bfloat16), "seq")
        head_part = tuple((member * mask_value for member in head_part))
        shared_part = tuple((member * mask_value for member in shared_part))
        if tick_index == 0:
            head_total = head_part
            shared_total = shared_part
        else:
            head_total = tuple((former + latter for former, latter in zip(head_total, head_part)))
            shared_total = tuple(
                (former + latter for former, latter in zip(shared_total, shared_part))
            )
        input_grads = store_slot(input_grads, grad_stream, clipped, is_valid)
        if tick_index + 1 < tick_count:
            back_arrived = shifted(grad_stream.astype(jnp.bfloat16), "section", -1).astype(
                grad_stream.dtype
            )
    anchor = out_total[0, 0].astype(jnp.float32) * 0.0
    head_total = (head_total[0] + anchor,) + head_total[1:]
    bc_part, bc_shapes = bc_box[0]
    bc_part = bc_part + anchor
    head_total, norm_sum, bc_rows = reduce_grads(head_total, shared_total[0], bc_part, tick_count)
    shared_total = (norm_sum,) + unpack_rows(bc_rows, bc_shapes, bc_rows.shape[-1])
    head_total = head_total[:3] + (out_total.astype(jnp.float32),) + head_total[3:]
    return (
        outputs_all[None],
        input_grads[None],
        shared_total[0][None],
        head_total[0][None],
        head_total[1][None],
        shared_total[1][None],
        head_total[2][None],
        head_total[4][None],
        head_total[5][None],
        shared_total[2][None],
        shared_total[3][None],
        head_total[6][None],
        head_total[7][None],
        head_total[8][None],
        head_total[9][None],
        head_total[3][None],
    )


def solution(mesh):
    return jax.shard_map(
        on_device,
        mesh=mesh,
        in_specs=(
            P(None, ("seq", "head"), None),
            P(None, ("seq", "head"), None),
            P(None, "seq"),
            P(None, "seq"),
            P("section", None),
            P("section", None, "head"),
            P("section", None, "head"),
            P("section", None, None),
            P("section", None, "head"),
            P("section", None, "head"),
            P("section", "head"),
            P("section", None, None),
            P("section", None),
            P("section", "head"),
            P("section", "head"),
            P("section", "head"),
            P("section", "head"),
            P("section", "head", None),
        ),
        out_specs=(
            P("section", None, ("seq", "head"), None),
            P("section", None, ("seq", "head"), None),
            P("section", None),
            P("section", None, "head"),
            P("section", None, "head"),
            P("section", None, None),
            P("section", None, "head"),
            P("section", None, "head"),
            P("section", "head"),
            P("section", None, None),
            P("section", None),
            P("section", "head"),
            P("section", "head"),
            P("section", "head"),
            P("section", "head"),
            P("section", "head", None),
        ),
        check_vma=False,
    )
```

```python
from functools import partial

import functools
import math

import jax
import jax.numpy as jnp
from jax import lax
from jax.experimental import pallas as pl
from jax.experimental.pallas import tpu as pltpu
from jax.sharding import PartitionSpec as P

DI = 4096
P_SIZE = 64
N = 128
KW = 4
SCAN_BLOCK = 256


MESH = pl.DeviceIdType.MESH


def _tick_valid(offset, sign, count):
    slot = offset + sign * lax.axis_index("section")
    return jnp.logical_and(slot >= 0, slot < count)


def _enter(barrier, h, n):
    @pl.when(h > 0)
    def _():
        pl.semaphore_signal(barrier, 1, device_id={"head": h - 1}, device_id_type=MESH)

    @pl.when(h < n - 1)
    def _():
        pl.semaphore_signal(barrier, 1, device_id={"head": h + 1}, device_id_type=MESH)

    @pl.when(jnp.logical_and(h > 0, h < n - 1))
    def _():
        pl.semaphore_wait(barrier, 2)

    @pl.when(jnp.logical_or(h == 0, h == n - 1))
    def _():
        pl.semaphore_wait(barrier, 1)


def gather_body(n, tick, x_ref, o_ref, land, send_r, send_l, recv):
    h = lax.axis_index("head")
    valid = _tick_valid(*tick)

    @pl.when(valid)
    def _():
        _enter(pltpu.get_barrier_semaphore(), h, n)

        def copy_right(s, k):
            src = x_ref if s == 0 else land.at[k]
            return pltpu.make_async_remote_copy(
                src_ref=src, dst_ref=land.at[k], send_sem=send_r.at[s], recv_sem=recv.at[k],
                device_id={"head": h + 1}, device_id_type=MESH)

        def copy_left(s, k):
            src = x_ref if s == 0 else land.at[k]
            return pltpu.make_async_remote_copy(
                src_ref=src, dst_ref=land.at[k], send_sem=send_l.at[s], recv_sem=recv.at[k],
                device_id={"head": h - 1}, device_id_type=MESH)

        for s in range(n):
            k_r = h - s
            k_l = h + s
            if s >= 1:
                @pl.when(k_r >= 0)
                def _():
                    pltpu.make_async_remote_copy(
                        src_ref=land.at[k_r], dst_ref=land.at[k_r], send_sem=send_r.at[0],
                        recv_sem=recv.at[k_r], device_id={"head": h}, device_id_type=MESH
                    ).wait_recv()

                @pl.when(k_l <= n - 1)
                def _():
                    pltpu.make_async_remote_copy(
                        src_ref=land.at[k_l], dst_ref=land.at[k_l], send_sem=send_l.at[0],
                        recv_sem=recv.at[k_l], device_id={"head": h}, device_id_type=MESH
                    ).wait_recv()
            if s <= n - 2:
                @pl.when(jnp.logical_and(k_r >= 0, h < n - 1))
                def _():
                    copy_right(s, k_r).start()

                @pl.when(jnp.logical_and(k_l <= n - 1, h > 0))
                def _():
                    copy_left(s, k_l).start()
        land[h] = x_ref[...]
        for s in range(n - 1):
            k_r = h - s
            k_l = h + s

            @pl.when(jnp.logical_and(k_r >= 0, h < n - 1))
            def _():
                copy_right(s, k_r).wait_send()

            @pl.when(jnp.logical_and(k_l <= n - 1, h > 0))
            def _():
                copy_left(s, k_l).wait_send()
        o_ref[...] = land[...]

    @pl.when(jnp.logical_not(valid))
    def _():
        o_ref[...] = jnp.zeros(o_ref.shape, o_ref.dtype)


def head_gather(x, tick, cid):
    n = lax.axis_size("head")
    rows, cols = x.shape
    return pl.pallas_call(
        functools.partial(gather_body, n, tick),
        out_shape=jax.ShapeDtypeStruct((n, rows, cols), x.dtype),
        in_specs=[pl.BlockSpec(memory_space=pltpu.VMEM)],
        out_specs=pl.BlockSpec(memory_space=pltpu.VMEM),
        scratch_shapes=[
            pltpu.VMEM((n, rows, cols), x.dtype),
            pltpu.SemaphoreType.DMA((n,)),
            pltpu.SemaphoreType.DMA((n,)),
            pltpu.SemaphoreType.DMA((n,)),
        ],
        compiler_params=pltpu.CompilerParams(collective_id=cid, has_side_effects=True),
    )(x)


def scatter_body(n, tick, p_ref, o_ref, recv_l, recv_r, send_l, send_r, ssem_l, ssem_r, rsem_l, rsem_r):
    h = lax.axis_index("head")
    valid = _tick_valid(*tick)
    link = send_r.dtype

    @pl.when(valid)
    def _():
        _enter(pltpu.get_barrier_semaphore(), h, n)

        def to_right(k):
            return pltpu.make_async_remote_copy(
                src_ref=send_r.at[k], dst_ref=recv_l.at[k], send_sem=ssem_r.at[k],
                recv_sem=rsem_l.at[k], device_id={"head": h + 1}, device_id_type=MESH)

        def to_left(k):
            return pltpu.make_async_remote_copy(
                src_ref=send_l.at[k], dst_ref=recv_r.at[k], send_sem=ssem_l.at[k],
                recv_sem=rsem_r.at[k], device_id={"head": h - 1}, device_id_type=MESH)

        def rightward(s):
            k_r = n - 1 - s

            @pl.when(k_r > h)
            def _():
                @pl.when(h > 0)
                def _():
                    to_right(k_r).wait_recv()
                    send_r[k_r] = (p_ref[k_r] + recv_l[k_r].astype(jnp.float32)).astype(link)

                @pl.when(h == 0)
                def _():
                    send_r[k_r] = p_ref[k_r].astype(link)

                to_right(k_r).start()

        def leftward(s):
            k_l = s

            @pl.when(k_l < h)
            def _():
                @pl.when(h < n - 1)
                def _():
                    to_left(k_l).wait_recv()
                    send_l[k_l] = (p_ref[k_l] + recv_r[k_l].astype(jnp.float32)).astype(link)

                @pl.when(h == n - 1)
                def _():
                    send_l[k_l] = p_ref[k_l].astype(link)

                to_left(k_l).start()

        for s in range(n - 1):

            @pl.when(2 * h < n)
            def _():
                rightward(s)
                leftward(s)

            @pl.when(2 * h >= n)
            def _():
                leftward(s)
                rightward(s)

        total = p_ref[h]

        @pl.when(h > 0)
        def _():
            to_right(h).wait_recv()

        @pl.when(h < n - 1)
        def _():
            to_left(h).wait_recv()

        left_part = jnp.where(h > 0, recv_l[h].astype(jnp.float32), 0.0)
        right_part = jnp.where(h < n - 1, recv_r[h].astype(jnp.float32), 0.0)
        o_ref[...] = (total + left_part + right_part).astype(o_ref.dtype)
        for s in range(n - 1):
            k_r = n - 1 - s
            k_l = s

            @pl.when(k_r > h)
            def _():
                to_right(k_r).wait_send()

            @pl.when(k_l < h)
            def _():
                to_left(k_l).wait_send()

    @pl.when(jnp.logical_not(valid))
    def _():
        o_ref[...] = jnp.zeros(o_ref.shape, o_ref.dtype)


def head_scatter(parts, tick, cid, link=jnp.bfloat16):
    n = lax.axis_size("head")
    _, rows, cols = parts.shape
    return pl.pallas_call(
        functools.partial(scatter_body, n, tick),
        out_shape=jax.ShapeDtypeStruct((rows, cols), jnp.float32),
        in_specs=[pl.BlockSpec(memory_space=pltpu.VMEM)],
        out_specs=pl.BlockSpec(memory_space=pltpu.VMEM),
        scratch_shapes=[
            pltpu.VMEM((n, rows, cols), link),
            pltpu.VMEM((n, rows, cols), link),
            pltpu.VMEM((n, rows, cols), link),
            pltpu.VMEM((n, rows, cols), link),
            pltpu.SemaphoreType.DMA((n,)),
            pltpu.SemaphoreType.DMA((n,)),
            pltpu.SemaphoreType.DMA((n,)),
            pltpu.SemaphoreType.DMA((n,)),
        ],
        compiler_params=pltpu.CompilerParams(collective_id=cid, has_side_effects=True),
    )(parts)


norm_eps = 1e-05
far_below = -1e30
highest = lax.Precision.DEFAULT


def shifted(value, axis, by):
    count = lax.axis_size(axis)
    pairs = [(i, i + by) for i in range(count) if 0 <= i + by < count]
    return lax.ppermute(value, axis, pairs)


def entering(value, axis, combine, identity):
    count, mine = (lax.axis_size(axis), lax.axis_index(axis))
    everything = jax.tree.map(lambda part: lax.all_gather(part, axis), value)
    before = jax.tree.map(
        lambda part, zero: jnp.broadcast_to(jnp.asarray(zero, part.dtype), part.shape),
        value,
        identity,
    )
    for k in range(count - 1):
        reached = k < mine
        new = combine(before, jax.tree.map(lambda part: part[k], everything))
        before = jax.tree.map(lambda a, b: jnp.where(reached, a, b), new, before)
    return before


def entering_2(value, axis, join, neutral):
    count = lax.axis_size(axis)
    place = lax.axis_index(axis)
    ahead = count - 1 - place
    gathered = jax.tree.map(
        lambda a, kind: lax.all_gather(a.astype(kind), axis),
        value,
        jax.tree.map(lambda a: jnp.bfloat16 if a.dtype == jnp.float32 else a.dtype, value),
    )
    state = jax.tree.map(lambda a, e: jnp.zeros_like(a) + jnp.asarray(e, a.dtype), value, neutral)
    for lap in range(count - 1):
        source = count - 1 - lap
        new = join(
            state,
            jax.tree.map(lambda a, own: a[source].astype(own.dtype), gathered, value),
        )
        active = lap < ahead
        state = jax.tree.map(lambda a, b: jnp.where(active, a, b), new, state)
    return state


def rms_scale(values):
    return lax.rsqrt(jnp.mean(values * values, axis=-1, keepdims=True) + norm_eps)


def silu_slope(values):
    logistic = jax.nn.sigmoid(values)
    return logistic * (1.0 + values * (1.0 - logistic))


def causal_conv(extended, marks_ext, weight, conv_bias):
    tap_count = weight.shape[0]
    length = extended.shape[0] - tap_count + 1
    counts = jnp.cumsum(marks_ext)
    conv_sum = jnp.zeros((length, extended.shape[1]), jnp.float32) + conv_bias
    for tap_index in range(tap_count):
        linked = (counts[tap_count - 1 :] == counts[tap_index : tap_index + length]).astype(
            jnp.float32
        )
        conv_sum = (
            conv_sum
            + linked[:, None] * weight[tap_index] * extended[tap_index : tap_index + length]
        )
    return conv_sum


def prepare(extended, dt_pre, marks_ext, alive_mask, conv_weight, conv_bias, dt_bias, a_log):
    inner_width = dt_pre.shape[1] * P_SIZE
    activated = jax.nn.silu(causal_conv(extended, marks_ext, conv_weight, conv_bias))
    inner_act = activated[:, :inner_width] * alive_mask[:, None]
    b_mat = activated[:, inner_width : inner_width + N]
    c_mat = activated[:, inner_width + N :]
    step_size = jax.nn.softplus(dt_pre + dt_bias) * alive_mask[:, None]
    log_decay = -step_size * jnp.exp(a_log)
    return (inner_act, step_size, log_decay, b_mat, c_mat)


def block_terms(inner_act, step_size, log_decay, b_mat, start_marks):
    blocks = inner_act.shape[0] // SCAN_BLOCK
    head_count = step_size.shape[1]
    x_blocks = inner_act.reshape(blocks, SCAN_BLOCK, head_count, P_SIZE)
    dt_blocks = step_size.reshape(blocks, SCAN_BLOCK, head_count)
    cum_decay = jnp.cumsum(log_decay.reshape(blocks, SCAN_BLOCK, head_count), axis=1)
    mark_count = jnp.cumsum(start_marks.reshape(blocks, SCAN_BLOCK), axis=1)
    b_blocks = b_mat.reshape(blocks, SCAN_BLOCK, N)
    last_cum = cum_decay[:, -1]
    last_mark = mark_count[:, -1]
    same_end = (mark_count == last_mark[:, None]).astype(jnp.float32)
    end_weight = jnp.exp(last_cum[:, None, :] - cum_decay) * same_end[:, :, None] * dt_blocks
    block_states = jnp.einsum(
        "cjh,cjhp,cjn->chpn", end_weight, x_blocks, b_blocks, precision=highest
    )
    block_decay = jnp.exp(last_cum) * (last_mark == 0).astype(jnp.float32)[:, None]
    return (block_decay, block_states, cum_decay, mark_count, x_blocks, dt_blocks)


def compose_blocks(block_decay, block_states, start_state):
    chain_state = start_state
    incoming = []
    for block_index in range(block_decay.shape[0]):
        incoming.append(chain_state)
        chain_state = (
            block_decay[block_index][:, None, None] * chain_state + block_states[block_index]
        )
    return (chain_state, jnp.stack(incoming))


def block_output(block_parts, b_mat, c_mat, skip, incoming):
    block_decay, block_states, cum_decay, mark_count, x_blocks, dt_blocks = block_parts
    blocks = cum_decay.shape[0]
    head_count = cum_decay.shape[2]
    b_blocks = b_mat.reshape(blocks, SCAN_BLOCK, N)
    c_blocks = c_mat.reshape(blocks, SCAN_BLOCK, N)
    inner_prod = jnp.einsum("cin,cjn->cij", c_blocks, b_blocks, precision=highest)
    arange_pos = jnp.arange(SCAN_BLOCK)
    linked = (arange_pos[:, None] >= arange_pos[None, :])[None] & (
        mark_count[:, :, None] == mark_count[:, None, :]
    )
    spread = jnp.where(
        linked[..., None], cum_decay[:, :, None, :] - cum_decay[:, None, :, :], far_below
    )
    weights = jnp.exp(spread) * inner_prod[..., None] * dt_blocks[:, None, :, :]
    y_intra = jnp.einsum(
        "cijh,cjhp->cihp", weights, x_blocks, precision=lax.Precision.DEFAULT
    )
    carry_in = jnp.exp(cum_decay) * (mark_count == 0).astype(jnp.float32)[:, :, None]
    y_inter = (
        jnp.einsum("cin,chpn->cihp", c_blocks, incoming, precision=highest) * carry_in[..., None]
    )
    mixed_out = y_intra + y_inter + skip[None, None, :, None] * x_blocks
    return mixed_out.reshape(blocks * SCAN_BLOCK, head_count * P_SIZE)


def local_front(marks_ext, alive_mask, extended, dt_pre, conv_weight, conv_bias, dt_bias, a_log):
    inner_act, step_size, log_decay, b_mat, c_mat = prepare(
        extended, dt_pre, marks_ext, alive_mask, conv_weight, conv_bias, dt_bias, a_log
    )
    block_parts = block_terms(inner_act, step_size, log_decay, b_mat, marks_ext[KW - 1 :])
    zero_state = jnp.zeros(block_parts[1].shape[1:], jnp.float32)
    total_state, _ = compose_blocks(block_parts[0], block_parts[1], zero_state)
    total_decay = jnp.prod(block_parts[0], axis=0)
    return (block_parts, b_mat, c_mat, total_decay, total_state)


def local_rear(block_parts, b_mat, c_mat, skip, start_state):
    _, incoming = compose_blocks(block_parts[0], block_parts[1], start_state)
    return block_output(block_parts, b_mat, c_mat, skip, incoming)


def local_pass(
    marks_ext,
    alive_mask,
    extended,
    dt_pre,
    conv_weight,
    conv_bias,
    dt_bias,
    a_log,
    skip,
    start_state,
):
    block_parts, b_mat, c_mat, total_decay, total_state = local_front(
        marks_ext, alive_mask, extended, dt_pre, conv_weight, conv_bias, dt_bias, a_log
    )
    return (local_rear(block_parts, b_mat, c_mat, skip, start_state), total_decay, total_state)


def chain_combine(earlier, later):
    return (earlier[0] * later[0], later[0][:, None, None] * earlier[1] + later[1])


def extend(pre_conv, start_marks, edge_rows, edge_marks):
    extended = jnp.concatenate([edge_rows, pre_conv], axis=0)
    marks_ext = jnp.concatenate([edge_marks.astype(jnp.int32), start_marks], axis=0)
    return (extended, marks_ext)


def mixer_forward(stream, start_marks, alive_mask, layer_weights, tick, ids):
    (
        norm_gain,
        w_main,
        w_low,
        w_bc,
        conv_weight,
        conv_bias,
        dt_bias,
        a_log,
        skip,
        gate_gain,
        w_out,
    ) = layer_weights
    inner_width = w_out.shape[0]
    normed = (stream * rms_scale(stream) * norm_gain).astype(jnp.bfloat16)
    gathered = head_gather(normed, tick, ids[0])
    gathered = gathered.reshape(-1, gathered.shape[-1])
    projected = jnp.dot(gathered, w_main, preferred_element_type=jnp.float32)
    gate_pre = projected[:, :inner_width]
    pre_conv = projected[:, inner_width : 2 * inner_width + 2 * N]
    dt_pre = projected[:, 2 * inner_width + 2 * N :]
    marks_float = start_marks.astype(jnp.float32)
    tail_from = pre_conv.shape[0] - KW + 1
    edge_parts = shifted((pre_conv[tail_from:], marks_float[tail_from:]), "seq", 1)
    extended, marks_ext = extend(pre_conv, start_marks, edge_parts[0], edge_parts[1])
    front_fn = partial(local_front, marks_ext, alive_mask)
    front_out, front_pull = jax.vjp(
        front_fn, extended, dt_pre, conv_weight, conv_bias, dt_bias, a_log
    )
    block_parts, b_mat, c_mat, total_decay, total_state = front_out
    neutral = (jnp.ones_like(total_decay), jnp.zeros_like(total_state))
    prefix = entering((total_decay, total_state), "seq", chain_combine, neutral)
    start_state = prefix[1]
    mixed_out, rear_pull = jax.vjp(local_rear, block_parts, b_mat, c_mat, skip, start_state)
    silu_gate = jax.nn.silu(gate_pre)
    gated_mix = mixed_out * silu_gate
    square_total = lax.psum(jnp.sum(gated_mix * gated_mix, axis=-1), "head")
    scale_out = lax.rsqrt(square_total / DI + norm_eps)
    normed_out = (gated_mix * scale_out[:, None] * gate_gain).astype(jnp.bfloat16)
    head_count = lax.axis_size("head")
    branch = head_scatter(
        jnp.dot(normed_out, w_out, preferred_element_type=jnp.float32).reshape(
            head_count, -1, w_out.shape[1]
        ),
        tick,
        ids[1],
    )
    saved = (
        stream,
        gathered,
        gate_pre,
        mixed_out,
        silu_gate,
        gated_mix,
        scale_out,
        normed_out,
        total_decay,
        start_state,
        front_pull,
        rear_pull,
    )
    return stream + branch, saved


def mixer_backward(grad_next, layer_weights, saved, mask_value, tick, ids, hook=None):
    (
        norm_gain,
        w_main,
        w_low,
        w_bc,
        conv_weight,
        conv_bias,
        dt_bias,
        a_log,
        skip,
        gate_gain,
        w_out,
    ) = layer_weights
    (
        stream,
        gathered,
        gate_pre,
        mixed_out,
        silu_gate,
        gated_mix,
        scale_out,
        normed_out,
        total_decay,
        start_state,
        front_pull,
        rear_pull,
    ) = saved
    inner_width = w_out.shape[0]
    grad_branch = grad_next.astype(jnp.bfloat16)
    shard_rows = head_gather(grad_branch, tick, ids[0])
    shard_rows = shard_rows.reshape(-1, shard_rows.shape[-1])
    g_w_out = lax.dot_general(
        normed_out, shard_rows, (((0,), (0,)), ((), ())), preferred_element_type=jnp.float32
    ) * mask_value
    grad_normed = lax.dot_general(
        shard_rows, w_out, (((1,), (1,)), ((), ())), preferred_element_type=jnp.float32
    )
    weighted = grad_normed * gate_gain
    g_gate_gain = jnp.sum(grad_normed * gated_mix * scale_out[:, None], axis=0)
    cross_sum = lax.psum(jnp.sum(weighted * gated_mix, axis=-1), "head")
    grad_gated = (
        scale_out[:, None] * weighted - gated_mix * (scale_out**3 * cross_sum / DI)[:, None]
    )
    grad_mixed = grad_gated * silu_gate
    grad_gate = (grad_gated * mixed_out * silu_slope(gate_pre)).astype(jnp.bfloat16)
    g_parts, g_b_mat, g_c_mat, g_skip, g_start = rear_pull(grad_mixed)
    neutral = (jnp.ones_like(total_decay), jnp.zeros_like(g_start))
    suffix = entering_2((total_decay, g_start), "seq", chain_combine, neutral)
    after_state = suffix[1]
    grad_decay = jnp.sum(after_state * start_state, axis=(1, 2))
    grad_ext, grad_dt_pre, g_conv_w, g_conv_b, g_dt_bias, g_a_log = front_pull(
        (g_parts, g_b_mat, g_c_mat, grad_decay, after_state)
    )
    returned = shifted(grad_ext[: KW - 1], "seq", -1)
    grad_pre = grad_ext[KW - 1 :]
    tail_from = grad_pre.shape[0] - KW + 1
    grad_pre = jnp.concatenate([grad_pre[:tail_from], grad_pre[tail_from:] + returned], axis=0)
    grad_inner = grad_pre[:, :inner_width].astype(jnp.bfloat16)
    grad_bc = grad_pre[:, inner_width:]
    grad_low = jnp.concatenate([grad_gate, grad_inner, grad_dt_pre.astype(jnp.bfloat16)], axis=1)
    w_bc_float = w_bc.astype(jnp.float32)
    g_w_bc = lax.dot_general(
        gathered,
        grad_bc.astype(jnp.bfloat16),
        (((0,), (0,)), ((), ())),
        preferred_element_type=jnp.float32,
    )
    main_term = lax.dot_general(
        grad_low, w_low, (((1,), (1,)), ((), ())), preferred_element_type=jnp.float32
    )
    side_term = lax.dot_general(
        grad_bc.astype(jnp.bfloat16),
        w_bc,
        (((1,), (1,)), ((), ())),
        preferred_element_type=jnp.float32,
    )
    head_count = lax.axis_size("head")
    lead = 0.0
    if hook is not None:
        lead = hook((g_w_bc, g_conv_w[:, inner_width:], g_conv_b[inner_width:]))
    grad_normed_in = head_scatter(
        (main_term + side_term + lead).reshape(head_count, -1, main_term.shape[1]), tick, ids[1]
    )
    scale_in = rms_scale(stream)
    g_norm_gain = jnp.sum(grad_normed_in * stream * scale_in, axis=0)
    weighted_in = grad_normed_in * norm_gain
    grad_stream = (
        grad_next
        + scale_in * weighted_in
        - stream * scale_in**3 * jnp.mean(weighted_in * stream, axis=-1, keepdims=True)
    )
    head_part = (
        g_conv_w[:, :inner_width],
        g_conv_b[:inner_width],
        g_dt_bias,
        g_a_log,
        g_skip,
        g_gate_gain,
    )
    shared_part = (g_norm_gain, g_w_bc, g_conv_w[:, inner_width:], g_conv_b[inner_width:])
    return (grad_stream, head_part, shared_part, g_w_out, (gathered, grad_low))


def pack_rows(members, width, multiple):
    rows = jnp.concatenate([member.reshape(-1, width) for member in members], axis=0)
    return jnp.pad(rows, ((0, -rows.shape[0] % multiple), (0, 0)))


def unpack_rows(rows, shapes, width):
    pieces = []
    start = 0
    for shape in shapes:
        count = math.prod(shape) // width
        pieces.append(rows[start : start + count].reshape(shape))
        start += count
    return tuple(pieces)


def reduce_grads(head_part, norm_part, bc_part, tick_count):
    bc_all = lax.all_gather(bc_part.astype(jnp.bfloat16), "seq")
    bc_sum = bc_all[0].astype(jnp.float32)
    for index in range(1, bc_all.shape[0]):
        bc_sum = bc_sum + bc_all[index].astype(jnp.float32)
    anchor = bc_all[0, 0, 0].astype(jnp.float32) * 0.0
    summed = lax.psum(
        tuple(member.astype(jnp.bfloat16) for member in (head_part[0] + anchor,) + head_part[1:3]),
        "seq",
    )
    head_sum = tuple(member.astype(jnp.float32) for member in summed) + tuple(
        lax.psum(member.astype(jnp.bfloat16), "seq").astype(jnp.float32)
        for member in head_part[3:]
    )
    bc_rows = head_gather(bc_sum, (0, 0, 1), 4 * tick_count + 1)
    norm_sum = lax.psum(norm_part, ("seq", "head"))
    return (head_sum, norm_sum, bc_rows.reshape(-1, bc_rows.shape[-1]))


def store_slot(buffer, value, slot_index, is_valid):
    current = lax.dynamic_index_in_dim(buffer, slot_index, 0, False)
    return lax.dynamic_update_index_in_dim(
        buffer, jnp.where(is_valid, value, current), slot_index, 0
    )


def on_device(
    inputs,
    cotangent,
    starts,
    live,
    norm_gain,
    w_gate,
    w_in,
    w_bc,
    w_dt,
    conv_x,
    conv_x_bias,
    conv_bc,
    conv_bc_bias,
    dt_bias,
    a_log,
    skip,
    gate_gain,
    w_out,
):
    section_count = lax.axis_size("section")
    section_index = lax.axis_index("section")
    micro_count = inputs.shape[0]
    tick_count = micro_count + section_count - 1
    w_main = jnp.concatenate([w_gate[0], w_in[0], w_bc[0], w_dt[0]], axis=1)
    w_low = jnp.concatenate([w_gate[0], w_in[0], w_dt[0]], axis=1)
    conv_weight = jnp.concatenate([conv_x[0], conv_bc[0]], axis=1).astype(jnp.float32)
    conv_bias = jnp.concatenate([conv_x_bias[0], conv_bc_bias[0]], axis=0)
    layer_weights = (
        norm_gain[0],
        w_main,
        w_low,
        w_bc[0],
        conv_weight,
        conv_bias,
        dt_bias[0],
        a_log[0],
        skip[0],
        gate_gain[0],
        w_out[0],
    )
    row_shape = inputs.shape[1:]
    outputs_all = jnp.zeros((micro_count,) + row_shape, jnp.float32)
    arrived = jnp.zeros(row_shape, jnp.float32)
    ticks = []
    for tick_index in range(tick_count):
        slot_index = tick_index - section_index
        is_valid = (slot_index >= 0) & (slot_index < micro_count)
        clipped = jnp.clip(slot_index, 0, micro_count - 1)
        fresh_rows = lax.dynamic_index_in_dim(inputs, clipped, 0, False).astype(jnp.float32)
        stream = jnp.where(section_index == 0, fresh_rows, arrived)
        start_marks = lax.dynamic_index_in_dim(starts, clipped, 0, False)
        alive_mask = lax.dynamic_index_in_dim(live, clipped, 0, False).astype(jnp.float32)
        result, saved = mixer_forward(
            stream,
            start_marks,
            alive_mask,
            layer_weights,
            (tick_index, -1, micro_count),
            (tick_index, tick_count + tick_index),
        )
        outputs_all = store_slot(outputs_all, result, clipped, is_valid)
        ticks.append((clipped, is_valid, saved))
        if tick_index + 1 < tick_count:
            arrived = shifted(result, "section", 1)
    back_arrived = jnp.zeros(row_shape, jnp.float32)
    input_grads = jnp.zeros((micro_count,) + row_shape, jnp.float32)
    head_count = lax.axis_size("head")
    bc_box = []
    low_pairs = []
    head_total = ()
    shared_total = ()
    for tick_index in range(tick_count):
        clipped, is_valid, saved = ticks[tick_count - 1 - tick_index]
        outer_grad = lax.dynamic_index_in_dim(cotangent, clipped, 0, False).astype(jnp.float32)
        grad_next = jnp.where(section_index == section_count - 1, outer_grad, back_arrived)
        mask_value = is_valid.astype(jnp.float32)
        hook = None
        if tick_index + 1 == tick_count:

            def hook(bc_local, mask_value=mask_value, earlier=shared_total):
                totals = tuple(
                    (prev + member * mask_value) if earlier else member * mask_value
                    for prev, member in zip(earlier[1:] or bc_local, bc_local)
                )
                rows = pack_rows(totals, totals[0].shape[-1], 8 * head_count)
                part = head_scatter(
                    rows.reshape(head_count, -1, rows.shape[-1]), (0, 0, 1), 4 * tick_count
                )
                bc_box.append((part, [member.shape for member in totals]))
                return part[0, 0] * 0.0

        grad_stream, head_part, shared_part, out_part, low_pair = mixer_backward(
            grad_next,
            layer_weights,
            saved,
            mask_value,
            (tick_count - 1 - tick_index, -1, micro_count),
            (2 * tick_count + tick_index, 3 * tick_count + tick_index),
            hook,
        )
        if tick_index == 0:
            out_total = out_part
        else:
            out_total = out_total + out_part
        if tick_index + 1 == tick_count:
            out_total = lax.psum(out_total.astype(jnp.bfloat16), "seq")
        low_pairs.append((low_pair[0], low_pair[1] * is_valid.astype(low_pair[1].dtype)))
        head_part = tuple((member * mask_value for member in head_part))
        shared_part = tuple((member * mask_value for member in shared_part))
        if tick_index == 0:
            head_total = head_part
            shared_total = shared_part
        else:
            head_total = tuple((former + latter for former, latter in zip(head_total, head_part)))
            shared_total = tuple(
                (former + latter for former, latter in zip(shared_total, shared_part))
            )
        input_grads = store_slot(input_grads, grad_stream, clipped, is_valid)
        if tick_index + 1 < tick_count:
            back_arrived = shifted(grad_stream.astype(jnp.bfloat16), "section", -1).astype(
                grad_stream.dtype
            )
    inner_width = w_out.shape[1]
    g_low = lax.dot_general(
        jnp.concatenate([pair[0] for pair in low_pairs], axis=0),
        jnp.concatenate([pair[1] for pair in low_pairs], axis=0),
        (((0,), (0,)), ((), ())),
        preferred_element_type=jnp.float32,
    )
    anchor = out_total[0, 0].astype(jnp.float32) * 0.0
    head_total = (
        g_low[:, :inner_width] + anchor,
        g_low[:, inner_width : 2 * inner_width],
        g_low[:, 2 * inner_width :],
    ) + head_total
    bc_part, bc_shapes = bc_box[0]
    bc_part = bc_part + anchor
    head_total, norm_sum, bc_rows = reduce_grads(head_total, shared_total[0], bc_part, tick_count)
    shared_total = (norm_sum,) + unpack_rows(bc_rows, bc_shapes, bc_rows.shape[-1])
    head_total = head_total[:3] + (out_total.astype(jnp.float32),) + head_total[3:]
    return (
        outputs_all[None],
        input_grads[None],
        shared_total[0][None],
        head_total[0][None],
        head_total[1][None],
        shared_total[1][None],
        head_total[2][None],
        head_total[4][None],
        head_total[5][None],
        shared_total[2][None],
        shared_total[3][None],
        head_total[6][None],
        head_total[7][None],
        head_total[8][None],
        head_total[9][None],
        head_total[3][None],
    )


def solution(mesh):
    return jax.shard_map(
        on_device,
        mesh=mesh,
        in_specs=(
            P(None, ("seq", "head"), None),
            P(None, ("seq", "head"), None),
            P(None, "seq"),
            P(None, "seq"),
            P("section", None),
            P("section", None, "head"),
            P("section", None, "head"),
            P("section", None, None),
            P("section", None, "head"),
            P("section", None, "head"),
            P("section", "head"),
            P("section", None, None),
            P("section", None),
            P("section", "head"),
            P("section", "head"),
            P("section", "head"),
            P("section", "head"),
            P("section", "head", None),
        ),
        out_specs=(
            P("section", None, ("seq", "head"), None),
            P("section", None, ("seq", "head"), None),
            P("section", None),
            P("section", None, "head"),
            P("section", None, "head"),
            P("section", None, None),
            P("section", None, "head"),
            P("section", None, "head"),
            P("section", "head"),
            P("section", None, None),
            P("section", None),
            P("section", "head"),
            P("section", "head"),
            P("section", "head"),
            P("section", "head"),
            P("section", "head", None),
        ),
        check_vma=False,
    )
```
